32 devices in a mesh: dp: 4 (over y, x), ctx: 2 (over core), tensor: 4 (over z).
Axes of the slice: x: 2, y: 2, z: 4, core: 2. Of those that a mesh axis runs over, the one named last changes fastest.
Arguments:
- inputs: bfloat16 [4, 1024, 2048], P('dp', 'ctx'), may hold values from -6 to 6
- segment_ids: int32 [4, 1024], P('dp', 'ctx'), may hold values from -1 to 1022, as said below
- attention_gain: float32 [2048], replicated, may hold values from 0.5 to 1.5
- query_weight: bfloat16 [2048, 2048], P(None, 'tensor'), may hold values from -0.125 to 0.125
- key_weight: bfloat16 [2048, 256], P(None, 'tensor'), may hold values from -0.125 to 0.125
- value_weight: bfloat16 [2048, 256], P(None, 'tensor'), may hold values from -0.125 to 0.125
- out_weight: bfloat16 [2048, 2048], P('tensor'), may hold values from -0.75 to 0.75
- feedforward_gain: float32 [2048], replicated, may hold values from 0.5 to 1.5
- gate_weight: bfloat16 [2048, 5632], P(None, 'tensor'), may hold values from -0.125 to 0.125
- up_weight: bfloat16 [2048, 5632], P(None, 'tensor'), may hold values from -0.125 to 0.125
- down_weight: bfloat16 [5632, 2048], P('tensor'), may hold values from -0.078125 to 0.078125
- cotangent: bfloat16 [4, 1024, 2048], P('dp', 'ctx'), may hold values from -6 to 6
Outputs:
- layer_out: bfloat16 [4, 1024, 2048], P('dp', 'ctx')
- grad_inputs: bfloat16 [4, 1024, 2048], P('dp', 'ctx')
- grad_attention_gain: float32 [2048], P(('dp', 'ctx'))
- grad_query_weight: float32 [2048, 2048], P(('dp', 'ctx'), 'tensor')
- grad_key_weight: float32 [2048, 256], P(('dp', 'ctx'), 'tensor')
- grad_value_weight: float32 [2048, 256], P(('dp', 'ctx'), 'tensor')
- grad_out_weight: float32 [2048, 2048], P('tensor', ('dp', 'ctx'))
- grad_feedforward_gain: float32 [2048], P(('dp', 'ctx'))
- grad_gate_weight: float32 [2048, 5632], P(('dp', 'ctx'), 'tensor')
- grad_up_weight: float32 [2048, 5632], P(('dp', 'ctx'), 'tensor')
- grad_down_weight: float32 [5632, 2048], P('tensor', ('dp', 'ctx'))
The draws below stay inside these ranges and needn't reach their ends.
Inputs may be any that keep to these rules, and one draw needn't show every extreme that they name: `segment_ids`: along each sequence the numbers start at 0 and rise by at most one from token to token over the documents; the last 1 to 128 tokens of every sequence are padding, marked -1. In every draw the first sequence holds documents of one token each and a single padding token.
All inputs are finite; a program needn't handle non-finite values.
Results may differ from the reference program's by a relative error of at most 0.018.
Values may be sent and summed in bfloat16 or wider, within the bound.
A program may use at most 192 MiB of HBM per device.

```python
import math
import jax
import jax.numpy as jnp
from jax import lax

D = 2048
HEADS = 32
KV_HEADS = 4
HEAD_DIM = 64
FF = 5632
SEQ_LEN = 1024
SEQS = 4


def draw_segment_ids(key, part):
    rate_key, start_key, pad_key = jax.random.split(key, 3)
    row_index = jnp.arange(SEQS, dtype=jnp.int32)[:, None]
    exponent = jax.random.randint(rate_key, (SEQS, 1), 0, 6)
    mean_length = jnp.maximum(jnp.right_shift(jnp.full((SEQS, 1), SEQ_LEN, jnp.int32), exponent), 2)
    mean_length = jnp.where(row_index == 0, 1, mean_length).astype(jnp.int32)
    token_index = jnp.arange(SEQ_LEN, dtype=jnp.int32)[None, :]
    starts = (jax.random.randint(start_key, (SEQS, SEQ_LEN), 0, mean_length) == 0) | (token_index == 0)
    numbers = jnp.cumsum(starts.astype(jnp.int32), axis=1) - 1
    padding = jax.random.randint(pad_key, (SEQS, 1), 1, SEQ_LEN // 8 + 1)
    padding = jnp.where(row_index == 0, 1, padding).astype(jnp.int32)
    return jnp.where(token_index >= SEQ_LEN - padding, -1, numbers).astype(jnp.int32)


def steps_of(rng, dims, cuts, least, largest):
    level, own = 1.0, jax.random.fold_in(rng, 6)
    for position, shards_of in cuts:
        heights = jnp.exp(jax.random.uniform(jax.random.fold_in(own, position), (shards_of,), jnp.float32, least / len(cuts), largest / len(cuts)))
        level = level * jnp.repeat(heights, dims[position] // shards_of).reshape([-1 if axis == position else 1 for axis in range(len(dims))])
    return level


def scatter_about(stream_key, dims, deviation, reach, cuts=(), kind=jnp.bfloat16):
    drawn = jax.random.normal(stream_key, dims, jnp.float32) * deviation
    if len(cuts) > 0:
        drawn = steps_of(stream_key, dims, cuts, -0.22, 0.18) * drawn
    return jnp.clip(drawn, min=-reach, max=reach).astype(kind)


def setup_inputs(seed: int = 0) -> dict:
    key_of = jax.random.split(jax.random.key(seed), 13)
    inputs = scatter_about(key_of[0], (SEQS, SEQ_LEN, D), 1.0, 6.0, ((0, 4), (1, 2)))
    segment_ids = draw_segment_ids(jax.random.fold_in(key_of[12], 71), 0)
    attention_gain = jnp.clip(1.0 + 0.1 * jax.random.normal(key_of[2], (D,), jnp.float32), 0.5, 1.5)
    query_weight = scatter_about(key_of[3], (D, HEADS * HEAD_DIM), D ** -0.5, 0.125, ((1, 4),))
    key_weight = scatter_about(key_of[4], (D, KV_HEADS * HEAD_DIM), D ** -0.5, 0.125, ((1, 4),))
    value_weight = scatter_about(key_of[5], (D, KV_HEADS * HEAD_DIM), D ** -0.5, 0.125, ((1, 4),))
    out_weight = scatter_about(key_of[6], (HEADS * HEAD_DIM, D), (HEADS * HEAD_DIM // 32) ** -0.5, 0.75, ((0, 4),))
    feedforward_gain = jnp.clip(1.0 + 0.1 * jax.random.normal(key_of[7], (D,), jnp.float32), 0.5, 1.5)
    gate_weight = scatter_about(key_of[8], (D, FF), D ** -0.5, 0.125, ((1, 4),))
    up_weight = scatter_about(key_of[9], (D, FF), D ** -0.5, 0.125, ((1, 4),))
    down_weight = scatter_about(key_of[10], (FF, D), FF ** -0.5, 0.078125, ((0, 4),))
    cotangent = scatter_about(key_of[11], (SEQS, SEQ_LEN, D), 1.0, 6.0, ((0, 4), (1, 2)))
    return dict(inputs=inputs, segment_ids=segment_ids, attention_gain=attention_gain, query_weight=query_weight, key_weight=key_weight, value_weight=value_weight, out_weight=out_weight, feedforward_gain=feedforward_gain, gate_weight=gate_weight, up_weight=up_weight, down_weight=down_weight, cotangent=cotangent)


epsilon = 1e-05
rope_base = 10000.0
masked_score = -1e+30
highest = lax.Precision.HIGHEST

@jax.custom_vjp
def low(v):
    return lax.optimization_barrier(v.astype(jnp.bfloat16)).astype(jnp.float32)

@jax.custom_vjp
def low_back(v):
    return v

def low_keep(v):
    return (low(v), None)

def low_pass(kept, grad):
    return (grad,)

def back_keep(v):
    return (v, None)

def back_low(kept, grad):
    return (low(grad),)
low.defvjp(low_keep, low_pass)
low_back.defvjp(back_keep, back_low)

def matmul_high(left, right):
    return jnp.dot(left, right, precision=highest, preferred_element_type=jnp.float32)

def positions_of(segment):
    token_index = jnp.arange(segment.shape[-1], dtype=jnp.int32)
    previous = jnp.concatenate([segment[..., :1] - 1, segment[..., :-1]], axis=-1)
    starts = jnp.where(segment != previous, token_index, 0).astype(jnp.int32)
    return (token_index - lax.cummax(starts, axis=segment.ndim - 1)).astype(jnp.int32)

def rotary_tables(positions):
    half_dim = HEAD_DIM // 2
    frequency = rope_base ** (-2.0 * jnp.arange(half_dim, dtype=jnp.float32) / HEAD_DIM)
    angles = positions.astype(jnp.float32)[..., None] * frequency
    return (jnp.cos(angles), jnp.sin(angles))

def rotate(values, cosine, sine_table):
    half_dim = values.shape[-1] // 2
    first = values[..., :half_dim]
    second = values[..., half_dim:]
    return jnp.concatenate([first * cosine - second * sine_table, second * cosine + first * sine_table], axis=-1)

def visible(query_seg, key_seg, first_row):
    query_pos = first_row + jnp.arange(query_seg.shape[0], dtype=jnp.int32)
    key_pos = jnp.arange(key_seg.shape[0], dtype=jnp.int32)
    same_doc = query_seg[:, None] == key_seg[None, :]
    causal = key_pos[None, :] <= query_pos[:, None]
    usable = (key_seg[None, :] >= 0) | (key_pos[None, :] == query_pos[:, None])
    return same_doc & causal & usable

def rms_norm(values, gain):
    inverse = lax.rsqrt(lax.optimization_barrier(jnp.mean(values * values, axis=-1, keepdims=True)) + epsilon)
    return values * inverse * gain

def block_forward(segment, hidden, attention_gain, query_weight, key_weight, value_weight, out_weight, feedforward_gain, gate_weight, up_weight, down_weight):
    length = hidden.shape[0]
    group_size = HEADS // KV_HEADS
    score_scale = 1.0 / math.sqrt(HEAD_DIM)
    cosine, sine_table = rotary_tables(positions_of(segment))
    cosine = cosine[:, None, :]
    sine_table = sine_table[:, None, :]
    normed = low(rms_norm(hidden, attention_gain))
    query_rows = low(rotate(low_back(matmul_high(normed, query_weight)).reshape(length, HEADS, HEAD_DIM), cosine, sine_table))
    key_rows = low(rotate(low_back(matmul_high(normed, key_weight)).reshape(length, KV_HEADS, HEAD_DIM), cosine, sine_table))
    value_rows = low(low_back(matmul_high(normed, value_weight))).reshape(length, KV_HEADS, HEAD_DIM)
    allowed = visible(segment, segment, 0)
    stacked = query_rows.reshape(length, KV_HEADS, group_size, HEAD_DIM).transpose(1, 2, 0, 3)

    def head_block(block_items):
        query_block, key_block, value_block = block_items
        raw_scores = low_back(jnp.einsum('gqd,kd->gqk', query_block, key_block, precision=highest))
        scores = jnp.where(allowed[None], raw_scores * score_scale, masked_score)
        attn_probs = jax.nn.softmax(scores, axis=-1)
        return jnp.einsum('gqk,kd->gqd', low(attn_probs), value_block, precision=highest)
    mixed_heads = lax.map(jax.checkpoint(head_block), (stacked, key_rows.transpose(1, 0, 2), value_rows.transpose(1, 0, 2)))
    mixed_heads = mixed_heads.transpose(2, 0, 1, 3).reshape(length, HEADS * HEAD_DIM)
    attended = low_back(matmul_high(low(low_back(mixed_heads)), out_weight))
    middle = hidden + attended
    normed_two = low(rms_norm(middle, feedforward_gain))
    gate_pre = low_back(matmul_high(normed_two, gate_weight))
    up_pre = low_back(matmul_high(normed_two, up_weight))
    inner_act = low(jax.nn.silu(gate_pre) * up_pre)
    return middle + low_back(matmul_high(inner_act, down_weight))

def reference(inputs, segment_ids, attention_gain, query_weight, key_weight, value_weight, out_weight, feedforward_gain, gate_weight, up_weight, down_weight, cotangent):
    float_weights = (attention_gain.astype(jnp.float32), query_weight.astype(jnp.float32), key_weight.astype(jnp.float32), value_weight.astype(jnp.float32), out_weight.astype(jnp.float32), feedforward_gain.astype(jnp.float32), gate_weight.astype(jnp.float32), up_weight.astype(jnp.float32), down_weight.astype(jnp.float32))

    def one_sequence(running, sequence):
        segment, hidden, upstream = sequence

        def forward(hidden_in, *weights):
            return block_forward(segment, hidden_in, *weights)
        result, pullback = jax.vjp(forward, hidden.astype(jnp.float32), *float_weights)
        gradients = pullback(upstream.astype(jnp.float32))
        running = tuple((total_part + gradient for total_part, gradient in zip(running, gradients[1:])))
        return (running, (result.astype(jnp.bfloat16), gradients[0].astype(jnp.bfloat16)))
    zero_sums = tuple((jnp.zeros(weight.shape, jnp.float32) for weight in float_weights))
    totals, (layer_out, grad_inputs) = lax.scan(one_sequence, zero_sums, (segment_ids, inputs, cotangent))
    return (layer_out, grad_inputs, totals[0], totals[1], totals[2], totals[3], totals[4], totals[5], totals[6], totals[7], totals[8])
```

```python
import functools
import math

import jax
import jax.numpy as jnp
from jax import lax
from jax.experimental import pallas as pl
from jax.experimental.pallas import tpu as pltpu
from jax.sharding import PartitionSpec as P

HEAD_DIM = 64


epsilon = 1e-05
rope_base = 10000.0
masked_score = -1e30


def positions_of(segment):
    token_index = jnp.arange(segment.shape[-1], dtype=jnp.int32)
    previous = jnp.concatenate([segment[..., :1] - 1, segment[..., :-1]], axis=-1)
    starts = jnp.where(segment != previous, token_index, 0)
    earlier = token_index[None, :] <= token_index[:, None]
    run_start = jnp.max(jnp.where(earlier, starts[..., None, :], 0), axis=-1)
    return token_index - run_start


MESH = pl.DeviceIdType.MESH
CHUNK = 32
MIB = 1 << 20


def greet_line(line_size):
    here = lax.axis_index("tensor")
    barrier = pltpu.get_barrier_semaphore()

    @pl.when(here > 0)
    def _():
        pl.semaphore_signal(barrier, inc=1, device_id={"tensor": here - 1}, device_id_type=MESH)

    @pl.when(here < line_size - 1)
    def _():
        pl.semaphore_signal(barrier, inc=1, device_id={"tensor": here + 1}, device_id_type=MESH)

    peers = jnp.where(here > 0, 1, 0) + jnp.where(here < line_size - 1, 1, 0)
    pl.semaphore_wait(barrier, peers)


def line_sum(line_size, own, finish, out_ref, held, acc_send, acc_recv, back_send, back_recv):
    here = lax.axis_index("tensor")
    last = line_size - 1
    count = held.shape[1]
    half = count * CHUNK

    def parts(stream):
        if stream == 0:
            return here, here + 1, here - 1
        return last - here, here - 1, here + 1

    def acc_copy(stream, i, target):
        return pltpu.make_async_remote_copy(
            src_ref=held.at[stream, i],
            dst_ref=held.at[stream, i],
            send_sem=acc_send.at[stream, i],
            recv_sem=acc_recv.at[stream, i],
            device_id={"tensor": target},
            device_id_type=MESH,
        )

    def rows_of(stream, i):
        return pl.ds(pl.multiple_of(stream * half + i * CHUNK, CHUNK), CHUNK)

    def back_copy(stream, i, target):
        return pltpu.make_async_remote_copy(
            src_ref=out_ref.at[rows_of(stream, i)],
            dst_ref=out_ref.at[rows_of(stream, i)],
            send_sem=back_send.at[stream, i],
            recv_sem=back_recv.at[stream, i],
            device_id={"tensor": target},
            device_id_type=MESH,
        )

    def step(k, carry):
        for stream in (0, 1):
            place, after, before = parts(stream)
            i = k - place

            @pl.when((i >= 0) & (i < count) & (place == 0))
            def _():
                held[stream, i] = own(stream, i).astype(jnp.bfloat16)
                acc_copy(stream, i, after).start()

            @pl.when((i >= 0) & (i < count) & (place > 0) & (place < last))
            def _():
                acc_copy(stream, i, after).wait_recv()
                held[stream, i] = (held[stream, i].astype(jnp.float32) + own(stream, i)).astype(
                    jnp.bfloat16
                )
                acc_copy(stream, i, after).start()

            @pl.when((i >= 0) & (i < count) & (place == last))
            def _():
                acc_copy(stream, i, before).wait_recv()
                total = held[stream, i].astype(jnp.float32) + own(stream, i)
                out_ref[rows_of(stream, i)] = finish(stream, i, total).astype(jnp.bfloat16)
                back_copy(stream, i, before).start()

            j = k - (2 * last - place)

            @pl.when((j >= 0) & (j < count) & (place < last))
            def _():
                back_copy(stream, j, before).wait_recv()

                @pl.when(place > 0)
                def _():
                    back_copy(stream, j, before).start()

        return carry

    lax.fori_loop(0, count + 2 * last, step, 0)

    def drain(i, carry):
        for stream in (0, 1):
            place, after, before = parts(stream)

            @pl.when(place < last)
            def _():
                acc_copy(stream, i, after).wait_send()

            @pl.when(place > 0)
            def _():
                back_copy(stream, i, before).wait_send()

        return carry

    lax.fori_loop(0, count, drain, 0)


def line_scratch(rows, width):
    count = rows // 2 // CHUNK
    return [
        pltpu.VMEM((2, count, CHUNK, width), jnp.bfloat16),
        pltpu.SemaphoreType.DMA((2, count)),
        pltpu.SemaphoreType.DMA((2, count)),
        pltpu.SemaphoreType.DMA((2, count)),
        pltpu.SemaphoreType.DMA((2, count)),
    ]


def tiled_products(pairs, partial):
    rows, width = partial.shape
    tile_m, tile_n = min(256, rows // 2), 512

    def tile(n, carry):
        columns = pl.ds(pl.multiple_of(n * tile_n, tile_n), tile_n)
        for m in range(rows // tile_m):
            block = slice(m * tile_m, (m + 1) * tile_m)
            total = None
            for left, right, transposed in pairs:
                if transposed:
                    term = lax.dot_general(
                        left[block],
                        right[columns, :],
                        (((1,), (1,)), ((), ())),
                        preferred_element_type=jnp.float32,
                    )
                else:
                    term = jnp.dot(
                        left[block], right[:, columns], preferred_element_type=jnp.float32
                    )
                total = term if total is None else total + term
            partial[block, columns] = total
        return carry

    lax.fori_loop(0, width // tile_n, tile, 0)


def own_rows(partial):
    half = partial.shape[0] // 2

    def own(stream, i):
        return partial[pl.ds(pl.multiple_of(stream * half + i * CHUNK, CHUNK), CHUNK)]

    return own


def chunk_rows(ref, stream, i):
    half = ref.shape[0] // 2
    return ref[pl.ds(pl.multiple_of(stream * half + i * CHUNK, CHUNK), CHUNK)]


def kept_rows(i):
    return pl.ds(pl.multiple_of(i * CHUNK, CHUNK), CHUNK)


def out_kernel(n, mixed, weight, inputs, gain, normed_two, middle, partial, *scratch):
    greet_line(n)
    tiled_products([(mixed, weight, False)], partial)

    def finish(stream, i, total):
        value = chunk_rows(inputs, stream, i).astype(jnp.float32) + total
        middle[kept_rows(i)] = value
        inverse = lax.rsqrt(jnp.mean(value * value, axis=-1, keepdims=True) + epsilon)
        return value * inverse * gain[...]

    line_sum(n, own_rows(partial), finish, normed_two, *scratch)


def down_kernel(n, inner, weight, middle, layer_out, partial, *scratch):
    greet_line(n)
    tiled_products([(inner, weight, False)], partial)

    def finish(stream, i, total):
        return middle[kept_rows(i)] + total

    line_sum(n, own_rows(partial), finish, layer_out, *scratch)


def back_two_kernel(
    n, gate, up, gate_weight, up_weight, upstream, middle, gain,
    grad_attended, grad_middle, grad_gain, partial, *scratch
):
    greet_line(n)
    grad_gain[...] = jnp.zeros_like(grad_gain)
    tiled_products([(gate, gate_weight, True), (up, up_weight, True)], partial)

    def finish(stream, i, total):
        value = middle[kept_rows(i)]
        inverse = lax.rsqrt(jnp.mean(value * value, axis=-1, keepdims=True) + epsilon)
        unit = value * inverse
        grad_gain[...] += jnp.sum(total * unit, axis=0, keepdims=True)
        scaled = total * gain[...]
        result = chunk_rows(upstream, stream, i).astype(jnp.float32) + inverse * (
            scaled - unit * jnp.mean(scaled * unit, axis=-1, keepdims=True)
        )
        grad_middle[kept_rows(i)] = result
        return result

    line_sum(n, own_rows(partial), finish, grad_attended, *scratch)


def back_one_kernel(
    n, query, key, value, query_weight, key_weight, value_weight, inputs, grad_middle, gain,
    grad_inputs, grad_gain, partial, *scratch
):
    greet_line(n)
    grad_gain[...] = jnp.zeros_like(grad_gain)
    tiled_products(
        [(query, query_weight, True), (key, key_weight, True), (value, value_weight, True)], partial
    )

    def finish(stream, i, total):
        hidden = chunk_rows(inputs, stream, i).astype(jnp.float32)
        inverse = lax.rsqrt(jnp.mean(hidden * hidden, axis=-1, keepdims=True) + epsilon)
        unit = hidden * inverse
        grad_gain[...] += jnp.sum(total * unit, axis=0, keepdims=True)
        scaled = total * gain[...]
        return grad_middle[kept_rows(i)] + inverse * (
            scaled - unit * jnp.mean(scaled * unit, axis=-1, keepdims=True)
        )

    line_sum(n, own_rows(partial), finish, grad_inputs, *scratch)


def line_call(kernel, line_size, rows, width, operands, outs, collective_id, limit):
    vmem = pl.BlockSpec(memory_space=pltpu.VMEM)
    return pl.pallas_call(
        functools.partial(kernel, line_size),
        out_shape=[jax.ShapeDtypeStruct(s, d) for s, d in outs],
        in_specs=[vmem] * len(operands),
        out_specs=[vmem] * len(outs),
        scratch_shapes=[pltpu.VMEM((rows, width), jnp.float32), *line_scratch(rows, width)],
        compiler_params=pltpu.CompilerParams(
            collective_id=collective_id, has_side_effects=True, vmem_limit_bytes=limit * MIB
        ),
    )(*operands)


def rotary_tables(positions):
    half_dim = HEAD_DIM // 2
    frequency = rope_base ** (-2.0 * jnp.arange(half_dim, dtype=jnp.float32) / HEAD_DIM)
    angles = positions.astype(jnp.float32)[..., None] * frequency
    return (jnp.cos(angles), jnp.sin(angles))


def rotate(values, cosine, sine_table):
    half_dim = values.shape[-1] // 2
    first = values[..., :half_dim]
    second = values[..., half_dim:]
    return jnp.concatenate(
        [first * cosine - second * sine_table, second * cosine + first * sine_table], axis=-1
    )


def visible(query_seg, key_seg, first_row):
    query_pos = first_row + jnp.arange(query_seg.shape[0], dtype=jnp.int32)
    key_pos = jnp.arange(key_seg.shape[0], dtype=jnp.int32)
    same_doc = query_seg[:, None] == key_seg[None, :]
    causal = key_pos[None, :] <= query_pos[:, None]
    usable = (key_seg[None, :] >= 0) | (key_pos[None, :] == query_pos[:, None])
    return same_doc & causal & usable


def body(
    inputs,
    segment_ids,
    attention_gain,
    query_weight,
    key_weight,
    value_weight,
    out_weight,
    feedforward_gain,
    gate_weight,
    up_weight,
    down_weight,
    cotangent,
):
    seq_count, span_len, model_width = inputs.shape
    row_count = seq_count * span_len
    query_heads = query_weight.shape[1] // HEAD_DIM
    kv_heads = key_weight.shape[1] // HEAD_DIM
    group_size = query_heads // kv_heads
    score_scale = 1.0 / math.sqrt(HEAD_DIM)
    offset = lax.axis_index("ctx") * span_len
    whole_segments = lax.all_gather(segment_ids, "ctx", axis=1, tiled=True)
    own_positions = lax.dynamic_slice_in_dim(positions_of(whole_segments), offset, span_len, 1)
    cosine, sine_table = rotary_tables(own_positions)
    cosine = cosine[:, :, None, :]
    sine_table = sine_table[:, :, None, :]
    hidden = inputs.astype(jnp.float32).reshape(row_count, model_width)
    inverse_one = lax.rsqrt(jnp.mean(hidden * hidden, axis=-1, keepdims=True) + epsilon)
    unit_one = hidden * inverse_one
    normed = (unit_one * attention_gain).astype(jnp.bfloat16)
    query_rows = rotate(
        jnp.dot(normed, query_weight, preferred_element_type=jnp.float32).reshape(
            seq_count, span_len, query_heads, HEAD_DIM
        ),
        cosine,
        sine_table,
    ).astype(jnp.bfloat16)
    key_rows = rotate(
        jnp.dot(normed, key_weight, preferred_element_type=jnp.float32).reshape(
            seq_count, span_len, kv_heads, HEAD_DIM
        ),
        cosine,
        sine_table,
    ).astype(jnp.bfloat16)
    value_rows = (
        jnp.dot(normed, value_weight, preferred_element_type=jnp.float32)
        .astype(jnp.bfloat16)
        .reshape(seq_count, span_len, kv_heads, HEAD_DIM)
    )
    all_keys, all_values = (
        lax.all_gather(key_rows, "ctx", axis=1, tiled=True),
        lax.all_gather(value_rows, "ctx", axis=1, tiled=True),
    )

    def attend(block_items):
        query_block, key_block, value_block, query_seg, key_seg = block_items
        allowed = visible(query_seg, key_seg, offset)
        grouped = query_block.reshape(span_len, kv_heads, group_size, HEAD_DIM)
        raw_scores = jnp.einsum(
            "qhgd,khd->hgqk", grouped, key_block, preferred_element_type=jnp.float32
        )
        scores = jnp.where(allowed, raw_scores * score_scale, masked_score)
        row_peak = jnp.max(scores, axis=-1, keepdims=True)
        shifted_exp = jnp.exp(scores - row_peak)
        denominator = jnp.sum(shifted_exp, axis=-1, keepdims=True)
        attn_probs = (shifted_exp / denominator).astype(jnp.bfloat16)
        mixed_block = jnp.einsum(
            "hgqk,khd->qhgd", attn_probs, value_block, preferred_element_type=jnp.float32
        )
        return (
            mixed_block.astype(jnp.bfloat16).reshape(span_len, query_heads * HEAD_DIM),
            row_peak + jnp.log(denominator),
        )

    mixed_heads, log_sums = lax.map(
        attend, (query_rows, all_keys, all_values, segment_ids, whole_segments)
    )
    mixed_flat = mixed_heads.reshape(row_count, query_heads * HEAD_DIM)
    line_size = lax.axis_size("tensor")
    flat = (row_count, model_width)
    kept = (row_count // 2, model_width)
    gain_one = attention_gain.reshape(1, model_width)
    gain_two = feedforward_gain.reshape(1, model_width)
    flat_inputs = inputs.reshape(flat)
    normed_two, middle = line_call(
        out_kernel, line_size, *flat,
        (mixed_flat, out_weight, flat_inputs, gain_two),
        [(flat, jnp.bfloat16), (kept, jnp.float32)], 1, 28,
    )
    gate_pre = jnp.dot(normed_two, gate_weight, preferred_element_type=jnp.float32)
    up_pre = jnp.dot(normed_two, up_weight, preferred_element_type=jnp.float32)
    sigmoid_gate = jax.nn.sigmoid(gate_pre)
    inner_act = (gate_pre * sigmoid_gate * up_pre).astype(jnp.bfloat16)
    [layer_out] = line_call(
        down_kernel, line_size, *flat,
        (inner_act, down_weight, middle), [(flat, jnp.bfloat16)], 2, 28,
    )
    layer_out = layer_out.reshape(seq_count, span_len, model_width)
    upstream = cotangent.reshape(row_count, model_width)
    grad_down = jnp.dot(inner_act.T, upstream, preferred_element_type=jnp.float32)
    grad_inner = jnp.dot(upstream, down_weight.T, preferred_element_type=jnp.float32)
    grad_up_pre = (grad_inner * gate_pre * sigmoid_gate).astype(jnp.bfloat16)
    grad_gate_pre = (
        grad_inner * up_pre * sigmoid_gate * (1.0 + gate_pre * (1.0 - sigmoid_gate))
    ).astype(jnp.bfloat16)
    grad_gate = jnp.dot(normed_two.T, grad_gate_pre, preferred_element_type=jnp.float32)
    grad_up = jnp.dot(normed_two.T, grad_up_pre, preferred_element_type=jnp.float32)
    grad_attended, grad_middle, grad_ffn_gain = line_call(
        back_two_kernel, line_size, *flat,
        (grad_gate_pre, grad_up_pre, gate_weight, up_weight, upstream, middle, gain_two),
        [(flat, jnp.bfloat16), (kept, jnp.float32), ((1, model_width), jnp.float32)], 3, 40,
    )
    grad_out_part = jnp.dot(mixed_flat.T, grad_attended, preferred_element_type=jnp.float32)
    grad_mixed = (
        jnp.dot(grad_attended, out_weight.T, preferred_element_type=jnp.float32)
        .astype(jnp.bfloat16)
        .reshape(seq_count, span_len, query_heads, HEAD_DIM)
    )

    def attend_back(block_items):
        query_block, key_block, value_block, query_seg, key_seg, grad_block, log_block = block_items
        allowed = visible(query_seg, key_seg, offset)
        grouped = query_block.reshape(span_len, kv_heads, group_size, HEAD_DIM)
        grad_grouped = grad_block.reshape(span_len, kv_heads, group_size, HEAD_DIM)
        raw_scores = jnp.einsum(
            "qhgd,khd->hgqk", grouped, key_block, preferred_element_type=jnp.float32
        )
        scores = jnp.where(allowed, raw_scores * score_scale, masked_score)
        attn_probs = jnp.exp(scores - log_block)
        rounded = attn_probs.astype(jnp.bfloat16)
        grad_values = jnp.einsum(
            "hgqk,qhgd->khd", rounded, grad_grouped, preferred_element_type=jnp.float32
        )
        grad_probs = jnp.einsum(
            "qhgd,khd->hgqk", grad_grouped, value_block, preferred_element_type=jnp.float32
        )
        row_dot = jnp.sum(attn_probs * grad_probs, axis=-1, keepdims=True)
        grad_scores = (attn_probs * (grad_probs - row_dot) * score_scale).astype(jnp.bfloat16)
        grad_queries = jnp.einsum(
            "hgqk,khd->qhgd", grad_scores, key_block, preferred_element_type=jnp.float32
        ).reshape(span_len, query_heads, HEAD_DIM)
        grad_keys = jnp.einsum(
            "hgqk,qhgd->khd", grad_scores, grouped, preferred_element_type=jnp.float32
        )
        return (grad_queries, grad_keys, grad_values)

    grad_queries, grad_keys, grad_values = lax.map(
        attend_back,
        (query_rows, all_keys, all_values, segment_ids, whole_segments, grad_mixed, log_sums),
    )
    own_grad_keys, own_grad_values = (
        lax.psum_scatter(grad_keys, "ctx", scatter_dimension=1, tiled=True),
        lax.psum_scatter(grad_values, "ctx", scatter_dimension=1, tiled=True),
    )
    grad_query_pre = (
        rotate(grad_queries, cosine, -sine_table)
        .astype(jnp.bfloat16)
        .reshape(row_count, query_heads * HEAD_DIM)
    )
    grad_key_pre = (
        rotate(own_grad_keys, cosine, -sine_table)
        .astype(jnp.bfloat16)
        .reshape(row_count, kv_heads * HEAD_DIM)
    )
    grad_value_pre = own_grad_values.astype(jnp.bfloat16).reshape(row_count, kv_heads * HEAD_DIM)
    grad_query = jnp.dot(normed.T, grad_query_pre, preferred_element_type=jnp.float32)
    grad_key = jnp.dot(normed.T, grad_key_pre, preferred_element_type=jnp.float32)
    grad_value = jnp.dot(normed.T, grad_value_pre, preferred_element_type=jnp.float32)
    grad_inputs, grad_attn_gain = line_call(
        back_one_kernel, line_size, *flat,
        (grad_query_pre, grad_key_pre, grad_value_pre, query_weight, key_weight, value_weight,
         flat_inputs, grad_middle, gain_one),
        [(flat, jnp.bfloat16), ((1, model_width), jnp.float32)], 4, 40,
    )
    grad_inputs = grad_inputs.reshape(seq_count, span_len, model_width)
    gain_grads = jnp.concatenate([grad_attn_gain, grad_ffn_gain], axis=0)
    place = lax.axis_index("tensor")
    owner = (place == 0) | (place == line_size - 1)
    gain_grads = lax.psum(jnp.where(owner, gain_grads, 0.0), ("dp", "ctx", "tensor"))
    shards = lax.axis_size("dp") * lax.axis_size("ctx")
    piece = model_width // shards
    shard = lax.axis_index("dp") * lax.axis_size("ctx") + lax.axis_index("ctx")
    gain_grads = lax.dynamic_slice_in_dim(gain_grads, shard * piece, piece, 1)
    reduced = (
        gain_grads[0],
        lax.psum_scatter(
            grad_query.astype(jnp.bfloat16), ("dp", "ctx"), scatter_dimension=0, tiled=True
        ).astype(jnp.float32),
        lax.psum_scatter(
            grad_key.astype(jnp.bfloat16), ("dp", "ctx"), scatter_dimension=0, tiled=True
        ).astype(jnp.float32),
        lax.psum_scatter(
            grad_value.astype(jnp.bfloat16), ("dp", "ctx"), scatter_dimension=0, tiled=True
        ).astype(jnp.float32),
        lax.psum_scatter(
            grad_out_part.astype(jnp.bfloat16), ("dp", "ctx"), scatter_dimension=1, tiled=True
        ).astype(jnp.float32),
        gain_grads[1],
        lax.psum_scatter(
            grad_gate.astype(jnp.bfloat16), ("dp", "ctx"), scatter_dimension=0, tiled=True
        ).astype(jnp.float32),
        lax.psum_scatter(
            grad_up.astype(jnp.bfloat16), ("dp", "ctx"), scatter_dimension=0, tiled=True
        ).astype(jnp.float32),
        lax.psum_scatter(
            grad_down.astype(jnp.bfloat16), ("dp", "ctx"), scatter_dimension=1, tiled=True
        ).astype(jnp.float32),
    )
    return (
        layer_out,
        grad_inputs,
        reduced[0],
        reduced[1],
        reduced[2],
        reduced[3],
        reduced[4],
        reduced[5],
        reduced[6],
        reduced[7],
        reduced[8],
    )


def solution(mesh):
    return jax.shard_map(
        body,
        mesh=mesh,
        in_specs=(
            P("dp", "ctx", None),
            P("dp", "ctx"),
            P(),
            P(None, "tensor"),
            P(None, "tensor"),
            P(None, "tensor"),
            P("tensor", None),
            P(),
            P(None, "tensor"),
            P(None, "tensor"),
            P("tensor", None),
            P("dp", "ctx", None),
        ),
        out_specs=(
            P("dp", "ctx", None),
            P("dp", "ctx", None),
            P(("dp", "ctx")),
            P(("dp", "ctx"), "tensor"),
            P(("dp", "ctx"), "tensor"),
            P(("dp", "ctx"), "tensor"),
            P("tensor", ("dp", "ctx")),
            P(("dp", "ctx")),
            P(("dp", "ctx"), "tensor"),
            P(("dp", "ctx"), "tensor"),
            P("tensor", ("dp", "ctx")),
        ),
        check_vma=False,
    )
```

```python
import functools
import math

import jax
import jax.numpy as jnp
from jax import lax
from jax.experimental import pallas as pl
from jax.experimental.pallas import tpu as pltpu
from jax.sharding import PartitionSpec as P

HEAD_DIM = 64


epsilon = 1e-05
rope_base = 10000.0
masked_score = -1e30


def positions_of(segment):
    token_index = jnp.arange(segment.shape[-1], dtype=jnp.int32)
    previous = jnp.concatenate([segment[..., :1] - 1, segment[..., :-1]], axis=-1)
    starts = jnp.where(segment != previous, token_index, 0)
    earlier = token_index[None, :] <= token_index[:, None]
    run_start = jnp.max(jnp.where(earlier, starts[..., None, :], 0), axis=-1)
    return token_index - run_start


MESH = pl.DeviceIdType.MESH
CHUNK = 32
MIB = 1 << 20


def greet_line(line_size):
    here = lax.axis_index("tensor")
    barrier = pltpu.get_barrier_semaphore()

    @pl.when(here > 0)
    def _():
        pl.semaphore_signal(barrier, inc=1, device_id={"tensor": here - 1}, device_id_type=MESH)

    @pl.when(here < line_size - 1)
    def _():
        pl.semaphore_signal(barrier, inc=1, device_id={"tensor": here + 1}, device_id_type=MESH)

    peers = jnp.where(here > 0, 1, 0) + jnp.where(here < line_size - 1, 1, 0)
    pl.semaphore_wait(barrier, peers)


class LineChannel:
    def __init__(self, line_size, own, finish, out_ref, held, acc_send, acc_recv, back_send, back_recv, lag=0):
        self.last = line_size - 1
        self.here = lax.axis_index("tensor")
        self.own, self.finish, self.out_ref, self.held = own, finish, out_ref, held
        self.acc_sems, self.back_sems = (acc_send, acc_recv), (back_send, back_recv)
        self.count = held.shape[1]
        self.lag = lag
        self.steps = lag + self.count + 2 * self.last

    def parts(self, stream):
        if stream == 0:
            return self.here, self.here + 1, self.here - 1
        return self.last - self.here, self.here - 1, self.here + 1

    def acc_copy(self, stream, i, target):
        return pltpu.make_async_remote_copy(
            src_ref=self.held.at[stream, i],
            dst_ref=self.held.at[stream, i],
            send_sem=self.acc_sems[0].at[stream, i],
            recv_sem=self.acc_sems[1].at[stream, i],
            device_id={"tensor": target},
            device_id_type=MESH,
        )

    def rows_of(self, stream, i):
        return pl.ds(pl.multiple_of((stream * self.count + i) * CHUNK, CHUNK), CHUNK)

    def back_copy(self, stream, i, target):
        return pltpu.make_async_remote_copy(
            src_ref=self.out_ref.at[self.rows_of(stream, i)],
            dst_ref=self.out_ref.at[self.rows_of(stream, i)],
            send_sem=self.back_sems[0].at[stream, i],
            recv_sem=self.back_sems[1].at[stream, i],
            device_id={"tensor": target},
            device_id_type=MESH,
        )

    def step(self, k):
        last, count, held = self.last, self.count, self.held
        for stream in (0, 1):
            place, after, before = self.parts(stream)
            i = k - self.lag - place
            inside = (i >= 0) & (i < count)

            @pl.when(inside & (place == 0))
            def _():
                held[stream, i] = self.own(stream, i).astype(jnp.bfloat16)
                self.acc_copy(stream, i, after).start()

            @pl.when(inside & (place > 0) & (place < last))
            def _():
                self.acc_copy(stream, i, after).wait_recv()
                held[stream, i] = (
                    held[stream, i].astype(jnp.float32) + self.own(stream, i)
                ).astype(jnp.bfloat16)
                self.acc_copy(stream, i, after).start()

            @pl.when(inside & (place == last))
            def _():
                self.acc_copy(stream, i, before).wait_recv()
                total = held[stream, i].astype(jnp.float32) + self.own(stream, i)
                result = self.finish(stream, i, total)
                self.out_ref[self.rows_of(stream, i)] = result.astype(jnp.bfloat16)
                self.back_copy(stream, i, before).start()

            j = k - self.lag - (2 * last - place)

            @pl.when((j >= 0) & (j < count) & (place < last))
            def _():
                self.back_copy(stream, j, before).wait_recv()

                @pl.when(place > 0)
                def _():
                    self.back_copy(stream, j, before).start()

    def drain(self):
        def sent(i, carry):
            for stream in (0, 1):
                place, after, before = self.parts(stream)

                @pl.when(place < self.last)
                def _():
                    self.acc_copy(stream, i, after).wait_send()

                @pl.when(place > 0)
                def _():
                    self.back_copy(stream, i, before).wait_send()

            return carry

        lax.fori_loop(0, self.count, sent, 0)


def line_sum(*args):
    channel = LineChannel(*args)

    def step(k, carry):
        channel.step(k)
        return carry

    lax.fori_loop(0, channel.steps, step, 0)
    channel.drain()


def greet_all(line_size, dp_size):
    here, row, core = lax.axis_index("tensor"), lax.axis_index("dp"), lax.axis_index("ctx")
    barrier = pltpu.get_barrier_semaphore()

    @pl.when(here > 0)
    def _():
        pl.semaphore_signal(barrier, inc=1, device_id={"tensor": here - 1}, device_id_type=MESH)

    @pl.when(here < line_size - 1)
    def _():
        pl.semaphore_signal(barrier, inc=1, device_id={"tensor": here + 1}, device_id_type=MESH)

    pl.semaphore_signal(barrier, inc=1, device_id={"ctx": 1 - core}, device_id_type=MESH)
    for r in range(dp_size - 1):
        peer = lax.rem(row + 1 + r, dp_size)
        pl.semaphore_signal(barrier, inc=1, device_id={"dp": peer}, device_id_type=MESH)
    peers = dp_size + jnp.where(here > 0, 1, 0) + jnp.where(here < line_size - 1, 1, 0)
    pl.semaphore_wait(barrier, peers)


class CoreExchange:
    def __init__(self, send, recv):
        self.send, self.recv, self.copies = send, recv, []
        self.core = lax.axis_index("ctx")

    def copy(self, src, dst):
        slot = len(self.copies)
        made = pltpu.make_async_remote_copy(
            src_ref=src,
            dst_ref=dst,
            send_sem=self.send.at[slot],
            recv_sem=self.recv.at[slot],
            device_id={"ctx": 1 - self.core},
            device_id_type=MESH,
        )
        made.start()
        self.copies.append(made)

    def rows(self, stacked):
        span = stacked.shape[0] // 2
        self.copy(stacked.at[pl.ds(0, span)], stacked.at[pl.ds(span, span)])

    def columns(self, held, other, piece, dp_size):
        for q in range(dp_size):
            block = (2 * q + 1 - self.core) * piece
            self.copy(
                held.at[:, pl.ds(pl.multiple_of(block, piece), piece)],
                other.at[:, pl.ds(q * piece, piece)],
            )

    def wait(self):
        for made in self.copies:
            made.wait()


class PlaneScatter:
    def __init__(self, dp_size, piece, sends, landings, send_sems, recv_sems, turned):
        self.dp_size, self.piece, self.turned = dp_size, piece, turned
        self.sends, self.landings = sends, landings
        self.send_sems, self.recv_sems = send_sems, recv_sems
        self.row, self.core = lax.axis_index("dp"), lax.axis_index("ctx")

    def turn(self, r, held, other):
        peer = lax.rem(self.row + 1 + r, self.dp_size)
        span = held.shape[0]
        block = pl.multiple_of((2 * peer + self.core) * self.piece, self.piece)
        self.turned[:, 0:span] = held[:, pl.ds(block, self.piece)].T
        place = pl.multiple_of(peer * self.piece, self.piece)
        self.turned[:, span : 2 * span] = other[:, pl.ds(place, self.piece)].T

    def copy(self, w, r):
        peer = lax.rem(self.row + 1 + r, self.dp_size)
        return pltpu.make_async_remote_copy(
            src_ref=self.sends[w].at[r],
            dst_ref=self.landings[w].at[r],
            send_sem=self.send_sems.at[w, r],
            recv_sem=self.recv_sems.at[w, r],
            device_id={"dp": peer},
            device_id_type=MESH,
        )

    def piece_of(self, w, r, stacked, own):
        width = stacked.shape[1]
        tile = 384

        def value(low, high):
            return jnp.dot(
                self.turned[...], stacked[:, low:high], preferred_element_type=jnp.float32
            )

        edges = [(low, min(low + tile, width)) for low in range(0, width, tile)]

        @pl.when(r < self.dp_size - 1)
        def _():
            for low, high in edges:
                self.sends[w][r, :, low:high] = value(low, high).astype(jnp.bfloat16)
            self.copy(w, r).start()

        @pl.when(r == self.dp_size - 1)
        def _():
            for low, high in edges:
                own[:, low:high] = value(low, high)

    def gather(self, w, own, load_sems=None):
        landed = self.landings[w]
        loads = []
        for r in range(self.dp_size - 1):
            self.copy(w, r).wait()
            if load_sems is not None:
                load = pltpu.make_async_copy(landed.at[r], self.sends[w].at[r], load_sems.at[r])
                load.start()
                loads.append(load)
        for load in loads:
            load.wait()
        if load_sems is not None:
            landed = self.sends[w]
        total = own[...]
        for r in range(self.dp_size - 1):
            total = total + landed[r].astype(jnp.float32)
        return total


def line_scratch(rows, width):
    count = rows // 2 // CHUNK
    return [
        pltpu.VMEM((2, count, CHUNK, width), jnp.bfloat16),
        pltpu.SemaphoreType.DMA((2, count)),
        pltpu.SemaphoreType.DMA((2, count)),
        pltpu.SemaphoreType.DMA((2, count)),
        pltpu.SemaphoreType.DMA((2, count)),
    ]


def tiled_products(pairs, partial):
    rows, width = partial.shape
    tile_m, tile_n = min(256, rows // 2), 512

    def tile(n, carry):
        columns = pl.ds(pl.multiple_of(n * tile_n, tile_n), tile_n)
        for m in range(rows // tile_m):
            block = slice(m * tile_m, (m + 1) * tile_m)
            total = None
            for left, right, transposed in pairs:
                if transposed:
                    term = lax.dot_general(
                        left[block],
                        right[columns, :],
                        (((1,), (1,)), ((), ())),
                        preferred_element_type=jnp.float32,
                    )
                else:
                    term = jnp.dot(
                        left[block], right[:, columns], preferred_element_type=jnp.float32
                    )
                total = term if total is None else total + term
            partial[block, columns] = total.astype(partial.dtype)
        return carry

    lax.fori_loop(0, width // tile_n, tile, 0)


def own_rows(partial):
    half = partial.shape[0] // 2

    def own(stream, i):
        return partial[pl.ds(pl.multiple_of(stream * half + i * CHUNK, CHUNK), CHUNK)]

    return own


def chunk_rows(ref, stream, i):
    half = ref.shape[0] // 2
    return ref[pl.ds(pl.multiple_of(stream * half + i * CHUNK, CHUNK), CHUNK)]


def kept_rows(i):
    return pl.ds(pl.multiple_of(i * CHUNK, CHUNK), CHUNK)


def out_kernel(n, mixed, weight, inputs, gain, normed_two, middle, partial, *scratch):
    greet_line(n)
    tiled_products([(mixed, weight, False)], partial)

    def finish(stream, i, total):
        value = chunk_rows(inputs, stream, i).astype(jnp.float32) + total
        middle[kept_rows(i)] = value
        inverse = lax.rsqrt(jnp.mean(value * value, axis=-1, keepdims=True) + epsilon)
        return value * inverse * gain[...]

    line_sum(n, own_rows(partial), finish, normed_two, *scratch)


def back_two_kernel(
    n, dp_size, gate_any, up_any, inner_any, gate_weight_any, up_weight_any, down_weight_any,
    upstream_any, normed_any, middle_any, gain,
    layer_out, grad_attended, grad_middle, grad_gain, grad_gate, grad_up, grad_down, land_gate, land_up, land_down,
    gate, up, inner, weight_a, weight_b, weight_c, upstream, normed, middle, upstream_other, normed_other,
    own_down, turned, send_gate, send_up, send_down,
    partial, second, load_sems, core_send, core_recv, plane_send, plane_recv,
    held_a, as_a, ar_a, bs_a, br_a, held_b, as_b, ar_b, bs_b, br_b,
):
    span = upstream.shape[0]
    loads = [
        pltpu.make_async_copy(src, dst, load_sems.at[at])
        for at, (src, dst) in enumerate([
            (gate_any, gate.at[pl.ds(0, span)]),
            (gate_weight_any, weight_a),
            (up_any, up.at[pl.ds(0, span)]),
            (up_weight_any, weight_b),
            (normed_any, normed),
            (inner_any, inner.at[pl.ds(0, span)]),
            (upstream_any, upstream),
            (middle_any, middle),
        ])
    ]
    for load in loads:
        load.start()
    greet_all(n, dp_size)
    grad_gain[...] = jnp.zeros_like(grad_gain)
    for load in loads:
        load.wait()
    exchange = CoreExchange(core_send, core_recv)
    exchange.rows(gate)
    exchange.columns(normed, normed_other, turned.shape[0], dp_size)
    exchange.rows(up)
    exchange.rows(inner)
    exchange.columns(upstream, upstream_other, turned.shape[0], dp_size)
    tiled_products([(gate, weight_a, True), (up, weight_b, True)], partial)
    down_load = pltpu.make_async_copy(down_weight_any, weight_c, load_sems.at[8])
    down_load.start()

    def finish_two(stream, i, total):
        value = middle[kept_rows(i)]
        inverse = lax.rsqrt(jnp.mean(value * value, axis=-1, keepdims=True) + epsilon)
        unit = value * inverse
        grad_gain[...] += jnp.sum(total * unit, axis=0, keepdims=True)
        scaled = total * gain[...]
        result = chunk_rows(upstream, stream, i).astype(jnp.float32) + inverse * (
            scaled - unit * jnp.mean(scaled * unit, axis=-1, keepdims=True)
        )
        grad_middle[kept_rows(i)] = result
        return result

    def finish_out(stream, i, total):
        return middle[kept_rows(i)] + total

    count = held_a.shape[1]
    first = LineChannel(n, own_rows(partial), finish_two, grad_attended, held_a, as_a, ar_a, bs_a, br_a)
    then = LineChannel(n, own_rows(second), finish_out, layer_out, held_b, as_b, ar_b, bs_b, br_b, lag=count)
    plane = PlaneScatter(
        dp_size, turned.shape[0], (send_gate, send_up, send_down), (land_gate, land_up, land_down),
        plane_send, plane_recv, turned,
    )
    def step(k, carry):
        first.step(k)
        then.step(k)

        @pl.when(k == 0)
        def _():
            down_load.wait()
            tiled_products([(inner, weight_c, False)], second)

        @pl.when(k == 1)
        def _():
            exchange.wait()

        task = k - 2
        r = task // 3

        @pl.when((task >= 0) & (task < 3 * dp_size))
        def _():
            kind = lax.rem(task, 3)

            @pl.when(kind == 0)
            def _():
                plane.turn(r, normed, normed_other)
                plane.piece_of(0, r, gate, grad_gate)

            @pl.when(kind == 1)
            def _():
                plane.piece_of(1, r, up, grad_up)

            @pl.when(kind == 2)
            def _():
                plane.turn(r, upstream, upstream_other)
                plane.piece_of(2, r, inner, own_down)

        return carry

    lax.fori_loop(0, max(then.steps, 2 + 3 * dp_size), step, 0)
    first.drain()
    then.drain()
    grad_gate[...] = plane.gather(0, grad_gate, load_sems)
    grad_up[...] = plane.gather(1, grad_up, load_sems)
    grad_down[...] = plane.gather(2, own_down, load_sems).T


def back_one_kernel(
    n, dp_size, pre_any, mixed_any, normed_any, attended_any, query_weight, key_weight, value_weight,
    inputs, grad_middle, gain, gain_two,
    grad_inputs, grad_gains, grad_qkv, grad_out,
    pre, mixed, normed, attended, normed_other, attended_other, own_out, turned,
    send_qkv, send_out, land_qkv, land_out,
    gain_line, gain_land, gain_sum, gain_plane, partial, load_sems, core_send, core_recv, plane_send, plane_recv,
    line_send, line_recv, spread_send, spread_recv,
    held, acc_send, acc_recv, back_send, back_recv,
):
    span, width = inputs.shape
    here, row, core = lax.axis_index("tensor"), lax.axis_index("dp"), lax.axis_index("ctx")
    loads = [
        pltpu.make_async_copy(src, dst, load_sems.at[at])
        for at, (src, dst) in enumerate([
            (pre_any, pre.at[pl.ds(0, span)]),
            (mixed_any, mixed.at[pl.ds(0, span)]),
            (normed_any, normed),
            (attended_any, attended),
        ])
    ]
    for load in loads:
        load.start()
    greet_plane_and_lines(n, dp_size)
    gain_line[...] = jnp.zeros_like(gain_line)
    gain_line[1:2, :] = gain_two[...]
    for load in loads:
        load.wait()
    exchange = CoreExchange(core_send, core_recv)
    exchange.rows(pre)
    exchange.columns(normed, normed_other, turned.shape[0], dp_size)
    exchange.rows(mixed)
    exchange.columns(attended, attended_other, turned.shape[0], dp_size)
    heads, head = query_weight.shape[1], key_weight.shape[1]

    def products(n_tile, carry):
        columns = pl.ds(pl.multiple_of(n_tile * 512, 512), 512)
        for low in range(0, span, span // 2):
            rows = slice(low, low + span // 2)
            partial[rows, columns] = (
                turned_dot(pre[rows, 0:heads], query_weight[columns, :])
                + turned_dot(pre[rows, heads : heads + head], key_weight[columns, :])
                + turned_dot(pre[rows, heads + head : heads + 2 * head], value_weight[columns, :])
            )
        return carry

    lax.fori_loop(0, width // 512, products, 0)

    def finish(stream, i, total):
        hidden = chunk_rows(inputs, stream, i).astype(jnp.float32)
        inverse = lax.rsqrt(jnp.mean(hidden * hidden, axis=-1, keepdims=True) + epsilon)
        unit = hidden * inverse
        gain_line[0:1, :] += jnp.sum(total * unit, axis=0, keepdims=True)
        scaled = total * gain[...]
        return grad_middle[kept_rows(i)] + inverse * (
            scaled - unit * jnp.mean(scaled * unit, axis=-1, keepdims=True)
        )

    channel = LineChannel(n, own_rows(partial), finish, grad_inputs, held, acc_send, acc_recv, back_send, back_recv)
    plane = PlaneScatter(
        dp_size, turned.shape[0], (send_qkv, send_out), (land_qkv, land_out), plane_send, plane_recv, turned
    )

    def line_copies(owner, hops):
        slot = 0 if owner == 0 else 1
        return [
            pltpu.make_async_remote_copy(
                src_ref=gain_line,
                dst_ref=gain_land.at[slot],
                send_sem=line_send.at[slot, hop - 1],
                recv_sem=line_recv.at[slot],
                device_id={"tensor": owner + hop if owner == 0 else owner - hop},
                device_id_type=MESH,
            )
            for hop in hops
        ]

    def step(k, carry):
        channel.step(k)

        @pl.when(k == 1)
        def _():
            exchange.wait()

        task = k - 2
        r = task // 2

        @pl.when((task >= 0) & (task < 2 * dp_size))
        def _():
            kind = lax.rem(task, 2)

            @pl.when(kind == 0)
            def _():
                plane.turn(r, normed, normed_other)
                plane.piece_of(0, r, pre, grad_qkv)

            @pl.when(kind == 1)
            def _():
                plane.turn(r, attended, attended_other)
                plane.piece_of(1, r, mixed, own_out)

        @pl.when(k == channel.count + n - 2)
        def _():
            for owner in (0, n - 1):

                @pl.when(here == owner)
                def _():
                    for made in line_copies(owner, range(1, n)):
                        made.start()

        return carry

    lax.fori_loop(0, max(channel.steps, 2 + 2 * dp_size), step, 0)
    piece = width // (2 * dp_size)
    gain_sum[...] = jnp.zeros_like(gain_sum)
    for owner in (0, n - 1):
        slot = 0 if owner == 0 else 1

        @pl.when(here == owner)
        def _():
            gain_sum[...] += gain_line[...]

        @pl.when(here != owner)
        def _():
            line_copies(owner, (1,))[0].wait_recv()
            gain_sum[...] += gain_land[slot]

    total_shards = 2 * dp_size
    place = 2 * row + core

    def spread(r):
        peer = lax.rem(place + 1 + r, total_shards)
        block = pl.multiple_of(peer * piece, piece)
        return pltpu.make_async_remote_copy(
            src_ref=gain_sum.at[:, pl.ds(block, piece)],
            dst_ref=gain_plane.at[r],
            send_sem=spread_send.at[r],
            recv_sem=spread_recv.at[r],
            device_id={"dp": peer // 2, "ctx": lax.rem(peer, 2)},
            device_id_type=MESH,
        )

    for r in range(total_shards - 1):
        spread(r).start()
    channel.drain()
    grad_qkv[...] = plane.gather(0, grad_qkv)
    grad_out[...] = plane.gather(1, own_out).T
    grad_gains[...] = gain_sum[:, pl.ds(pl.multiple_of(place * piece, piece), piece)]
    for r in range(total_shards - 1):
        spread(r).wait()
        grad_gains[...] += gain_plane[r]
    for owner in (0, n - 1):

        @pl.when(here == owner)
        def _():
            for made in line_copies(owner, range(1, n)):
                made.wait_send()


def turned_dot(left, right):
    return lax.dot_general(
        left, right, (((1,), (1,)), ((), ())), preferred_element_type=jnp.float32
    )


def greet_plane_and_lines(line_size, dp_size):
    here, row, core = lax.axis_index("tensor"), lax.axis_index("dp"), lax.axis_index("ctx")
    barrier = pltpu.get_barrier_semaphore()
    for hop in range(1, line_size):
        other = lax.rem(here + hop, line_size)
        pl.semaphore_signal(barrier, inc=1, device_id={"tensor": other}, device_id_type=MESH)
    total = 2 * dp_size
    for hop in range(1, total):
        peer = lax.rem(2 * row + core + hop, total)
        pl.semaphore_signal(
            barrier, inc=1, device_id={"dp": peer // 2, "ctx": lax.rem(peer, 2)}, device_id_type=MESH
        )
    pl.semaphore_wait(barrier, line_size - 1 + total - 1)


def back_two_call(line_size, dp_size, operands):
    gate, up, inner, gate_weight, up_weight, down_weight, upstream, normed, middle, gain = operands
    span, hidden = gate.shape
    width = upstream.shape[1]
    piece = width // (2 * dp_size)
    low, full = jnp.bfloat16, jnp.float32
    vmem, outside = pl.BlockSpec(memory_space=pltpu.VMEM), pl.BlockSpec(memory_space=pl.ANY)
    outs = [
        ((span, width), low), ((span, width), low), ((span // 2, width), full), ((1, width), full),
        ((piece, hidden), full), ((piece, hidden), full), ((hidden, piece), full),
    ]
    outs += [((dp_size - 1, piece, hidden), low)] * 3
    dma = pltpu.SemaphoreType.DMA
    others = (dp_size - 1, piece, hidden)
    scratch = [
        *[pltpu.VMEM((2 * span, hidden), low)] * 3,
        *[pltpu.VMEM((width, hidden), low)] * 2, pltpu.VMEM((hidden, width), low),
        pltpu.VMEM((span, width), low), pltpu.VMEM((span, width), low), pltpu.VMEM((span // 2, width), full),
        pltpu.VMEM((span, width // 2), low), pltpu.VMEM((span, width // 2), low),
        pltpu.VMEM((piece, hidden), full), pltpu.VMEM((piece, 2 * span), low),
        *[pltpu.VMEM(others, low)] * 3,
        pltpu.VMEM((span, width), full), pltpu.VMEM((span, width), low),
        dma((9,)), dma((3 + 2 * dp_size,)), dma((3 + 2 * dp_size,)),
        dma((3, dp_size - 1)), dma((3, dp_size - 1)),
        *line_scratch(span, width), *line_scratch(span, width),
    ]
    return pl.pallas_call(
        functools.partial(back_two_kernel, line_size, dp_size),
        out_shape=[jax.ShapeDtypeStruct(s, d) for s, d in outs],
        in_specs=[outside] * 9 + [vmem],
        out_specs=[vmem] * (len(outs) - 3) + [outside] * 3,
        scratch_shapes=scratch,
        compiler_params=pltpu.CompilerParams(
            collective_id=3, has_side_effects=True, vmem_limit_bytes=62 * MIB
        ),
    )(*operands)


def back_one_call(line_size, dp_size, operands):
    pre, mixed, normed = operands[:3]
    span, heads = mixed.shape
    width = normed.shape[1]
    piece = width // (2 * dp_size)
    low, full = jnp.bfloat16, jnp.float32
    vmem, outside = pl.BlockSpec(memory_space=pltpu.VMEM), pl.BlockSpec(memory_space=pl.ANY)
    wide = pre.shape[1]
    outs = [
        ((span, width), low), ((8, piece), full), ((piece, wide), full), ((heads, piece), full),
    ]
    dma = pltpu.SemaphoreType.DMA
    scratch = [
        pltpu.VMEM((2 * span, wide), low), pltpu.VMEM((2 * span, heads), low),
        pltpu.VMEM((span, width), low), pltpu.VMEM((span, width), low),
        pltpu.VMEM((span, width // 2), low), pltpu.VMEM((span, width // 2), low),
        pltpu.VMEM((piece, heads), full), pltpu.VMEM((piece, 2 * span), low),
        pltpu.VMEM((dp_size - 1, piece, wide), low), pltpu.VMEM((dp_size - 1, piece, heads), low),
        pltpu.VMEM((dp_size - 1, piece, wide), low), pltpu.VMEM((dp_size - 1, piece, heads), low),
        pltpu.VMEM((8, width), full), pltpu.VMEM((2, 8, width), full), pltpu.VMEM((8, width), full),
        pltpu.VMEM((2 * dp_size - 1, 8, piece), full),
        pltpu.VMEM((span, width), full),
        dma((4,)), dma((2 + 2 * dp_size,)), dma((2 + 2 * dp_size,)),
        dma((2, dp_size - 1)), dma((2, dp_size - 1)),
        dma((2, line_size - 1)), dma((2,)), dma((2 * dp_size - 1,)), dma((2 * dp_size - 1,)),
        *line_scratch(span, width),
    ]
    return pl.pallas_call(
        functools.partial(back_one_kernel, line_size, dp_size),
        out_shape=[jax.ShapeDtypeStruct(s, d) for s, d in outs],
        in_specs=[outside] * 4 + [vmem] * (len(operands) - 4),
        out_specs=[vmem] * len(outs),
        scratch_shapes=scratch,
        compiler_params=pltpu.CompilerParams(
            collective_id=4, has_side_effects=True, vmem_limit_bytes=50 * MIB
        ),
    )(*operands)


def line_call(kernel, line_size, rows, width, operands, outs, collective_id, limit):
    vmem = pl.BlockSpec(memory_space=pltpu.VMEM)
    return pl.pallas_call(
        functools.partial(kernel, line_size),
        out_shape=[jax.ShapeDtypeStruct(s, d) for s, d in outs],
        in_specs=[vmem] * len(operands),
        out_specs=[vmem] * len(outs),
        scratch_shapes=[pltpu.VMEM((rows, width), jnp.float32), *line_scratch(rows, width)],
        compiler_params=pltpu.CompilerParams(
            collective_id=collective_id, has_side_effects=True, vmem_limit_bytes=limit * MIB
        ),
    )(*operands)


def rotary_tables(positions):
    half_dim = HEAD_DIM // 2
    frequency = rope_base ** (-2.0 * jnp.arange(half_dim, dtype=jnp.float32) / HEAD_DIM)
    angles = positions.astype(jnp.float32)[..., None] * frequency
    return (jnp.cos(angles), jnp.sin(angles))


def rotate(values, cosine, sine_table):
    half_dim = values.shape[-1] // 2
    first = values[..., :half_dim]
    second = values[..., half_dim:]
    return jnp.concatenate(
        [first * cosine - second * sine_table, second * cosine + first * sine_table], axis=-1
    )


def visible(query_seg, key_seg, first_row):
    query_pos = first_row + jnp.arange(query_seg.shape[0], dtype=jnp.int32)
    key_pos = jnp.arange(key_seg.shape[0], dtype=jnp.int32)
    same_doc = query_seg[:, None] == key_seg[None, :]
    causal = key_pos[None, :] <= query_pos[:, None]
    usable = (key_seg[None, :] >= 0) | (key_pos[None, :] == query_pos[:, None])
    return same_doc & causal & usable


def plain_body(
    inputs,
    segment_ids,
    attention_gain,
    query_weight,
    key_weight,
    value_weight,
    out_weight,
    feedforward_gain,
    gate_weight,
    up_weight,
    down_weight,
    cotangent,
):
    seq_count, span_len, model_width = inputs.shape
    row_count = seq_count * span_len
    query_heads = query_weight.shape[1] // HEAD_DIM
    kv_heads = key_weight.shape[1] // HEAD_DIM
    group_size = query_heads // kv_heads
    score_scale = 1.0 / math.sqrt(HEAD_DIM)
    offset = lax.axis_index("ctx") * span_len
    whole_segments = lax.all_gather(segment_ids, "ctx", axis=1, tiled=True)
    own_positions = lax.dynamic_slice_in_dim(positions_of(whole_segments), offset, span_len, 1)
    cosine, sine_table = rotary_tables(own_positions)
    cosine = cosine[:, :, None, :]
    sine_table = sine_table[:, :, None, :]
    hidden = inputs.astype(jnp.float32).reshape(row_count, model_width)
    inverse_one = lax.rsqrt(jnp.mean(hidden * hidden, axis=-1, keepdims=True) + epsilon)
    unit_one = hidden * inverse_one
    normed = (unit_one * attention_gain).astype(jnp.bfloat16)
    query_rows = rotate(
        jnp.dot(normed, query_weight, preferred_element_type=jnp.float32).reshape(
            seq_count, span_len, query_heads, HEAD_DIM
        ),
        cosine,
        sine_table,
    ).astype(jnp.bfloat16)
    key_rows = rotate(
        jnp.dot(normed, key_weight, preferred_element_type=jnp.float32).reshape(
            seq_count, span_len, kv_heads, HEAD_DIM
        ),
        cosine,
        sine_table,
    ).astype(jnp.bfloat16)
    value_rows = (
        jnp.dot(normed, value_weight, preferred_element_type=jnp.float32)
        .astype(jnp.bfloat16)
        .reshape(seq_count, span_len, kv_heads, HEAD_DIM)
    )
    all_keys, all_values = (
        lax.all_gather(key_rows, "ctx", axis=1, tiled=True),
        lax.all_gather(value_rows, "ctx", axis=1, tiled=True),
    )

    def attend(block_items):
        query_block, key_block, value_block, query_seg, key_seg = block_items
        allowed = visible(query_seg, key_seg, offset)
        grouped = query_block.reshape(span_len, kv_heads, group_size, HEAD_DIM)
        raw_scores = jnp.einsum(
            "qhgd,khd->hgqk", grouped, key_block, preferred_element_type=jnp.float32
        )
        scores = jnp.where(allowed, raw_scores * score_scale, masked_score)
        row_peak = jnp.max(scores, axis=-1, keepdims=True)
        shifted_exp = jnp.exp(scores - row_peak)
        denominator = jnp.sum(shifted_exp, axis=-1, keepdims=True)
        attn_probs = (shifted_exp / denominator).astype(jnp.bfloat16)
        mixed_block = jnp.einsum(
            "hgqk,khd->qhgd", attn_probs, value_block, preferred_element_type=jnp.float32
        )
        return (
            mixed_block.astype(jnp.bfloat16).reshape(span_len, query_heads * HEAD_DIM),
            row_peak + jnp.log(denominator),
        )

    mixed_heads, log_sums = lax.map(
        attend, (query_rows, all_keys, all_values, segment_ids, whole_segments)
    )
    mixed_flat = mixed_heads.reshape(row_count, query_heads * HEAD_DIM)
    attended = lax.psum(
        jnp.dot(mixed_flat, out_weight, preferred_element_type=jnp.float32), "tensor"
    )
    middle = hidden + attended
    inverse_two = lax.rsqrt(jnp.mean(middle * middle, axis=-1, keepdims=True) + epsilon)
    unit_two = middle * inverse_two
    normed_two = (unit_two * feedforward_gain).astype(jnp.bfloat16)
    gate_pre = jnp.dot(normed_two, gate_weight, preferred_element_type=jnp.float32)
    up_pre = jnp.dot(normed_two, up_weight, preferred_element_type=jnp.float32)
    sigmoid_gate = jax.nn.sigmoid(gate_pre)
    inner_act = (gate_pre * sigmoid_gate * up_pre).astype(jnp.bfloat16)
    feed_out = lax.psum(
        jnp.dot(inner_act, down_weight, preferred_element_type=jnp.float32).astype(jnp.bfloat16),
        "tensor",
    ).astype(jnp.float32)
    layer_out = (middle + feed_out).astype(jnp.bfloat16).reshape(seq_count, span_len, model_width)
    upstream = cotangent.reshape(row_count, model_width)
    grad_down = jnp.dot(inner_act.T, upstream, preferred_element_type=jnp.float32)
    grad_inner = jnp.dot(upstream, down_weight.T, preferred_element_type=jnp.float32)
    grad_up_pre = (grad_inner * gate_pre * sigmoid_gate).astype(jnp.bfloat16)
    grad_gate_pre = (
        grad_inner * up_pre * sigmoid_gate * (1.0 + gate_pre * (1.0 - sigmoid_gate))
    ).astype(jnp.bfloat16)
    grad_gate = jnp.dot(normed_two.T, grad_gate_pre, preferred_element_type=jnp.float32)
    grad_up = jnp.dot(normed_two.T, grad_up_pre, preferred_element_type=jnp.float32)
    grad_normed_two = lax.psum(
        jnp.dot(grad_gate_pre, gate_weight.T, preferred_element_type=jnp.float32)
        + jnp.dot(grad_up_pre, up_weight.T, preferred_element_type=jnp.float32),
        "tensor",
    )
    grad_ffn_gain = jnp.sum(grad_normed_two * unit_two, axis=0)
    scaled_two = grad_normed_two * feedforward_gain
    grad_middle = upstream.astype(jnp.float32) + inverse_two * (
        scaled_two - unit_two * jnp.mean(scaled_two * unit_two, axis=-1, keepdims=True)
    )
    grad_attended = grad_middle.astype(jnp.bfloat16)
    grad_out_part = jnp.dot(mixed_flat.T, grad_attended, preferred_element_type=jnp.float32)
    grad_mixed = (
        jnp.dot(grad_attended, out_weight.T, preferred_element_type=jnp.float32)
        .astype(jnp.bfloat16)
        .reshape(seq_count, span_len, query_heads, HEAD_DIM)
    )

    def attend_back(block_items):
        query_block, key_block, value_block, query_seg, key_seg, grad_block, log_block = block_items
        allowed = visible(query_seg, key_seg, offset)
        grouped = query_block.reshape(span_len, kv_heads, group_size, HEAD_DIM)
        grad_grouped = grad_block.reshape(span_len, kv_heads, group_size, HEAD_DIM)
        raw_scores = jnp.einsum(
            "qhgd,khd->hgqk", grouped, key_block, preferred_element_type=jnp.float32
        )
        scores = jnp.where(allowed, raw_scores * score_scale, masked_score)
        attn_probs = jnp.exp(scores - log_block)
        rounded = attn_probs.astype(jnp.bfloat16)
        grad_values = jnp.einsum(
            "hgqk,qhgd->khd", rounded, grad_grouped, preferred_element_type=jnp.float32
        )
        grad_probs = jnp.einsum(
            "qhgd,khd->hgqk", grad_grouped, value_block, preferred_element_type=jnp.float32
        )
        row_dot = jnp.sum(attn_probs * grad_probs, axis=-1, keepdims=True)
        grad_scores = (attn_probs * (grad_probs - row_dot) * score_scale).astype(jnp.bfloat16)
        grad_queries = jnp.einsum(
            "hgqk,khd->qhgd", grad_scores, key_block, preferred_element_type=jnp.float32
        ).reshape(span_len, query_heads, HEAD_DIM)
        grad_keys = jnp.einsum(
            "hgqk,qhgd->khd", grad_scores, grouped, preferred_element_type=jnp.float32
        )
        return (grad_queries, grad_keys, grad_values)

    grad_queries, grad_keys, grad_values = lax.map(
        attend_back,
        (query_rows, all_keys, all_values, segment_ids, whole_segments, grad_mixed, log_sums),
    )
    own_grad_keys, own_grad_values = (
        lax.psum_scatter(grad_keys, "ctx", scatter_dimension=1, tiled=True),
        lax.psum_scatter(grad_values, "ctx", scatter_dimension=1, tiled=True),
    )
    grad_query_pre = (
        rotate(grad_queries, cosine, -sine_table)
        .astype(jnp.bfloat16)
        .reshape(row_count, query_heads * HEAD_DIM)
    )
    grad_key_pre = (
        rotate(own_grad_keys, cosine, -sine_table)
        .astype(jnp.bfloat16)
        .reshape(row_count, kv_heads * HEAD_DIM)
    )
    grad_value_pre = own_grad_values.astype(jnp.bfloat16).reshape(row_count, kv_heads * HEAD_DIM)
    grad_query = jnp.dot(normed.T, grad_query_pre, preferred_element_type=jnp.float32)
    grad_key = jnp.dot(normed.T, grad_key_pre, preferred_element_type=jnp.float32)
    grad_value = jnp.dot(normed.T, grad_value_pre, preferred_element_type=jnp.float32)
    grad_normed = lax.psum(
        (
            jnp.dot(grad_query_pre, query_weight.T, preferred_element_type=jnp.float32)
            + jnp.dot(grad_key_pre, key_weight.T, preferred_element_type=jnp.float32)
            + jnp.dot(grad_value_pre, value_weight.T, preferred_element_type=jnp.float32)
        ).astype(jnp.bfloat16),
        "tensor",
    ).astype(jnp.float32)
    grad_attn_gain = jnp.sum(grad_normed * unit_one, axis=0)
    scaled_one = grad_normed * attention_gain
    grad_hidden = grad_middle + inverse_one * (
        scaled_one - unit_one * jnp.mean(scaled_one * unit_one, axis=-1, keepdims=True)
    )
    grad_inputs = grad_hidden.astype(jnp.bfloat16).reshape(seq_count, span_len, model_width)
    reduced = (
        lax.psum_scatter(
            grad_attn_gain.astype(jnp.bfloat16), ("dp", "ctx"), scatter_dimension=0, tiled=True
        ).astype(jnp.float32),
        lax.psum_scatter(
            grad_query.astype(jnp.bfloat16), ("dp", "ctx"), scatter_dimension=0, tiled=True
        ).astype(jnp.float32),
        lax.psum_scatter(
            grad_key.astype(jnp.bfloat16), ("dp", "ctx"), scatter_dimension=0, tiled=True
        ).astype(jnp.float32),
        lax.psum_scatter(
            grad_value.astype(jnp.bfloat16), ("dp", "ctx"), scatter_dimension=0, tiled=True
        ).astype(jnp.float32),
        lax.psum_scatter(
            grad_out_part.astype(jnp.bfloat16), ("dp", "ctx"), scatter_dimension=1, tiled=True
        ).astype(jnp.float32),
        lax.psum_scatter(
            grad_ffn_gain.astype(jnp.bfloat16), ("dp", "ctx"), scatter_dimension=0, tiled=True
        ).astype(jnp.float32),
        lax.psum_scatter(
            grad_gate.astype(jnp.bfloat16), ("dp", "ctx"), scatter_dimension=0, tiled=True
        ).astype(jnp.float32),
        lax.psum_scatter(
            grad_up.astype(jnp.bfloat16), ("dp", "ctx"), scatter_dimension=0, tiled=True
        ).astype(jnp.float32),
        lax.psum_scatter(
            grad_down.astype(jnp.bfloat16), ("dp", "ctx"), scatter_dimension=1, tiled=True
        ).astype(jnp.float32),
    )
    return (
        layer_out,
        grad_inputs,
        reduced[0],
        reduced[1],
        reduced[2],
        reduced[3],
        reduced[4],
        reduced[5],
        reduced[6],
        reduced[7],
        reduced[8],
    )


def fast_body(
    inputs,
    segment_ids,
    attention_gain,
    query_weight,
    key_weight,
    value_weight,
    out_weight,
    feedforward_gain,
    gate_weight,
    up_weight,
    down_weight,
    cotangent,
):
    seq_count, span_len, model_width = inputs.shape
    row_count = seq_count * span_len
    query_heads = query_weight.shape[1] // HEAD_DIM
    kv_heads = key_weight.shape[1] // HEAD_DIM
    group_size = query_heads // kv_heads
    score_scale = 1.0 / math.sqrt(HEAD_DIM)
    offset = lax.axis_index("ctx") * span_len
    whole_segments = lax.all_gather(segment_ids, "ctx", axis=1, tiled=True)
    own_positions = lax.dynamic_slice_in_dim(positions_of(whole_segments), offset, span_len, 1)
    cosine, sine_table = rotary_tables(own_positions)
    cosine = cosine[:, :, None, :]
    sine_table = sine_table[:, :, None, :]
    hidden = inputs.astype(jnp.float32).reshape(row_count, model_width)
    inverse_one = lax.rsqrt(jnp.mean(hidden * hidden, axis=-1, keepdims=True) + epsilon)
    unit_one = hidden * inverse_one
    normed = (unit_one * attention_gain).astype(jnp.bfloat16)
    query_rows = rotate(
        jnp.dot(normed, query_weight, preferred_element_type=jnp.float32).reshape(
            seq_count, span_len, query_heads, HEAD_DIM
        ),
        cosine,
        sine_table,
    ).astype(jnp.bfloat16)
    key_rows = rotate(
        jnp.dot(normed, key_weight, preferred_element_type=jnp.float32).reshape(
            seq_count, span_len, kv_heads, HEAD_DIM
        ),
        cosine,
        sine_table,
    ).astype(jnp.bfloat16)
    value_rows = (
        jnp.dot(normed, value_weight, preferred_element_type=jnp.float32)
        .astype(jnp.bfloat16)
        .reshape(seq_count, span_len, kv_heads, HEAD_DIM)
    )
    all_keys, all_values = (
        lax.all_gather(key_rows, "ctx", axis=1, tiled=True),
        lax.all_gather(value_rows, "ctx", axis=1, tiled=True),
    )

    def attend(block_items):
        query_block, key_block, value_block, query_seg, key_seg = block_items
        allowed = visible(query_seg, key_seg, offset)
        grouped = query_block.reshape(span_len, kv_heads, group_size, HEAD_DIM)
        raw_scores = jnp.einsum(
            "qhgd,khd->hgqk", grouped, key_block, preferred_element_type=jnp.float32
        )
        scores = jnp.where(allowed, raw_scores * score_scale, masked_score)
        row_peak = jnp.max(scores, axis=-1, keepdims=True)
        shifted_exp = jnp.exp(scores - row_peak)
        denominator = jnp.sum(shifted_exp, axis=-1, keepdims=True)
        attn_probs = (shifted_exp / denominator).astype(jnp.bfloat16)
        mixed_block = jnp.einsum(
            "hgqk,khd->qhgd", attn_probs, value_block, preferred_element_type=jnp.float32
        )
        return (
            mixed_block.astype(jnp.bfloat16).reshape(span_len, query_heads * HEAD_DIM),
            row_peak + jnp.log(denominator),
        )

    mixed_heads, log_sums = lax.map(
        attend, (query_rows, all_keys, all_values, segment_ids, whole_segments)
    )
    mixed_flat = mixed_heads.reshape(row_count, query_heads * HEAD_DIM)
    line_size, dp_size = lax.axis_size("tensor"), lax.axis_size("dp")
    flat = (row_count, model_width)
    kept = (row_count // 2, model_width)
    gain_one = attention_gain.reshape(1, model_width)
    gain_two = feedforward_gain.reshape(1, model_width)
    flat_inputs = inputs.reshape(flat)
    normed_two, middle = line_call(
        out_kernel, line_size, *flat,
        (mixed_flat, out_weight, flat_inputs, gain_two),
        [(flat, jnp.bfloat16), (kept, jnp.float32)], 1, 28,
    )
    gate_pre = jnp.dot(normed_two, gate_weight, preferred_element_type=jnp.float32)
    up_pre = jnp.dot(normed_two, up_weight, preferred_element_type=jnp.float32)
    sigmoid_gate = jax.nn.sigmoid(gate_pre)
    inner_act = (gate_pre * sigmoid_gate * up_pre).astype(jnp.bfloat16)
    upstream = cotangent.reshape(row_count, model_width)
    grad_inner = jnp.dot(upstream, down_weight.T, preferred_element_type=jnp.float32)
    grad_up_pre = (grad_inner * gate_pre * sigmoid_gate).astype(jnp.bfloat16)
    grad_gate_pre = (
        grad_inner * up_pre * sigmoid_gate * (1.0 + gate_pre * (1.0 - sigmoid_gate))
    ).astype(jnp.bfloat16)
    layer_out, grad_attended, grad_middle, grad_ffn_gain, grad_gate, grad_up, grad_down, *_ = back_two_call(
        line_size, dp_size,
        (grad_gate_pre, grad_up_pre, inner_act, gate_weight, up_weight, down_weight,
         upstream, normed_two, middle, gain_two),
    )
    layer_out = layer_out.reshape(seq_count, span_len, model_width)
    grad_mixed = (
        jnp.dot(grad_attended, out_weight.T, preferred_element_type=jnp.float32)
        .astype(jnp.bfloat16)
        .reshape(seq_count, span_len, query_heads, HEAD_DIM)
    )

    def attend_back(block_items):
        query_block, key_block, value_block, query_seg, key_seg, grad_block, log_block = block_items
        allowed = visible(query_seg, key_seg, offset)
        grouped = query_block.reshape(span_len, kv_heads, group_size, HEAD_DIM)
        grad_grouped = grad_block.reshape(span_len, kv_heads, group_size, HEAD_DIM)
        raw_scores = jnp.einsum(
            "qhgd,khd->hgqk", grouped, key_block, preferred_element_type=jnp.float32
        )
        scores = jnp.where(allowed, raw_scores * score_scale, masked_score)
        attn_probs = jnp.exp(scores - log_block)
        rounded = attn_probs.astype(jnp.bfloat16)
        grad_values = jnp.einsum(
            "hgqk,qhgd->khd", rounded, grad_grouped, preferred_element_type=jnp.float32
        )
        grad_probs = jnp.einsum(
            "qhgd,khd->hgqk", grad_grouped, value_block, preferred_element_type=jnp.float32
        )
        row_dot = jnp.sum(attn_probs * grad_probs, axis=-1, keepdims=True)
        grad_scores = (attn_probs * (grad_probs - row_dot) * score_scale).astype(jnp.bfloat16)
        grad_queries = jnp.einsum(
            "hgqk,khd->qhgd", grad_scores, key_block, preferred_element_type=jnp.float32
        ).reshape(span_len, query_heads, HEAD_DIM)
        grad_keys = jnp.einsum(
            "hgqk,qhgd->khd", grad_scores, grouped, preferred_element_type=jnp.float32
        )
        return (grad_queries, grad_keys, grad_values)

    grad_queries, grad_keys, grad_values = lax.map(
        attend_back,
        (query_rows, all_keys, all_values, segment_ids, whole_segments, grad_mixed, log_sums),
    )
    own_grad_keys, own_grad_values = (
        lax.psum_scatter(grad_keys, "ctx", scatter_dimension=1, tiled=True),
        lax.psum_scatter(grad_values, "ctx", scatter_dimension=1, tiled=True),
    )
    grad_query_pre = (
        rotate(grad_queries, cosine, -sine_table)
        .astype(jnp.bfloat16)
        .reshape(row_count, query_heads * HEAD_DIM)
    )
    grad_key_pre = (
        rotate(own_grad_keys, cosine, -sine_table)
        .astype(jnp.bfloat16)
        .reshape(row_count, kv_heads * HEAD_DIM)
    )
    grad_value_pre = own_grad_values.astype(jnp.bfloat16).reshape(row_count, kv_heads * HEAD_DIM)
    grad_pre = jnp.concatenate([grad_query_pre, grad_key_pre, grad_value_pre], axis=1)
    grad_inputs, gains, grad_qkv, grad_out = back_one_call(
        line_size, dp_size,
        (grad_pre, mixed_flat, normed, grad_attended, query_weight, key_weight, value_weight,
         flat_inputs, grad_middle, gain_one, grad_ffn_gain),
    )
    heads_width, head_width = query_weight.shape[1], key_weight.shape[1]
    return (
        layer_out,
        grad_inputs.reshape(seq_count, span_len, model_width),
        gains[0],
        grad_qkv[:, :heads_width],
        grad_qkv[:, heads_width : heads_width + head_width],
        grad_qkv[:, heads_width + head_width :],
        grad_out,
        gains[1],
        grad_gate,
        grad_up,
        grad_down,
    )


def body(mesh, *arrays):
    inputs = arrays[0]
    span_len, model_width = inputs.shape[1:]
    dp_size, ctx_size, line_size = mesh.shape["dp"], mesh.shape["ctx"], mesh.shape["tensor"]
    piece = model_width // (dp_size * ctx_size)
    fits = inputs.shape[0] == 1 and ctx_size == 2 and dp_size > 1 and line_size > 1
    if fits and piece % 128 == 0 and span_len % (2 * CHUNK) == 0:
        return fast_body(*arrays)
    return plain_body(*arrays)


def solution(mesh):
    return jax.shard_map(
        functools.partial(body, mesh),
        mesh=mesh,
        in_specs=(
            P("dp", "ctx", None),
            P("dp", "ctx"),
            P(),
            P(None, "tensor"),
            P(None, "tensor"),
            P(None, "tensor"),
            P("tensor", None),
            P(),
            P(None, "tensor"),
            P(None, "tensor"),
            P("tensor", None),
            P("dp", "ctx", None),
        ),
        out_specs=(
            P("dp", "ctx", None),
            P("dp", "ctx", None),
            P(("dp", "ctx")),
            P(("dp", "ctx"), "tensor"),
            P(("dp", "ctx"), "tensor"),
            P(("dp", "ctx"), "tensor"),
            P("tensor", ("dp", "ctx")),
            P(("dp", "ctx")),
            P(("dp", "ctx"), "tensor"),
            P(("dp", "ctx"), "tensor"),
            P("tensor", ("dp", "ctx")),
        ),
        check_vma=False,
    )
```

```python
import functools
import math

import jax
import jax.numpy as jnp
from jax import lax
from jax.experimental import pallas as pl
from jax.experimental.pallas import tpu as pltpu
from jax.sharding import PartitionSpec as P

HEAD_DIM = 64


epsilon = 1e-05
rope_base = 10000.0
masked_score = -1e30


def positions_of(segment):
    token_index = jnp.arange(segment.shape[-1], dtype=jnp.int32)
    previous = jnp.concatenate([segment[..., :1] - 1, segment[..., :-1]], axis=-1)
    starts = jnp.where(segment != previous, token_index, 0)
    earlier = token_index[None, :] <= token_index[:, None]
    run_start = jnp.max(jnp.where(earlier, starts[..., None, :], 0), axis=-1)
    return token_index - run_start


MESH = pl.DeviceIdType.MESH
CHUNK = 32
MIB = 1 << 20
FRONT_MIB, BACK_MIB = 60, 62


def rotary_tables(positions):
    half_dim = HEAD_DIM // 2
    frequency = rope_base ** (-2.0 * jnp.arange(half_dim, dtype=jnp.float32) / HEAD_DIM)
    angles = positions.astype(jnp.float32)[..., None] * frequency
    return (jnp.cos(angles), jnp.sin(angles))


def rotate(values, cosine, sine_table):
    half_dim = values.shape[-1] // 2
    first = values[..., :half_dim]
    second = values[..., half_dim:]
    return jnp.concatenate(
        [first * cosine - second * sine_table, second * cosine + first * sine_table], axis=-1
    )


def visible(query_seg, key_seg, first_row):
    query_pos = first_row + jnp.arange(query_seg.shape[0], dtype=jnp.int32)
    key_pos = jnp.arange(key_seg.shape[0], dtype=jnp.int32)
    same_doc = query_seg[:, None] == key_seg[None, :]
    causal = key_pos[None, :] <= query_pos[:, None]
    usable = (key_seg[None, :] >= 0) | (key_pos[None, :] == query_pos[:, None])
    return same_doc & causal & usable


def turned_dot(left, right):
    return lax.dot_general(
        left, right, (((1,), (1,)), ((), ())), preferred_element_type=jnp.float32
    )


def remote(src, dst, send, recv, **device):
    return pltpu.make_async_remote_copy(
        src_ref=src, dst_ref=dst, send_sem=send, recv_sem=recv, device_id=device, device_id_type=MESH
    )


class Line:
    def __init__(self, line_size, own, finish, place, out_ref, held, acc_send, acc_recv, back_send, back_recv):
        self.last = line_size - 1
        self.here = lax.axis_index("tensor")
        self.own, self.finish, self.place = own, finish, place
        self.out_ref, self.held = out_ref, held
        self.acc_sems, self.back_sems = (acc_send, acc_recv), (back_send, back_recv)
        self.count = held.shape[1]

    def parts(self, stream):
        if stream == 0:
            return self.here, self.here + 1, self.here - 1
        return self.last - self.here, self.here - 1, self.here + 1

    def acc_copy(self, stream, i, target):
        ref = self.held.at[stream, i]
        return remote(ref, ref, self.acc_sems[0].at[stream, i], self.acc_sems[1].at[stream, i], tensor=target)

    def rows_of(self, stream, i):
        return pl.ds(pl.multiple_of(self.place(stream, i), CHUNK), CHUNK)

    def back_copy(self, stream, i, target):
        ref = self.out_ref.at[self.rows_of(stream, i)]
        return remote(ref, ref, self.back_sems[0].at[stream, i], self.back_sems[1].at[stream, i], tensor=target)

    def step(self, k, begin=0, size=None):
        last, held = self.last, self.held
        size = self.count if size is None else size
        for stream in (0, 1):
            place, after, before = self.parts(stream)
            inside = (k >= place) & (k < place + size)
            i = begin + k - place

            @pl.when(inside & (place == 0))
            def _():
                held[stream, i] = self.own(stream, i).astype(jnp.bfloat16)
                self.acc_copy(stream, i, after).start()

            @pl.when(inside & (place > 0) & (place < last))
            def _():
                self.acc_copy(stream, i, after).wait_recv()
                held[stream, i] = (held[stream, i].astype(jnp.float32) + self.own(stream, i)).astype(jnp.bfloat16)
                self.acc_copy(stream, i, after).start()

            @pl.when(inside & (place == last))
            def _():
                self.acc_copy(stream, i, before).wait_recv()
                total = held[stream, i].astype(jnp.float32) + self.own(stream, i)
                self.out_ref[self.rows_of(stream, i)] = self.finish(stream, i, total).astype(jnp.bfloat16)
                self.back_copy(stream, i, before).start()

            back = k - (2 * last - place)
            j = begin + back

            @pl.when((back >= 0) & (back < size) & (place < last))
            def _():
                self.back_copy(stream, j, before).wait_recv()

                @pl.when(place > 0)
                def _():
                    self.back_copy(stream, j, before).start()

    def drain(self):
        def sent(i, carry):
            for stream in (0, 1):
                place, after, before = self.parts(stream)

                @pl.when(place < self.last)
                def _():
                    self.acc_copy(stream, i, after).wait_send()

                @pl.when(place > 0)
                def _():
                    self.back_copy(stream, i, before).wait_send()

            return carry

        lax.fori_loop(0, self.count, sent, 0)


def line_scratch(rows, width):
    count = rows // 2 // CHUNK
    return [
        pltpu.VMEM((2, count, CHUNK, width), jnp.bfloat16),
        *[pltpu.SemaphoreType.DMA((2, count))] * 4,
    ]


def greet(line, core, plane, full_line=False):
    here, row, side = lax.axis_index("tensor"), lax.axis_index("dp"), lax.axis_index("ctx")
    barrier = pltpu.get_barrier_semaphore()
    peers = 0

    def call(**device):
        pl.semaphore_signal(barrier, inc=1, device_id=device, device_id_type=MESH)

    if full_line:
        for hop in range(1, line):
            call(tensor=lax.rem(here + hop, line))
        peers += line - 1
    else:

        @pl.when(here > 0)
        def _():
            call(tensor=here - 1)

        @pl.when(here < line - 1)
        def _():
            call(tensor=here + 1)

        peers = jnp.where(here > 0, 1, 0) + jnp.where(here < line - 1, 1, 0)
    if plane:
        for hop in range(1, 2 * plane):
            peer = lax.rem(2 * row + side + hop, 2 * plane)
            call(dp=peer // 2, ctx=lax.rem(peer, 2))
        peers += 2 * plane - 1
    elif core:
        call(ctx=1 - side)
        peers += 1
    pl.semaphore_wait(barrier, peers)


def kept_rows(i):
    return pl.ds(pl.multiple_of(i * CHUNK, CHUNK), CHUNK)


def rotate_lanes(values, cosine, signed_sine, back=False):
    lane = lax.broadcasted_iota(jnp.int32, values.shape, 1)
    swapped = jnp.where(
        lax.rem(lane, HEAD_DIM) < HEAD_DIM // 2,
        pltpu.roll(values, 128 - HEAD_DIM // 2, 1),
        pltpu.roll(values, HEAD_DIM // 2, 1),
    )
    turn = swapped * signed_sine
    return values * cosine - turn if back else values * cosine + turn


def key_lanes(values, turned):
    lane = lax.broadcasted_iota(jnp.int32, values.shape, 1)
    return jnp.where(lane < HEAD_DIM, turned, values)


def fill_bias(bias, seg_col, seg_row, first, keys, block):
    key_seg = seg_col[0:keys]
    query_seg = seg_row[:, first : first + block]
    key_pos = lax.broadcasted_iota(jnp.int32, (keys, block), 0)
    query_pos = first + lax.broadcasted_iota(jnp.int32, (keys, block), 1)
    usable = (key_seg >= 0) | (key_pos == query_pos)
    allowed = (key_seg == query_seg) & (key_pos <= query_pos) & usable
    bias[0:keys, :] = jnp.where(allowed, 0.0, masked_score)


def wide_tiles(width):
    return width // 256, width % 256


def inverse_rms(values):
    return lax.rsqrt(jnp.mean(values * values, axis=-1, keepdims=True) + epsilon)


def front_kernel(
    n,
    inputs_any, cosine, signed_sine, seg_col, seg_row, gain_one, gain_two,
    query_weight_any, kv_weight_any, out_weight_any, gate_weight_any, up_weight_any, down_weight_any, upstream_any,
    query_out, kv_out, log_out, mixed_out, normed_out, normed_two_out, gate_out, up_out, inner_out, second_out,
    attended_out, middle_out, grad_middle_out, gain_out,
    inputs, normed, query_weight, kv_weight, out_weight, query, kv, kv_turned, logs, mixed, bias,
    gate_weight, up_weight, down_weight, upstream, grad_inner, normed_two, gate, up, inner,
    partial, second, attended, middle, grad_middle,
    load_sems, store_sems, core_send, core_recv, *line_refs,
):
    span, width = inputs.shape
    hidden = gate.shape[1]
    core = lax.axis_index("ctx")
    half, block = span // 2, span // 4
    line_one, line_two = line_refs[:5], line_refs[5:]
    count = line_one[0].shape[1]
    part = count // 2

    def load(at, src, dst):
        made = pltpu.make_async_copy(src, dst, load_sems.at[at])
        made.start()
        return made

    def ordered(stream, i):
        return (i // part) * half + stream * block + lax.rem(i, part) * CHUNK

    def moved(at):
        return (0, 2, 1, 3)[at] * block

    load_inputs = load(0, inputs_any, inputs)
    load_query = load(1, query_weight_any, query_weight)
    load_kv = load(2, kv_weight_any, kv_weight)
    load_out = load(3, out_weight_any, out_weight)
    load_up = [
        load(4 + b, upstream_any.at[pl.ds(b * block, block)], upstream.at[pl.ds(moved(b), block)]) for b in range(4)
    ]
    load_down = load(8, down_weight_any, down_weight)
    load_gate = load(9, gate_weight_any, gate_weight)
    load_up_weight = load(10, up_weight_any, up_weight)
    greet(n, True, 0)
    load_inputs.wait()

    def norm_rows(b, carry):
        rows = pl.ds(pl.multiple_of(b * 64, 64), 64)
        value = inputs[rows].astype(jnp.float32)
        normed[rows] = (value * inverse_rms(value) * gain_one[...]).astype(jnp.bfloat16)
        return carry

    lax.fori_loop(0, span // 64, norm_rows, 0)
    load_kv.wait()
    own_rows = pl.ds(pl.multiple_of(core * span, span), span)
    raw = jnp.dot(normed[...], kv_weight[...], preferred_element_type=jnp.float32)
    kv[own_rows] = key_lanes(raw, rotate_lanes(raw, cosine[...], signed_sine[...])).astype(jnp.bfloat16)

    def kv_copy():
        return remote(kv.at[own_rows], kv.at[own_rows], core_send.at[0], core_recv.at[0], ctx=1 - core)

    def kv_arrival():
        rows = pl.ds(0, span)
        return remote(kv.at[rows], kv.at[rows], core_send.at[0], core_recv.at[0], ctx=1 - core)

    @pl.when(core == 0)
    def _():
        kv_copy().start()

    load_query.wait()
    for low in range(0, span, half):
        rows = slice(low, low + half)
        raw = jnp.dot(normed[rows], query_weight[...], preferred_element_type=jnp.float32)
        for lanes in range(0, raw.shape[1], 128):
            turned = rotate_lanes(raw[:, lanes : lanes + 128], cosine[rows], signed_sine[rows])
            query[rows, lanes : lanes + 128] = turned.astype(jnp.bfloat16) * (HEAD_DIM ** -0.5)

    @pl.when(core == 1)
    def _():
        kv_arrival().wait_recv()

    kv_turned[...] = kv[...].T

    def attend(side, at):
        keys = side * span + (at + 1) * half
        rows = slice(at * half, (at + 1) * half)
        fill_bias(bias, seg_col, seg_row, side * span + at * half, keys, half)

        def pair(index, carry):
            lanes = pl.ds(pl.multiple_of(index * 128, 128), 128)
            both = query[rows, lanes]
            outs = []
            for which in (0, 1):
                scores = turned_dot(kv[0:keys, 0:HEAD_DIM], both[:, which * HEAD_DIM : (which + 1) * HEAD_DIM])
                scores = scores + bias[0:keys, :]
                peak = jnp.max(scores, axis=0, keepdims=True)
                grown = jnp.exp(scores - peak)
                total = jnp.sum(grown, axis=0, keepdims=True)
                logs[pl.ds(2 * index + which, 1), rows] = peak + jnp.log(total)
                out = jnp.dot(
                    kv_turned[HEAD_DIM : 2 * HEAD_DIM, 0:keys],
                    grown.astype(jnp.bfloat16),
                    preferred_element_type=jnp.float32,
                )
                outs.append(out / total)
            mixed[rows, lanes] = jnp.concatenate(outs, axis=0).T.astype(jnp.bfloat16)
            return carry

        lax.fori_loop(0, query.shape[1] // 128, pair, 0)

    for side in (0, 1):

        @pl.when(core == side)
        def _():
            attend(side, 0)
            attend(side, 1)

    load_out.wait()

    def out_tile(t, carry):
        columns = pl.ds(pl.multiple_of(t * 512, 512), 512)
        for b in (0, 2):
            value = jnp.dot(
                mixed[b * block : (b + 2) * block], out_weight[:, columns], preferred_element_type=jnp.float32
            )
            partial[moved(b) : moved(b) + block, columns] = value[:block]
            partial[moved(b + 1) : moved(b + 1) + block, columns] = value[block:]
        return carry

    lax.fori_loop(0, width // 512, out_tile, 0)

    def rows_at(start):
        return pl.ds(pl.multiple_of(start, CHUNK), CHUNK)

    def own(stream, i):
        return partial[rows_at(ordered(stream, i))]

    def finish_one(stream, i, total):
        value = inputs[rows_at((stream * count + i) * CHUNK)].astype(jnp.float32) + total
        middle[kept_rows(i)] = value
        return value * inverse_rms(value) * gain_two[...]

    gain_out[...] = jnp.zeros_like(gain_out)

    def finish_two(stream, i, total):
        value = middle[kept_rows(i)]
        inverse = inverse_rms(value)
        unit = value * inverse
        gain_out[0:1, :] += jnp.sum(total * unit, axis=0, keepdims=True)
        scaled = total * gain_two[...]
        result = upstream[rows_at(ordered(stream, i))].astype(jnp.float32) + inverse * (
            scaled - unit * jnp.mean(scaled * unit, axis=-1, keepdims=True)
        )
        grad_middle[kept_rows(i)] = result
        return result

    first = Line(n, own, finish_one, ordered, normed_two, *line_one)
    then = Line(n, own, finish_two, ordered, attended, *line_two)
    tiles, rest = wide_tiles(hidden)
    tile_count = tiles + (1 if rest else 0)

    def each_tile(t, work):
        @pl.when(t < tiles)
        def _():
            work(pl.ds(pl.multiple_of(t * 256, 256), 256))

        if rest:

            @pl.when(t == tiles)
            def _():
                work(pl.ds(tiles * 256, rest))

    def inner_tile(columns):
        grad_inner[:, columns] = turned_dot(upstream[...], down_weight[columns, :])

    def forward_tile(rows, columns):
        gated = jnp.dot(normed_two[rows], gate_weight[:, columns], preferred_element_type=jnp.float32)
        upped = jnp.dot(normed_two[rows], up_weight[:, columns], preferred_element_type=jnp.float32)
        sig = jax.nn.sigmoid(gated)
        act = gated * sig
        grad = grad_inner[rows, columns]
        inner[rows, columns] = (act * upped).astype(jnp.bfloat16)
        up[rows, columns] = (grad * act).astype(jnp.bfloat16)
        gate[rows, columns] = (grad * upped * sig * (1.0 + gated * (1.0 - sig))).astype(jnp.bfloat16)

    def back_tile(rows, t):
        columns = pl.ds(pl.multiple_of(t * 512, 512), 512)
        partial[rows, columns] = turned_dot(gate[rows], gate_weight[columns, :]) + turned_dot(
            up[rows], up_weight[columns, :]
        )

    def second_tile(rows, t):
        columns = pl.ds(pl.multiple_of(t * 512, 512), 512)
        second[rows, columns] = jnp.dot(
            inner[rows], down_weight[:, columns], preferred_element_type=jnp.float32
        ).astype(jnp.bfloat16)

    last = n - 1
    base_one = part + 2 * last
    base_two = max(count + 2 * last, base_one + 4)
    steps = base_two + 3 + part + 2 * last
    each = -(-tile_count // 2)

    def store(at, src, dst):
        return pltpu.make_async_copy(src, dst, store_sems.at[at])

    def stores(at, src, dst):
        return [
            store(at + b, src.at[pl.ds(moved(b), block)], dst.at[pl.ds(b * block, block)]) for b in range(4)
        ]

    early = [
        store(0, query, query_out), store(1, kv, kv_out), store(2, logs, log_out), store(3, mixed, mixed_out),
        store(4, normed, normed_out),
    ]
    hidden_stores = [(5, normed_two, normed_two_out), (9, gate, gate_out), (13, up, up_out), (17, inner, inner_out)]

    for made in early:
        made.start()

    def step(k, carry):
        first.step(k)
        then.step(k - (base_one + 3), 0, part)
        then.step(k - (base_two + 3), part, part)

        @pl.when(k == 0)
        def _():
            for made in load_up:
                made.wait()
            load_down.wait()
            load_gate.wait()
            load_up_weight.wait()

        @pl.when((k >= 1) & (k <= tile_count))
        def _():
            each_tile(k - 1, inner_tile)

        late = jnp.where(k >= base_two, 1, 0)
        phase = k - jnp.where(k >= base_two, base_two, base_one)
        rows = pl.ds(pl.multiple_of(late * half, half), half)

        @pl.when((phase >= 0) & (phase < 2))
        def _():
            def tile(t, carry):
                each_tile(t, functools.partial(forward_tile, rows))
                return carry

            lax.fori_loop(phase * each, jnp.minimum((phase + 1) * each, tile_count), tile, 0)

        @pl.when(phase == 2)
        def _():
            def tile(t, carry):
                back_tile(rows, t)
                return carry

            lax.fori_loop(0, width // 512, tile, 0)

        @pl.when(k == base_two + 3)
        def _():
            for at, src, dst in hidden_stores:
                for made in stores(at, src, dst):
                    made.start()

        after = k - (base_two + 4)

        @pl.when((after >= 0) & (after < 4))
        def _():
            for low in (0, half):
                second_tile(pl.ds(low, half), after)

        return carry

    lax.fori_loop(0, steps, step, 0)
    late_stores = [
        *stores(21, second, second_out), *stores(25, attended, attended_out),
        store(29, middle, middle_out), store(30, grad_middle, grad_middle_out),
    ]
    for made in late_stores:
        made.start()
    first.drain()
    then.drain()

    @pl.when(core == 0)
    def _():
        kv_copy().wait_send()

    for made in [*early, *late_stores]:
        made.wait()
    for at, src, dst in hidden_stores:
        for made in stores(at, src, dst):
            made.wait()


def front_call(line_size, operands):
    inputs = operands[0]
    query_weight, kv_weight, out_weight, gate_weight = operands[7:11]
    span, width = inputs.shape
    heads, hidden = query_weight.shape[1], gate_weight.shape[1]
    low, full = jnp.bfloat16, jnp.float32
    vmem, outside = pl.BlockSpec(memory_space=pltpu.VMEM), pl.BlockSpec(memory_space=pl.ANY)
    dma = pltpu.SemaphoreType.DMA
    outs = [
        ((span, heads), low), ((2 * span, 128), low), ((heads // HEAD_DIM, span), full), ((span, heads), low),
        ((span, width), low), ((span, width), low), *[((span, hidden), low)] * 3, ((span, width), low),
        ((span, width), low), ((span // 2, width), full), ((span // 2, width), full), ((8, width), full),
    ]
    scratch = [
        pltpu.VMEM((span, width), low), pltpu.VMEM((span, width), low), pltpu.VMEM((width, heads), low),
        pltpu.VMEM((width, 128), low), pltpu.VMEM((heads, width), low), pltpu.VMEM((span, heads), low),
        pltpu.VMEM((2 * span, 128), low), pltpu.VMEM((128, 2 * span), low),
        pltpu.VMEM((heads // HEAD_DIM, span), full), pltpu.VMEM((span, heads), low),
        pltpu.VMEM((2 * span, span // 2), full),
        pltpu.VMEM((width, hidden), low), pltpu.VMEM((width, hidden), low), pltpu.VMEM((hidden, width), low),
        pltpu.VMEM((span, width), low), pltpu.VMEM((span, hidden), full), pltpu.VMEM((span, width), low),
        *[pltpu.VMEM((span, hidden), low)] * 3,
        pltpu.VMEM((span, width), full), pltpu.VMEM((span, width), low), pltpu.VMEM((span, width), low),
        pltpu.VMEM((span // 2, width), full), pltpu.VMEM((span // 2, width), full),
        dma((11,)), dma((31,)), dma((1,)), dma((1,)),
        *line_scratch(span, width), *line_scratch(span, width),
    ]
    return pl.pallas_call(
        functools.partial(front_kernel, line_size),
        out_shape=[jax.ShapeDtypeStruct(s, d) for s, d in outs],
        in_specs=[outside] + [vmem] * 6 + [outside] * 7,
        out_specs=[outside] * 13 + [vmem],
        scratch_shapes=scratch,
        compiler_params=pltpu.CompilerParams(
            collective_id=1, has_side_effects=True, vmem_limit_bytes=FRONT_MIB * MIB
        ),
    )(*operands)


RING = 5


def back_kernel(
    n, dp_size,
    query_any, kv_any, logs, mixed_any, cosine, signed_sine, seg_col, seg_row, inputs_any, normed_any, normed_two_any,
    gate_any, up_any, inner_any, second_any, attended_any, middle_any, grad_middle_any, gain_one, gain_two_grad,
    query_weight_any, kv_weight_any, out_weight_any, upstream_any,
    layer_out, grad_inputs, grad_gains, grad_qkv, grad_out, grad_gate, grad_up, grad_down,
    land_gate, land_up, land_down, land_qkv, land_out,
    query, kv, kv_turned, grad_mixed, mixed, attended, normed_cols, attended_cols, two_cols, upstream_cols,
    gate, up, inner, pre, query_weight, kv_weight, out_weight, grad_middle, middle, inputs,
    ring, send_qkv, send_out, own_down, own_out, turned, bias, kv_grad, kv_grad_other,
    gain_line, gain_land, gain_sum, gain_plane,
    load_sems, core_send, core_recv, ring_send, ring_recv, plane_send, plane_recv, line_send, line_recv,
    spread_send, spread_recv, *line_refs,
):
    span, width = attended.shape
    heads, piece = query.shape[1], turned.shape[0]
    here, row, core = lax.axis_index("tensor"), lax.axis_index("dp"), lax.axis_index("ctx")
    half = span // 2
    line_out, line_in = line_refs[:5], line_refs[5:]
    count = line_out[0].shape[1]
    last = n - 1
    loads = []

    def load(src, dst):
        made = pltpu.make_async_copy(src, dst, load_sems.at[len(loads)])
        made.start()
        loads.append(made)
        return made

    own_half = pl.ds(pl.multiple_of(jnp.where(here == 0, half, 0), half), half)
    first_loads = [
        load(second_any, layer_out), load(middle_any, middle),
        load(attended_any, attended), load(out_weight_any, out_weight), load(query_any, query), load(kv_any, kv),
    ]

    def load_cols(src, dst):
        made = []
        for q in range(dp_size):
            block = pl.multiple_of((2 * q + core) * piece, piece)
            made.append(load(src.at[:, pl.ds(block, piece)], dst.at[pl.ds(0, span), pl.ds(q * piece, piece)]))
        return made

    ffn_loads = [
        load(gate_any, gate.at[pl.ds(0, span)]), load(up_any, up.at[pl.ds(0, span)]),
        load(inner_any, inner.at[pl.ds(0, span)]), *load_cols(normed_two_any, two_cols),
        *load_cols(upstream_any, upstream_cols),
    ]
    late_loads = [
        load(query_weight_any, query_weight), load(kv_weight_any, kv_weight),
        load(grad_middle_any, grad_middle), load(inputs_any.at[own_half], inputs),
        load(mixed_any, mixed.at[pl.ds(0, span)]), *load_cols(normed_any, normed_cols),
        *load_cols(attended_any, attended_cols),
    ]
    greet(n, True, dp_size, full_line=True)
    slots = []

    def swap(src, dst):
        at = len(slots)
        slots.append(at)
        return remote(src, dst, core_send.at[at], core_recv.at[at], ctx=1 - core)

    def swap_rows(src, dst):
        return swap(src, dst.at[pl.ds(span, span)])

    def swap_cols(src, dst):
        made = []
        for q in range(dp_size):
            block = pl.multiple_of((2 * q + 1 - core) * piece, piece)
            made.append(
                swap(src.at[:, pl.ds(block, piece)], dst.at[pl.ds(span, span), pl.ds(q * piece, piece)])
            )
        return made

    ffn_swaps = [
        swap_rows(gate_any, gate), *swap_cols(normed_two_any, two_cols), swap_rows(up_any, up),
        swap_rows(inner_any, inner), *swap_cols(upstream_any, upstream_cols),
    ]
    late_swaps = [
        swap_rows(mixed_any, mixed), *swap_cols(attended_any, attended_cols), *swap_cols(normed_any, normed_cols),
    ]
    for made in [*ffn_swaps, *late_swaps]:
        made.start()
    pre_slot, kv_slot = len(slots), len(slots) + 1

    def pre_swap():
        return remote(
            pre.at[pl.ds(0, span)], pre.at[pl.ds(span, span)], core_send.at[pre_slot], core_recv.at[pre_slot],
            ctx=1 - core,
        )

    def kv_swap():
        return remote(
            kv_grad.at[pl.ds(0, span)], kv_grad_other, core_send.at[kv_slot], core_recv.at[kv_slot], ctx=1 - core
        )

    gain_line[...] = jnp.zeros_like(gain_line)
    gain_line[1:2, :] = gain_two_grad[0:1, :]
    kv_grad[...] = jnp.zeros_like(kv_grad)
    for made in first_loads:
        made.wait()
    kv_turned[...] = kv[...].T

    def rows_at(start):
        return pl.ds(pl.multiple_of(start, CHUNK), CHUNK)

    def plain(stream, i):
        return (stream * count + i) * CHUNK

    def finish_out(stream, i, total):
        return middle[kept_rows(i)] + total

    def finish_in(stream, i, total):
        hidden = inputs[kept_rows(i)].astype(jnp.float32)
        inverse = inverse_rms(hidden)
        unit = hidden * inverse
        gain_line[0:1, :] += jnp.sum(total * unit, axis=0, keepdims=True)
        scaled = total * gain_one[...]
        return grad_middle[kept_rows(i)] + inverse * (
            scaled - unit * jnp.mean(scaled * unit, axis=-1, keepdims=True)
        )

    out_line = Line(
        n, lambda s, i: layer_out[rows_at(plain(s, i))].astype(jnp.float32), finish_out, plain, layer_out, *line_out
    )
    in_line = Line(
        n, lambda s, i: grad_inputs[rows_at(plain(s, i))].astype(jnp.float32), finish_in, plain, grad_inputs, *line_in
    )

    def attend_back(side, at, index):
        keys = side * span + (at + 1) * half
        rows = slice(at * half, (at + 1) * half)
        lanes = pl.ds(pl.multiple_of(index * 128, 128), 128)

        @pl.when(index == 0)
        def _():
            fill_bias(bias, seg_col, seg_row, side * span + at * half, keys, half)

        both_query, both_grad = query[rows, lanes], grad_mixed[rows, lanes]
        outs, parts = [], None
        for which in (0, 1):
            head = slice(which * HEAD_DIM, (which + 1) * HEAD_DIM)
            query_head, grad_head = both_query[:, head], both_grad[:, head]
            scores = turned_dot(kv[0:keys, 0:HEAD_DIM], query_head) + bias[0:keys, :]
            probs = jnp.exp(scores - logs[pl.ds(2 * index + which, 1), rows])
            grad_probs = turned_dot(kv[0:keys, HEAD_DIM : 2 * HEAD_DIM], grad_head)
            both = probs * grad_probs
            grad_scores = (both - probs * jnp.sum(both, axis=0, keepdims=True)).astype(jnp.bfloat16)
            grad_key = jnp.dot(grad_scores, query_head, preferred_element_type=jnp.float32)
            grad_value = jnp.dot(probs.astype(jnp.bfloat16), grad_head, preferred_element_type=jnp.float32)
            part = jnp.concatenate([grad_key, grad_value], axis=1)
            parts = part if parts is None else parts + part
            outs.append(
                jnp.dot(kv_turned[0:HEAD_DIM, 0:keys], grad_scores, preferred_element_type=jnp.float32)
            )
        kv_grad[0:keys] += parts
        grad_query = jnp.concatenate(outs, axis=0).T * (HEAD_DIM ** -0.5)
        pre[rows, lanes] = rotate_lanes(grad_query, cosine[rows], signed_sine[rows], back=True).astype(jnp.bfloat16)

    pairs = heads // 128
    tasks = 2 * pairs

    def attend_task(task):
        for side in (0, 1):
            for at in (0, 1):

                @pl.when((core == side) & (task // pairs == at))
                def _():
                    attend_back(side, at, lax.rem(task, pairs))

    own_grad = pl.ds(pl.multiple_of(core * span, span), span)

    def finish_pre():
        @pl.when(core == 0)
        def _():
            kv_swap().wait_recv()
            kv_grad[0:span] += kv_grad_other[...]

        raw = kv_grad[own_grad]
        turned_back = rotate_lanes(raw, cosine[...], signed_sine[...], back=True)
        pre[0:span, heads : heads + 128] = key_lanes(raw, turned_back).astype(jnp.bfloat16)

    def in_products():
        def tile(t, carry):
            columns = pl.ds(pl.multiple_of(t * 512, 512), 512)
            for low in (0, half):
                rows = slice(low, low + half)
                grad_inputs[rows, columns] = (
                    turned_dot(pre[rows, 0:heads], query_weight[columns, :])
                    + turned_dot(pre[rows, heads : heads + 128], kv_weight[columns, :])
                ).astype(jnp.bfloat16)
            return carry

        lax.fori_loop(0, width // 512, tile, 0)

    def peer_of(r):
        return lax.rem(row + 1 + r, dp_size)

    def turn(r, cols):
        block = pl.multiple_of(peer_of(r) * piece, piece)
        turned[...] = cols[:, pl.ds(block, piece)].T

    def tiles_of(stacked):
        wide = stacked.shape[1]
        return [(low, min(low + 384, wide)) for low in range(0, wide, 384)]

    def piece_value(stacked, low, high):
        return jnp.dot(turned[...], stacked[:, low:high], preferred_element_type=jnp.float32)

    landings = (land_gate, land_up, land_down)

    def ring_copy(w, r, at):
        return remote(
            ring.at[lax.rem(at, RING)], landings[w].at[r], ring_send.at[at], ring_recv.at[w, r], dp=peer_of(r)
        )

    def ring_piece(w, r, stacked, own):
        at = 3 * r + w

        @pl.when(r < dp_size - 1)
        def _():
            slot = lax.rem(at, RING)

            @pl.when(at >= RING)
            def _():
                ring_copy(w, r, at - RING).wait_send()

            for low, high in tiles_of(stacked):
                ring[slot, :, low:high] = piece_value(stacked, low, high).astype(jnp.bfloat16)
            ring_copy(w, r, at).start()

        @pl.when(r == dp_size - 1)
        def _():
            for low, high in tiles_of(stacked):
                own[:, low:high] = piece_value(stacked, low, high)

    sends, lands = (send_qkv, send_out), (land_qkv, land_out)

    def plane_copy(w, r):
        return remote(sends[w].at[r], lands[w].at[r], plane_send.at[w, r], plane_recv.at[w, r], dp=peer_of(r))

    def plane_piece(w, r, stacked, own):
        @pl.when(r < dp_size - 1)
        def _():
            for low, high in tiles_of(stacked):
                sends[w][r, :, low:high] = piece_value(stacked, low, high).astype(jnp.bfloat16)
            plane_copy(w, r).start()

        @pl.when(r == dp_size - 1)
        def _():
            for low, high in tiles_of(stacked):
                own[:, low:high] = piece_value(stacked, low, high)

    def line_copies(owner, hops):
        slot = 0 if owner == 0 else 1
        return [
            remote(
                gain_line, gain_land.at[slot], line_send.at[slot, hop - 1], line_recv.at[slot],
                tensor=owner + hop if owner == 0 else owner - hop,
            )
            for hop in hops
        ]

    lag = tasks + 2
    ffn_tasks = 3 * dp_size
    out_base = max(ffn_tasks + 1, lag + 1)
    steps = max(lag + count + 2 * last, out_base + dp_size)

    def step(k, carry):
        out_line.step(k)
        in_line.step(k - lag)

        @pl.when(k == 0)
        def _():
            grad_mixed[...] = turned_dot(attended[...], out_weight[...]).astype(jnp.bfloat16)

        @pl.when((k >= 1) & (k <= tasks))
        def _():
            attend_task(k - 1)

        @pl.when((k == tasks) & (core == 1))
        def _():
            kv_swap().start()

        @pl.when(k == 1)
        def _():
            for made in ffn_loads:
                made.wait()
            for made in ffn_swaps:
                made.wait()

        @pl.when(k == tasks)
        def _():
            for made in late_loads:
                made.wait()
            for made in late_swaps:
                made.wait()

        @pl.when(k == tasks + 1)
        def _():
            finish_pre()
            in_products()
            pre_swap().start()

        task = k - 1
        r, kind = task // 3, lax.rem(task, 3)
        ffn = (task >= 0) & (task < ffn_tasks)

        @pl.when(ffn & (kind == 0))
        def _():
            turn(r, two_cols)
            ring_piece(0, r, gate, grad_gate)

        @pl.when(ffn & (kind == 1))
        def _():
            ring_piece(1, r, up, grad_up)

        @pl.when(ffn & (kind == 2))
        def _():
            turn(r, upstream_cols)
            ring_piece(2, r, inner, own_down)

        @pl.when(k == out_base)
        def _():
            pre_swap().wait()

        at = k - out_base

        @pl.when((at >= 0) & (at < dp_size))
        def _():
            turn(at, attended_cols)
            plane_piece(1, at, mixed, own_out)
            turn(at, normed_cols)
            plane_piece(0, at, pre, grad_qkv)

        @pl.when(k == lag + count + last - 1)
        def _():
            for owner in (0, last):

                @pl.when(here == owner)
                def _():
                    for made in line_copies(owner, range(1, n)):
                        made.start()

        return carry

    lax.fori_loop(0, steps, step, 0)
    shard = width // (2 * dp_size)
    gain_sum[...] = jnp.zeros_like(gain_sum)
    for owner in (0, last):
        slot = 0 if owner == 0 else 1

        @pl.when(here == owner)
        def _():
            gain_sum[...] += gain_line[...]

        @pl.when(here != owner)
        def _():
            line_copies(owner, (1,))[0].wait_recv()
            gain_sum[...] += gain_land[slot]

    shards = 2 * dp_size
    place = 2 * row + core

    def spread(r):
        peer = lax.rem(place + 1 + r, shards)
        block = pl.multiple_of(peer * shard, shard)
        return remote(
            gain_sum.at[:, pl.ds(block, shard)], gain_plane.at[r], spread_send.at[r], spread_recv.at[r],
            dp=peer // 2, ctx=lax.rem(peer, 2),
        )

    for r in range(shards - 1):
        spread(r).start()
    out_line.drain()
    in_line.drain()

    @pl.when(core == 1)
    def _():
        kv_swap().wait_send()

    pads = (gate, up, inner)
    fetches = []
    for r in range(dp_size - 1):
        for w in range(3):
            ring_copy(w, r, 3 * r + w).wait_recv()
            fetch = pltpu.make_async_copy(
                landings[w].at[r], pads[w].at[pl.ds(r * piece, piece)], load_sems.at[len(fetches)]
            )
            fetch.start()
            fetches.append(fetch)
    for at in range(max(0, 3 * (dp_size - 1) - RING), 3 * (dp_size - 1)):
        ring_copy(at % 3, at // 3, at).wait_send()
    for fetch in fetches:
        fetch.wait()

    def landed(w):
        total = pads[w][0:piece].astype(jnp.float32)
        for r in range(1, dp_size - 1):
            total = total + pads[w][r * piece : (r + 1) * piece].astype(jnp.float32)
        return total

    grad_gate[...] += landed(0)
    grad_up[...] += landed(1)
    grad_down[...] = (own_down[...] + landed(2)).T
    fetches = []
    for r in range(dp_size - 1):
        for w in (0, 1):
            plane_copy(w, r).wait()
            fetch = pltpu.make_async_copy(lands[w].at[r], sends[w].at[r], load_sems.at[len(fetches)])
            fetch.start()
            fetches.append(fetch)
    for fetch in fetches:
        fetch.wait()
    for r in range(dp_size - 1):
        grad_qkv[...] += send_qkv[r].astype(jnp.float32)
        own_out[...] += send_out[r].astype(jnp.float32)
    grad_out[...] = own_out[...].T
    grad_gains[...] = gain_sum[:, pl.ds(pl.multiple_of(place * shard, shard), shard)]
    for r in range(shards - 1):
        spread(r).wait()
        grad_gains[...] += gain_plane[r]
    for owner in (0, last):

        @pl.when(here == owner)
        def _():
            for made in line_copies(owner, range(1, n)):
                made.wait_send()


def back_call(line_size, dp_size, operands):
    query, kv, logs, mixed = operands[:4]
    gate = operands[11]
    span, heads = query.shape
    width, hidden = operands[9].shape[1], gate.shape[1]
    piece = width // (2 * dp_size)
    wide = heads + 128
    low, full = jnp.bfloat16, jnp.float32
    vmem, outside = pl.BlockSpec(memory_space=pltpu.VMEM), pl.BlockSpec(memory_space=pl.ANY)
    dma = pltpu.SemaphoreType.DMA
    others = dp_size - 1
    outs = [
        ((span, width), low), ((span, width), low), ((8, piece), full), ((piece, wide), full), ((heads, piece), full),
        ((piece, hidden), full), ((piece, hidden), full), ((hidden, piece), full),
        *[((others, piece, hidden), low)] * 3, ((others, piece, wide), low), ((others, piece, heads), low),
    ]
    core_copies = 4 + 4 * dp_size + 2
    scratch = [
        pltpu.VMEM((span, heads), low), pltpu.VMEM((2 * span, 128), low), pltpu.VMEM((128, 2 * span), low),
        pltpu.VMEM((span, heads), low), pltpu.VMEM((2 * span, heads), low), pltpu.VMEM((span, width), low),
        *[pltpu.VMEM((2 * span, width // 2), low)] * 4,
        *[pltpu.VMEM((2 * span, hidden), low)] * 3, pltpu.VMEM((2 * span, wide), low),
        pltpu.VMEM((width, heads), low), pltpu.VMEM((width, 128), low), pltpu.VMEM((heads, width), low),
        pltpu.VMEM((span // 2, width), full), pltpu.VMEM((span // 2, width), full), pltpu.VMEM((span // 2, width), low),
        pltpu.VMEM((RING, piece, hidden), low), pltpu.VMEM((others, piece, wide), low),
        pltpu.VMEM((others, piece, heads), low), pltpu.VMEM((piece, hidden), full), pltpu.VMEM((piece, heads), full),
        pltpu.VMEM((piece, 2 * span), low), pltpu.VMEM((2 * span, span // 2), full),
        pltpu.VMEM((2 * span, 128), full), pltpu.VMEM((span, 128), full),
        pltpu.VMEM((8, width), full), pltpu.VMEM((2, 8, width), full), pltpu.VMEM((8, width), full),
        pltpu.VMEM((2 * dp_size - 1, 8, piece), full),
        dma((16 + 4 * dp_size + 6,)), dma((core_copies,)), dma((core_copies,)),
        dma((3 * others,)), dma((3, others)), dma((2, others)), dma((2, others)),
        dma((2, line_size - 1)), dma((2,)), dma((2 * dp_size - 1,)), dma((2 * dp_size - 1,)),
        *line_scratch(span, width), *line_scratch(span, width),
    ]
    spaces = [outside, outside, vmem, outside, vmem, vmem, vmem, vmem] + [outside] * 10 + [vmem, vmem] + [outside] * 4
    return pl.pallas_call(
        functools.partial(back_kernel, line_size, dp_size),
        out_shape=[jax.ShapeDtypeStruct(s, d) for s, d in outs],
        in_specs=spaces,
        out_specs=[vmem] * 8 + [outside] * 5,
        scratch_shapes=scratch,
        compiler_params=pltpu.CompilerParams(
            collective_id=2, has_side_effects=True, vmem_limit_bytes=BACK_MIB * MIB
        ),
    )(*operands)


def plain_body(
    inputs,
    segment_ids,
    attention_gain,
    query_weight,
    key_weight,
    value_weight,
    out_weight,
    feedforward_gain,
    gate_weight,
    up_weight,
    down_weight,
    cotangent,
):
    seq_count, span_len, model_width = inputs.shape
    row_count = seq_count * span_len
    query_heads = query_weight.shape[1] // HEAD_DIM
    kv_heads = key_weight.shape[1] // HEAD_DIM
    group_size = query_heads // kv_heads
    score_scale = 1.0 / math.sqrt(HEAD_DIM)
    offset = lax.axis_index("ctx") * span_len
    whole_segments = lax.all_gather(segment_ids, "ctx", axis=1, tiled=True)
    own_positions = lax.dynamic_slice_in_dim(positions_of(whole_segments), offset, span_len, 1)
    cosine, sine_table = rotary_tables(own_positions)
    cosine = cosine[:, :, None, :]
    sine_table = sine_table[:, :, None, :]
    hidden = inputs.astype(jnp.float32).reshape(row_count, model_width)
    inverse_one = lax.rsqrt(jnp.mean(hidden * hidden, axis=-1, keepdims=True) + epsilon)
    unit_one = hidden * inverse_one
    normed = (unit_one * attention_gain).astype(jnp.bfloat16)
    query_rows = rotate(
        jnp.dot(normed, query_weight, preferred_element_type=jnp.float32).reshape(
            seq_count, span_len, query_heads, HEAD_DIM
        ),
        cosine,
        sine_table,
    ).astype(jnp.bfloat16)
    key_rows = rotate(
        jnp.dot(normed, key_weight, preferred_element_type=jnp.float32).reshape(
            seq_count, span_len, kv_heads, HEAD_DIM
        ),
        cosine,
        sine_table,
    ).astype(jnp.bfloat16)
    value_rows = (
        jnp.dot(normed, value_weight, preferred_element_type=jnp.float32)
        .astype(jnp.bfloat16)
        .reshape(seq_count, span_len, kv_heads, HEAD_DIM)
    )
    all_keys, all_values = (
        lax.all_gather(key_rows, "ctx", axis=1, tiled=True),
        lax.all_gather(value_rows, "ctx", axis=1, tiled=True),
    )

    def attend(block_items):
        query_block, key_block, value_block, query_seg, key_seg = block_items
        allowed = visible(query_seg, key_seg, offset)
        grouped = query_block.reshape(span_len, kv_heads, group_size, HEAD_DIM)
        raw_scores = jnp.einsum(
            "qhgd,khd->hgqk", grouped, key_block, preferred_element_type=jnp.float32
        )
        scores = jnp.where(allowed, raw_scores * score_scale, masked_score)
        row_peak = jnp.max(scores, axis=-1, keepdims=True)
        shifted_exp = jnp.exp(scores - row_peak)
        denominator = jnp.sum(shifted_exp, axis=-1, keepdims=True)
        attn_probs = (shifted_exp / denominator).astype(jnp.bfloat16)
        mixed_block = jnp.einsum(
            "hgqk,khd->qhgd", attn_probs, value_block, preferred_element_type=jnp.float32
        )
        return (
            mixed_block.astype(jnp.bfloat16).reshape(span_len, query_heads * HEAD_DIM),
            row_peak + jnp.log(denominator),
        )

    mixed_heads, log_sums = lax.map(
        attend, (query_rows, all_keys, all_values, segment_ids, whole_segments)
    )
    mixed_flat = mixed_heads.reshape(row_count, query_heads * HEAD_DIM)
    attended = lax.psum(
        jnp.dot(mixed_flat, out_weight, preferred_element_type=jnp.float32), "tensor"
    )
    middle = hidden + attended
    inverse_two = lax.rsqrt(jnp.mean(middle * middle, axis=-1, keepdims=True) + epsilon)
    unit_two = middle * inverse_two
    normed_two = (unit_two * feedforward_gain).astype(jnp.bfloat16)
    gate_pre = jnp.dot(normed_two, gate_weight, preferred_element_type=jnp.float32)
    up_pre = jnp.dot(normed_two, up_weight, preferred_element_type=jnp.float32)
    sigmoid_gate = jax.nn.sigmoid(gate_pre)
    inner_act = (gate_pre * sigmoid_gate * up_pre).astype(jnp.bfloat16)
    feed_out = lax.psum(
        jnp.dot(inner_act, down_weight, preferred_element_type=jnp.float32).astype(jnp.bfloat16),
        "tensor",
    ).astype(jnp.float32)
    layer_out = (middle + feed_out).astype(jnp.bfloat16).reshape(seq_count, span_len, model_width)
    upstream = cotangent.reshape(row_count, model_width)
    grad_down = jnp.dot(inner_act.T, upstream, preferred_element_type=jnp.float32)
    grad_inner = jnp.dot(upstream, down_weight.T, preferred_element_type=jnp.float32)
    grad_up_pre = (grad_inner * gate_pre * sigmoid_gate).astype(jnp.bfloat16)
    grad_gate_pre = (
        grad_inner * up_pre * sigmoid_gate * (1.0 + gate_pre * (1.0 - sigmoid_gate))
    ).astype(jnp.bfloat16)
    grad_gate = jnp.dot(normed_two.T, grad_gate_pre, preferred_element_type=jnp.float32)
    grad_up = jnp.dot(normed_two.T, grad_up_pre, preferred_element_type=jnp.float32)
    grad_normed_two = lax.psum(
        jnp.dot(grad_gate_pre, gate_weight.T, preferred_element_type=jnp.float32)
        + jnp.dot(grad_up_pre, up_weight.T, preferred_element_type=jnp.float32),
        "tensor",
    )
    grad_ffn_gain = jnp.sum(grad_normed_two * unit_two, axis=0)
    scaled_two = grad_normed_two * feedforward_gain
    grad_middle = upstream.astype(jnp.float32) + inverse_two * (
        scaled_two - unit_two * jnp.mean(scaled_two * unit_two, axis=-1, keepdims=True)
    )
    grad_attended = grad_middle.astype(jnp.bfloat16)
    grad_out_part = jnp.dot(mixed_flat.T, grad_attended, preferred_element_type=jnp.float32)
    grad_mixed = (
        jnp.dot(grad_attended, out_weight.T, preferred_element_type=jnp.float32)
        .astype(jnp.bfloat16)
        .reshape(seq_count, span_len, query_heads, HEAD_DIM)
    )

    def attend_back(block_items):
        query_block, key_block, value_block, query_seg, key_seg, grad_block, log_block = block_items
        allowed = visible(query_seg, key_seg, offset)
        grouped = query_block.reshape(span_len, kv_heads, group_size, HEAD_DIM)
        grad_grouped = grad_block.reshape(span_len, kv_heads, group_size, HEAD_DIM)
        raw_scores = jnp.einsum(
            "qhgd,khd->hgqk", grouped, key_block, preferred_element_type=jnp.float32
        )
        scores = jnp.where(allowed, raw_scores * score_scale, masked_score)
        attn_probs = jnp.exp(scores - log_block)
        rounded = attn_probs.astype(jnp.bfloat16)
        grad_values = jnp.einsum(
            "hgqk,qhgd->khd", rounded, grad_grouped, preferred_element_type=jnp.float32
        )
        grad_probs = jnp.einsum(
            "qhgd,khd->hgqk", grad_grouped, value_block, preferred_element_type=jnp.float32
        )
        row_dot = jnp.sum(attn_probs * grad_probs, axis=-1, keepdims=True)
        grad_scores = (attn_probs * (grad_probs - row_dot) * score_scale).astype(jnp.bfloat16)
        grad_queries = jnp.einsum(
            "hgqk,khd->qhgd", grad_scores, key_block, preferred_element_type=jnp.float32
        ).reshape(span_len, query_heads, HEAD_DIM)
        grad_keys = jnp.einsum(
            "hgqk,qhgd->khd", grad_scores, grouped, preferred_element_type=jnp.float32
        )
        return (grad_queries, grad_keys, grad_values)

    grad_queries, grad_keys, grad_values = lax.map(
        attend_back,
        (query_rows, all_keys, all_values, segment_ids, whole_segments, grad_mixed, log_sums),
    )
    own_grad_keys, own_grad_values = (
        lax.psum_scatter(grad_keys, "ctx", scatter_dimension=1, tiled=True),
        lax.psum_scatter(grad_values, "ctx", scatter_dimension=1, tiled=True),
    )
    grad_query_pre = (
        rotate(grad_queries, cosine, -sine_table)
        .astype(jnp.bfloat16)
        .reshape(row_count, query_heads * HEAD_DIM)
    )
    grad_key_pre = (
        rotate(own_grad_keys, cosine, -sine_table)
        .astype(jnp.bfloat16)
        .reshape(row_count, kv_heads * HEAD_DIM)
    )
    grad_value_pre = own_grad_values.astype(jnp.bfloat16).reshape(row_count, kv_heads * HEAD_DIM)
    grad_query = jnp.dot(normed.T, grad_query_pre, preferred_element_type=jnp.float32)
    grad_key = jnp.dot(normed.T, grad_key_pre, preferred_element_type=jnp.float32)
    grad_value = jnp.dot(normed.T, grad_value_pre, preferred_element_type=jnp.float32)
    grad_normed = lax.psum(
        (
            jnp.dot(grad_query_pre, query_weight.T, preferred_element_type=jnp.float32)
            + jnp.dot(grad_key_pre, key_weight.T, preferred_element_type=jnp.float32)
            + jnp.dot(grad_value_pre, value_weight.T, preferred_element_type=jnp.float32)
        ).astype(jnp.bfloat16),
        "tensor",
    ).astype(jnp.float32)
    grad_attn_gain = jnp.sum(grad_normed * unit_one, axis=0)
    scaled_one = grad_normed * attention_gain
    grad_hidden = grad_middle + inverse_one * (
        scaled_one - unit_one * jnp.mean(scaled_one * unit_one, axis=-1, keepdims=True)
    )
    grad_inputs = grad_hidden.astype(jnp.bfloat16).reshape(seq_count, span_len, model_width)
    reduced = (
        lax.psum_scatter(
            grad_attn_gain.astype(jnp.bfloat16), ("dp", "ctx"), scatter_dimension=0, tiled=True
        ).astype(jnp.float32),
        lax.psum_scatter(
            grad_query.astype(jnp.bfloat16), ("dp", "ctx"), scatter_dimension=0, tiled=True
        ).astype(jnp.float32),
        lax.psum_scatter(
            grad_key.astype(jnp.bfloat16), ("dp", "ctx"), scatter_dimension=0, tiled=True
        ).astype(jnp.float32),
        lax.psum_scatter(
            grad_value.astype(jnp.bfloat16), ("dp", "ctx"), scatter_dimension=0, tiled=True
        ).astype(jnp.float32),
        lax.psum_scatter(
            grad_out_part.astype(jnp.bfloat16), ("dp", "ctx"), scatter_dimension=1, tiled=True
        ).astype(jnp.float32),
        lax.psum_scatter(
            grad_ffn_gain.astype(jnp.bfloat16), ("dp", "ctx"), scatter_dimension=0, tiled=True
        ).astype(jnp.float32),
        lax.psum_scatter(
            grad_gate.astype(jnp.bfloat16), ("dp", "ctx"), scatter_dimension=0, tiled=True
        ).astype(jnp.float32),
        lax.psum_scatter(
            grad_up.astype(jnp.bfloat16), ("dp", "ctx"), scatter_dimension=0, tiled=True
        ).astype(jnp.float32),
        lax.psum_scatter(
            grad_down.astype(jnp.bfloat16), ("dp", "ctx"), scatter_dimension=1, tiled=True
        ).astype(jnp.float32),
    )
    return (
        layer_out,
        grad_inputs,
        reduced[0],
        reduced[1],
        reduced[2],
        reduced[3],
        reduced[4],
        reduced[5],
        reduced[6],
        reduced[7],
        reduced[8],
    )


def fast_body(
    inputs, segment_ids, attention_gain, query_weight, key_weight, value_weight, out_weight, feedforward_gain,
    gate_weight, up_weight, down_weight, cotangent,
):
    _, span_len, model_width = inputs.shape
    line_size, dp_size = lax.axis_size("tensor"), lax.axis_size("dp")
    offset = lax.axis_index("ctx") * span_len
    whole_segments = lax.all_gather(segment_ids, "ctx", axis=1, tiled=True)
    positions = lax.dynamic_slice_in_dim(positions_of(whole_segments), offset, span_len, 1)
    cosine, sine_table = rotary_tables(positions[0])
    cosine = jnp.tile(cosine, (1, 4))
    signed_sine = jnp.concatenate([-sine_table, sine_table, -sine_table, sine_table], axis=1)
    seg_col, seg_row = whole_segments.reshape(-1, 1), whole_segments.reshape(1, -1)
    flat_inputs = inputs.reshape(span_len, model_width)
    upstream = cotangent.reshape(span_len, model_width)
    gain_one, gain_two = attention_gain.reshape(1, -1), feedforward_gain.reshape(1, -1)
    kv_weight = jnp.concatenate([key_weight, value_weight], axis=1)
    (
        query, kv, logs, mixed, normed, normed_two, gate, up, inner, second, attended, middle, grad_middle, gain_grad,
    ) = front_call(
        line_size,
        (
            flat_inputs, cosine, signed_sine, seg_col, seg_row, gain_one, gain_two,
            query_weight, kv_weight, out_weight, gate_weight, up_weight, down_weight, upstream,
        ),
    )
    layer_out, grad_inputs, gains, grad_qkv, grad_out, grad_gate, grad_up, grad_down, *_ = back_call(
        line_size, dp_size,
        (
            query, kv, logs, mixed, cosine, signed_sine, seg_col, seg_row, flat_inputs, normed, normed_two,
            gate, up, inner, second, attended, middle, grad_middle, gain_one, gain_grad,
            query_weight, kv_weight, out_weight, upstream,
        ),
    )
    heads, head = query_weight.shape[1], key_weight.shape[1]
    shape = (1, span_len, model_width)
    return (
        layer_out.reshape(shape), grad_inputs.reshape(shape), gains[0],
        grad_qkv[:, :heads], grad_qkv[:, heads : heads + head], grad_qkv[:, heads + head :],
        grad_out, gains[1], grad_gate, grad_up, grad_down,
    )


def body(mesh, *arrays):
    inputs = arrays[0]
    span_len, model_width = inputs.shape[1:]
    dp_size, ctx_size, line_size = mesh.shape["dp"], mesh.shape["ctx"], mesh.shape["tensor"]
    piece = model_width // (dp_size * ctx_size)
    fits = inputs.shape[0] == 1 and ctx_size == 2 and dp_size > 1 and line_size > 1
    if fits and piece % 128 == 0 and span_len % (2 * CHUNK) == 0:
        return fast_body(*arrays)
    return plain_body(*arrays)


def solution(mesh):
    return jax.shard_map(
        functools.partial(body, mesh),
        mesh=mesh,
        in_specs=(
            P("dp", "ctx", None),
            P("dp", "ctx"),
            P(),
            P(None, "tensor"),
            P(None, "tensor"),
            P(None, "tensor"),
            P("tensor", None),
            P(),
            P(None, "tensor"),
            P(None, "tensor"),
            P("tensor", None),
            P("dp", "ctx", None),
        ),
        out_specs=(
            P("dp", "ctx", None),
            P("dp", "ctx", None),
            P(("dp", "ctx")),
            P(("dp", "ctx"), "tensor"),
            P(("dp", "ctx"), "tensor"),
            P(("dp", "ctx"), "tensor"),
            P("tensor", ("dp", "ctx")),
            P(("dp", "ctx")),
            P(("dp", "ctx"), "tensor"),
            P(("dp", "ctx"), "tensor"),
            P("tensor", ("dp", "ctx")),
        ),
        check_vma=False,
    )
```

```python
import functools
import math

import jax
import jax.numpy as jnp
from jax import lax
from jax.experimental import pallas as pl
from jax.experimental.pallas import tpu as pltpu
from jax.sharding import PartitionSpec as P

HEAD_DIM = 64


epsilon = 1e-05
rope_base = 10000.0
masked_score = -1e30


def positions_of(segment):
    token_index = jnp.arange(segment.shape[-1], dtype=jnp.int32)
    previous = jnp.concatenate([segment[..., :1] - 1, segment[..., :-1]], axis=-1)
    starts = jnp.where(segment != previous, token_index, 0)
    earlier = token_index[None, :] <= token_index[:, None]
    run_start = jnp.max(jnp.where(earlier, starts[..., None, :], 0), axis=-1)
    return token_index - run_start


MESH = pl.DeviceIdType.MESH
CHUNK = 16
HOP = 2
MIB = 1 << 20
FRONT_MIB, BACK_MIB = 62, 62


def rotary_tables(positions):
    half_dim = HEAD_DIM // 2
    frequency = rope_base ** (-2.0 * jnp.arange(half_dim, dtype=jnp.float32) / HEAD_DIM)
    angles = positions.astype(jnp.float32)[..., None] * frequency
    return (jnp.cos(angles), jnp.sin(angles))


def rotate(values, cosine, sine_table):
    half_dim = values.shape[-1] // 2
    first = values[..., :half_dim]
    second = values[..., half_dim:]
    return jnp.concatenate(
        [first * cosine - second * sine_table, second * cosine + first * sine_table], axis=-1
    )


def visible(query_seg, key_seg, first_row):
    query_pos = first_row + jnp.arange(query_seg.shape[0], dtype=jnp.int32)
    key_pos = jnp.arange(key_seg.shape[0], dtype=jnp.int32)
    same_doc = query_seg[:, None] == key_seg[None, :]
    causal = key_pos[None, :] <= query_pos[:, None]
    usable = (key_seg[None, :] >= 0) | (key_pos[None, :] == query_pos[:, None])
    return same_doc & causal & usable


def turned_dot(left, right):
    return lax.dot_general(
        left, right, (((1,), (1,)), ((), ())), preferred_element_type=jnp.float32
    )


def remote(src, dst, send, recv, **device):
    return pltpu.make_async_remote_copy(
        src_ref=src, dst_ref=dst, send_sem=send, recv_sem=recv, device_id=device, device_id_type=MESH
    )


class Line:
    def __init__(self, line_size, own, finish, place, out_ref, held, acc_send, acc_recv, back_send, back_recv):
        self.last = line_size - 1
        self.here = lax.axis_index("tensor")
        self.own, self.finish, self.place = own, finish, place
        self.out_ref, self.held = out_ref, held
        self.acc_sems, self.back_sems = (acc_send, acc_recv), (back_send, back_recv)
        self.count = held.shape[1]

    def parts(self, stream):
        if stream == 0:
            return self.here, self.here + 1, self.here - 1
        return self.last - self.here, self.here - 1, self.here + 1

    def acc_copy(self, stream, i, target):
        ref = self.held.at[stream, i]
        return remote(ref, ref, self.acc_sems[0].at[stream, i], self.acc_sems[1].at[stream, i], tensor=target)

    def rows_of(self, stream, i):
        return pl.ds(pl.multiple_of(self.place(stream, i), CHUNK), CHUNK)

    def back_copy(self, stream, i, target):
        ref = self.out_ref.at[self.rows_of(stream, i)]
        return remote(ref, ref, self.back_sems[0].at[stream, i], self.back_sems[1].at[stream, i], tensor=target)

    def step(self, k, begin=0, size=None):
        last, held = self.last, self.held
        size = self.count if size is None else size
        for stream in (0, 1):
            place, after, before = self.parts(stream)
            due = k - HOP * place
            inside = (due >= 0) & (due < size)
            i = begin + due

            @pl.when(inside & (place == 0))
            def _():
                held[stream, i] = self.own(stream, i).astype(jnp.bfloat16)
                self.acc_copy(stream, i, after).start()

            @pl.when(inside & (place > 0) & (place < last))
            def _():
                self.acc_copy(stream, i, after).wait_recv()
                held[stream, i] = (held[stream, i].astype(jnp.float32) + self.own(stream, i)).astype(jnp.bfloat16)
                self.acc_copy(stream, i, after).start()

            @pl.when(inside & (place == last))
            def _():
                self.acc_copy(stream, i, before).wait_recv()
                total = held[stream, i].astype(jnp.float32) + self.own(stream, i)
                self.out_ref[self.rows_of(stream, i)] = self.finish(stream, i, total).astype(jnp.bfloat16)
                self.back_copy(stream, i, before).start()

            back = k - HOP * (2 * last - place)
            j = begin + back

            @pl.when((back >= 0) & (back < size) & (place < last))
            def _():
                self.back_copy(stream, j, before).wait_recv()

                @pl.when(place > 0)
                def _():
                    self.back_copy(stream, j, before).start()

    def drain(self):
        def sent(i, carry):
            for stream in (0, 1):
                place, after, before = self.parts(stream)

                @pl.when(place < self.last)
                def _():
                    self.acc_copy(stream, i, after).wait_send()

                @pl.when(place > 0)
                def _():
                    self.back_copy(stream, i, before).wait_send()

            return carry

        lax.fori_loop(0, self.count, sent, 0)


def line_scratch(rows, width):
    count = rows // 2 // CHUNK
    return [
        pltpu.VMEM((2, count, CHUNK, width), jnp.bfloat16),
        *[pltpu.SemaphoreType.DMA((2, count))] * 4,
    ]


def greet(line, core, plane, full_line=False):
    here, row, side = lax.axis_index("tensor"), lax.axis_index("dp"), lax.axis_index("ctx")
    barrier = pltpu.get_barrier_semaphore()
    peers = 0

    def call(**device):
        pl.semaphore_signal(barrier, inc=1, device_id=device, device_id_type=MESH)

    if full_line:
        for hop in range(1, line):
            call(tensor=lax.rem(here + hop, line))
        peers += line - 1
    else:

        @pl.when(here > 0)
        def _():
            call(tensor=here - 1)

        @pl.when(here < line - 1)
        def _():
            call(tensor=here + 1)

        peers = jnp.where(here > 0, 1, 0) + jnp.where(here < line - 1, 1, 0)
    if plane:
        for hop in range(1, 2 * plane):
            peer = lax.rem(2 * row + side + hop, 2 * plane)
            call(dp=peer // 2, ctx=lax.rem(peer, 2))
        peers += 2 * plane - 1
    elif core:
        call(ctx=1 - side)
        peers += 1
    pl.semaphore_wait(barrier, peers)


def kept_rows(i):
    return pl.ds(pl.multiple_of(i * CHUNK, CHUNK), CHUNK)


def rotate_lanes(values, cosine, signed_sine, back=False):
    lane = lax.broadcasted_iota(jnp.int32, values.shape, 1)
    swapped = jnp.where(
        lax.rem(lane, HEAD_DIM) < HEAD_DIM // 2,
        pltpu.roll(values, 128 - HEAD_DIM // 2, 1),
        pltpu.roll(values, HEAD_DIM // 2, 1),
    )
    turn = swapped * signed_sine
    return values * cosine - turn if back else values * cosine + turn


def key_lanes(values, turned):
    lane = lax.broadcasted_iota(jnp.int32, values.shape, 1)
    return jnp.where(lane < HEAD_DIM, turned, values)


def fill_bias(bias, seg_col, seg_row, first, keys, block):
    key_seg = seg_col[0:keys]
    query_seg = seg_row[:, first : first + block]
    key_pos = lax.broadcasted_iota(jnp.int32, (keys, block), 0)
    query_pos = first + lax.broadcasted_iota(jnp.int32, (keys, block), 1)
    usable = (key_seg >= 0) | (key_pos == query_pos)
    allowed = (key_seg == query_seg) & (key_pos <= query_pos) & usable
    bias[0:keys, :] = jnp.where(allowed, 0.0, masked_score)


def wide_tiles(width):
    return width // 256, width % 256


def inverse_rms(values):
    return lax.rsqrt(jnp.mean(values * values, axis=-1, keepdims=True) + epsilon)


def front_kernel(
    n, dp_size,
    inputs_any, segments, frequency, gain_one, gain_two,
    query_weight_any, key_weight_any, value_weight_any, out_weight_any, gate_weight_any, up_weight_any, down_weight_any, upstream_any,
    seg_out, cosine_out, sine_out, query_out, kv_out, log_out, mixed_out, normed_out, normed_two_out, up_out, inner_out, second_out,
    attended_out, middle_out, grad_middle_out, land_gate, gain_out, own_gate,
    seg_all, seg_row, seg_col, cosine, signed_sine,
    inputs, normed, query_weight, kv_weight, out_weight, query, kv, kv_turned, logs, mixed, bias,
    gate_weight, up_weight, down_weight, upstream, grad_inner, normed_two, gate, up, inner,
    partial, middle, grad_middle, two_other, turned, send_gate,
    load_sems, store_sems, core_send, core_recv, plane_send, plane_recv, *line_refs,
):
    span, width = inputs.shape
    hidden, piece = gate.shape[1], turned.shape[0]
    row, core = lax.axis_index("dp"), lax.axis_index("ctx")
    half, block = span // 2, span // 4
    second, attended = normed, inputs
    line_one, line_two = line_refs[:5], line_refs[5:]
    count = line_one[0].shape[1]
    part = count // 2

    def load(at, src, dst):
        made = pltpu.make_async_copy(src, dst, load_sems.at[at])
        made.start()
        return made

    def ordered(stream, i):
        return (i // part) * half + stream * block + lax.rem(i, part) * CHUNK

    def moved(at):
        return (0, 2, 1, 3)[at] * block

    load_inputs = load(0, inputs_any, inputs)
    load_query = load(1, query_weight_any, query_weight)
    load_kv = [
        load(2, key_weight_any, kv_weight.at[pl.ds(0, HEAD_DIM)]),
        load(11, value_weight_any, kv_weight.at[pl.ds(HEAD_DIM, HEAD_DIM)]),
    ]
    load_out = load(3, out_weight_any, out_weight)
    load_up = [
        load(4 + b, upstream_any.at[pl.ds(b * block, block)], upstream.at[pl.ds(moved(b), block)]) for b in range(4)
    ]
    load_down = load(8, down_weight_any, down_weight)
    load_gate = load(9, gate_weight_any, gate_weight)
    load_up_weight = load(10, up_weight_any, up_weight)
    seg_all[core] = jnp.broadcast_to(segments[...], seg_all.shape[1:])
    greet(n, True, dp_size)

    def seg_copy():
        return remote(seg_all.at[core], seg_all.at[core], core_send.at[1], core_recv.at[1], ctx=1 - core)

    seg_copy().start()
    load_inputs.wait()

    def norm_rows(b, carry):
        rows = pl.ds(pl.multiple_of(b * 64, 64), 64)
        value = inputs[rows].astype(jnp.float32)
        normed[rows] = (value * inverse_rms(value) * gain_one[...]).astype(jnp.bfloat16)
        return carry

    lax.fori_loop(0, span // 64, norm_rows, 0)
    seg_copy().wait()
    for side in (0, 1):
        seg_row[:, side * span : (side + 1) * span] = seg_all[side, 0:1]
        seg_col[side * span : (side + 1) * span] = seg_all[side].T[:, 0:1]
    own_seg = seg_all[core, 0:1]
    key_pos = lax.broadcasted_iota(jnp.int32, (2 * span, span), 0)
    query_pos = core * span + lax.broadcasted_iota(jnp.int32, (2 * span, span), 1)
    before = (seg_col[...] == own_seg) & (key_pos < query_pos)
    position = jnp.sum(jnp.where(before, 1.0, 0.0), axis=0, keepdims=True)
    angles = jnp.broadcast_to(position, (8, span)).T[:, 0:1] * frequency[...]
    lane = lax.broadcasted_iota(jnp.int32, angles.shape, 1)
    cosine[...] = jnp.cos(angles)
    sine = jnp.sin(angles)
    signed_sine[...] = jnp.where(lax.rem(lane, HEAD_DIM) < HEAD_DIM // 2, -sine, sine)
    for made in load_kv:
        made.wait()
    own_rows = pl.ds(pl.multiple_of(core * span, span), span)
    raw = turned_dot(normed[...], kv_weight[...])
    kv[own_rows] = key_lanes(raw, rotate_lanes(raw, cosine[...], signed_sine[...])).astype(jnp.bfloat16)

    def kv_copy():
        return remote(kv.at[own_rows], kv.at[own_rows], core_send.at[0], core_recv.at[0], ctx=1 - core)

    def kv_arrival():
        rows = pl.ds(0, span)
        return remote(kv.at[rows], kv.at[rows], core_send.at[0], core_recv.at[0], ctx=1 - core)

    @pl.when(core == 0)
    def _():
        kv_copy().start()

    load_query.wait()
    for low in range(0, span, half):
        rows = slice(low, low + half)
        raw = jnp.dot(normed[rows], query_weight[...], preferred_element_type=jnp.float32)
        for lanes in range(0, raw.shape[1], 128):
            rotated = rotate_lanes(raw[:, lanes : lanes + 128], cosine[rows], signed_sine[rows])
            query[rows, lanes : lanes + 128] = rotated.astype(jnp.bfloat16) * (HEAD_DIM ** -0.5)

    @pl.when(core == 1)
    def _():
        kv_arrival().wait_recv()

    kv_turned[...] = kv[...].T

    def attend(side, at):
        keys = side * span + (at + 1) * half
        rows = slice(at * half, (at + 1) * half)
        fill_bias(bias, seg_col, seg_row, side * span + at * half, keys, half)

        def pair(index, carry):
            lanes = pl.ds(pl.multiple_of(index * 128, 128), 128)
            both = query[rows, lanes]
            outs = []
            for which in (0, 1):
                scores = turned_dot(kv[0:keys, 0:HEAD_DIM], both[:, which * HEAD_DIM : (which + 1) * HEAD_DIM])
                scores = scores + bias[0:keys, :]
                peak = jnp.max(scores, axis=0, keepdims=True)
                grown = jnp.exp(scores - peak)
                total = jnp.sum(grown, axis=0, keepdims=True)
                logs[pl.ds(2 * index + which, 1), rows] = peak + jnp.log(total)
                out = jnp.dot(
                    kv_turned[HEAD_DIM : 2 * HEAD_DIM, 0:keys],
                    grown.astype(jnp.bfloat16),
                    preferred_element_type=jnp.float32,
                )
                outs.append(out / total)
            mixed[rows, lanes] = jnp.concatenate(outs, axis=0).T.astype(jnp.bfloat16)
            return carry

        lax.fori_loop(0, query.shape[1] // 128, pair, 0)

    for side in (0, 1):

        @pl.when(core == side)
        def _():
            attend(side, 0)
            attend(side, 1)

    load_out.wait()

    def out_tile(t, carry):
        columns = pl.ds(pl.multiple_of(t * 512, 512), 512)
        for b in (0, 2):
            value = jnp.dot(
                mixed[b * block : (b + 2) * block], out_weight[:, columns], preferred_element_type=jnp.float32
            )
            partial[moved(b) : moved(b) + block, columns] = value[:block]
            partial[moved(b + 1) : moved(b + 1) + block, columns] = value[block:]
        return carry

    lax.fori_loop(0, width // 512, out_tile, 0)

    def rows_at(start):
        return pl.ds(pl.multiple_of(start, CHUNK), CHUNK)

    def own(stream, i):
        return partial[rows_at(ordered(stream, i))]

    def finish_one(stream, i, total):
        value = inputs[rows_at((stream * count + i) * CHUNK)].astype(jnp.float32) + total
        middle[kept_rows(i)] = value
        return value * inverse_rms(value) * gain_two[...]

    gain_out[...] = jnp.zeros_like(gain_out)

    def finish_two(stream, i, total):
        value = middle[kept_rows(i)]
        inverse = inverse_rms(value)
        unit = value * inverse
        gain_out[0:1, :] += jnp.sum(total * unit, axis=0, keepdims=True)
        scaled = total * gain_two[...]
        result = upstream[rows_at(ordered(stream, i))].astype(jnp.float32) + inverse * (
            scaled - unit * jnp.mean(scaled * unit, axis=-1, keepdims=True)
        )
        grad_middle[kept_rows(i)] = result
        return result

    first = Line(n, own, finish_one, ordered, normed_two, *line_one)
    then = Line(n, own, finish_two, ordered, attended, *line_two)
    tiles, rest = wide_tiles(hidden)
    tile_count = tiles + (1 if rest else 0)

    def each_tile(t, work):
        @pl.when(t < tiles)
        def _():
            work(pl.ds(pl.multiple_of(t * 256, 256), 256))

        if rest:

            @pl.when(t == tiles)
            def _():
                work(pl.ds(tiles * 256, rest))

    def inner_tile(columns):
        grad_inner[:, columns] = turned_dot(upstream[...], down_weight[columns, :])

    def forward_tile(rows, columns):
        gated = jnp.dot(normed_two[rows], gate_weight[:, columns], preferred_element_type=jnp.float32)
        upped = jnp.dot(normed_two[rows], up_weight[:, columns], preferred_element_type=jnp.float32)
        sig = jax.nn.sigmoid(gated)
        act = gated * sig
        grad = grad_inner[rows, columns]
        inner[rows, columns] = (act * upped).astype(jnp.bfloat16)
        up[rows, columns] = (grad * act).astype(jnp.bfloat16)
        gate[rows, columns] = (grad * upped * sig * (1.0 + gated * (1.0 - sig))).astype(jnp.bfloat16)

    def back_tile(rows, t):
        columns = pl.ds(pl.multiple_of(t * 512, 512), 512)
        partial[rows, columns] = turned_dot(gate[rows], gate_weight[columns, :]) + turned_dot(
            up[rows], up_weight[columns, :]
        )

    def second_tile(rows, t):
        columns = pl.ds(pl.multiple_of(t * 512, 512), 512)
        second[rows, columns] = jnp.dot(
            inner[rows], down_weight[:, columns], preferred_element_type=jnp.float32
        ).astype(jnp.bfloat16)

    last = n - 1
    trip = 2 * HOP * last
    each = 2
    forward_steps, back_steps = -(-tile_count // each), width // 1024
    work = forward_steps + back_steps
    base_one = part + trip
    base_two = max(count + trip, base_one + work + 1)
    steps = base_two + work + part + trip

    def store(at, src, dst):
        return pltpu.make_async_copy(src, dst, store_sems.at[at])

    def stores(at, src, dst):
        return [
            store(at + b, src.at[pl.ds(moved(b), block)], dst.at[pl.ds(b * block, block)]) for b in range(4)
        ]

    early = [
        store(0, query, query_out), store(1, kv, kv_out), store(2, logs, log_out), store(3, mixed, mixed_out),
        store(31, seg_row, seg_out), store(32, cosine, cosine_out),
        store(33, signed_sine, sine_out),
    ]
    hidden_stores = [(5, normed_two, normed_two_out), (13, up, up_out), (17, inner, inner_out)]

    def gate_swaps():
        made = [
            remote(
                gate.at[pl.ds(0, span)], gate.at[pl.ds(span, span)], core_send.at[2], core_recv.at[2], ctx=1 - core
            )
        ]
        for q in range(dp_size):
            columns = pl.ds(pl.multiple_of((2 * q + 1 - core) * piece, piece), piece)
            made.append(
                remote(
                    normed_two.at[:, columns], two_other.at[:, pl.ds(q * piece, piece)],
                    core_send.at[3 + q], core_recv.at[3 + q], ctx=1 - core,
                )
            )
        return made

    def peer_of(r):
        return lax.rem(row + 1 + r, dp_size)

    def gate_copy(r):
        return remote(send_gate.at[r], land_gate.at[r], plane_send.at[r], plane_recv.at[r], dp=peer_of(r))

    def gate_piece(r):
        peer = peer_of(r)
        columns = pl.ds(pl.multiple_of((2 * peer + core) * piece, piece), piece)
        turned[:, 0:span] = normed_two[:, columns].T
        turned[:, span : 2 * span] = two_other[:, pl.ds(pl.multiple_of(peer * piece, piece), piece)].T
        edges = [(low, min(low + 384, hidden)) for low in range(0, hidden, 384)]

        @pl.when(r < dp_size - 1)
        def _():
            for low, high in edges:
                send_gate[r, :, low:high] = jnp.dot(
                    turned[...], gate[:, low:high], preferred_element_type=jnp.float32
                ).astype(jnp.bfloat16)
            gate_copy(r).start()

        @pl.when(r == dp_size - 1)
        def _():
            for low, high in edges:
                own_gate[:, low:high] = jnp.dot(turned[...], gate[:, low:high], preferred_element_type=jnp.float32)

    keep_normed = store(4, normed, normed_out)
    for made in [*early, keep_normed]:
        made.start()

    def step(k, carry):
        first.step(k)
        then.step(k - (base_one + work), 0, part)
        then.step(k - (base_two + work), part, part)

        @pl.when(k == 0)
        def _():
            for made in load_up:
                made.wait()
            load_down.wait()
            load_gate.wait()
            load_up_weight.wait()

        @pl.when((k >= 1) & (k <= tile_count))
        def _():
            each_tile(k - 1, inner_tile)

        late = jnp.where(k >= base_two, 1, 0)
        phase = k - jnp.where(k >= base_two, base_two, base_one)
        rows = pl.ds(pl.multiple_of(late * half, half), half)

        @pl.when((phase >= 0) & (phase < forward_steps))
        def _():
            def tile(t, carry):
                each_tile(t, functools.partial(forward_tile, rows))
                return carry

            lax.fori_loop(phase * each, jnp.minimum((phase + 1) * each, tile_count), tile, 0)

        @pl.when((phase >= forward_steps) & (phase < work))
        def _():
            for t in (0, 1):
                back_tile(rows, 2 * (phase - forward_steps) + t)

        @pl.when(k == base_two + work)
        def _():
            for at, src, dst in hidden_stores:
                for made in stores(at, src, dst):
                    made.start()

        @pl.when(k == base_two + forward_steps)
        def _():
            for made in gate_swaps():
                made.start()

        @pl.when(k == base_two + work + 1)
        def _():
            keep_normed.wait()
            for made in gate_swaps():
                made.wait()

        gate_task = k - (base_two + work + 1)

        @pl.when((gate_task >= 0) & (gate_task < dp_size))
        def _():
            gate_piece(gate_task)

        after = gate_task - dp_size

        @pl.when((after >= 0) & (after < 4))
        def _():
            for low in (0, half):
                second_tile(pl.ds(low, half), after)

        return carry

    lax.fori_loop(0, steps, step, 0)
    late_stores = [
        *stores(21, second, second_out), *stores(25, attended, attended_out),
        store(29, middle, middle_out), store(30, grad_middle, grad_middle_out),
    ]
    for made in late_stores:
        made.start()
    first.drain()
    then.drain()

    @pl.when(core == 0)
    def _():
        kv_copy().wait_send()

    for r in range(dp_size - 1):
        gate_copy(r).wait()
    for made in [*early, *late_stores]:
        made.wait()
    for at, src, dst in hidden_stores:
        for made in stores(at, src, dst):
            made.wait()


def front_call(line_size, dp_size, operands):
    inputs = operands[0]
    query_weight, out_weight, gate_weight = operands[5], operands[8], operands[9]
    span, width = inputs.shape
    heads, hidden = query_weight.shape[1], gate_weight.shape[1]
    piece = width // (2 * dp_size)
    low, full = jnp.bfloat16, jnp.float32
    vmem, outside = pl.BlockSpec(memory_space=pltpu.VMEM), pl.BlockSpec(memory_space=pl.ANY)
    dma = pltpu.SemaphoreType.DMA
    outs = [
        ((1, 2 * span), jnp.int32), ((span, 128), full), ((span, 128), full),
        ((span, heads), low), ((2 * span, 128), low), ((heads // HEAD_DIM, span), full), ((span, heads), low),
        ((span, width), low), ((span, width), low), *[((span, hidden), low)] * 2, ((span, width), low),
        ((span, width), low), ((span // 2, width), full), ((span // 2, width), full),
        ((dp_size - 1, piece, hidden), low), ((8, width), full), ((piece, hidden), full),
    ]
    scratch = [
        pltpu.VMEM((2, 8, span), jnp.int32), pltpu.VMEM((1, 2 * span), jnp.int32),
        pltpu.VMEM((2 * span, 1), jnp.int32), pltpu.VMEM((span, 128), full), pltpu.VMEM((span, 128), full),
        pltpu.VMEM((span, width), low), pltpu.VMEM((span, width), low), pltpu.VMEM((width, heads), low),
        pltpu.VMEM((128, width), low), pltpu.VMEM((heads, width), low), pltpu.VMEM((span, heads), low),
        pltpu.VMEM((2 * span, 128), low), pltpu.VMEM((128, 2 * span), low),
        pltpu.VMEM((heads // HEAD_DIM, span), full), pltpu.VMEM((span, heads), low),
        pltpu.VMEM((2 * span, span // 2), full),
        pltpu.VMEM((width, hidden), low), pltpu.VMEM((width, hidden), low), pltpu.VMEM((hidden, width), low),
        pltpu.VMEM((span, width), low), pltpu.VMEM((span, hidden), full), pltpu.VMEM((span, width), low),
        pltpu.VMEM((2 * span, hidden), low), *[pltpu.VMEM((span, hidden), low)] * 2,
        pltpu.VMEM((span, width), full),
        pltpu.VMEM((span // 2, width), full), pltpu.VMEM((span // 2, width), full),
        pltpu.VMEM((span, width // 2), low), pltpu.VMEM((piece, 2 * span), low),
        pltpu.VMEM((dp_size - 1, piece, hidden), low),
        dma((12,)), dma((34,)), dma((3 + dp_size,)), dma((3 + dp_size,)), dma((dp_size - 1,)), dma((dp_size - 1,)),
        *line_scratch(span, width), *line_scratch(span, width),
    ]
    return pl.pallas_call(
        functools.partial(front_kernel, line_size, dp_size),
        out_shape=[jax.ShapeDtypeStruct(s, d) for s, d in outs],
        in_specs=[outside] + [vmem] * 4 + [outside] * 8,
        out_specs=[outside] * 16 + [vmem] * 2,
        scratch_shapes=scratch,
        compiler_params=pltpu.CompilerParams(
            collective_id=1, has_side_effects=True, vmem_limit_bytes=FRONT_MIB * MIB
        ),
    )(*operands)


def back_kernel(
    n, dp_size,
    query_any, kv_any, logs, mixed_any, cosine, signed_sine, seg_row, inputs_any, normed_any, normed_two_any,
    up_any, inner_any, second_any, attended_any, middle_any, grad_middle_any, gain_one, gain_two_grad,
    query_weight_any, key_weight_any, value_weight_any, out_weight_any, upstream_any,
    layer_out, grad_inputs, grad_gains, grad_qkv, own_out, grad_up, own_down,
    land_up, land_down, land_qkv, land_out,
    query, kv, kv_turned, grad_mixed, mixed, attended, normed_cols, attended_cols, two_cols, upstream_cols,
    up, inner, pre, query_weight, kv_weight, out_weight, grad_middle, middle, inputs,
    ring, send_qkv, send_out, turned, seg_col, bias, kv_grad, kv_grad_other,
    gain_line, gain_land, gain_sum, gain_plane,
    load_sems, core_send, core_recv, ring_send, ring_recv, plane_send, plane_recv, line_send, line_recv,
    spread_send, spread_recv, *line_refs,
):
    span, width = attended.shape
    heads, piece = query.shape[1], turned.shape[0]
    here, row, core = lax.axis_index("tensor"), lax.axis_index("dp"), lax.axis_index("ctx")
    half = span // 2
    line_out, line_in = line_refs[:5], line_refs[5:]
    count = line_out[0].shape[1]
    last = n - 1
    loads = []

    def load(src, dst):
        made = pltpu.make_async_copy(src, dst, load_sems.at[len(loads)])
        made.start()
        loads.append(made)
        return made

    own_half = pl.ds(pl.multiple_of(jnp.where(here == 0, half, 0), half), half)
    first_loads = [
        load(second_any, layer_out), load(middle_any, middle),
        load(attended_any, attended), load(out_weight_any, out_weight), load(query_any, query), load(kv_any, kv),
    ]

    def load_cols(src, dst):
        made = []
        for q in range(dp_size):
            block = pl.multiple_of((2 * q + core) * piece, piece)
            made.append(load(src.at[:, pl.ds(block, piece)], dst.at[pl.ds(0, span), pl.ds(q * piece, piece)]))
        return made

    up_loads = [load(up_any, up.at[pl.ds(0, span)]), *load_cols(normed_two_any, two_cols)]
    inner_loads = [load(inner_any, inner.at[pl.ds(0, span)]), *load_cols(upstream_any, upstream_cols)]
    late_loads = [
        load(query_weight_any, query_weight), load(key_weight_any, kv_weight.at[pl.ds(0, HEAD_DIM)]),
        load(value_weight_any, kv_weight.at[pl.ds(HEAD_DIM, HEAD_DIM)]),
        load(grad_middle_any, grad_middle), load(inputs_any.at[own_half], inputs),
        load(mixed_any, mixed.at[pl.ds(0, span)]), *load_cols(normed_any, normed_cols),
        *load_cols(attended_any, attended_cols),
    ]
    greet(n, True, dp_size, full_line=True)
    slots = []

    def swap(src, dst):
        at = len(slots)
        slots.append(at)
        return remote(src, dst, core_send.at[at], core_recv.at[at], ctx=1 - core)

    def swap_rows(src, dst):
        return swap(src, dst.at[pl.ds(span, span)])

    def swap_cols(src, dst):
        made = []
        for q in range(dp_size):
            block = pl.multiple_of((2 * q + 1 - core) * piece, piece)
            made.append(
                swap(src.at[:, pl.ds(block, piece)], dst.at[pl.ds(span, span), pl.ds(q * piece, piece)])
            )
        return made

    up_swaps = [swap_rows(up_any, up), *swap_cols(normed_two_any, two_cols)]
    inner_swaps = [swap_rows(inner_any, inner), *swap_cols(upstream_any, upstream_cols)]
    late_swaps = [
        swap_rows(mixed_any, mixed), *swap_cols(attended_any, attended_cols), *swap_cols(normed_any, normed_cols),
    ]
    for made in [*up_swaps, *inner_swaps, *late_swaps]:
        made.start()
    pre_slot, kv_slot = len(slots), len(slots) + 1

    def pre_swap():
        return remote(
            pre.at[pl.ds(0, span)], pre.at[pl.ds(span, span)], core_send.at[pre_slot], core_recv.at[pre_slot],
            ctx=1 - core,
        )

    def kv_swap():
        return remote(
            kv_grad.at[pl.ds(0, span)], kv_grad_other, core_send.at[kv_slot], core_recv.at[kv_slot], ctx=1 - core
        )

    gain_line[...] = jnp.zeros_like(gain_line)
    gain_line[1:2, :] = gain_two_grad[0:1, :]
    kv_grad[...] = jnp.zeros_like(kv_grad)
    seg_col[...] = jnp.broadcast_to(seg_row[...], (8, 2 * span)).T[:, 0:1]
    for made in first_loads:
        made.wait()
    kv_turned[...] = kv[...].T

    def rows_at(start):
        return pl.ds(pl.multiple_of(start, CHUNK), CHUNK)

    def plain(stream, i):
        return (stream * count + i) * CHUNK

    def finish_out(stream, i, total):
        return middle[kept_rows(i)] + total

    def finish_in(stream, i, total):
        hidden = inputs[kept_rows(i)].astype(jnp.float32)
        inverse = inverse_rms(hidden)
        unit = hidden * inverse
        gain_line[0:1, :] += jnp.sum(total * unit, axis=0, keepdims=True)
        scaled = total * gain_one[...]
        return grad_middle[kept_rows(i)] + inverse * (
            scaled - unit * jnp.mean(scaled * unit, axis=-1, keepdims=True)
        )

    out_line = Line(
        n, lambda s, i: layer_out[rows_at(plain(s, i))].astype(jnp.float32), finish_out, plain, layer_out, *line_out
    )
    in_line = Line(
        n, lambda s, i: grad_inputs[rows_at(plain(s, i))].astype(jnp.float32), finish_in, plain, grad_inputs, *line_in
    )

    def attend_back(side, at, index):
        keys = side * span + (at + 1) * half
        rows = slice(at * half, (at + 1) * half)
        lanes = pl.ds(pl.multiple_of(index * 128, 128), 128)

        @pl.when(index == 0)
        def _():
            fill_bias(bias, seg_col, seg_row, side * span + at * half, keys, half)

        both_query, both_grad = query[rows, lanes], grad_mixed[rows, lanes]
        outs, parts = [], None
        for which in (0, 1):
            head = slice(which * HEAD_DIM, (which + 1) * HEAD_DIM)
            query_head, grad_head = both_query[:, head], both_grad[:, head]
            scores = turned_dot(kv[0:keys, 0:HEAD_DIM], query_head) + bias[0:keys, :]
            probs = jnp.exp(scores - logs[pl.ds(2 * index + which, 1), rows])
            grad_probs = turned_dot(kv[0:keys, HEAD_DIM : 2 * HEAD_DIM], grad_head)
            both = probs * grad_probs
            grad_scores = (both - probs * jnp.sum(both, axis=0, keepdims=True)).astype(jnp.bfloat16)
            grad_key = jnp.dot(grad_scores, query_head, preferred_element_type=jnp.float32)
            grad_value = jnp.dot(probs.astype(jnp.bfloat16), grad_head, preferred_element_type=jnp.float32)
            part = jnp.concatenate([grad_key, grad_value], axis=1)
            parts = part if parts is None else parts + part
            outs.append(
                jnp.dot(kv_turned[0:HEAD_DIM, 0:keys], grad_scores, preferred_element_type=jnp.float32)
            )
        kv_grad[0:keys] += parts
        grad_query = jnp.concatenate(outs, axis=0).T * (HEAD_DIM ** -0.5)
        pre[rows, lanes] = rotate_lanes(grad_query, cosine[rows], signed_sine[rows], back=True).astype(jnp.bfloat16)

    pairs = heads // 128
    tasks = 2 * pairs

    def attend_task(task):
        for side in (0, 1):
            for at in (0, 1):

                @pl.when((core == side) & (task // pairs == at))
                def _():
                    attend_back(side, at, lax.rem(task, pairs))

    own_grad = pl.ds(pl.multiple_of(core * span, span), span)

    def finish_pre():
        @pl.when(core == 0)
        def _():
            kv_swap().wait_recv()
            kv_grad[0:span] += kv_grad_other[...]

        raw = kv_grad[own_grad]
        turned_back = rotate_lanes(raw, cosine[...], signed_sine[...], back=True)
        pre[0:span, heads : heads + 128] = key_lanes(raw, turned_back).astype(jnp.bfloat16)

    def in_products():
        def tile(t, carry):
            columns = pl.ds(pl.multiple_of(t * 512, 512), 512)
            for low in (0, half):
                rows = slice(low, low + half)
                grad_inputs[rows, columns] = (
                    turned_dot(pre[rows, 0:heads], query_weight[columns, :])
                    + jnp.dot(
                        pre[rows, heads : heads + 128], kv_weight[:, columns], preferred_element_type=jnp.float32
                    )
                ).astype(jnp.bfloat16)
            return carry

        lax.fori_loop(0, width // 512, tile, 0)

    def peer_of(r):
        return lax.rem(row + 1 + r, dp_size)

    def turn(r, cols):
        block = pl.multiple_of(peer_of(r) * piece, piece)
        turned[...] = cols[:, pl.ds(block, piece)].T

    def tiles_of(stacked):
        wide = stacked.shape[1]
        return [(low, min(low + 384, wide)) for low in range(0, wide, 384)]

    def piece_value(stacked, low, high):
        return jnp.dot(turned[...], stacked[:, low:high], preferred_element_type=jnp.float32)

    landings = (land_up, land_down)
    others = dp_size - 1

    def ring_copy(w, r, at):
        return remote(
            ring.at[at], landings[w].at[r], ring_send.at[at], ring_recv.at[w, r], dp=peer_of(r)
        )

    def ring_piece(w, r, stacked, own):
        at = others * w + r

        @pl.when(r < dp_size - 1)
        def _():
            slot = at

            for low, high in tiles_of(stacked):
                ring[slot, :, low:high] = piece_value(stacked, low, high).astype(jnp.bfloat16)
            ring_copy(w, r, at).start()

        @pl.when(r == dp_size - 1)
        def _():
            for low, high in tiles_of(stacked):
                own[:, low:high] = piece_value(stacked, low, high)

    sends, lands = (send_qkv, send_out), (land_qkv, land_out)

    def plane_copy(w, r):
        return remote(sends[w].at[r], lands[w].at[r], plane_send.at[w, r], plane_recv.at[w, r], dp=peer_of(r))

    def plane_piece(w, r, stacked, own):
        @pl.when(r < dp_size - 1)
        def _():
            for low, high in tiles_of(stacked):
                sends[w][r, :, low:high] = piece_value(stacked, low, high).astype(jnp.bfloat16)
            plane_copy(w, r).start()

        @pl.when(r == dp_size - 1)
        def _():
            for low, high in tiles_of(stacked):
                own[:, low:high] = piece_value(stacked, low, high)

    def line_copies(owner, hops):
        slot = 0 if owner == 0 else 1
        return [
            remote(
                gain_line, gain_land.at[slot], line_send.at[slot, hop - 1], line_recv.at[slot],
                tensor=owner + hop if owner == 0 else owner - hop,
            )
            for hop in hops
        ]

    lag = tasks + 2
    ffn_tasks = 2 * dp_size
    out_base = max(ffn_tasks + 1, lag + 1)
    steps = max(lag + count + 2 * HOP * last, out_base + dp_size)

    def step(k, carry):
        out_line.step(k)
        in_line.step(k - lag)

        @pl.when(k == 0)
        def _():
            grad_mixed[...] = turned_dot(attended[...], out_weight[...]).astype(jnp.bfloat16)

        @pl.when((k >= 1) & (k <= tasks))
        def _():
            attend_task(k - 1)

        @pl.when((k == tasks) & (core == 1))
        def _():
            kv_swap().start()

        @pl.when(k == 1)
        def _():
            for made in [*up_loads, *up_swaps]:
                made.wait()

        @pl.when(k == dp_size + 1)
        def _():
            for made in [*inner_loads, *inner_swaps]:
                made.wait()

        @pl.when(k == tasks)
        def _():
            for made in late_loads:
                made.wait()
            for made in late_swaps:
                made.wait()

        @pl.when(k == tasks + 1)
        def _():
            finish_pre()
            in_products()
            pre_swap().start()

        r = k - 1

        @pl.when((r >= 0) & (r < dp_size))
        def _():
            turn(r, two_cols)
            ring_piece(0, r, up, grad_up)

        @pl.when((r >= dp_size) & (r < 2 * dp_size))
        def _():
            turn(r - dp_size, upstream_cols)
            ring_piece(1, r - dp_size, inner, own_down)

        @pl.when(k == out_base)
        def _():
            pre_swap().wait()

        at = k - out_base

        @pl.when((at >= 0) & (at < dp_size))
        def _():
            turn(at, attended_cols)
            plane_piece(1, at, mixed, own_out)
            turn(at, normed_cols)
            plane_piece(0, at, pre, grad_qkv)

        @pl.when(k == lag + count + HOP * last - 1)
        def _():
            for owner in (0, last):

                @pl.when(here == owner)
                def _():
                    for made in line_copies(owner, range(1, n)):
                        made.start()

        return carry

    lax.fori_loop(0, steps, step, 0)
    shard = width // (2 * dp_size)
    gain_sum[...] = jnp.zeros_like(gain_sum)
    for owner in (0, last):
        slot = 0 if owner == 0 else 1

        @pl.when(here == owner)
        def _():
            gain_sum[...] += gain_line[...]

        @pl.when(here != owner)
        def _():
            line_copies(owner, (1,))[0].wait_recv()
            gain_sum[...] += gain_land[slot]

    shards = 2 * dp_size
    place = 2 * row + core

    def spread(r):
        peer = lax.rem(place + 1 + r, shards)
        block = pl.multiple_of(peer * shard, shard)
        return remote(
            gain_sum.at[:, pl.ds(block, shard)], gain_plane.at[r], spread_send.at[r], spread_recv.at[r],
            dp=peer // 2, ctx=lax.rem(peer, 2),
        )

    for r in range(shards - 1):
        spread(r).start()
    out_line.drain()
    in_line.drain()

    @pl.when(core == 1)
    def _():
        kv_swap().wait_send()

    for r in range(others):
        for w in (0, 1):
            ring_copy(w, r, others * w + r).wait()
            plane_copy(w, r).wait()
    grad_gains[...] = gain_sum[:, pl.ds(pl.multiple_of(place * shard, shard), shard)]
    for r in range(shards - 1):
        spread(r).wait()
        grad_gains[...] += gain_plane[r]
    for owner in (0, last):

        @pl.when(here == owner)
        def _():
            for made in line_copies(owner, range(1, n)):
                made.wait_send()


def back_call(line_size, dp_size, operands):
    query, kv, logs, mixed = operands[:4]
    span, heads = query.shape
    width, hidden = operands[8].shape[1], operands[10].shape[1]
    piece = width // (2 * dp_size)
    wide = heads + 128
    low, full = jnp.bfloat16, jnp.float32
    vmem, outside = pl.BlockSpec(memory_space=pltpu.VMEM), pl.BlockSpec(memory_space=pl.ANY)
    dma = pltpu.SemaphoreType.DMA
    others = dp_size - 1
    outs = [
        ((span, width), low), ((span, width), low), ((8, piece), full), ((piece, wide), full), ((piece, heads), full),
        ((piece, hidden), full), ((piece, hidden), full),
        *[((others, piece, hidden), low)] * 2, ((others, piece, wide), low), ((others, piece, heads), low),
    ]
    core_copies = 3 + 4 * dp_size + 2
    scratch = [
        pltpu.VMEM((span, heads), low), pltpu.VMEM((2 * span, 128), low), pltpu.VMEM((128, 2 * span), low),
        pltpu.VMEM((span, heads), low), pltpu.VMEM((2 * span, heads), low), pltpu.VMEM((span, width), low),
        *[pltpu.VMEM((2 * span, width // 2), low)] * 4,
        *[pltpu.VMEM((2 * span, hidden), low)] * 2, pltpu.VMEM((2 * span, wide), low),
        pltpu.VMEM((width, heads), low), pltpu.VMEM((128, width), low), pltpu.VMEM((heads, width), low),
        pltpu.VMEM((span // 2, width), full), pltpu.VMEM((span // 2, width), full), pltpu.VMEM((span // 2, width), low),
        pltpu.VMEM((2 * others, piece, hidden), low), pltpu.VMEM((others, piece, wide), low),
        pltpu.VMEM((others, piece, heads), low),
        pltpu.VMEM((piece, 2 * span), low), pltpu.VMEM((2 * span, 1), jnp.int32), pltpu.VMEM((2 * span, span // 2), full),
        pltpu.VMEM((2 * span, 128), full), pltpu.VMEM((span, 128), full),
        pltpu.VMEM((8, width), full), pltpu.VMEM((2, 8, width), full), pltpu.VMEM((8, width), full),
        pltpu.VMEM((2 * dp_size - 1, 8, piece), full),
        dma((17 + 4 * dp_size + 6,)), dma((core_copies,)), dma((core_copies,)),
        dma((2 * others,)), dma((2, others)), dma((2, others)), dma((2, others)),
        dma((2, line_size - 1)), dma((2,)), dma((2 * dp_size - 1,)), dma((2 * dp_size - 1,)),
        *line_scratch(span, width), *line_scratch(span, width),
    ]
    spaces = [outside, outside, vmem, outside, vmem, vmem, vmem] + [outside] * 9 + [vmem, vmem] + [outside] * 5
    return pl.pallas_call(
        functools.partial(back_kernel, line_size, dp_size),
        out_shape=[jax.ShapeDtypeStruct(s, d) for s, d in outs],
        in_specs=spaces,
        out_specs=[vmem] * 7 + [outside] * 4,
        scratch_shapes=scratch,
        compiler_params=pltpu.CompilerParams(
            collective_id=2, has_side_effects=True, vmem_limit_bytes=BACK_MIB * MIB
        ),
    )(*operands)


def settle_kernel(
    layer_any, inputs_any, gains, qkv_any, out_any, gate_any, up_any, down_any,
    land_gate, land_up, land_down, land_qkv, land_out,
    layer_out, grad_inputs, gain_one, grad_query, grad_key, grad_value, grad_out, gain_two, grad_gate, grad_up, grad_down,
    own_qkv, own_out, own_gate, own_up, own_down, far_qkv, far_out, far_gate, far_up, far_down,
    turned_kv, turned_out, turned_down, in_sems, out_sems,
):
    whole = [
        pltpu.make_async_copy(layer_any, layer_out, out_sems.at[0]),
        pltpu.make_async_copy(inputs_any, grad_inputs, out_sems.at[1]),
    ]
    owns = ((qkv_any, own_qkv), (out_any, own_out), (gate_any, own_gate), (up_any, own_up), (down_any, own_down))
    fars = ((land_qkv, far_qkv), (land_out, far_out), (land_gate, far_gate), (land_up, far_up), (land_down, far_down))
    loads = [
        (
            pltpu.make_async_copy(*own, in_sems.at[0, at]),
            pltpu.make_async_copy(*far, in_sems.at[1, at]),
        )
        for at, (own, far) in enumerate(zip(owns, fars))
    ]
    for pair in loads:
        for made in pair:
            made.start()
    for made in whole:
        made.start()
    gain_one[...] = gains[0:1]
    gain_two[...] = gains[1:2]

    def settle(at, own, far):
        for made in loads[at]:
            made.wait()
        total = own[...]
        for r in range(far.shape[0]):
            total = total + far[r].astype(jnp.float32)
        return total

    def put(at, src, dst):
        made = pltpu.make_async_copy(src, dst, out_sems.at[at])
        made.start()
        whole.append(made)

    heads = grad_query.shape[1]
    own_qkv[...] = settle(0, own_qkv, far_qkv)
    put(2, own_qkv.at[:, pl.ds(0, heads)], grad_query)
    turned_kv[...] = own_qkv[:, heads:].T
    put(3, turned_kv.at[pl.ds(0, HEAD_DIM)], grad_key)
    put(4, turned_kv.at[pl.ds(HEAD_DIM, HEAD_DIM)], grad_value)
    turned_out[...] = settle(1, own_out, far_out).T
    put(5, turned_out, grad_out)
    own_gate[...] = settle(2, own_gate, far_gate)
    put(6, own_gate, grad_gate)
    own_up[...] = settle(3, own_up, far_up)
    put(7, own_up, grad_up)
    turned_down[...] = settle(4, own_down, far_down).T
    put(8, turned_down, grad_down)
    for made in whole:
        made.wait()


def settle_call(operands):
    layer_out, _, gains, qkv, out, gate = operands[:6]
    piece, wide = qkv.shape
    heads, hidden = out.shape[1], gate.shape[1]
    others = operands[8].shape[0]
    low, full = jnp.bfloat16, jnp.float32
    vmem, outside = pl.BlockSpec(memory_space=pltpu.VMEM), pl.BlockSpec(memory_space=pl.ANY)
    outs = [
        (layer_out.shape, low), (layer_out.shape, low), ((1, piece), full), ((piece, heads), full),
        ((HEAD_DIM, piece), full), ((HEAD_DIM, piece), full), ((heads, piece), full), ((1, piece), full),
        ((piece, hidden), full), ((piece, hidden), full), ((hidden, piece), full),
    ]
    shapes = [(piece, wide), (piece, heads), *[(piece, hidden)] * 3]
    scratch = [
        *[pltpu.VMEM(shape, full) for shape in shapes], *[pltpu.VMEM((others, *shape), low) for shape in shapes],
        pltpu.VMEM((wide - heads, piece), full), pltpu.VMEM((heads, piece), full), pltpu.VMEM((hidden, piece), full),
        pltpu.SemaphoreType.DMA((2, 5)), pltpu.SemaphoreType.DMA((9,)),
    ]
    return pl.pallas_call(
        settle_kernel,
        out_shape=[jax.ShapeDtypeStruct(s, d) for s, d in outs],
        in_specs=[outside, outside, vmem] + [outside] * 10,
        out_specs=[outside, outside, vmem] + [outside] * 4 + [vmem] + [outside] * 3,
        scratch_shapes=scratch,
        compiler_params=pltpu.CompilerParams(vmem_limit_bytes=40 * MIB),
    )(*operands)


def plain_body(
    inputs,
    segment_ids,
    attention_gain,
    query_weight,
    key_weight,
    value_weight,
    out_weight,
    feedforward_gain,
    gate_weight,
    up_weight,
    down_weight,
    cotangent,
):
    seq_count, span_len, model_width = inputs.shape
    row_count = seq_count * span_len
    query_heads = query_weight.shape[1] // HEAD_DIM
    kv_heads = key_weight.shape[1] // HEAD_DIM
    group_size = query_heads // kv_heads
    score_scale = 1.0 / math.sqrt(HEAD_DIM)
    offset = lax.axis_index("ctx") * span_len
    whole_segments = lax.all_gather(segment_ids, "ctx", axis=1, tiled=True)
    own_positions = lax.dynamic_slice_in_dim(positions_of(whole_segments), offset, span_len, 1)
    cosine, sine_table = rotary_tables(own_positions)
    cosine = cosine[:, :, None, :]
    sine_table = sine_table[:, :, None, :]
    hidden = inputs.astype(jnp.float32).reshape(row_count, model_width)
    inverse_one = lax.rsqrt(jnp.mean(hidden * hidden, axis=-1, keepdims=True) + epsilon)
    unit_one = hidden * inverse_one
    normed = (unit_one * attention_gain).astype(jnp.bfloat16)
    query_rows = rotate(
        jnp.dot(normed, query_weight, preferred_element_type=jnp.float32).reshape(
            seq_count, span_len, query_heads, HEAD_DIM
        ),
        cosine,
        sine_table,
    ).astype(jnp.bfloat16)
    key_rows = rotate(
        jnp.dot(normed, key_weight, preferred_element_type=jnp.float32).reshape(
            seq_count, span_len, kv_heads, HEAD_DIM
        ),
        cosine,
        sine_table,
    ).astype(jnp.bfloat16)
    value_rows = (
        jnp.dot(normed, value_weight, preferred_element_type=jnp.float32)
        .astype(jnp.bfloat16)
        .reshape(seq_count, span_len, kv_heads, HEAD_DIM)
    )
    all_keys, all_values = (
        lax.all_gather(key_rows, "ctx", axis=1, tiled=True),
        lax.all_gather(value_rows, "ctx", axis=1, tiled=True),
    )

    def attend(block_items):
        query_block, key_block, value_block, query_seg, key_seg = block_items
        allowed = visible(query_seg, key_seg, offset)
        grouped = query_block.reshape(span_len, kv_heads, group_size, HEAD_DIM)
        raw_scores = jnp.einsum(
            "qhgd,khd->hgqk", grouped, key_block, preferred_element_type=jnp.float32
        )
        scores = jnp.where(allowed, raw_scores * score_scale, masked_score)
        row_peak = jnp.max(scores, axis=-1, keepdims=True)
        shifted_exp = jnp.exp(scores - row_peak)
        denominator = jnp.sum(shifted_exp, axis=-1, keepdims=True)
        attn_probs = (shifted_exp / denominator).astype(jnp.bfloat16)
        mixed_block = jnp.einsum(
            "hgqk,khd->qhgd", attn_probs, value_block, preferred_element_type=jnp.float32
        )
        return (
            mixed_block.astype(jnp.bfloat16).reshape(span_len, query_heads * HEAD_DIM),
            row_peak + jnp.log(denominator),
        )

    mixed_heads, log_sums = lax.map(
        attend, (query_rows, all_keys, all_values, segment_ids, whole_segments)
    )
    mixed_flat = mixed_heads.reshape(row_count, query_heads * HEAD_DIM)
    attended = lax.psum(
        jnp.dot(mixed_flat, out_weight, preferred_element_type=jnp.float32), "tensor"
    )
    middle = hidden + attended
    inverse_two = lax.rsqrt(jnp.mean(middle * middle, axis=-1, keepdims=True) + epsilon)
    unit_two = middle * inverse_two
    normed_two = (unit_two * feedforward_gain).astype(jnp.bfloat16)
    gate_pre = jnp.dot(normed_two, gate_weight, preferred_element_type=jnp.float32)
    up_pre = jnp.dot(normed_two, up_weight, preferred_element_type=jnp.float32)
    sigmoid_gate = jax.nn.sigmoid(gate_pre)
    inner_act = (gate_pre * sigmoid_gate * up_pre).astype(jnp.bfloat16)
    feed_out = lax.psum(
        jnp.dot(inner_act, down_weight, preferred_element_type=jnp.float32).astype(jnp.bfloat16),
        "tensor",
    ).astype(jnp.float32)
    layer_out = (middle + feed_out).astype(jnp.bfloat16).reshape(seq_count, span_len, model_width)
    upstream = cotangent.reshape(row_count, model_width)
    grad_down = jnp.dot(inner_act.T, upstream, preferred_element_type=jnp.float32)
    grad_inner = jnp.dot(upstream, down_weight.T, preferred_element_type=jnp.float32)
    grad_up_pre = (grad_inner * gate_pre * sigmoid_gate).astype(jnp.bfloat16)
    grad_gate_pre = (
        grad_inner * up_pre * sigmoid_gate * (1.0 + gate_pre * (1.0 - sigmoid_gate))
    ).astype(jnp.bfloat16)
    grad_gate = jnp.dot(normed_two.T, grad_gate_pre, preferred_element_type=jnp.float32)
    grad_up = jnp.dot(normed_two.T, grad_up_pre, preferred_element_type=jnp.float32)
    grad_normed_two = lax.psum(
        jnp.dot(grad_gate_pre, gate_weight.T, preferred_element_type=jnp.float32)
        + jnp.dot(grad_up_pre, up_weight.T, preferred_element_type=jnp.float32),
        "tensor",
    )
    grad_ffn_gain = jnp.sum(grad_normed_two * unit_two, axis=0)
    scaled_two = grad_normed_two * feedforward_gain
    grad_middle = upstream.astype(jnp.float32) + inverse_two * (
        scaled_two - unit_two * jnp.mean(scaled_two * unit_two, axis=-1, keepdims=True)
    )
    grad_attended = grad_middle.astype(jnp.bfloat16)
    grad_out_part = jnp.dot(mixed_flat.T, grad_attended, preferred_element_type=jnp.float32)
    grad_mixed = (
        jnp.dot(grad_attended, out_weight.T, preferred_element_type=jnp.float32)
        .astype(jnp.bfloat16)
        .reshape(seq_count, span_len, query_heads, HEAD_DIM)
    )

    def attend_back(block_items):
        query_block, key_block, value_block, query_seg, key_seg, grad_block, log_block = block_items
        allowed = visible(query_seg, key_seg, offset)
        grouped = query_block.reshape(span_len, kv_heads, group_size, HEAD_DIM)
        grad_grouped = grad_block.reshape(span_len, kv_heads, group_size, HEAD_DIM)
        raw_scores = jnp.einsum(
            "qhgd,khd->hgqk", grouped, key_block, preferred_element_type=jnp.float32
        )
        scores = jnp.where(allowed, raw_scores * score_scale, masked_score)
        attn_probs = jnp.exp(scores - log_block)
        rounded = attn_probs.astype(jnp.bfloat16)
        grad_values = jnp.einsum(
            "hgqk,qhgd->khd", rounded, grad_grouped, preferred_element_type=jnp.float32
        )
        grad_probs = jnp.einsum(
            "qhgd,khd->hgqk", grad_grouped, value_block, preferred_element_type=jnp.float32
        )
        row_dot = jnp.sum(attn_probs * grad_probs, axis=-1, keepdims=True)
        grad_scores = (attn_probs * (grad_probs - row_dot) * score_scale).astype(jnp.bfloat16)
        grad_queries = jnp.einsum(
            "hgqk,khd->qhgd", grad_scores, key_block, preferred_element_type=jnp.float32
        ).reshape(span_len, query_heads, HEAD_DIM)
        grad_keys = jnp.einsum(
            "hgqk,qhgd->khd", grad_scores, grouped, preferred_element_type=jnp.float32
        )
        return (grad_queries, grad_keys, grad_values)

    grad_queries, grad_keys, grad_values = lax.map(
        attend_back,
        (query_rows, all_keys, all_values, segment_ids, whole_segments, grad_mixed, log_sums),
    )
    own_grad_keys, own_grad_values = (
        lax.psum_scatter(grad_keys, "ctx", scatter_dimension=1, tiled=True),
        lax.psum_scatter(grad_values, "ctx", scatter_dimension=1, tiled=True),
    )
    grad_query_pre = (
        rotate(grad_queries, cosine, -sine_table)
        .astype(jnp.bfloat16)
        .reshape(row_count, query_heads * HEAD_DIM)
    )
    grad_key_pre = (
        rotate(own_grad_keys, cosine, -sine_table)
        .astype(jnp.bfloat16)
        .reshape(row_count, kv_heads * HEAD_DIM)
    )
    grad_value_pre = own_grad_values.astype(jnp.bfloat16).reshape(row_count, kv_heads * HEAD_DIM)
    grad_query = jnp.dot(normed.T, grad_query_pre, preferred_element_type=jnp.float32)
    grad_key = jnp.dot(normed.T, grad_key_pre, preferred_element_type=jnp.float32)
    grad_value = jnp.dot(normed.T, grad_value_pre, preferred_element_type=jnp.float32)
    grad_normed = lax.psum(
        (
            jnp.dot(grad_query_pre, query_weight.T, preferred_element_type=jnp.float32)
            + jnp.dot(grad_key_pre, key_weight.T, preferred_element_type=jnp.float32)
            + jnp.dot(grad_value_pre, value_weight.T, preferred_element_type=jnp.float32)
        ).astype(jnp.bfloat16),
        "tensor",
    ).astype(jnp.float32)
    grad_attn_gain = jnp.sum(grad_normed * unit_one, axis=0)
    scaled_one = grad_normed * attention_gain
    grad_hidden = grad_middle + inverse_one * (
        scaled_one - unit_one * jnp.mean(scaled_one * unit_one, axis=-1, keepdims=True)
    )
    grad_inputs = grad_hidden.astype(jnp.bfloat16).reshape(seq_count, span_len, model_width)
    reduced = (
        lax.psum_scatter(
            grad_attn_gain.astype(jnp.bfloat16), ("dp", "ctx"), scatter_dimension=0, tiled=True
        ).astype(jnp.float32),
        lax.psum_scatter(
            grad_query.astype(jnp.bfloat16), ("dp", "ctx"), scatter_dimension=0, tiled=True
        ).astype(jnp.float32),
        lax.psum_scatter(
            grad_key.astype(jnp.bfloat16), ("dp", "ctx"), scatter_dimension=0, tiled=True
        ).astype(jnp.float32),
        lax.psum_scatter(
            grad_value.astype(jnp.bfloat16), ("dp", "ctx"), scatter_dimension=0, tiled=True
        ).astype(jnp.float32),
        lax.psum_scatter(
            grad_out_part.astype(jnp.bfloat16), ("dp", "ctx"), scatter_dimension=1, tiled=True
        ).astype(jnp.float32),
        lax.psum_scatter(
            grad_ffn_gain.astype(jnp.bfloat16), ("dp", "ctx"), scatter_dimension=0, tiled=True
        ).astype(jnp.float32),
        lax.psum_scatter(
            grad_gate.astype(jnp.bfloat16), ("dp", "ctx"), scatter_dimension=0, tiled=True
        ).astype(jnp.float32),
        lax.psum_scatter(
            grad_up.astype(jnp.bfloat16), ("dp", "ctx"), scatter_dimension=0, tiled=True
        ).astype(jnp.float32),
        lax.psum_scatter(
            grad_down.astype(jnp.bfloat16), ("dp", "ctx"), scatter_dimension=1, tiled=True
        ).astype(jnp.float32),
    )
    return (
        layer_out,
        grad_inputs,
        reduced[0],
        reduced[1],
        reduced[2],
        reduced[3],
        reduced[4],
        reduced[5],
        reduced[6],
        reduced[7],
        reduced[8],
    )


def fast_body(
    inputs, segment_ids, attention_gain, query_weight, key_weight, value_weight, out_weight, feedforward_gain,
    gate_weight, up_weight, down_weight, cotangent,
):
    _, span_len, model_width = inputs.shape
    line_size, dp_size = lax.axis_size("tensor"), lax.axis_size("dp")
    half_dim = HEAD_DIM // 2
    frequency = rope_base ** (-2.0 * jnp.arange(half_dim, dtype=jnp.float32) / HEAD_DIM)
    frequency = jnp.tile(frequency, 4).reshape(1, 128)
    flat_inputs = inputs.reshape(span_len, model_width)
    upstream = cotangent.reshape(span_len, model_width)
    gain_one, gain_two = attention_gain.reshape(1, -1), feedforward_gain.reshape(1, -1)
    key_turned, value_turned = key_weight.T, value_weight.T
    (
        seg_row, cosine, signed_sine, query, kv, logs, mixed, normed, normed_two, up, inner, second, attended,
        middle, grad_middle, land_gate, gain_grad, own_gate,
    ) = front_call(
        line_size, dp_size,
        (
            flat_inputs, segment_ids, frequency, gain_one, gain_two, query_weight, key_turned, value_turned, out_weight,
            gate_weight, up_weight, down_weight, upstream,
        ),
    )
    (
        layer_out, grad_inputs, gains, own_qkv, own_out, own_up, own_down, land_up, land_down, land_qkv, land_out
    ) = back_call(
        line_size, dp_size,
        (
            query, kv, logs, mixed, cosine, signed_sine, seg_row, flat_inputs, normed, normed_two,
            up, inner, second, attended, middle, grad_middle, gain_one, gain_grad,
            query_weight, key_turned, value_turned, out_weight, upstream,
        ),
    )
    layer_out, grad_inputs, gain_a, grad_query, grad_key, grad_value, grad_out, gain_b, *ffn = settle_call(
        (
            layer_out, grad_inputs, gains, own_qkv, own_out, own_gate, own_up, own_down,
            land_gate, land_up, land_down, land_qkv, land_out,
        )
    )
    shape = (1, span_len, model_width)
    return (
        layer_out.reshape(shape), grad_inputs.reshape(shape), gain_a[0], grad_query, grad_key.T, grad_value.T,
        grad_out, gain_b[0], *ffn,
    )


def body(mesh, *arrays):
    inputs = arrays[0]
    span_len, model_width = inputs.shape[1:]
    dp_size, ctx_size, line_size = mesh.shape["dp"], mesh.shape["ctx"], mesh.shape["tensor"]
    piece = model_width // (dp_size * ctx_size)
    fits = inputs.shape[0] == 1 and ctx_size == 2 and dp_size > 1 and line_size > 1
    if fits and piece % 128 == 0 and span_len % (2 * CHUNK) == 0:
        return fast_body(*arrays)
    return plain_body(*arrays)


def solution(mesh):
    return jax.shard_map(
        functools.partial(body, mesh),
        mesh=mesh,
        in_specs=(
            P("dp", "ctx", None),
            P("dp", "ctx"),
            P(),
            P(None, "tensor"),
            P(None, "tensor"),
            P(None, "tensor"),
            P("tensor", None),
            P(),
            P(None, "tensor"),
            P(None, "tensor"),
            P("tensor", None),
            P("dp", "ctx", None),
        ),
        out_specs=(
            P("dp", "ctx", None),
            P("dp", "ctx", None),
            P(("dp", "ctx")),
            P(("dp", "ctx"), "tensor"),
            P(("dp", "ctx"), "tensor"),
            P(("dp", "ctx"), "tensor"),
            P("tensor", ("dp", "ctx")),
            P(("dp", "ctx")),
            P(("dp", "ctx"), "tensor"),
            P(("dp", "ctx"), "tensor"),
            P("tensor", ("dp", "ctx")),
        ),
        check_vma=False,
    )
```

```python
import functools
import math

import jax
import jax.numpy as jnp
from jax import lax
from jax.experimental import pallas as pl
from jax.experimental.pallas import tpu as pltpu
from jax.sharding import PartitionSpec as P

HEAD_DIM = 64


epsilon = 1e-05
rope_base = 10000.0
masked_score = -1e30


def positions_of(segment):
    token_index = jnp.arange(segment.shape[-1], dtype=jnp.int32)
    previous = jnp.concatenate([segment[..., :1] - 1, segment[..., :-1]], axis=-1)
    starts = jnp.where(segment != previous, token_index, 0)
    earlier = token_index[None, :] <= token_index[:, None]
    run_start = jnp.max(jnp.where(earlier, starts[..., None, :], 0), axis=-1)
    return token_index - run_start


MESH = pl.DeviceIdType.MESH
CHUNK = 16
HOP = 2
MIB = 1 << 20
FRONT_MIB, BACK_MIB = 62, 62


def rotary_tables(positions):
    half_dim = HEAD_DIM // 2
    frequency = rope_base ** (-2.0 * jnp.arange(half_dim, dtype=jnp.float32) / HEAD_DIM)
    angles = positions.astype(jnp.float32)[..., None] * frequency
    return (jnp.cos(angles), jnp.sin(angles))


def rotate(values, cosine, sine_table):
    half_dim = values.shape[-1] // 2
    first = values[..., :half_dim]
    second = values[..., half_dim:]
    return jnp.concatenate(
        [first * cosine - second * sine_table, second * cosine + first * sine_table], axis=-1
    )


def visible(query_seg, key_seg, first_row):
    query_pos = first_row + jnp.arange(query_seg.shape[0], dtype=jnp.int32)
    key_pos = jnp.arange(key_seg.shape[0], dtype=jnp.int32)
    same_doc = query_seg[:, None] == key_seg[None, :]
    causal = key_pos[None, :] <= query_pos[:, None]
    usable = (key_seg[None, :] >= 0) | (key_pos[None, :] == query_pos[:, None])
    return same_doc & causal & usable


def turned_dot(left, right):
    return lax.dot_general(
        left, right, (((1,), (1,)), ((), ())), preferred_element_type=jnp.float32
    )


def remote(src, dst, send, recv, **device):
    return pltpu.make_async_remote_copy(
        src_ref=src, dst_ref=dst, send_sem=send, recv_sem=recv, device_id=device, device_id_type=MESH
    )


class Line:
    def __init__(self, line_size, own, finish, place, out_ref, held, acc_send, acc_recv, back_send, back_recv, base=0):
        self.base = base
        self.last = line_size - 1
        self.here = lax.axis_index("tensor")
        self.own, self.finish, self.place = own, finish, place
        self.out_ref, self.held = out_ref, held
        self.acc_sems, self.back_sems = (acc_send, acc_recv), (back_send, back_recv)
        self.count = held.shape[1]

    def parts(self, stream):
        if stream == 0:
            return self.here, self.here + 1, self.here - 1
        return self.last - self.here, self.here - 1, self.here + 1

    def acc_copy(self, stream, i, target):
        at = i - self.base
        ref = self.held.at[stream, at]
        return remote(ref, ref, self.acc_sems[0].at[stream, at], self.acc_sems[1].at[stream, at], tensor=target)

    def rows_of(self, stream, i):
        return pl.ds(pl.multiple_of(self.place(stream, i), CHUNK), CHUNK)

    def back_copy(self, stream, i, target):
        at = i - self.base
        ref = self.out_ref.at[self.rows_of(stream, i)]
        return remote(ref, ref, self.back_sems[0].at[stream, at], self.back_sems[1].at[stream, at], tensor=target)

    def step(self, k, begin=0, size=None):
        last, held = self.last, self.held
        size = self.count if size is None else size
        for stream in (0, 1):
            place, after, before = self.parts(stream)
            due = k - HOP * place
            inside = (due >= 0) & (due < size)
            i = begin + due

            @pl.when(inside & (place == 0))
            def _():
                held[stream, i - self.base] = self.own(stream, i).astype(jnp.bfloat16)
                self.acc_copy(stream, i, after).start()

            @pl.when(inside & (place > 0) & (place < last))
            def _():
                self.acc_copy(stream, i, after).wait_recv()
                at = i - self.base
                held[stream, at] = (held[stream, at].astype(jnp.float32) + self.own(stream, i)).astype(jnp.bfloat16)
                self.acc_copy(stream, i, after).start()

            @pl.when(inside & (place == last))
            def _():
                self.acc_copy(stream, i, before).wait_recv()
                total = held[stream, i - self.base].astype(jnp.float32) + self.own(stream, i)
                self.out_ref[self.rows_of(stream, i)] = self.finish(stream, i, total).astype(jnp.bfloat16)
                self.back_copy(stream, i, before).start()

            back = k - HOP * (2 * last - place)
            j = begin + back

            @pl.when((back >= 0) & (back < size) & (place < last))
            def _():
                self.back_copy(stream, j, before).wait_recv()

                @pl.when(place > 0)
                def _():
                    self.back_copy(stream, j, before).start()

    def drain(self):
        def sent(at, carry):
            i = at + self.base
            for stream in (0, 1):
                place, after, before = self.parts(stream)

                @pl.when(place < self.last)
                def _():
                    self.acc_copy(stream, i, after).wait_send()

                @pl.when(place > 0)
                def _():
                    self.back_copy(stream, i, before).wait_send()

            return carry

        lax.fori_loop(0, self.count, sent, 0)


def line_scratch(rows, width, share=1):
    count = rows // 2 // CHUNK // share
    return [
        pltpu.VMEM((2, count, CHUNK, width), jnp.bfloat16),
        *[pltpu.SemaphoreType.DMA((2, count))] * 4,
    ]


def greet(line, core, plane, full_line=False):
    here, row, side = lax.axis_index("tensor"), lax.axis_index("dp"), lax.axis_index("ctx")
    barrier = pltpu.get_barrier_semaphore()
    peers = 0

    def call(**device):
        pl.semaphore_signal(barrier, inc=1, device_id=device, device_id_type=MESH)

    if full_line:
        for hop in range(1, line):
            call(tensor=lax.rem(here + hop, line))
        peers += line - 1
    else:

        @pl.when(here > 0)
        def _():
            call(tensor=here - 1)

        @pl.when(here < line - 1)
        def _():
            call(tensor=here + 1)

        peers = jnp.where(here > 0, 1, 0) + jnp.where(here < line - 1, 1, 0)
    if plane:
        for hop in range(1, 2 * plane):
            peer = lax.rem(2 * row + side + hop, 2 * plane)
            call(dp=peer // 2, ctx=lax.rem(peer, 2))
        peers += 2 * plane - 1
    elif core:
        call(ctx=1 - side)
        peers += 1
    pl.semaphore_wait(barrier, peers)


def kept_rows(i):
    return pl.ds(pl.multiple_of(i * CHUNK, CHUNK), CHUNK)


def rotate_lanes(values, cosine, signed_sine, back=False):
    lane = lax.broadcasted_iota(jnp.int32, values.shape, 1)
    swapped = jnp.where(
        lax.rem(lane, HEAD_DIM) < HEAD_DIM // 2,
        pltpu.roll(values, 128 - HEAD_DIM // 2, 1),
        pltpu.roll(values, HEAD_DIM // 2, 1),
    )
    turn = swapped * signed_sine
    return values * cosine - turn if back else values * cosine + turn


def key_lanes(values, turned):
    lane = lax.broadcasted_iota(jnp.int32, values.shape, 1)
    return jnp.where(lane < HEAD_DIM, turned, values)


def fill_bias(bias, seg_col, seg_row, first, keys, block):
    key_seg = seg_col[0:keys]
    query_seg = seg_row[:, first : first + block]
    key_pos = lax.broadcasted_iota(jnp.int32, (keys, block), 0)
    query_pos = first + lax.broadcasted_iota(jnp.int32, (keys, block), 1)
    usable = (key_seg >= 0) | (key_pos == query_pos)
    allowed = (key_seg == query_seg) & (key_pos <= query_pos) & usable
    bias[0:keys, :] = jnp.where(allowed, 0.0, masked_score)


def wide_tiles(width):
    return width // 256, width % 256


def inverse_rms(values):
    return lax.rsqrt(jnp.mean(values * values, axis=-1, keepdims=True) + epsilon)


def front_kernel(
    n, dp_size,
    inputs_any, segments, frequency, gain_one, gain_two,
    query_weight_any, key_weight_any, value_weight_any, out_weight_any, gate_weight_any, up_weight_any, down_weight_any, upstream_any,
    seg_out, cosine_out, sine_out, query_out, kv_out, log_out, mixed_out, normed_cols, two_cols, upstream_cols, up_out, inner_out, second_out,
    attended_out, middle_out, grad_middle_out, land_gate, land_up, own_gate, gain_out,
    seg_all, seg_row, seg_col, cosine, signed_sine,
    inputs, normed, kv_weight, query, kv, kv_turned, logs, mixed, bias,
    gate_weight, up_weight, down_weight, upstream, grad_inner, normed_two, gate, up, inner,
    partial, middle, grad_middle, two_other, turned, send_gate, send_up,
    load_sems, store_sems, core_send, core_recv, plane_send, plane_recv, *line_refs,
):
    span, width = inputs.shape
    hidden, piece = gate.shape[1], turned.shape[0]
    row, core = lax.axis_index("dp"), lax.axis_index("ctx")
    half, block = span // 2, span // 4
    second, attended = normed, inputs
    line_one, line_two, line_three = line_refs[:5], line_refs[5:10], line_refs[10:]
    count, heads = line_one[0].shape[1], query.shape[1]
    part = count // 2

    def load(at, src, dst):
        made = pltpu.make_async_copy(src, dst, load_sems.at[at])
        made.start()
        return made

    def ordered(stream, i):
        return (i // part) * half + stream * block + lax.rem(i, part) * CHUNK

    def moved(at):
        return (0, 2, 1, 3)[at] * block

    load_inputs = load(0, inputs_any, inputs)
    query_weight = gate_weight.at[:, pl.ds(0, heads)]
    out_weight = down_weight.at[pl.ds(0, heads)]
    load_query = load(1, query_weight_any, query_weight)
    load_kv = [
        load(2, key_weight_any, kv_weight.at[pl.ds(0, HEAD_DIM)]),
        load(11, value_weight_any, kv_weight.at[pl.ds(HEAD_DIM, HEAD_DIM)]),
    ]
    load_out = load(3, out_weight_any, out_weight)
    load_up = [
        load(4 + b, upstream_any.at[pl.ds(b * block, block)], upstream.at[pl.ds(moved(b), block)]) for b in range(4)
    ]
    load_up_weight = load(10, up_weight_any, up_weight)
    seg_all[core] = jnp.broadcast_to(segments[...], seg_all.shape[1:])
    greet(n, True, dp_size)

    def seg_copy():
        return remote(seg_all.at[core], seg_all.at[core], core_send.at[1], core_recv.at[1], ctx=1 - core)

    seg_copy().start()
    load_inputs.wait()

    def norm_rows(b, carry):
        rows = pl.ds(pl.multiple_of(b * 64, 64), 64)
        value = inputs[rows].astype(jnp.float32)
        normed[rows] = (value * inverse_rms(value) * gain_one[...]).astype(jnp.bfloat16)
        return carry

    lax.fori_loop(0, span // 64, norm_rows, 0)
    seg_copy().wait()
    for side in (0, 1):
        seg_row[:, side * span : (side + 1) * span] = seg_all[side, 0:1]
        seg_col[side * span : (side + 1) * span] = seg_all[side].T[:, 0:1]
    own_seg = seg_all[core, 0:1]
    key_pos = lax.broadcasted_iota(jnp.int32, (2 * span, span), 0)
    query_pos = core * span + lax.broadcasted_iota(jnp.int32, (2 * span, span), 1)
    before = (seg_col[...] == own_seg) & (key_pos < query_pos)
    position = jnp.sum(jnp.where(before, 1.0, 0.0), axis=0, keepdims=True)
    angles = jnp.broadcast_to(position, (8, span)).T[:, 0:1] * frequency[...]
    lane = lax.broadcasted_iota(jnp.int32, angles.shape, 1)
    cosine[...] = jnp.cos(angles)
    sine = jnp.sin(angles)
    signed_sine[...] = jnp.where(lax.rem(lane, HEAD_DIM) < HEAD_DIM // 2, -sine, sine)
    for made in load_kv:
        made.wait()
    own_rows = pl.ds(pl.multiple_of(core * span, span), span)
    raw = turned_dot(normed[...], kv_weight[...])
    kv[own_rows] = key_lanes(raw, rotate_lanes(raw, cosine[...], signed_sine[...])).astype(jnp.bfloat16)

    def kv_copy():
        return remote(kv.at[own_rows], kv.at[own_rows], core_send.at[0], core_recv.at[0], ctx=1 - core)

    def kv_arrival():
        rows = pl.ds(0, span)
        return remote(kv.at[rows], kv.at[rows], core_send.at[0], core_recv.at[0], ctx=1 - core)

    @pl.when(core == 0)
    def _():
        kv_copy().start()

    load_query.wait()
    for low in range(0, span, half):
        rows = slice(low, low + half)
        raw = jnp.dot(normed[rows], query_weight[...], preferred_element_type=jnp.float32)
        for lanes in range(0, raw.shape[1], 128):
            rotated = rotate_lanes(raw[:, lanes : lanes + 128], cosine[rows], signed_sine[rows])
            query[rows, lanes : lanes + 128] = rotated.astype(jnp.bfloat16) * (HEAD_DIM ** -0.5)
    load_gate = load(9, gate_weight_any, gate_weight)

    @pl.when(core == 1)
    def _():
        kv_arrival().wait_recv()

    kv_turned[...] = kv[...].T

    def attend(side, at):
        keys = side * span + (at + 1) * half
        rows = slice(at * half, (at + 1) * half)
        fill_bias(bias, seg_col, seg_row, side * span + at * half, keys, half)

        def pair(index, carry):
            lanes = pl.ds(pl.multiple_of(index * 128, 128), 128)
            both = query[rows, lanes]
            outs = []
            for which in (0, 1):
                scores = turned_dot(kv[0:keys, 0:HEAD_DIM], both[:, which * HEAD_DIM : (which + 1) * HEAD_DIM])
                scores = scores + bias[0:keys, :]
                peak = jnp.max(scores, axis=0, keepdims=True)
                grown = jnp.exp(scores - peak)
                total = jnp.sum(grown, axis=0, keepdims=True)
                logs[pl.ds(2 * index + which, 1), rows] = peak + jnp.log(total)
                out = jnp.dot(
                    kv_turned[HEAD_DIM : 2 * HEAD_DIM, 0:keys],
                    grown.astype(jnp.bfloat16),
                    preferred_element_type=jnp.float32,
                )
                outs.append(out / total)
            mixed[rows, lanes] = jnp.concatenate(outs, axis=0).T.astype(jnp.bfloat16)
            return carry

        lax.fori_loop(0, query.shape[1] // 128, pair, 0)

    for side in (0, 1):

        @pl.when(core == side)
        def _():
            attend(side, 0)
            attend(side, 1)

    load_out.wait()

    def out_tile(t, carry):
        columns = pl.ds(pl.multiple_of(t * 512, 512), 512)
        for b in (0, 2):
            value = jnp.dot(
                mixed[b * block : (b + 2) * block], out_weight[:, columns], preferred_element_type=jnp.float32
            )
            partial[moved(b) : moved(b) + block, columns] = value[:block]
            partial[moved(b + 1) : moved(b + 1) + block, columns] = value[block:]
        return carry

    lax.fori_loop(0, width // 512, out_tile, 0)
    load_down = load(8, down_weight_any, down_weight)

    def rows_at(start):
        return pl.ds(pl.multiple_of(start, CHUNK), CHUNK)

    def own(stream, i):
        return partial[rows_at(ordered(stream, i))]

    def finish_one(stream, i, total):
        value = inputs[rows_at((stream * count + i) * CHUNK)].astype(jnp.float32) + total
        middle[kept_rows(i)] = value
        return value * inverse_rms(value) * gain_two[...]

    gain_out[...] = jnp.zeros_like(gain_out)

    def finish_two(stream, i, total):
        value = middle[kept_rows(i)]
        inverse = inverse_rms(value)
        unit = value * inverse
        gain_out[0:1, :] += jnp.sum(total * unit, axis=0, keepdims=True)
        scaled = total * gain_two[...]
        result = upstream[rows_at(ordered(stream, i))].astype(jnp.float32) + inverse * (
            scaled - unit * jnp.mean(scaled * unit, axis=-1, keepdims=True)
        )
        grad_middle[kept_rows(i)] = result
        return result

    first = Line(n, own, finish_one, ordered, normed_two, *line_one)
    then = Line(n, own, finish_two, ordered, attended, *line_two)
    third = Line(
        n,
        lambda stream, i: second[rows_at(ordered(stream, i))].astype(jnp.float32),
        lambda stream, i, total: middle[kept_rows(i)] + total,
        ordered, second, *line_three,
    )
    tiles, rest = wide_tiles(hidden)
    tile_count = tiles + (1 if rest else 0)

    def each_tile(t, work):
        @pl.when(t < tiles)
        def _():
            work(pl.ds(pl.multiple_of(t * 256, 256), 256))

        if rest:

            @pl.when(t == tiles)
            def _():
                work(pl.ds(tiles * 256, rest))

    def inner_tile(columns):
        grad_inner[:, columns] = turned_dot(upstream[...], down_weight[columns, :])

    def forward_tile(rows, columns):
        gated = jnp.dot(normed_two[rows], gate_weight[:, columns], preferred_element_type=jnp.float32)
        upped = jnp.dot(normed_two[rows], up_weight[:, columns], preferred_element_type=jnp.float32)
        sig = jax.nn.sigmoid(gated)
        act = gated * sig
        grad = grad_inner[rows, columns]
        inner[rows, columns] = (act * upped).astype(jnp.bfloat16)
        up[rows, columns] = (grad * act).astype(jnp.bfloat16)
        gate[rows, columns] = (grad * upped * sig * (1.0 + gated * (1.0 - sig))).astype(jnp.bfloat16)

    def back_tile(rows, t):
        columns = pl.ds(pl.multiple_of(t * 512, 512), 512)
        partial[rows, columns] = turned_dot(gate[rows], gate_weight[columns, :]) + turned_dot(
            up[rows], up_weight[columns, :]
        )

    def second_tile(rows, t):
        columns = pl.ds(pl.multiple_of(t * 512, 512), 512)
        second[rows, columns] = jnp.dot(
            inner[rows], down_weight[:, columns], preferred_element_type=jnp.float32
        ).astype(jnp.bfloat16)

    last = n - 1
    trip = 2 * HOP * last
    each = 2
    forward_steps, back_steps = -(-tile_count // each), width // 1024
    work = forward_steps + back_steps
    base_one = part + trip
    second_steps = width // 1024
    base_two = max(count + trip, base_one + work + second_steps)
    third_base = base_one + work + second_steps
    steps = max(base_two + work + part + trip, third_base + part + trip)

    def store(at, src, dst):
        return pltpu.make_async_copy(src, dst, store_sems.at[at])

    def stores(at, src, dst):
        return [
            store(at + b, src.at[pl.ds(moved(b), block)], dst.at[pl.ds(b * block, block)]) for b in range(4)
        ]

    early = [
        store(0, query, query_out), store(1, kv, kv_out), store(2, logs, log_out), store(3, mixed, mixed_out.at[pl.ds(0, span)]),
        store(31, seg_row, seg_out), store(32, cosine, cosine_out),
        store(33, signed_sine, sine_out),
    ]
    own_slots, far_slots = [], []

    def own_columns(src, dst):
        made = []
        for q in range(dp_size):
            columns = pl.ds(pl.multiple_of((2 * q + core) * piece, piece), piece)
            at = 34 + len(own_slots)
            own_slots.append(at)
            made.append(store(at, src.at[:, columns], dst.at[pl.ds(0, span), pl.ds(q * piece, piece)]))
        return made

    def far_copy(src, dst):
        at = 3 + dp_size + len(far_slots)
        far_slots.append(at)
        return remote(src, dst, core_send.at[at], core_recv.at[at], ctx=1 - core)

    def far_columns(src, dst):
        made = []
        for q in range(dp_size):
            columns = pl.ds(pl.multiple_of((2 * q + 1 - core) * piece, piece), piece)
            made.append(far_copy(src.at[:, columns], dst.at[pl.ds(span, span), pl.ds(q * piece, piece)]))
        return made

    normed_moves = [*own_columns(normed, normed_cols), *far_columns(normed, normed_cols)]
    upstream_moves = [*own_columns(upstream, upstream_cols), *far_columns(upstream, upstream_cols)]
    mixed_move = far_copy(mixed, mixed_out.at[pl.ds(span, span)])
    hidden_moves = [
        store(6, inner, inner_out.at[pl.ds(0, span)]), far_copy(inner, inner_out.at[pl.ds(span, span)]),
        *own_columns(normed_two, two_cols),
    ]
    up_slot = 3 + dp_size + len(far_slots)
    two_moves = [store(7, two_other, two_cols.at[pl.ds(span, span)]), store(5, up, up_out)]
    second_stores = stores(21, second, second_out)
    middle_store = store(29, middle, middle_out)

    def gate_swaps():
        made = [
            remote(
                ref.at[pl.ds(0, span)], ref.at[pl.ds(span, span)], core_send.at[at], core_recv.at[at], ctx=1 - core
            )
            for ref, at in ((gate, 2), (up, up_slot))
        ]
        for q in range(dp_size):
            columns = pl.ds(pl.multiple_of((2 * q + 1 - core) * piece, piece), piece)
            made.append(
                remote(
                    normed_two.at[:, columns], two_other.at[:, pl.ds(q * piece, piece)],
                    core_send.at[3 + q], core_recv.at[3 + q], ctx=1 - core,
                )
            )
        return made

    def peer_of(r):
        return lax.rem(row + 1 + r, dp_size)

    sends, lands = (send_gate, send_up), (land_gate, land_up)

    def gate_copy(w, r):
        return remote(sends[w].at[r], lands[w].at[r], plane_send.at[w, r], plane_recv.at[w, r], dp=peer_of(r))

    def turn_two(r):
        peer = peer_of(r)
        columns = pl.ds(pl.multiple_of((2 * peer + core) * piece, piece), piece)
        turned[:, 0:span] = normed_two[:, columns].T
        turned[:, span : 2 * span] = two_other[:, pl.ds(pl.multiple_of(peer * piece, piece), piece)].T

    edges = [(low, min(low + 384, hidden)) for low in range(0, hidden, 384)]

    def gate_piece(w, r):
        for low, high in edges:
            sends[w][r, :, low:high] = jnp.dot(
                turned[...], (gate, up)[w][:, low:high], preferred_element_type=jnp.float32
            ).astype(jnp.bfloat16)
        gate_copy(w, r).start()

    def own_piece():
        for low, high in edges:
            partial[0:piece, low:high] = jnp.dot(turned[...], gate[:, low:high], preferred_element_type=jnp.float32)

    own_store = store(4, partial.at[pl.ds(0, piece), pl.ds(0, hidden)], own_gate)

    for made in [*early, *normed_moves, mixed_move]:
        made.start()

    def step(k, carry):
        first.step(k)
        then.step(k - (base_one + work), 0, part)
        then.step(k - (base_two + work), part, part)
        third.step(k - third_base)

        @pl.when(k == 0)
        def _():
            for made in load_up:
                made.wait()
            for made in upstream_moves:
                made.start()

        @pl.when(k == 2)
        def _():
            load_down.wait()
            load_gate.wait()
            load_up_weight.wait()

        @pl.when((k >= 2) & (k < 2 + tile_count))
        def _():
            each_tile(k - 2, inner_tile)

        @pl.when(k == base_one)
        def _():
            for made in normed_moves:
                made.wait()

        @pl.when(k == base_two)
        def _():
            middle_store.start()

        late = jnp.where(k >= base_two, 1, 0)
        phase = k - jnp.where(k >= base_two, base_two, base_one)
        rows = pl.ds(pl.multiple_of(late * half, half), half)

        @pl.when((phase >= 0) & (phase < forward_steps))
        def _():
            def tile(t, carry):
                each_tile(t, functools.partial(forward_tile, rows))
                return carry

            lax.fori_loop(phase * each, jnp.minimum((phase + 1) * each, tile_count), tile, 0)

        @pl.when((phase >= forward_steps) & (phase < work))
        def _():
            for t in (0, 1):
                back_tile(rows, 2 * (phase - forward_steps) + t)

        @pl.when((phase >= work) & (phase < work + second_steps))
        def _():
            for t in (0, 1):
                second_tile(rows, 2 * (phase - work) + t)

        @pl.when(k == base_two + work)
        def _():
            for made in hidden_moves:
                made.start()

        @pl.when(k == base_two + forward_steps)
        def _():
            for made in gate_swaps():
                made.start()

        @pl.when(k == base_two + work + 1)
        def _():
            for made in gate_swaps():
                made.wait()
            for made in two_moves:
                made.start()

        gate_task = k - (base_two + work + 1)

        @pl.when((gate_task >= 0) & (gate_task < dp_size - 1))
        def _():
            turn_two(gate_task)
            gate_piece(0, gate_task)

            @pl.when(gate_task < dp_size - 2)
            def _():
                gate_piece(1, gate_task)

        @pl.when(k == base_two + work + part + HOP * last)
        def _():
            turn_two(dp_size - 1)
            own_piece()
            own_store.start()

        @pl.when(k == base_two + work + second_steps)
        def _():
            for b in (1, 3):
                second_stores[b].start()

        return carry

    lax.fori_loop(0, steps, step, 0)
    late_stores = [
        second_stores[0], second_stores[2], *stores(25, attended, attended_out), store(30, grad_middle, grad_middle_out),
    ]
    for made in late_stores:
        made.start()
    first.drain()
    then.drain()
    third.drain()

    @pl.when(core == 0)
    def _():
        kv_copy().wait_send()

    for r in range(dp_size - 1):
        for w in ((0, 1) if r < dp_size - 2 else (0,)):
            gate_copy(w, r).wait()
    for made in [
        *early, mixed_move, *upstream_moves, *hidden_moves, *two_moves, own_store, middle_store, second_stores[1], second_stores[3],
        *late_stores,
    ]:
        made.wait()


def front_call(line_size, dp_size, operands):
    inputs = operands[0]
    query_weight, out_weight, gate_weight = operands[5], operands[8], operands[9]
    span, width = inputs.shape
    heads, hidden = query_weight.shape[1], gate_weight.shape[1]
    piece = width // (2 * dp_size)
    low, full = jnp.bfloat16, jnp.float32
    vmem, outside = pl.BlockSpec(memory_space=pltpu.VMEM), pl.BlockSpec(memory_space=pl.ANY)
    dma = pltpu.SemaphoreType.DMA
    outs = [
        ((1, 2 * span), jnp.int32), ((span, 128), full), ((span, 128), full),
        ((span, heads), low), ((2 * span, 128), low), ((heads // HEAD_DIM, span), full), ((2 * span, heads), low),
        *[((2 * span, width // 2), low)] * 3, *[((2 * span, hidden), low)] * 2, ((span, width), low),
        ((span, width), low), ((span // 2, width), full), ((span // 2, width), full),
        ((dp_size - 1, piece, hidden), low), ((dp_size - 2, piece, hidden), low), ((piece, hidden), full), ((8, width), full),
    ]
    scratch = [
        pltpu.VMEM((2, 8, span), jnp.int32), pltpu.VMEM((1, 2 * span), jnp.int32),
        pltpu.VMEM((2 * span, 1), jnp.int32), pltpu.VMEM((span, 128), full), pltpu.VMEM((span, 128), full),
        pltpu.VMEM((span, width), low), pltpu.VMEM((span, width), low),
        pltpu.VMEM((128, width), low), pltpu.VMEM((span, heads), low),
        pltpu.VMEM((2 * span, 128), low), pltpu.VMEM((128, 2 * span), low),
        pltpu.VMEM((heads // HEAD_DIM, span), full), pltpu.VMEM((span, heads), low),
        pltpu.VMEM((2 * span, span // 2), full),
        pltpu.VMEM((width, hidden), low), pltpu.VMEM((width, hidden), low), pltpu.VMEM((hidden, width), low),
        pltpu.VMEM((span, width), low), pltpu.VMEM((span, hidden), full), pltpu.VMEM((span, width), low),
        *[pltpu.VMEM((2 * span, hidden), low)] * 2, pltpu.VMEM((span, hidden), low),
        pltpu.VMEM((span, width), full),
        pltpu.VMEM((span // 2, width), full), pltpu.VMEM((span // 2, width), full),
        pltpu.VMEM((span, width // 2), low), pltpu.VMEM((piece, 2 * span), low),
        pltpu.VMEM((dp_size - 1, piece, hidden), low), pltpu.VMEM((dp_size - 2, piece, hidden), low),
        dma((12,)), dma((34 + 3 * dp_size,)), dma((6 + 3 * dp_size,)), dma((6 + 3 * dp_size,)),
        dma((2, dp_size - 1)), dma((2, dp_size - 1)),
        *line_scratch(span, width), *line_scratch(span, width), *line_scratch(span, width, 2),
    ]
    return pl.pallas_call(
        functools.partial(front_kernel, line_size, dp_size),
        out_shape=[jax.ShapeDtypeStruct(s, d) for s, d in outs],
        in_specs=[outside] + [vmem] * 4 + [outside] * 8,
        out_specs=[outside] * 19 + [vmem],
        scratch_shapes=scratch,
        compiler_params=pltpu.CompilerParams(
            collective_id=1, has_side_effects=True, vmem_limit_bytes=FRONT_MIB * MIB
        ),
    )(*operands)


def back_kernel(
    n, dp_size,
    query_any, kv_any, logs, mixed_any, cosine, signed_sine, seg_row, inputs_any, normed_any, two_any, upstream_any,
    up_any, inner_any, second_any, attended_any, middle_any, grad_middle_any, gain_one, gain_two_grad,
    query_weight_any, key_weight_any, value_weight_any, out_weight_any,
    layer_out, grad_inputs, grad_gains, grad_qkv, own_out, grad_up, own_down,
    land_up, land_down, land_qkv, land_out,
    query, kv, kv_turned, grad_mixed, mixed, attended, normed_cols, two_cols, upstream_cols, attended_other,
    up, inner, pre, query_weight, kv_weight, out_weight, grad_middle, middle, inputs,
    ring, send_qkv, send_out, turned, seg_col, bias, kv_grad, kv_grad_other,
    gain_line, gain_land, gain_sum, gain_plane,
    load_sems, core_send, core_recv, ring_send, ring_recv, plane_send, plane_recv, line_send, line_recv,
    spread_send, spread_recv, *line_refs,
):
    span, width = attended.shape
    heads, piece = query.shape[1], turned.shape[0]
    here, row, core = lax.axis_index("tensor"), lax.axis_index("dp"), lax.axis_index("ctx")
    half = span // 2
    line_out, line_in = line_refs[:5], line_refs[5:]
    count, part = line_in[0].shape[1], line_out[0].shape[1]
    last = n - 1
    loads = []

    def load(src, dst):
        made = pltpu.make_async_copy(src, dst, load_sems.at[len(loads)])
        made.start()
        loads.append(made)
        return made

    own_half = pl.ds(pl.multiple_of(jnp.where(here == 0, half, 0), half), half)
    line_loads = [load(second_any, layer_out), load(middle_any, middle)]
    mixed_loads = [load(attended_any, attended), load(out_weight_any, out_weight)]
    attend_loads = [load(query_any, query), load(kv_any, kv)]

    up_loads = [load(two_any, two_cols), load(up_any, up)]
    inner_loads = [load(upstream_any, upstream_cols), load(inner_any, inner)]
    late_loads = [
        load(query_weight_any, query_weight), load(key_weight_any, kv_weight.at[pl.ds(0, HEAD_DIM)]),
        load(value_weight_any, kv_weight.at[pl.ds(HEAD_DIM, HEAD_DIM)]),
        load(grad_middle_any, grad_middle), load(inputs_any.at[own_half], inputs),
        load(mixed_any, mixed), load(normed_any, normed_cols),
    ]
    greet(n, True, dp_size, full_line=True)
    pre_slot, kv_slot = dp_size, dp_size + 1

    def attended_swaps():
        made = []
        for q in range(dp_size):
            columns = pl.ds(pl.multiple_of((2 * q + 1 - core) * piece, piece), piece)
            made.append(
                remote(
                    attended.at[:, columns], attended_other.at[:, pl.ds(q * piece, piece)],
                    core_send.at[q], core_recv.at[q], ctx=1 - core,
                )
            )
        return made

    def pre_swap():
        return remote(
            pre.at[pl.ds(0, span)], pre.at[pl.ds(span, span)], core_send.at[pre_slot], core_recv.at[pre_slot],
            ctx=1 - core,
        )

    def kv_swap():
        return remote(
            kv_grad.at[pl.ds(0, span)], kv_grad_other, core_send.at[kv_slot], core_recv.at[kv_slot], ctx=1 - core
        )

    gain_line[...] = jnp.zeros_like(gain_line)
    gain_line[1:2, :] = gain_two_grad[0:1, :]
    kv_grad[...] = jnp.zeros_like(kv_grad)
    seg_col[...] = jnp.broadcast_to(seg_row[...], (8, 2 * span)).T[:, 0:1]
    for made in line_loads:
        made.wait()

    def rows_at(start):
        return pl.ds(pl.multiple_of(start, CHUNK), CHUNK)

    def plain(stream, i):
        return (stream * count + i) * CHUNK

    def finish_out(stream, i, total):
        return middle[kept_rows(i)] + total

    def finish_in(stream, i, total):
        hidden = inputs[kept_rows(i)].astype(jnp.float32)
        inverse = inverse_rms(hidden)
        unit = hidden * inverse
        gain_line[0:1, :] += jnp.sum(total * unit, axis=0, keepdims=True)
        scaled = total * gain_one[...]
        return grad_middle[kept_rows(i)] + inverse * (
            scaled - unit * jnp.mean(scaled * unit, axis=-1, keepdims=True)
        )

    out_line = Line(
        n, lambda s, i: layer_out[rows_at(plain(s, i))].astype(jnp.float32), finish_out, plain, layer_out, *line_out,
        base=count - part,
    )
    in_line = Line(
        n, lambda s, i: grad_inputs[rows_at(plain(s, i))].astype(jnp.float32), finish_in, plain, grad_inputs, *line_in
    )

    def attend_back(side, at, index):
        keys = side * span + (at + 1) * half
        rows = slice(at * half, (at + 1) * half)
        lanes = pl.ds(pl.multiple_of(index * 128, 128), 128)

        @pl.when(index == 0)
        def _():
            fill_bias(bias, seg_col, seg_row, side * span + at * half, keys, half)

        both_query, both_grad = query[rows, lanes], grad_mixed[rows, lanes]
        outs, parts = [], None
        for which in (0, 1):
            head = slice(which * HEAD_DIM, (which + 1) * HEAD_DIM)
            query_head, grad_head = both_query[:, head], both_grad[:, head]
            scores = turned_dot(kv[0:keys, 0:HEAD_DIM], query_head) + bias[0:keys, :]
            probs = jnp.exp(scores - logs[pl.ds(2 * index + which, 1), rows])
            grad_probs = turned_dot(kv[0:keys, HEAD_DIM : 2 * HEAD_DIM], grad_head)
            both = probs * grad_probs
            grad_scores = (both - probs * jnp.sum(both, axis=0, keepdims=True)).astype(jnp.bfloat16)
            grad_key = jnp.dot(grad_scores, query_head, preferred_element_type=jnp.float32)
            grad_value = jnp.dot(probs.astype(jnp.bfloat16), grad_head, preferred_element_type=jnp.float32)
            part = jnp.concatenate([grad_key, grad_value], axis=1)
            parts = part if parts is None else parts + part
            outs.append(
                jnp.dot(kv_turned[0:HEAD_DIM, 0:keys], grad_scores, preferred_element_type=jnp.float32)
            )
        kv_grad[0:keys] += parts
        grad_query = jnp.concatenate(outs, axis=0).T * (HEAD_DIM ** -0.5)
        pre[rows, lanes] = rotate_lanes(grad_query, cosine[rows], signed_sine[rows], back=True).astype(jnp.bfloat16)

    pairs = heads // 128
    tasks = 2 * pairs

    def attend_task(task):
        for side in (0, 1):
            for at in (0, 1):

                @pl.when((core == side) & (task // pairs == at))
                def _():
                    attend_back(side, at, lax.rem(task, pairs))

    own_grad = pl.ds(pl.multiple_of(core * span, span), span)

    def finish_pre():
        @pl.when(core == 0)
        def _():
            kv_swap().wait_recv()
            kv_grad[0:span] += kv_grad_other[...]

        raw = kv_grad[own_grad]
        turned_back = rotate_lanes(raw, cosine[...], signed_sine[...], back=True)
        pre[0:span, heads : heads + 128] = key_lanes(raw, turned_back).astype(jnp.bfloat16)

    def in_products():
        def tile(t, carry):
            columns = pl.ds(pl.multiple_of(t * 512, 512), 512)
            for low in (0, half):
                rows = slice(low, low + half)
                grad_inputs[rows, columns] = (
                    turned_dot(pre[rows, 0:heads], query_weight[columns, :])
                    + jnp.dot(
                        pre[rows, heads : heads + 128], kv_weight[:, columns], preferred_element_type=jnp.float32
                    )
                ).astype(jnp.bfloat16)
            return carry

        lax.fori_loop(0, width // 512, tile, 0)

    def peer_of(r):
        return lax.rem(row + 1 + r, dp_size)

    def turn(r, cols):
        block = pl.multiple_of(peer_of(r) * piece, piece)
        turned[...] = cols[:, pl.ds(block, piece)].T

    def turn_attended(r):
        peer = peer_of(r)
        columns = pl.ds(pl.multiple_of((2 * peer + core) * piece, piece), piece)
        turned[:, 0:span] = attended[:, columns].T
        turned[:, span : 2 * span] = attended_other[:, pl.ds(pl.multiple_of(peer * piece, piece), piece)].T

    def tiles_of(stacked):
        wide = stacked.shape[1]
        return [(low, min(low + 384, wide)) for low in range(0, wide, 384)]

    def piece_value(stacked, low, high):
        return jnp.dot(turned[...], stacked[:, low:high], preferred_element_type=jnp.float32)

    others = dp_size - 1

    def ring_copy(at):
        r = others - 1 if at == 0 else at - 1
        land = land_up.at[0] if at == 0 else land_down.at[at - 1]
        return remote(ring.at[at], land, ring_send.at[at], ring_recv.at[at], dp=peer_of(r))

    def ring_piece(at, cols, stacked):
        turn(others - 1 if at == 0 else at - 1, cols)
        for low, high in tiles_of(stacked):
            ring[at, :, low:high] = piece_value(stacked, low, high).astype(jnp.bfloat16)
        ring_copy(at).start()

    def kept_piece(cols, stacked, own):
        turn(others, cols)
        for low, high in tiles_of(stacked):
            own[:, low:high] = piece_value(stacked, low, high)

    sends, lands = (send_qkv, send_out), (land_qkv, land_out)

    def plane_copy(w, r):
        return remote(sends[w].at[r], lands[w].at[r], plane_send.at[w, r], plane_recv.at[w, r], dp=peer_of(r))

    def plane_piece(w, r, stacked, own):
        @pl.when(r < dp_size - 1)
        def _():
            for low, high in tiles_of(stacked):
                sends[w][r, :, low:high] = piece_value(stacked, low, high).astype(jnp.bfloat16)
            plane_copy(w, r).start()

        @pl.when(r == dp_size - 1)
        def _():
            for low, high in tiles_of(stacked):
                own[:, low:high] = piece_value(stacked, low, high)

    def line_copies(owner, hops):
        slot = 0 if owner == 0 else 1
        return [
            remote(
                gain_line, gain_land.at[slot], line_send.at[slot, hop - 1], line_recv.at[slot],
                tensor=owner + hop if owner == 0 else owner - hop,
            )
            for hop in hops
        ]

    shard = width // (2 * dp_size)
    shards = 2 * dp_size
    place = 2 * row + core

    def spread(r):
        peer = lax.rem(place + 1 + r, shards)
        block = pl.multiple_of(peer * shard, shard)
        return remote(
            gain_sum.at[:, pl.ds(block, shard)], gain_plane.at[r], spread_send.at[r], spread_recv.at[r],
            dp=peer // 2, ctx=lax.rem(peer, 2),
        )

    def gather_gains():
        gain_sum[...] = jnp.zeros_like(gain_sum)
        for owner in (0, last):
            slot = 0 if owner == 0 else 1

            @pl.when(here == owner)
            def _():
                gain_sum[...] += gain_line[...]

            @pl.when(here != owner)
            def _():
                line_copies(owner, (1,))[0].wait_recv()
                gain_sum[...] += gain_land[slot]
        for r in range(shards - 1):
            spread(r).start()

    lag = tasks + 2
    ring_steps = [1, 3, 6] + [lag + at for at in range(dp_size - 3)]
    out_base = lag + 1
    steps = max(lag + count + 2 * HOP * last, out_base + dp_size)

    def step(k, carry):
        out_line.step(k, count - part, part)
        in_line.step(k - lag)

        @pl.when(k == 0)
        def _():
            for made in [*mixed_loads, *attend_loads]:
                made.wait()
            for made in attended_swaps():
                made.start()
            kv_turned[...] = kv[...].T
            grad_mixed[...] = turned_dot(attended[...], out_weight[...]).astype(jnp.bfloat16)

        @pl.when((k >= 1) & (k <= tasks))
        def _():
            attend_task(k - 1)

        @pl.when((k == tasks) & (core == 1))
        def _():
            kv_swap().start()

        @pl.when(k == 1)
        def _():
            for made in up_loads:
                made.wait()

        @pl.when(k == ring_steps[1])
        def _():
            for made in inner_loads:
                made.wait()

        @pl.when(k == tasks)
        def _():
            for made in [*late_loads, *attended_swaps()]:
                made.wait()

        @pl.when(k == tasks + 1)
        def _():
            finish_pre()
            in_products()
            pre_swap().start()

        for at in range(dp_size):

            @pl.when(k == ring_steps[at])
            def _():
                ring_piece(at, *((two_cols, up) if at == 0 else (upstream_cols, inner)))

        @pl.when(k == lag + dp_size)
        def _():
            kept_piece(two_cols, up, grad_up)

        @pl.when(k == lag + dp_size + 1)
        def _():
            kept_piece(upstream_cols, inner, own_down)

        @pl.when(k == out_base)
        def _():
            pre_swap().wait()

        at = k - out_base

        @pl.when((at >= 0) & (at < dp_size))
        def _():
            turn_attended(at)
            plane_piece(1, at, mixed, own_out)
            turn(at, normed_cols)
            plane_piece(0, at, pre, grad_qkv)

        @pl.when(k == lag + count + HOP * last - 1)
        def _():
            for owner in (0, last):

                @pl.when(here == owner)
                def _():
                    for made in line_copies(owner, range(1, n)):
                        made.start()

        @pl.when(k == lag + count + HOP * last + 3)
        def _():
            gather_gains()

        return carry

    lax.fori_loop(0, steps, step, 0)
    out_line.drain()
    in_line.drain()

    @pl.when(core == 1)
    def _():
        kv_swap().wait_send()

    for at in range(dp_size):
        ring_copy(at).wait()
    for r in range(others):
        for w in (0, 1):
            plane_copy(w, r).wait()
    grad_gains[...] = gain_sum[:, pl.ds(pl.multiple_of(place * shard, shard), shard)]
    for r in range(shards - 1):
        spread(r).wait()
        grad_gains[...] += gain_plane[r]
    for owner in (0, last):

        @pl.when(here == owner)
        def _():
            for made in line_copies(owner, range(1, n)):
                made.wait_send()


def back_call(line_size, dp_size, operands):
    query = operands[0]
    span, heads = query.shape
    width, hidden = operands[7].shape[1], operands[11].shape[1]
    piece = width // (2 * dp_size)
    wide = heads + 128
    low, full = jnp.bfloat16, jnp.float32
    vmem, outside = pl.BlockSpec(memory_space=pltpu.VMEM), pl.BlockSpec(memory_space=pl.ANY)
    dma = pltpu.SemaphoreType.DMA
    others = dp_size - 1
    outs = [
        ((span, width), low), ((span, width), low), ((8, piece), full), ((piece, wide), full), ((piece, heads), full),
        ((piece, hidden), full), ((piece, hidden), full),
        ((1, piece, hidden), low), ((others, piece, hidden), low), ((others, piece, wide), low), ((others, piece, heads), low),
    ]
    core_copies = dp_size + 2
    scratch = [
        pltpu.VMEM((span, heads), low), pltpu.VMEM((2 * span, 128), low), pltpu.VMEM((128, 2 * span), low),
        pltpu.VMEM((span, heads), low), pltpu.VMEM((2 * span, heads), low), pltpu.VMEM((span, width), low),
        *[pltpu.VMEM((2 * span, width // 2), low)] * 3, pltpu.VMEM((span, width // 2), low),
        *[pltpu.VMEM((2 * span, hidden), low)] * 2, pltpu.VMEM((2 * span, wide), low),
        pltpu.VMEM((width, heads), low), pltpu.VMEM((128, width), low), pltpu.VMEM((heads, width), low),
        pltpu.VMEM((span // 2, width), full), pltpu.VMEM((span // 2, width), full), pltpu.VMEM((span // 2, width), low),
        pltpu.VMEM((dp_size, piece, hidden), low), pltpu.VMEM((others, piece, wide), low),
        pltpu.VMEM((others, piece, heads), low),
        pltpu.VMEM((piece, 2 * span), low), pltpu.VMEM((2 * span, 1), jnp.int32), pltpu.VMEM((2 * span, span // 2), full),
        pltpu.VMEM((2 * span, 128), full), pltpu.VMEM((span, 128), full),
        pltpu.VMEM((8, width), full), pltpu.VMEM((2, 8, width), full), pltpu.VMEM((8, width), full),
        pltpu.VMEM((2 * dp_size - 1, 8, piece), full),
        dma((17,)), dma((core_copies,)), dma((core_copies,)),
        dma((dp_size,)), dma((dp_size,)), dma((2, others)), dma((2, others)),
        dma((2, line_size - 1)), dma((2,)), dma((2 * dp_size - 1,)), dma((2 * dp_size - 1,)),
        *line_scratch(span, width, 2), *line_scratch(span, width),
    ]
    spaces = [outside, outside, vmem, outside, vmem, vmem, vmem] + [outside] * 10 + [vmem, vmem] + [outside] * 4
    return pl.pallas_call(
        functools.partial(back_kernel, line_size, dp_size),
        out_shape=[jax.ShapeDtypeStruct(s, d) for s, d in outs],
        in_specs=spaces,
        out_specs=[vmem] * 7 + [outside] * 4,
        scratch_shapes=scratch,
        compiler_params=pltpu.CompilerParams(
            collective_id=2, has_side_effects=True, vmem_limit_bytes=BACK_MIB * MIB
        ),
    )(*operands)


def settle_kernel(
    layer_any, inputs_any, gains, qkv_any, out_any, gate_any, up_any, down_any,
    land_gate, land_up, land_up_last, land_down, land_qkv, land_out,
    layer_out, grad_inputs, gain_one, grad_query, grad_key, grad_value, grad_out, gain_two, grad_gate, grad_up, grad_down,
    own_qkv, own_out, own_gate, own_up, own_down, far_qkv, far_out, far_gate, far_up, far_down,
    turned_kv, turned_out, turned_down, layer_held, inputs_held, in_sems, out_sems,
):
    whole, early = [], land_up.shape[0]
    passed = [
        pltpu.make_async_copy(layer_any, layer_held, in_sems.at[0, 5]),
        pltpu.make_async_copy(inputs_any, inputs_held, in_sems.at[1, 5]),
        pltpu.make_async_copy(land_up_last, far_up.at[pl.ds(early, 1)], in_sems.at[0, 6]),
    ]
    owns = ((qkv_any, own_qkv), (out_any, own_out), (gate_any, own_gate), (up_any, own_up), (down_any, own_down))
    fars = (
        (land_qkv, far_qkv), (land_out, far_out), (land_gate, far_gate), (land_up, far_up.at[pl.ds(0, early)]),
        (land_down, far_down),
    )
    loads = [
        (
            pltpu.make_async_copy(*own, in_sems.at[0, at]),
            pltpu.make_async_copy(*far, in_sems.at[1, at]),
        )
        for at, (own, far) in enumerate(zip(owns, fars))
    ]
    for pair in loads:
        for made in pair:
            made.start()
    for made in passed:
        made.start()
    gain_one[...] = gains[0:1]
    gain_two[...] = gains[1:2]

    def settle(at, own, far):
        for made in loads[at]:
            made.wait()
        total = own[...]
        for r in range(far.shape[0]):
            total = total + far[r].astype(jnp.float32)
        return total

    def put(at, src, dst):
        made = pltpu.make_async_copy(src, dst, out_sems.at[at])
        made.start()
        whole.append(made)

    heads = grad_query.shape[1]
    own_qkv[...] = settle(0, own_qkv, far_qkv)
    put(2, own_qkv.at[:, pl.ds(0, heads)], grad_query)
    turned_kv[...] = own_qkv[:, heads:].T
    put(3, turned_kv.at[pl.ds(0, HEAD_DIM)], grad_key)
    put(4, turned_kv.at[pl.ds(HEAD_DIM, HEAD_DIM)], grad_value)
    turned_out[...] = settle(1, own_out, far_out).T
    put(5, turned_out, grad_out)
    passed[0].wait()
    put(0, layer_held, layer_out)
    own_gate[...] = settle(2, own_gate, far_gate)
    put(6, own_gate, grad_gate)
    passed[2].wait()
    own_up[...] = settle(3, own_up, far_up)
    put(7, own_up, grad_up)
    passed[1].wait()
    put(1, inputs_held, grad_inputs)
    turned_down[...] = settle(4, own_down, far_down).T
    put(8, turned_down, grad_down)
    for made in whole:
        made.wait()


def settle_call(operands):
    layer_out, _, gains, qkv, out, gate = operands[:6]
    piece, wide = qkv.shape
    heads, hidden = out.shape[1], gate.shape[1]
    others = operands[8].shape[0]
    low, full = jnp.bfloat16, jnp.float32
    vmem, outside = pl.BlockSpec(memory_space=pltpu.VMEM), pl.BlockSpec(memory_space=pl.ANY)
    outs = [
        (layer_out.shape, low), (layer_out.shape, low), ((1, piece), full), ((piece, heads), full),
        ((HEAD_DIM, piece), full), ((HEAD_DIM, piece), full), ((heads, piece), full), ((1, piece), full),
        ((piece, hidden), full), ((piece, hidden), full), ((hidden, piece), full),
    ]
    shapes = [(piece, wide), (piece, heads), *[(piece, hidden)] * 3]
    scratch = [
        *[pltpu.VMEM(shape, full) for shape in shapes], *[pltpu.VMEM((others, *shape), low) for shape in shapes],
        pltpu.VMEM((wide - heads, piece), full), pltpu.VMEM((heads, piece), full), pltpu.VMEM((hidden, piece), full),
        pltpu.VMEM(layer_out.shape, low), pltpu.VMEM(layer_out.shape, low),
        pltpu.SemaphoreType.DMA((2, 7)), pltpu.SemaphoreType.DMA((9,)),
    ]
    return pl.pallas_call(
        settle_kernel,
        out_shape=[jax.ShapeDtypeStruct(s, d) for s, d in outs],
        in_specs=[outside, outside, vmem] + [outside] * 11,
        out_specs=[outside, outside, vmem] + [outside] * 4 + [vmem] + [outside] * 3,
        scratch_shapes=scratch,
        compiler_params=pltpu.CompilerParams(vmem_limit_bytes=62 * MIB),
    )(*operands)


def plain_body(
    inputs,
    segment_ids,
    attention_gain,
    query_weight,
    key_weight,
    value_weight,
    out_weight,
    feedforward_gain,
    gate_weight,
    up_weight,
    down_weight,
    cotangent,
):
    seq_count, span_len, model_width = inputs.shape
    row_count = seq_count * span_len
    query_heads = query_weight.shape[1] // HEAD_DIM
    kv_heads = key_weight.shape[1] // HEAD_DIM
    group_size = query_heads // kv_heads
    score_scale = 1.0 / math.sqrt(HEAD_DIM)
    offset = lax.axis_index("ctx") * span_len
    whole_segments = lax.all_gather(segment_ids, "ctx", axis=1, tiled=True)
    own_positions = lax.dynamic_slice_in_dim(positions_of(whole_segments), offset, span_len, 1)
    cosine, sine_table = rotary_tables(own_positions)
    cosine = cosine[:, :, None, :]
    sine_table = sine_table[:, :, None, :]
    hidden = inputs.astype(jnp.float32).reshape(row_count, model_width)
    inverse_one = lax.rsqrt(jnp.mean(hidden * hidden, axis=-1, keepdims=True) + epsilon)
    unit_one = hidden * inverse_one
    normed = (unit_one * attention_gain).astype(jnp.bfloat16)
    query_rows = rotate(
        jnp.dot(normed, query_weight, preferred_element_type=jnp.float32).reshape(
            seq_count, span_len, query_heads, HEAD_DIM
        ),
        cosine,
        sine_table,
    ).astype(jnp.bfloat16)
    key_rows = rotate(
        jnp.dot(normed, key_weight, preferred_element_type=jnp.float32).reshape(
            seq_count, span_len, kv_heads, HEAD_DIM
        ),
        cosine,
        sine_table,
    ).astype(jnp.bfloat16)
    value_rows = (
        jnp.dot(normed, value_weight, preferred_element_type=jnp.float32)
        .astype(jnp.bfloat16)
        .reshape(seq_count, span_len, kv_heads, HEAD_DIM)
    )
    all_keys, all_values = (
        lax.all_gather(key_rows, "ctx", axis=1, tiled=True),
        lax.all_gather(value_rows, "ctx", axis=1, tiled=True),
    )

    def attend(block_items):
        query_block, key_block, value_block, query_seg, key_seg = block_items
        allowed = visible(query_seg, key_seg, offset)
        grouped = query_block.reshape(span_len, kv_heads, group_size, HEAD_DIM)
        raw_scores = jnp.einsum(
            "qhgd,khd->hgqk", grouped, key_block, preferred_element_type=jnp.float32
        )
        scores = jnp.where(allowed, raw_scores * score_scale, masked_score)
        row_peak = jnp.max(scores, axis=-1, keepdims=True)
        shifted_exp = jnp.exp(scores - row_peak)
        denominator = jnp.sum(shifted_exp, axis=-1, keepdims=True)
        attn_probs = (shifted_exp / denominator).astype(jnp.bfloat16)
        mixed_block = jnp.einsum(
            "hgqk,khd->qhgd", attn_probs, value_block, preferred_element_type=jnp.float32
        )
        return (
            mixed_block.astype(jnp.bfloat16).reshape(span_len, query_heads * HEAD_DIM),
            row_peak + jnp.log(denominator),
        )

    mixed_heads, log_sums = lax.map(
        attend, (query_rows, all_keys, all_values, segment_ids, whole_segments)
    )
    mixed_flat = mixed_heads.reshape(row_count, query_heads * HEAD_DIM)
    attended = lax.psum(
        jnp.dot(mixed_flat, out_weight, preferred_element_type=jnp.float32), "tensor"
    )
    middle = hidden + attended
    inverse_two = lax.rsqrt(jnp.mean(middle * middle, axis=-1, keepdims=True) + epsilon)
    unit_two = middle * inverse_two
    normed_two = (unit_two * feedforward_gain).astype(jnp.bfloat16)
    gate_pre = jnp.dot(normed_two, gate_weight, preferred_element_type=jnp.float32)
    up_pre = jnp.dot(normed_two, up_weight, preferred_element_type=jnp.float32)
    sigmoid_gate = jax.nn.sigmoid(gate_pre)
    inner_act = (gate_pre * sigmoid_gate * up_pre).astype(jnp.bfloat16)
    feed_out = lax.psum(
        jnp.dot(inner_act, down_weight, preferred_element_type=jnp.float32).astype(jnp.bfloat16),
        "tensor",
    ).astype(jnp.float32)
    layer_out = (middle + feed_out).astype(jnp.bfloat16).reshape(seq_count, span_len, model_width)
    upstream = cotangent.reshape(row_count, model_width)
    grad_down = jnp.dot(inner_act.T, upstream, preferred_element_type=jnp.float32)
    grad_inner = jnp.dot(upstream, down_weight.T, preferred_element_type=jnp.float32)
    grad_up_pre = (grad_inner * gate_pre * sigmoid_gate).astype(jnp.bfloat16)
    grad_gate_pre = (
        grad_inner * up_pre * sigmoid_gate * (1.0 + gate_pre * (1.0 - sigmoid_gate))
    ).astype(jnp.bfloat16)
    grad_gate = jnp.dot(normed_two.T, grad_gate_pre, preferred_element_type=jnp.float32)
    grad_up = jnp.dot(normed_two.T, grad_up_pre, preferred_element_type=jnp.float32)
    grad_normed_two = lax.psum(
        jnp.dot(grad_gate_pre, gate_weight.T, preferred_element_type=jnp.float32)
        + jnp.dot(grad_up_pre, up_weight.T, preferred_element_type=jnp.float32),
        "tensor",
    )
    grad_ffn_gain = jnp.sum(grad_normed_two * unit_two, axis=0)
    scaled_two = grad_normed_two * feedforward_gain
    grad_middle = upstream.astype(jnp.float32) + inverse_two * (
        scaled_two - unit_two * jnp.mean(scaled_two * unit_two, axis=-1, keepdims=True)
    )
    grad_attended = grad_middle.astype(jnp.bfloat16)
    grad_out_part = jnp.dot(mixed_flat.T, grad_attended, preferred_element_type=jnp.float32)
    grad_mixed = (
        jnp.dot(grad_attended, out_weight.T, preferred_element_type=jnp.float32)
        .astype(jnp.bfloat16)
        .reshape(seq_count, span_len, query_heads, HEAD_DIM)
    )

    def attend_back(block_items):
        query_block, key_block, value_block, query_seg, key_seg, grad_block, log_block = block_items
        allowed = visible(query_seg, key_seg, offset)
        grouped = query_block.reshape(span_len, kv_heads, group_size, HEAD_DIM)
        grad_grouped = grad_block.reshape(span_len, kv_heads, group_size, HEAD_DIM)
        raw_scores = jnp.einsum(
            "qhgd,khd->hgqk", grouped, key_block, preferred_element_type=jnp.float32
        )
        scores = jnp.where(allowed, raw_scores * score_scale, masked_score)
        attn_probs = jnp.exp(scores - log_block)
        rounded = attn_probs.astype(jnp.bfloat16)
        grad_values = jnp.einsum(
            "hgqk,qhgd->khd", rounded, grad_grouped, preferred_element_type=jnp.float32
        )
        grad_probs = jnp.einsum(
            "qhgd,khd->hgqk", grad_grouped, value_block, preferred_element_type=jnp.float32
        )
        row_dot = jnp.sum(attn_probs * grad_probs, axis=-1, keepdims=True)
        grad_scores = (attn_probs * (grad_probs - row_dot) * score_scale).astype(jnp.bfloat16)
        grad_queries = jnp.einsum(
            "hgqk,khd->qhgd", grad_scores, key_block, preferred_element_type=jnp.float32
        ).reshape(span_len, query_heads, HEAD_DIM)
        grad_keys = jnp.einsum(
            "hgqk,qhgd->khd", grad_scores, grouped, preferred_element_type=jnp.float32
        )
        return (grad_queries, grad_keys, grad_values)

    grad_queries, grad_keys, grad_values = lax.map(
        attend_back,
        (query_rows, all_keys, all_values, segment_ids, whole_segments, grad_mixed, log_sums),
    )
    own_grad_keys, own_grad_values = (
        lax.psum_scatter(grad_keys, "ctx", scatter_dimension=1, tiled=True),
        lax.psum_scatter(grad_values, "ctx", scatter_dimension=1, tiled=True),
    )
    grad_query_pre = (
        rotate(grad_queries, cosine, -sine_table)
        .astype(jnp.bfloat16)
        .reshape(row_count, query_heads * HEAD_DIM)
    )
    grad_key_pre = (
        rotate(own_grad_keys, cosine, -sine_table)
        .astype(jnp.bfloat16)
        .reshape(row_count, kv_heads * HEAD_DIM)
    )
    grad_value_pre = own_grad_values.astype(jnp.bfloat16).reshape(row_count, kv_heads * HEAD_DIM)
    grad_query = jnp.dot(normed.T, grad_query_pre, preferred_element_type=jnp.float32)
    grad_key = jnp.dot(normed.T, grad_key_pre, preferred_element_type=jnp.float32)
    grad_value = jnp.dot(normed.T, grad_value_pre, preferred_element_type=jnp.float32)
    grad_normed = lax.psum(
        (
            jnp.dot(grad_query_pre, query_weight.T, preferred_element_type=jnp.float32)
            + jnp.dot(grad_key_pre, key_weight.T, preferred_element_type=jnp.float32)
            + jnp.dot(grad_value_pre, value_weight.T, preferred_element_type=jnp.float32)
        ).astype(jnp.bfloat16),
        "tensor",
    ).astype(jnp.float32)
    grad_attn_gain = jnp.sum(grad_normed * unit_one, axis=0)
    scaled_one = grad_normed * attention_gain
    grad_hidden = grad_middle + inverse_one * (
        scaled_one - unit_one * jnp.mean(scaled_one * unit_one, axis=-1, keepdims=True)
    )
    grad_inputs = grad_hidden.astype(jnp.bfloat16).reshape(seq_count, span_len, model_width)
    reduced = (
        lax.psum_scatter(
            grad_attn_gain.astype(jnp.bfloat16), ("dp", "ctx"), scatter_dimension=0, tiled=True
        ).astype(jnp.float32),
        lax.psum_scatter(
            grad_query.astype(jnp.bfloat16), ("dp", "ctx"), scatter_dimension=0, tiled=True
        ).astype(jnp.float32),
        lax.psum_scatter(
            grad_key.astype(jnp.bfloat16), ("dp", "ctx"), scatter_dimension=0, tiled=True
        ).astype(jnp.float32),
        lax.psum_scatter(
            grad_value.astype(jnp.bfloat16), ("dp", "ctx"), scatter_dimension=0, tiled=True
        ).astype(jnp.float32),
        lax.psum_scatter(
            grad_out_part.astype(jnp.bfloat16), ("dp", "ctx"), scatter_dimension=1, tiled=True
        ).astype(jnp.float32),
        lax.psum_scatter(
            grad_ffn_gain.astype(jnp.bfloat16), ("dp", "ctx"), scatter_dimension=0, tiled=True
        ).astype(jnp.float32),
        lax.psum_scatter(
            grad_gate.astype(jnp.bfloat16), ("dp", "ctx"), scatter_dimension=0, tiled=True
        ).astype(jnp.float32),
        lax.psum_scatter(
            grad_up.astype(jnp.bfloat16), ("dp", "ctx"), scatter_dimension=0, tiled=True
        ).astype(jnp.float32),
        lax.psum_scatter(
            grad_down.astype(jnp.bfloat16), ("dp", "ctx"), scatter_dimension=1, tiled=True
        ).astype(jnp.float32),
    )
    return (
        layer_out,
        grad_inputs,
        reduced[0],
        reduced[1],
        reduced[2],
        reduced[3],
        reduced[4],
        reduced[5],
        reduced[6],
        reduced[7],
        reduced[8],
    )


def fast_body(
    inputs, segment_ids, attention_gain, query_weight, key_weight, value_weight, out_weight, feedforward_gain,
    gate_weight, up_weight, down_weight, cotangent,
):
    _, span_len, model_width = inputs.shape
    line_size, dp_size = lax.axis_size("tensor"), lax.axis_size("dp")
    half_dim = HEAD_DIM // 2
    frequency = rope_base ** (-2.0 * jnp.arange(half_dim, dtype=jnp.float32) / HEAD_DIM)
    frequency = jnp.tile(frequency, 4).reshape(1, 128)
    flat_inputs = inputs.reshape(span_len, model_width)
    upstream = cotangent.reshape(span_len, model_width)
    gain_one, gain_two = attention_gain.reshape(1, -1), feedforward_gain.reshape(1, -1)
    key_turned, value_turned = key_weight.T, value_weight.T
    (
        seg_row, cosine, signed_sine, query, kv, logs, mixed, normed, two, upstream_cols, up, inner, second, attended,
        middle, grad_middle, land_gate, land_up, own_gate, gain_grad,
    ) = front_call(
        line_size, dp_size,
        (
            flat_inputs, segment_ids, frequency, gain_one, gain_two, query_weight, key_turned, value_turned, out_weight,
            gate_weight, up_weight, down_weight, upstream,
        ),
    )
    (
        layer_out, grad_inputs, gains, own_qkv, own_out, own_up, own_down, land_up_last, land_down, land_qkv,
        land_out,
    ) = back_call(
        line_size, dp_size,
        (
            query, kv, logs, mixed, cosine, signed_sine, seg_row, flat_inputs, normed, two, upstream_cols,
            up, inner, second, attended, middle, grad_middle, gain_one, gain_grad,
            query_weight, key_turned, value_turned, out_weight,
        ),
    )
    layer_out, grad_inputs, gain_a, grad_query, grad_key, grad_value, grad_out, gain_b, *ffn = settle_call(
        (
            layer_out, grad_inputs, gains, own_qkv, own_out, own_gate, own_up, own_down,
            land_gate, land_up, land_up_last, land_down, land_qkv, land_out,
        )
    )
    shape = (1, span_len, model_width)
    return (
        layer_out.reshape(shape), grad_inputs.reshape(shape), gain_a[0], grad_query, grad_key.T, grad_value.T,
        grad_out, gain_b[0], *ffn,
    )


def body(mesh, *arrays):
    inputs = arrays[0]
    span_len, model_width = inputs.shape[1:]
    dp_size, ctx_size, line_size = mesh.shape["dp"], mesh.shape["ctx"], mesh.shape["tensor"]
    piece = model_width // (dp_size * ctx_size)
    fits = inputs.shape[0] == 1 and ctx_size == 2 and dp_size > 2 and line_size > 1
    if fits and piece % 128 == 0 and span_len % (2 * CHUNK) == 0:
        return fast_body(*arrays)
    return plain_body(*arrays)


def solution(mesh):
    return jax.shard_map(
        functools.partial(body, mesh),
        mesh=mesh,
        in_specs=(
            P("dp", "ctx", None),
            P("dp", "ctx"),
            P(),
            P(None, "tensor"),
            P(None, "tensor"),
            P(None, "tensor"),
            P("tensor", None),
            P(),
            P(None, "tensor"),
            P(None, "tensor"),
            P("tensor", None),
            P("dp", "ctx", None),
        ),
        out_specs=(
            P("dp", "ctx", None),
            P("dp", "ctx", None),
            P(("dp", "ctx")),
            P(("dp", "ctx"), "tensor"),
            P(("dp", "ctx"), "tensor"),
            P(("dp", "ctx"), "tensor"),
            P("tensor", ("dp", "ctx")),
            P(("dp", "ctx")),
            P(("dp", "ctx"), "tensor"),
            P(("dp", "ctx"), "tensor"),
            P("tensor", ("dp", "ctx")),
        ),
        check_vma=False,
    )
```

```python
import functools
import math

import jax
import jax.numpy as jnp
from jax import lax
from jax.experimental import pallas as pl
from jax.experimental.pallas import tpu as pltpu
from jax.sharding import PartitionSpec as P

HEAD_DIM = 64


epsilon = 1e-05
rope_base = 10000.0
masked_score = -1e30


def positions_of(segment):
    token_index = jnp.arange(segment.shape[-1], dtype=jnp.int32)
    previous = jnp.concatenate([segment[..., :1] - 1, segment[..., :-1]], axis=-1)
    starts = jnp.where(segment != previous, token_index, 0)
    earlier = token_index[None, :] <= token_index[:, None]
    run_start = jnp.max(jnp.where(earlier, starts[..., None, :], 0), axis=-1)
    return token_index - run_start


MESH = pl.DeviceIdType.MESH
CHUNK, HOP = 16, 2
BACK_CHUNK, BACK_HOP = 32, 2
TASKS = 1
RINGS = [1, 2, 4]
MIB = 1 << 20
FRONT_MIB, BACK_MIB = 62, 62


def rotary_tables(positions):
    half_dim = HEAD_DIM // 2
    frequency = rope_base ** (-2.0 * jnp.arange(half_dim, dtype=jnp.float32) / HEAD_DIM)
    angles = positions.astype(jnp.float32)[..., None] * frequency
    return (jnp.cos(angles), jnp.sin(angles))


def rotate(values, cosine, sine_table):
    half_dim = values.shape[-1] // 2
    first = values[..., :half_dim]
    second = values[..., half_dim:]
    return jnp.concatenate(
        [first * cosine - second * sine_table, second * cosine + first * sine_table], axis=-1
    )


def visible(query_seg, key_seg, first_row):
    query_pos = first_row + jnp.arange(query_seg.shape[0], dtype=jnp.int32)
    key_pos = jnp.arange(key_seg.shape[0], dtype=jnp.int32)
    same_doc = query_seg[:, None] == key_seg[None, :]
    causal = key_pos[None, :] <= query_pos[:, None]
    usable = (key_seg[None, :] >= 0) | (key_pos[None, :] == query_pos[:, None])
    return same_doc & causal & usable


def turned_dot(left, right):
    return lax.dot_general(
        left, right, (((1,), (1,)), ((), ())), preferred_element_type=jnp.float32
    )


def remote(src, dst, send, recv, **device):
    return pltpu.make_async_remote_copy(
        src_ref=src, dst_ref=dst, send_sem=send, recv_sem=recv, device_id=device, device_id_type=MESH
    )


class Line:
    def __init__(self, line_size, own, finish, place, out_ref, held, acc_send, acc_recv, back_send, back_recv, base=0, hop=HOP):
        self.base, self.hop = base, hop
        self.last = line_size - 1
        self.here = lax.axis_index("tensor")
        self.own, self.finish, self.place = own, finish, place
        self.out_ref, self.held = out_ref, held
        self.acc_sems, self.back_sems = (acc_send, acc_recv), (back_send, back_recv)
        self.count, self.chunk = held.shape[1:3]

    def parts(self, stream):
        if stream == 0:
            return self.here, self.here + 1, self.here - 1
        return self.last - self.here, self.here - 1, self.here + 1

    def acc_copy(self, stream, i, target):
        at = i - self.base
        ref = self.held.at[stream, at]
        return remote(ref, ref, self.acc_sems[0].at[stream, at], self.acc_sems[1].at[stream, at], tensor=target)

    def rows_of(self, stream, i):
        return pl.ds(pl.multiple_of(self.place(stream, i), self.chunk), self.chunk)

    def back_copy(self, stream, i, target):
        at = i - self.base
        ref = self.out_ref.at[self.rows_of(stream, i)]
        return remote(ref, ref, self.back_sems[0].at[stream, at], self.back_sems[1].at[stream, at], tensor=target)

    def step(self, k, begin=0, size=None):
        size = self.count if size is None else size

        @pl.when((k >= 0) & (k < size + 2 * self.hop * self.last))
        def _():
            for stream in (0, 1):
                self.stream_step(k, stream, begin, size)

    def stream_step(self, k, stream, begin, size):
        last, held = self.last, self.held
        place, after, before = self.parts(stream)
        due = k - self.hop * place
        i = begin + due
        at = i - self.base

        @pl.when((due >= 0) & (due < size))
        def _():
            @pl.when(place == 0)
            def _():
                held[stream, at] = self.own(stream, i).astype(jnp.bfloat16)
                self.acc_copy(stream, i, after).start()

            @pl.when(place > 0)
            def _():
                self.acc_copy(stream, i, after).wait_recv()

                @pl.when(place < last)
                def _():
                    held[stream, at] = (held[stream, at].astype(jnp.float32) + self.own(stream, i)).astype(jnp.bfloat16)
                    self.acc_copy(stream, i, after).start()

                @pl.when(place == last)
                def _():
                    total = held[stream, at].astype(jnp.float32) + self.own(stream, i)
                    self.out_ref[self.rows_of(stream, i)] = self.finish(stream, i, total).astype(jnp.bfloat16)
                    self.back_copy(stream, i, before).start()

        back = k - self.hop * (2 * last - place)
        j = begin + back

        @pl.when((back >= 0) & (back < size) & (place < last))
        def _():
            self.back_copy(stream, j, before).wait_recv()

            @pl.when(place > 0)
            def _():
                self.back_copy(stream, j, before).start()

    def drain(self):
        def sent(at, carry):
            i = at + self.base
            for stream in (0, 1):
                place, after, before = self.parts(stream)

                @pl.when(place < self.last)
                def _():
                    self.acc_copy(stream, i, after).wait_send()

                @pl.when(place > 0)
                def _():
                    self.back_copy(stream, i, before).wait_send()

            return carry

        lax.fori_loop(0, self.count, sent, 0)


def line_scratch(rows, width, share=1, chunk=CHUNK):
    count = rows // 2 // chunk // share
    return [
        pltpu.VMEM((2, count, chunk, width), jnp.bfloat16),
        *[pltpu.SemaphoreType.DMA((2, count))] * 4,
    ]


def greet(line, core, plane, full_line=False):
    here, row, side = lax.axis_index("tensor"), lax.axis_index("dp"), lax.axis_index("ctx")
    barrier = pltpu.get_barrier_semaphore()
    peers = 0

    def call(**device):
        pl.semaphore_signal(barrier, inc=1, device_id=device, device_id_type=MESH)

    if full_line:
        for hop in range(1, line):
            call(tensor=lax.rem(here + hop, line))
        peers += line - 1
    else:

        @pl.when(here > 0)
        def _():
            call(tensor=here - 1)

        @pl.when(here < line - 1)
        def _():
            call(tensor=here + 1)

        peers = jnp.where(here > 0, 1, 0) + jnp.where(here < line - 1, 1, 0)
    if plane:
        for hop in range(1, 2 * plane):
            peer = lax.rem(2 * row + side + hop, 2 * plane)
            call(dp=peer // 2, ctx=lax.rem(peer, 2))
        peers += 2 * plane - 1
    elif core:
        call(ctx=1 - side)
        peers += 1
    pl.semaphore_wait(barrier, peers)


def kept_rows(i, chunk=CHUNK):
    return pl.ds(pl.multiple_of(i * chunk, chunk), chunk)


def rotate_lanes(values, cosine, signed_sine, back=False):
    lane = lax.broadcasted_iota(jnp.int32, values.shape, 1)
    swapped = jnp.where(
        lax.rem(lane, HEAD_DIM) < HEAD_DIM // 2,
        pltpu.roll(values, 128 - HEAD_DIM // 2, 1),
        pltpu.roll(values, HEAD_DIM // 2, 1),
    )
    turn = swapped * signed_sine
    return values * cosine - turn if back else values * cosine + turn


def key_lanes(values, turned):
    lane = lax.broadcasted_iota(jnp.int32, values.shape, 1)
    return jnp.where(lane < HEAD_DIM, turned, values)


def fill_bias(bias, seg_col, seg_row, first, keys, block):
    key_seg = seg_col[0:keys]
    query_seg = seg_row[:, first : first + block]
    key_pos = lax.broadcasted_iota(jnp.int32, (keys, block), 0)
    query_pos = first + lax.broadcasted_iota(jnp.int32, (keys, block), 1)
    usable = (key_seg >= 0) | (key_pos == query_pos)
    allowed = (key_seg == query_seg) & (key_pos <= query_pos) & usable
    bias[0:keys, :] = jnp.where(allowed, 0.0, masked_score)


def wide_tiles(width):
    return width // 256, width % 256


def inverse_rms(values):
    return lax.rsqrt(jnp.mean(values * values, axis=-1, keepdims=True) + epsilon)


def front_kernel(
    n, dp_size,
    inputs_any, segments, frequency, gain_one, gain_two,
    query_weight_any, key_weight_any, value_weight_any, out_weight_any, gate_weight_any, up_weight_any, down_weight_any, upstream_any,
    seg_out, cosine_out, sine_out, query_out, kv_out, log_out, mixed_out, normed_cols, two_cols, upstream_cols, up_out, inner_out, second_out,
    attended_out, middle_out, grad_middle_out, land_gate, land_up, own_gate, gain_out,
    seg_all, seg_row, seg_col, cosine, signed_sine,
    inputs, normed, kv_weight, query, kv, kv_turned, logs, mixed, bias,
    gate_weight, up_weight, down_weight, upstream, grad_inner, normed_two, gate, up, inner,
    partial, middle, grad_middle, two_other, turned, send_gate, send_up,
    load_sems, store_sems, core_send, core_recv, plane_send, plane_recv, *line_refs,
):
    span, width = inputs.shape
    hidden, piece = gate.shape[1], turned.shape[0]
    row, core = lax.axis_index("dp"), lax.axis_index("ctx")
    half, block = span // 2, span // 4
    second, attended = normed, inputs
    line_one, line_two, line_three = line_refs[:5], line_refs[5:10], line_refs[10:]
    count, heads = line_one[0].shape[1], query.shape[1]
    part = count // 2

    def load(at, src, dst):
        made = pltpu.make_async_copy(src, dst, load_sems.at[at])
        made.start()
        return made

    def ordered(stream, i):
        return (i // part) * half + stream * block + lax.rem(i, part) * CHUNK

    def moved(at):
        return (0, 2, 1, 3)[at] * block

    load_inputs = load(0, inputs_any, inputs)
    query_weight = gate_weight.at[:, pl.ds(0, heads)]
    out_weight = down_weight.at[pl.ds(0, heads)]
    load_query = load(1, query_weight_any, query_weight)
    load_kv = [
        load(2, key_weight_any, kv_weight.at[pl.ds(0, HEAD_DIM)]),
        load(11, value_weight_any, kv_weight.at[pl.ds(HEAD_DIM, HEAD_DIM)]),
    ]
    load_out = load(3, out_weight_any, out_weight)
    load_up = [
        load(4 + b, upstream_any.at[pl.ds(b * block, block)], upstream.at[pl.ds(moved(b), block)]) for b in range(4)
    ]
    load_up_weight = load(10, up_weight_any, up_weight)
    seg_all[core] = jnp.broadcast_to(segments[...], seg_all.shape[1:])
    greet(n, True, dp_size)

    def seg_copy():
        return remote(seg_all.at[core], seg_all.at[core], core_send.at[1], core_recv.at[1], ctx=1 - core)

    seg_copy().start()
    load_inputs.wait()

    def norm_rows(b, carry):
        rows = pl.ds(pl.multiple_of(b * 64, 64), 64)
        value = inputs[rows].astype(jnp.float32)
        normed[rows] = (value * inverse_rms(value) * gain_one[...]).astype(jnp.bfloat16)
        return carry

    lax.fori_loop(0, span // 64, norm_rows, 0)
    seg_copy().wait()
    for side in (0, 1):
        seg_row[:, side * span : (side + 1) * span] = seg_all[side, 0:1]
        seg_col[side * span : (side + 1) * span] = seg_all[side].T[:, 0:1]
    own_seg = seg_all[core, 0:1]
    key_pos = lax.broadcasted_iota(jnp.int32, (2 * span, span), 0)
    query_pos = core * span + lax.broadcasted_iota(jnp.int32, (2 * span, span), 1)
    before = (seg_col[...] == own_seg) & (key_pos < query_pos)
    position = jnp.sum(jnp.where(before, 1.0, 0.0), axis=0, keepdims=True)
    angles = jnp.broadcast_to(position, (8, span)).T[:, 0:1] * frequency[...]
    lane = lax.broadcasted_iota(jnp.int32, angles.shape, 1)
    cosine[...] = jnp.cos(angles)
    sine = jnp.sin(angles)
    signed_sine[...] = jnp.where(lax.rem(lane, HEAD_DIM) < HEAD_DIM // 2, -sine, sine)
    for made in load_kv:
        made.wait()
    own_rows = pl.ds(pl.multiple_of(core * span, span), span)
    raw = turned_dot(normed[...], kv_weight[...])
    kv[own_rows] = key_lanes(raw, rotate_lanes(raw, cosine[...], signed_sine[...])).astype(jnp.bfloat16)

    def kv_copy():
        return remote(kv.at[own_rows], kv.at[own_rows], core_send.at[0], core_recv.at[0], ctx=1 - core)

    def kv_arrival():
        rows = pl.ds(0, span)
        return remote(kv.at[rows], kv.at[rows], core_send.at[0], core_recv.at[0], ctx=1 - core)

    @pl.when(core == 0)
    def _():
        kv_copy().start()

    load_query.wait()
    for low in range(0, span, half):
        rows = slice(low, low + half)
        raw = jnp.dot(normed[rows], query_weight[...], preferred_element_type=jnp.float32)
        for lanes in range(0, raw.shape[1], 128):
            rotated = rotate_lanes(raw[:, lanes : lanes + 128], cosine[rows], signed_sine[rows])
            query[rows, lanes : lanes + 128] = rotated.astype(jnp.bfloat16) * (HEAD_DIM ** -0.5)
    load_gate = load(9, gate_weight_any, gate_weight)

    @pl.when(core == 1)
    def _():
        kv_arrival().wait_recv()

    kv_turned[...] = kv[...].T

    def attend(side, at):
        keys = side * span + (at + 1) * half
        rows = slice(at * half, (at + 1) * half)
        fill_bias(bias, seg_col, seg_row, side * span + at * half, keys, half)

        def pair(index, carry):
            lanes = pl.ds(pl.multiple_of(index * 128, 128), 128)
            both = query[rows, lanes]
            outs = []
            for which in (0, 1):
                scores = turned_dot(kv[0:keys, 0:HEAD_DIM], both[:, which * HEAD_DIM : (which + 1) * HEAD_DIM])
                scores = scores + bias[0:keys, :]
                peak = jnp.max(scores, axis=0, keepdims=True)
                grown = jnp.exp(scores - peak)
                total = jnp.sum(grown, axis=0, keepdims=True)
                logs[pl.ds(2 * index + which, 1), rows] = peak + jnp.log(total)
                out = jnp.dot(
                    kv_turned[HEAD_DIM : 2 * HEAD_DIM, 0:keys],
                    grown.astype(jnp.bfloat16),
                    preferred_element_type=jnp.float32,
                )
                outs.append(out / total)
            mixed[rows, lanes] = jnp.concatenate(outs, axis=0).T.astype(jnp.bfloat16)
            return carry

        lax.fori_loop(0, query.shape[1] // 128, pair, 0)

    for side in (0, 1):

        @pl.when(core == side)
        def _():
            attend(side, 0)
            attend(side, 1)

    load_out.wait()

    def out_tile(t, carry):
        columns = pl.ds(pl.multiple_of(t * 512, 512), 512)
        for b in (0, 2):
            value = jnp.dot(
                mixed[b * block : (b + 2) * block], out_weight[:, columns], preferred_element_type=jnp.float32
            )
            partial[moved(b) : moved(b) + block, columns] = value[:block]
            partial[moved(b + 1) : moved(b + 1) + block, columns] = value[block:]
        return carry

    lax.fori_loop(0, width // 512, out_tile, 0)
    load_down = load(8, down_weight_any, down_weight)

    def rows_at(start):
        return pl.ds(pl.multiple_of(start, CHUNK), CHUNK)

    def own(stream, i):
        return partial[rows_at(ordered(stream, i))]

    def finish_one(stream, i, total):
        value = inputs[rows_at((stream * count + i) * CHUNK)].astype(jnp.float32) + total
        middle[kept_rows(i)] = value
        return value * inverse_rms(value) * gain_two[...]

    gain_out[...] = jnp.zeros_like(gain_out)

    def finish_two(stream, i, total):
        value = middle[kept_rows(i)]
        inverse = inverse_rms(value)
        unit = value * inverse
        gain_out[0:1, :] += jnp.sum(total * unit, axis=0, keepdims=True)
        scaled = total * gain_two[...]
        result = upstream[rows_at(ordered(stream, i))].astype(jnp.float32) + inverse * (
            scaled - unit * jnp.mean(scaled * unit, axis=-1, keepdims=True)
        )
        grad_middle[kept_rows(i)] = result
        return result

    first = Line(n, own, finish_one, ordered, normed_two, *line_one)
    then = Line(n, own, finish_two, ordered, attended, *line_two)
    third = Line(
        n,
        lambda stream, i: second[rows_at(ordered(stream, i))].astype(jnp.float32),
        lambda stream, i, total: middle[kept_rows(i)] + total,
        ordered, second, *line_three,
    )
    tiles, rest = wide_tiles(hidden)
    tile_count = tiles + (1 if rest else 0)

    def each_tile(t, work):
        @pl.when(t < tiles)
        def _():
            work(pl.ds(pl.multiple_of(t * 256, 256), 256))

        if rest:

            @pl.when(t == tiles)
            def _():
                work(pl.ds(tiles * 256, rest))

    def inner_tile(columns):
        grad_inner[:, columns] = turned_dot(upstream[...], down_weight[columns, :])

    def forward_tile(rows, columns):
        gated = jnp.dot(normed_two[rows], gate_weight[:, columns], preferred_element_type=jnp.float32)
        upped = jnp.dot(normed_two[rows], up_weight[:, columns], preferred_element_type=jnp.float32)
        sig = jax.nn.sigmoid(gated)
        act = gated * sig
        grad = grad_inner[rows, columns]
        inner[rows, columns] = (act * upped).astype(jnp.bfloat16)
        up[rows, columns] = (grad * act).astype(jnp.bfloat16)
        gate[rows, columns] = (grad * upped * sig * (1.0 + gated * (1.0 - sig))).astype(jnp.bfloat16)

    def back_tile(rows, t):
        columns = pl.ds(pl.multiple_of(t * 512, 512), 512)
        partial[rows, columns] = turned_dot(gate[rows], gate_weight[columns, :]) + turned_dot(
            up[rows], up_weight[columns, :]
        )

    def second_tile(rows, t):
        columns = pl.ds(pl.multiple_of(t * 512, 512), 512)
        second[rows, columns] = jnp.dot(
            inner[rows], down_weight[:, columns], preferred_element_type=jnp.float32
        ).astype(jnp.bfloat16)

    last = n - 1
    trip = 2 * HOP * last
    each = 2
    forward_steps, back_steps = -(-tile_count // each), width // 1024
    work = forward_steps + back_steps
    base_one = part + trip
    second_steps = width // 1024
    base_two = max(count + trip, base_one + work + second_steps)
    third_base = base_one + work + second_steps
    steps = max(base_two + work + part + trip, third_base + part + trip)

    def store(at, src, dst):
        return pltpu.make_async_copy(src, dst, store_sems.at[at])

    def stores(at, src, dst):
        return [
            store(at + b, src.at[pl.ds(moved(b), block)], dst.at[pl.ds(b * block, block)]) for b in range(4)
        ]

    early = [
        store(0, query, query_out), store(1, kv, kv_out), store(2, logs, log_out), store(3, mixed, mixed_out.at[pl.ds(0, span)]),
        store(31, seg_row, seg_out), store(32, cosine, cosine_out),
        store(33, signed_sine, sine_out),
    ]
    own_slots, far_slots = [], []

    def own_columns(src, dst):
        made = []
        for q in range(dp_size):
            columns = pl.ds(pl.multiple_of((2 * q + core) * piece, piece), piece)
            at = 34 + len(own_slots)
            own_slots.append(at)
            made.append(store(at, src.at[:, columns], dst.at[pl.ds(0, span), pl.ds(q * piece, piece)]))
        return made

    def far_copy(src, dst):
        at = 3 + dp_size + len(far_slots)
        far_slots.append(at)
        return remote(src, dst, core_send.at[at], core_recv.at[at], ctx=1 - core)

    def far_columns(src, dst):
        made = []
        for q in range(dp_size):
            columns = pl.ds(pl.multiple_of((2 * q + 1 - core) * piece, piece), piece)
            made.append(far_copy(src.at[:, columns], dst.at[pl.ds(span, span), pl.ds(q * piece, piece)]))
        return made

    normed_moves = [*own_columns(normed, normed_cols), *far_columns(normed, normed_cols)]
    upstream_moves = [*own_columns(upstream, upstream_cols), *far_columns(upstream, upstream_cols)]
    mixed_move = far_copy(mixed, mixed_out.at[pl.ds(span, span)])
    hidden_moves = [
        store(6, inner, inner_out.at[pl.ds(0, span)]), far_copy(inner, inner_out.at[pl.ds(span, span)]),
        *own_columns(normed_two, two_cols),
    ]
    up_slot = 3 + dp_size + len(far_slots)
    two_moves = [store(7, two_other, two_cols.at[pl.ds(span, span)]), store(5, up, up_out)]
    second_stores = stores(21, second, second_out)
    middle_store = store(29, middle, middle_out)

    def gate_swaps():
        made = [
            remote(
                ref.at[pl.ds(0, span)], ref.at[pl.ds(span, span)], core_send.at[at], core_recv.at[at], ctx=1 - core
            )
            for ref, at in ((gate, 2), (up, up_slot))
        ]
        for q in range(dp_size):
            columns = pl.ds(pl.multiple_of((2 * q + 1 - core) * piece, piece), piece)
            made.append(
                remote(
                    normed_two.at[:, columns], two_other.at[:, pl.ds(q * piece, piece)],
                    core_send.at[3 + q], core_recv.at[3 + q], ctx=1 - core,
                )
            )
        return made

    def peer_of(r):
        return lax.rem(row + 1 + r, dp_size)

    sends, lands = (send_gate, send_up), (land_gate, land_up)

    def gate_copy(w, r):
        return remote(sends[w].at[r], lands[w].at[r], plane_send.at[w, r], plane_recv.at[w, r], dp=peer_of(r))

    def turn_two(r):
        peer = peer_of(r)
        columns = pl.ds(pl.multiple_of((2 * peer + core) * piece, piece), piece)
        turned[:, 0:span] = normed_two[:, columns].T
        turned[:, span : 2 * span] = two_other[:, pl.ds(pl.multiple_of(peer * piece, piece), piece)].T

    edges = [(low, min(low + 384, hidden)) for low in range(0, hidden, 384)]

    def gate_piece(w, r):
        for low, high in edges:
            sends[w][r, :, low:high] = jnp.dot(
                turned[...], (gate, up)[w][:, low:high], preferred_element_type=jnp.float32
            ).astype(jnp.bfloat16)
        gate_copy(w, r).start()

    def own_piece():
        for low, high in edges:
            partial[0:piece, low:high] = jnp.dot(turned[...], gate[:, low:high], preferred_element_type=jnp.float32)

    own_store = store(4, partial.at[pl.ds(0, piece), pl.ds(0, hidden)], own_gate)

    for made in [*early, *normed_moves, mixed_move]:
        made.start()

    def step(k, carry):
        first.step(k)
        if base_two == base_one + part:
            then.step(k - (base_one + work))
        else:
            then.step(k - (base_one + work), 0, part)
            then.step(k - (base_two + work), part, part)
        third.step(k - third_base)

        @pl.when(k == 0)
        def _():
            for made in load_up:
                made.wait()
            for made in upstream_moves:
                made.start()

        @pl.when(k == 2)
        def _():
            load_down.wait()
            load_gate.wait()
            load_up_weight.wait()

        @pl.when((k >= 2) & (k < 2 + tile_count))
        def _():
            each_tile(k - 2, inner_tile)

        @pl.when(k == base_one)
        def _():
            for made in normed_moves:
                made.wait()

        @pl.when(k == base_two)
        def _():
            middle_store.start()

        late = jnp.where(k >= base_two, 1, 0)
        phase = k - jnp.where(k >= base_two, base_two, base_one)
        rows = pl.ds(pl.multiple_of(late * half, half), half)

        @pl.when((phase >= 0) & (phase < forward_steps))
        def _():
            def tile(t, carry):
                each_tile(t, functools.partial(forward_tile, rows))
                return carry

            lax.fori_loop(phase * each, jnp.minimum((phase + 1) * each, tile_count), tile, 0)

        @pl.when((phase >= forward_steps) & (phase < work))
        def _():
            for t in (0, 1):
                back_tile(rows, 2 * (phase - forward_steps) + t)

        @pl.when((phase >= work) & (phase < work + second_steps))
        def _():
            for t in (0, 1):
                second_tile(rows, 2 * (phase - work) + t)

        @pl.when(k == base_two + work)
        def _():
            for made in hidden_moves:
                made.start()

        @pl.when(k == base_two + forward_steps)
        def _():
            for made in gate_swaps():
                made.start()

        @pl.when(k == base_two + work + 1)
        def _():
            for made in gate_swaps():
                made.wait()
            for made in two_moves:
                made.start()

        gate_task = k - (base_two + work + 1)

        @pl.when((gate_task >= 0) & (gate_task < dp_size - 1))
        def _():
            turn_two(gate_task)
            gate_piece(0, gate_task)

            @pl.when(gate_task < dp_size - 2)
            def _():
                gate_piece(1, gate_task)

        @pl.when(k == base_two + work + part + HOP * last)
        def _():
            turn_two(dp_size - 1)
            own_piece()
            own_store.start()

        @pl.when(k == base_two + work + second_steps)
        def _():
            for b in (1, 3):
                second_stores[b].start()

        return carry

    lax.fori_loop(0, steps, step, 0)
    late_stores = [
        second_stores[0], second_stores[2], *stores(25, attended, attended_out), store(30, grad_middle, grad_middle_out),
    ]
    for made in late_stores:
        made.start()
    first.drain()
    then.drain()
    third.drain()

    @pl.when(core == 0)
    def _():
        kv_copy().wait_send()

    for r in range(dp_size - 1):
        for w in ((0, 1) if r < dp_size - 2 else (0,)):
            gate_copy(w, r).wait()
    for made in [
        *early, mixed_move, *upstream_moves, *hidden_moves, *two_moves, own_store, middle_store, second_stores[1], second_stores[3],
        *late_stores,
    ]:
        made.wait()


def front_call(line_size, dp_size, operands):
    inputs = operands[0]
    query_weight, out_weight, gate_weight = operands[5], operands[8], operands[9]
    span, width = inputs.shape
    heads, hidden = query_weight.shape[1], gate_weight.shape[1]
    piece = width // (2 * dp_size)
    low, full = jnp.bfloat16, jnp.float32
    vmem, outside = pl.BlockSpec(memory_space=pltpu.VMEM), pl.BlockSpec(memory_space=pl.ANY)
    dma = pltpu.SemaphoreType.DMA
    outs = [
        ((1, 2 * span), jnp.int32), ((span, 128), full), ((span, 128), full),
        ((span, heads), low), ((2 * span, 128), low), ((heads // HEAD_DIM, span), full), ((2 * span, heads), low),
        *[((2 * span, width // 2), low)] * 3, *[((2 * span, hidden), low)] * 2, ((span, width), low),
        ((span, width), low), ((span // 2, width), full), ((span // 2, width), full),
        ((dp_size - 1, piece, hidden), low), ((dp_size - 2, piece, hidden), low), ((piece, hidden), full), ((8, width), full),
    ]
    scratch = [
        pltpu.VMEM((2, 8, span), jnp.int32), pltpu.VMEM((1, 2 * span), jnp.int32),
        pltpu.VMEM((2 * span, 1), jnp.int32), pltpu.VMEM((span, 128), full), pltpu.VMEM((span, 128), full),
        pltpu.VMEM((span, width), low), pltpu.VMEM((span, width), low),
        pltpu.VMEM((128, width), low), pltpu.VMEM((span, heads), low),
        pltpu.VMEM((2 * span, 128), low), pltpu.VMEM((128, 2 * span), low),
        pltpu.VMEM((heads // HEAD_DIM, span), full), pltpu.VMEM((span, heads), low),
        pltpu.VMEM((2 * span, span // 2), full),
        pltpu.VMEM((width, hidden), low), pltpu.VMEM((width, hidden), low), pltpu.VMEM((hidden, width), low),
        pltpu.VMEM((span, width), low), pltpu.VMEM((span, hidden), full), pltpu.VMEM((span, width), low),
        *[pltpu.VMEM((2 * span, hidden), low)] * 2, pltpu.VMEM((span, hidden), low),
        pltpu.VMEM((span, width), full),
        pltpu.VMEM((span // 2, width), full), pltpu.VMEM((span // 2, width), full),
        pltpu.VMEM((span, width // 2), low), pltpu.VMEM((piece, 2 * span), low),
        pltpu.VMEM((dp_size - 1, piece, hidden), low), pltpu.VMEM((dp_size - 2, piece, hidden), low),
        dma((12,)), dma((34 + 3 * dp_size,)), dma((6 + 3 * dp_size,)), dma((6 + 3 * dp_size,)),
        dma((2, dp_size - 1)), dma((2, dp_size - 1)),
        *line_scratch(span, width), *line_scratch(span, width), *line_scratch(span, width, 2),
    ]
    return pl.pallas_call(
        functools.partial(front_kernel, line_size, dp_size),
        out_shape=[jax.ShapeDtypeStruct(s, d) for s, d in outs],
        in_specs=[outside] + [vmem] * 4 + [outside] * 8,
        out_specs=[outside] * 19 + [vmem],
        scratch_shapes=scratch,
        compiler_params=pltpu.CompilerParams(
            collective_id=1, has_side_effects=True, vmem_limit_bytes=FRONT_MIB * MIB
        ),
    )(*operands)


def back_kernel(
    n, dp_size,
    query_any, kv_any, logs, mixed_any, cosine, signed_sine, seg_row, inputs_any, normed_any, two_any, upstream_any,
    up_any, inner_any, second_any, attended_any, middle_any, grad_middle_any, gain_one, gain_two_grad,
    query_weight_any, key_weight_any, value_weight_any, out_weight_any,
    layer_out, grad_inputs, grad_gains, grad_qkv, own_out, grad_up, own_down,
    land_up, land_down, land_qkv, land_out,
    query, kv, kv_turned, grad_mixed, mixed, attended, normed_cols, two_cols, upstream_cols, attended_other,
    up, inner, pre, query_weight, kv_weight, out_weight, grad_middle, middle, inputs,
    ring, send_qkv, send_out, turned, seg_col, bias, kv_grad, kv_grad_other,
    gain_line, gain_land, gain_sum, gain_plane,
    load_sems, core_send, core_recv, ring_send, ring_recv, plane_send, plane_recv, line_send, line_recv,
    spread_send, spread_recv, *line_refs,
):
    span, width = attended.shape
    heads, piece = query.shape[1], turned.shape[0]
    here, row, core = lax.axis_index("tensor"), lax.axis_index("dp"), lax.axis_index("ctx")
    half = span // 2
    line_out, line_in = line_refs[:5], line_refs[5:]
    count, part = line_in[0].shape[1], line_out[0].shape[1]
    last = n - 1
    loads = []

    def load(src, dst):
        made = pltpu.make_async_copy(src, dst, load_sems.at[len(loads)])
        made.start()
        loads.append(made)
        return made

    own_half = pl.ds(pl.multiple_of(jnp.where(here == 0, half, 0), half), half)
    line_loads = [load(second_any, layer_out), load(middle_any, middle)]
    mixed_loads = [load(attended_any, attended), load(out_weight_any, out_weight)]
    attend_loads = [load(query_any, query), load(kv_any, kv)]

    up_loads = [load(two_any, two_cols), load(up_any, up)]
    inner_loads = [load(upstream_any, upstream_cols), load(inner_any, inner)]
    late_loads = [
        load(query_weight_any, query_weight), load(key_weight_any, kv_weight.at[pl.ds(0, HEAD_DIM)]),
        load(value_weight_any, kv_weight.at[pl.ds(HEAD_DIM, HEAD_DIM)]),
        load(grad_middle_any, grad_middle), load(inputs_any.at[own_half], inputs),
        load(mixed_any, mixed), load(normed_any, normed_cols),
    ]
    greet(n, True, dp_size, full_line=True)
    pre_slot, kv_slot = dp_size, dp_size + 1

    def attended_swaps():
        made = []
        for q in range(dp_size):
            columns = pl.ds(pl.multiple_of((2 * q + 1 - core) * piece, piece), piece)
            made.append(
                remote(
                    attended.at[:, columns], attended_other.at[:, pl.ds(q * piece, piece)],
                    core_send.at[q], core_recv.at[q], ctx=1 - core,
                )
            )
        return made

    def pre_swap():
        return remote(
            pre.at[pl.ds(0, span)], pre.at[pl.ds(span, span)], core_send.at[pre_slot], core_recv.at[pre_slot],
            ctx=1 - core,
        )

    def kv_swap():
        return remote(
            kv_grad.at[pl.ds(0, span)], kv_grad_other, core_send.at[kv_slot], core_recv.at[kv_slot], ctx=1 - core
        )

    gain_line[...] = jnp.zeros_like(gain_line)
    gain_line[1:2, :] = gain_two_grad[0:1, :]
    kv_grad[...] = jnp.zeros_like(kv_grad)
    seg_col[...] = jnp.broadcast_to(seg_row[...], (8, 2 * span)).T[:, 0:1]
    for made in line_loads:
        made.wait()

    def rows_at(start):
        return pl.ds(pl.multiple_of(start, BACK_CHUNK), BACK_CHUNK)

    def plain(stream, i):
        return (stream * count + i) * BACK_CHUNK

    def finish_out(stream, i, total):
        return middle[kept_rows(i, BACK_CHUNK)] + total

    def finish_in(stream, i, total):
        hidden = inputs[kept_rows(i, BACK_CHUNK)].astype(jnp.float32)
        inverse = inverse_rms(hidden)
        unit = hidden * inverse
        gain_line[0:1, :] += jnp.sum(total * unit, axis=0, keepdims=True)
        scaled = total * gain_one[...]
        return grad_middle[kept_rows(i, BACK_CHUNK)] + inverse * (
            scaled - unit * jnp.mean(scaled * unit, axis=-1, keepdims=True)
        )

    out_line = Line(
        n, lambda s, i: layer_out[rows_at(plain(s, i))].astype(jnp.float32), finish_out, plain, layer_out, *line_out,
        base=count - part, hop=BACK_HOP,
    )
    in_line = Line(
        n, lambda s, i: grad_inputs[rows_at(plain(s, i))].astype(jnp.float32), finish_in, plain, grad_inputs, *line_in,
        hop=BACK_HOP,
    )

    def attend_back(side, at, index):
        keys = side * span + (at + 1) * half
        rows = slice(at * half, (at + 1) * half)
        lanes = pl.ds(pl.multiple_of(index * 128, 128), 128)

        @pl.when(index == 0)
        def _():
            fill_bias(bias, seg_col, seg_row, side * span + at * half, keys, half)

        both_query, both_grad = query[rows, lanes], grad_mixed[rows, lanes]
        outs, parts = [], None
        for which in (0, 1):
            head = slice(which * HEAD_DIM, (which + 1) * HEAD_DIM)
            query_head, grad_head = both_query[:, head], both_grad[:, head]
            scores = turned_dot(kv[0:keys, 0:HEAD_DIM], query_head) + bias[0:keys, :]
            probs = jnp.exp(scores - logs[pl.ds(2 * index + which, 1), rows])
            grad_probs = turned_dot(kv[0:keys, HEAD_DIM : 2 * HEAD_DIM], grad_head)
            both = probs * grad_probs
            grad_scores = (both - probs * jnp.sum(both, axis=0, keepdims=True)).astype(jnp.bfloat16)
            grad_key = jnp.dot(grad_scores, query_head, preferred_element_type=jnp.float32)
            grad_value = jnp.dot(probs.astype(jnp.bfloat16), grad_head, preferred_element_type=jnp.float32)
            part = jnp.concatenate([grad_key, grad_value], axis=1)
            parts = part if parts is None else parts + part
            outs.append(
                jnp.dot(kv_turned[0:HEAD_DIM, 0:keys], grad_scores, preferred_element_type=jnp.float32)
            )
        kv_grad[0:keys] += parts
        grad_query = jnp.concatenate(outs, axis=0).T * (HEAD_DIM ** -0.5)
        pre[rows, lanes] = rotate_lanes(grad_query, cosine[rows], signed_sine[rows], back=True).astype(jnp.bfloat16)

    pairs = heads // 128
    tasks = 2 * pairs

    def attend_task(task):
        for side in (0, 1):
            for at in (0, 1):

                @pl.when((core == side) & (task // pairs == at))
                def _():
                    attend_back(side, at, lax.rem(task, pairs))

    own_grad = pl.ds(pl.multiple_of(core * span, span), span)

    def finish_pre():
        @pl.when(core == 0)
        def _():
            kv_swap().wait_recv()
            kv_grad[0:span] += kv_grad_other[...]

        raw = kv_grad[own_grad]
        turned_back = rotate_lanes(raw, cosine[...], signed_sine[...], back=True)
        pre[0:span, heads : heads + 128] = key_lanes(raw, turned_back).astype(jnp.bfloat16)

    def in_products():
        def tile(t, carry):
            columns = pl.ds(pl.multiple_of(t * 512, 512), 512)
            for low in (0, half):
                rows = slice(low, low + half)
                grad_inputs[rows, columns] = (
                    turned_dot(pre[rows, 0:heads], query_weight[columns, :])
                    + jnp.dot(
                        pre[rows, heads : heads + 128], kv_weight[:, columns], preferred_element_type=jnp.float32
                    )
                ).astype(jnp.bfloat16)
            return carry

        lax.fori_loop(0, width // 512, tile, 0)

    def peer_of(r):
        return lax.rem(row + 1 + r, dp_size)

    def turn(r, cols):
        block = pl.multiple_of(peer_of(r) * piece, piece)
        turned[...] = cols[:, pl.ds(block, piece)].T

    def turn_attended(r):
        peer = peer_of(r)
        columns = pl.ds(pl.multiple_of((2 * peer + core) * piece, piece), piece)
        turned[:, 0:span] = attended[:, columns].T
        turned[:, span : 2 * span] = attended_other[:, pl.ds(pl.multiple_of(peer * piece, piece), piece)].T

    def tiles_of(stacked):
        wide = stacked.shape[1]
        return [(low, min(low + 384, wide)) for low in range(0, wide, 384)]

    def piece_value(stacked, low, high):
        return jnp.dot(turned[...], stacked[:, low:high], preferred_element_type=jnp.float32)

    others = dp_size - 1

    def ring_copy(at):
        r = others - 1 if at == 0 else at - 1
        land = land_up.at[0] if at == 0 else land_down.at[at - 1]
        return remote(ring.at[at], land, ring_send.at[at], ring_recv.at[at], dp=peer_of(r))

    def ring_piece(at, cols, stacked):
        turn(others - 1 if at == 0 else at - 1, cols)
        for low, high in tiles_of(stacked):
            ring[at, :, low:high] = piece_value(stacked, low, high).astype(jnp.bfloat16)
        ring_copy(at).start()

    def kept_piece(cols, stacked, own):
        turn(others, cols)
        for low, high in tiles_of(stacked):
            own[:, low:high] = piece_value(stacked, low, high)

    sends, lands = (send_qkv, send_out), (land_qkv, land_out)

    def plane_copy(w, r):
        return remote(sends[w].at[r], lands[w].at[r], plane_send.at[w, r], plane_recv.at[w, r], dp=peer_of(r))

    def plane_piece(w, r, stacked, own):
        @pl.when(r < dp_size - 1)
        def _():
            for low, high in tiles_of(stacked):
                sends[w][r, :, low:high] = piece_value(stacked, low, high).astype(jnp.bfloat16)
            plane_copy(w, r).start()

        @pl.when(r == dp_size - 1)
        def _():
            for low, high in tiles_of(stacked):
                own[:, low:high] = piece_value(stacked, low, high)

    def line_copies(owner, hops):
        slot = 0 if owner == 0 else 1
        return [
            remote(
                gain_line, gain_land.at[slot], line_send.at[slot, hop - 1], line_recv.at[slot],
                tensor=owner + hop if owner == 0 else owner - hop,
            )
            for hop in hops
        ]

    shard = width // (2 * dp_size)
    shards = 2 * dp_size
    place = 2 * row + core

    def spread(r):
        peer = lax.rem(place + 1 + r, shards)
        block = pl.multiple_of(peer * shard, shard)
        return remote(
            gain_sum.at[:, pl.ds(block, shard)], gain_plane.at[r], spread_send.at[r], spread_recv.at[r],
            dp=peer // 2, ctx=lax.rem(peer, 2),
        )

    def gather_gains():
        gain_sum[...] = jnp.zeros_like(gain_sum)
        for owner in (0, last):
            slot = 0 if owner == 0 else 1

            @pl.when(here == owner)
            def _():
                gain_sum[...] += gain_line[...]

            @pl.when(here != owner)
            def _():
                line_copies(owner, (1,))[0].wait_recv()
                gain_sum[...] += gain_land[slot]
        for r in range(shards - 1):
            spread(r).start()

    attend_steps = tasks // TASKS
    lag = attend_steps + 2
    ring_steps = RINGS + [lag + at for at in range(dp_size - 3)]
    out_base = lag + 1
    steps = max(lag + count + 2 * BACK_HOP * last, out_base + dp_size)

    def step(k, carry):
        out_line.step(k, count - part, part)
        in_line.step(k - lag)

        @pl.when(k == 0)
        def _():
            for made in [*mixed_loads, *attend_loads]:
                made.wait()
            for made in attended_swaps():
                made.start()
            kv_turned[...] = kv[...].T
            grad_mixed[...] = turned_dot(attended[...], out_weight[...]).astype(jnp.bfloat16)

        @pl.when((k >= 1) & (k <= attend_steps))
        def _():
            def task(more, carry):
                attend_task(TASKS * (k - 1) + more)
                return carry

            lax.fori_loop(0, TASKS, task, 0)

        @pl.when((k == attend_steps) & (core == 1))
        def _():
            kv_swap().start()

        @pl.when(k == 1)
        def _():
            for made in up_loads:
                made.wait()

        @pl.when(k == ring_steps[1])
        def _():
            for made in inner_loads:
                made.wait()

        @pl.when(k == attend_steps)
        def _():
            for made in [*late_loads, *attended_swaps()]:
                made.wait()

        @pl.when(k == attend_steps + 1)
        def _():
            finish_pre()
            in_products()
            pre_swap().start()

        for at in range(dp_size):

            @pl.when(k == ring_steps[at])
            def _():
                ring_piece(at, *((two_cols, up) if at == 0 else (upstream_cols, inner)))

        @pl.when(k == lag + dp_size)
        def _():
            kept_piece(two_cols, up, grad_up)

        @pl.when(k == lag + dp_size + 1)
        def _():
            kept_piece(upstream_cols, inner, own_down)

        @pl.when(k == out_base)
        def _():
            pre_swap().wait()

        at = k - out_base

        @pl.when((at >= 0) & (at < dp_size))
        def _():
            turn_attended(at)
            plane_piece(1, at, mixed, own_out)
            turn(at, normed_cols)
            plane_piece(0, at, pre, grad_qkv)

        @pl.when(k == lag + count + BACK_HOP * last - 1)
        def _():
            for owner in (0, last):

                @pl.when(here == owner)
                def _():
                    for made in line_copies(owner, range(1, n)):
                        made.start()

        @pl.when(k == min(lag + count + BACK_HOP * last + 3, steps - 1))
        def _():
            gather_gains()

        return carry

    lax.fori_loop(0, steps, step, 0)
    out_line.drain()
    in_line.drain()

    @pl.when(core == 1)
    def _():
        kv_swap().wait_send()

    for at in range(dp_size):
        ring_copy(at).wait()
    for r in range(others):
        for w in (0, 1):
            plane_copy(w, r).wait()
    grad_gains[...] = gain_sum[:, pl.ds(pl.multiple_of(place * shard, shard), shard)]
    for r in range(shards - 1):
        spread(r).wait()
        grad_gains[...] += gain_plane[r]
    for owner in (0, last):

        @pl.when(here == owner)
        def _():
            for made in line_copies(owner, range(1, n)):
                made.wait_send()


def back_call(line_size, dp_size, operands):
    query = operands[0]
    span, heads = query.shape
    width, hidden = operands[7].shape[1], operands[11].shape[1]
    piece = width // (2 * dp_size)
    wide = heads + 128
    low, full = jnp.bfloat16, jnp.float32
    vmem, outside = pl.BlockSpec(memory_space=pltpu.VMEM), pl.BlockSpec(memory_space=pl.ANY)
    dma = pltpu.SemaphoreType.DMA
    others = dp_size - 1
    outs = [
        ((span, width), low), ((span, width), low), ((8, piece), full), ((piece, wide), full), ((piece, heads), full),
        ((piece, hidden), full), ((piece, hidden), full),
        ((1, piece, hidden), low), ((others, piece, hidden), low), ((others, piece, wide), low), ((others, piece, heads), low),
    ]
    core_copies = dp_size + 2
    scratch = [
        pltpu.VMEM((span, heads), low), pltpu.VMEM((2 * span, 128), low), pltpu.VMEM((128, 2 * span), low),
        pltpu.VMEM((span, heads), low), pltpu.VMEM((2 * span, heads), low), pltpu.VMEM((span, width), low),
        *[pltpu.VMEM((2 * span, width // 2), low)] * 3, pltpu.VMEM((span, width // 2), low),
        *[pltpu.VMEM((2 * span, hidden), low)] * 2, pltpu.VMEM((2 * span, wide), low),
        pltpu.VMEM((width, heads), low), pltpu.VMEM((128, width), low), pltpu.VMEM((heads, width), low),
        pltpu.VMEM((span // 2, width), full), pltpu.VMEM((span // 2, width), full), pltpu.VMEM((span // 2, width), low),
        pltpu.VMEM((dp_size, piece, hidden), low), pltpu.VMEM((others, piece, wide), low),
        pltpu.VMEM((others, piece, heads), low),
        pltpu.VMEM((piece, 2 * span), low), pltpu.VMEM((2 * span, 1), jnp.int32), pltpu.VMEM((2 * span, span // 2), full),
        pltpu.VMEM((2 * span, 128), full), pltpu.VMEM((span, 128), full),
        pltpu.VMEM((8, width), full), pltpu.VMEM((2, 8, width), full), pltpu.VMEM((8, width), full),
        pltpu.VMEM((2 * dp_size - 1, 8, piece), full),
        dma((17,)), dma((core_copies,)), dma((core_copies,)),
        dma((dp_size,)), dma((dp_size,)), dma((2, others)), dma((2, others)),
        dma((2, line_size - 1)), dma((2,)), dma((2 * dp_size - 1,)), dma((2 * dp_size - 1,)),
        *line_scratch(span, width, 2, BACK_CHUNK), *line_scratch(span, width, 1, BACK_CHUNK),
    ]
    spaces = [outside, outside, vmem, outside, vmem, vmem, vmem] + [outside] * 10 + [vmem, vmem] + [outside] * 4
    return pl.pallas_call(
        functools.partial(back_kernel, line_size, dp_size),
        out_shape=[jax.ShapeDtypeStruct(s, d) for s, d in outs],
        in_specs=spaces,
        out_specs=[vmem] * 7 + [outside] * 4,
        scratch_shapes=scratch,
        compiler_params=pltpu.CompilerParams(
            collective_id=2, has_side_effects=True, vmem_limit_bytes=BACK_MIB * MIB
        ),
    )(*operands)


def settle_kernel(
    layer_any, inputs_any, gains, qkv_any, out_any, gate_any, up_any, down_any,
    land_gate, land_up, land_up_last, land_down, land_qkv, land_out,
    layer_out, grad_inputs, gain_one, grad_query, grad_key, grad_value, grad_out, gain_two, grad_gate, grad_up, grad_down,
    own_qkv, own_out, own_gate, own_up, own_down, far_qkv, far_out, far_gate, far_up, far_down,
    turned_kv, turned_out, turned_down, layer_held, inputs_held, in_sems, out_sems,
):
    whole, early = [], land_up.shape[0]
    passed = [
        pltpu.make_async_copy(layer_any, layer_held, in_sems.at[0, 5]),
        pltpu.make_async_copy(inputs_any, inputs_held, in_sems.at[1, 5]),
        pltpu.make_async_copy(land_up_last, far_up.at[pl.ds(early, 1)], in_sems.at[0, 6]),
    ]
    owns = ((qkv_any, own_qkv), (out_any, own_out), (gate_any, own_gate), (up_any, own_up), (down_any, own_down))
    fars = (
        (land_qkv, far_qkv), (land_out, far_out), (land_gate, far_gate), (land_up, far_up.at[pl.ds(0, early)]),
        (land_down, far_down),
    )
    loads = [
        (
            pltpu.make_async_copy(*own, in_sems.at[0, at]),
            pltpu.make_async_copy(*far, in_sems.at[1, at]),
        )
        for at, (own, far) in enumerate(zip(owns, fars))
    ]
    for pair in loads:
        for made in pair:
            made.start()
    for made in passed:
        made.start()
    gain_one[...] = gains[0:1]
    gain_two[...] = gains[1:2]

    def settle(at, own, far):
        for made in loads[at]:
            made.wait()
        total = own[...]
        for r in range(far.shape[0]):
            total = total + far[r].astype(jnp.float32)
        return total

    def put(at, src, dst):
        made = pltpu.make_async_copy(src, dst, out_sems.at[at])
        made.start()
        whole.append(made)

    heads = grad_query.shape[1]
    own_qkv[...] = settle(0, own_qkv, far_qkv)
    put(2, own_qkv.at[:, pl.ds(0, heads)], grad_query)
    turned_kv[...] = own_qkv[:, heads:].T
    put(3, turned_kv.at[pl.ds(0, HEAD_DIM)], grad_key)
    put(4, turned_kv.at[pl.ds(HEAD_DIM, HEAD_DIM)], grad_value)
    turned_out[...] = settle(1, own_out, far_out).T
    put(5, turned_out, grad_out)
    passed[0].wait()
    put(0, layer_held, layer_out)
    own_gate[...] = settle(2, own_gate, far_gate)
    put(6, own_gate, grad_gate)
    passed[2].wait()
    own_up[...] = settle(3, own_up, far_up)
    put(7, own_up, grad_up)
    passed[1].wait()
    put(1, inputs_held, grad_inputs)
    turned_down[...] = settle(4, own_down, far_down).T
    put(8, turned_down, grad_down)
    for made in whole:
        made.wait()


def settle_call(operands):
    layer_out, _, gains, qkv, out, gate = operands[:6]
    piece, wide = qkv.shape
    heads, hidden = out.shape[1], gate.shape[1]
    others = operands[8].shape[0]
    low, full = jnp.bfloat16, jnp.float32
    vmem, outside = pl.BlockSpec(memory_space=pltpu.VMEM), pl.BlockSpec(memory_space=pl.ANY)
    outs = [
        (layer_out.shape, low), (layer_out.shape, low), ((1, piece), full), ((piece, heads), full),
        ((HEAD_DIM, piece), full), ((HEAD_DIM, piece), full), ((heads, piece), full), ((1, piece), full),
        ((piece, hidden), full), ((piece, hidden), full), ((hidden, piece), full),
    ]
    shapes = [(piece, wide), (piece, heads), *[(piece, hidden)] * 3]
    scratch = [
        *[pltpu.VMEM(shape, full) for shape in shapes], *[pltpu.VMEM((others, *shape), low) for shape in shapes],
        pltpu.VMEM((wide - heads, piece), full), pltpu.VMEM((heads, piece), full), pltpu.VMEM((hidden, piece), full),
        pltpu.VMEM(layer_out.shape, low), pltpu.VMEM(layer_out.shape, low),
        pltpu.SemaphoreType.DMA((2, 7)), pltpu.SemaphoreType.DMA((9,)),
    ]
    return pl.pallas_call(
        settle_kernel,
        out_shape=[jax.ShapeDtypeStruct(s, d) for s, d in outs],
        in_specs=[outside, outside, vmem] + [outside] * 11,
        out_specs=[outside, outside, vmem] + [outside] * 4 + [vmem] + [outside] * 3,
        scratch_shapes=scratch,
        compiler_params=pltpu.CompilerParams(vmem_limit_bytes=62 * MIB),
    )(*operands)


def plain_body(
    inputs,
    segment_ids,
    attention_gain,
    query_weight,
    key_weight,
    value_weight,
    out_weight,
    feedforward_gain,
    gate_weight,
    up_weight,
    down_weight,
    cotangent,
):
    seq_count, span_len, model_width = inputs.shape
    row_count = seq_count * span_len
    query_heads = query_weight.shape[1] // HEAD_DIM
    kv_heads = key_weight.shape[1] // HEAD_DIM
    group_size = query_heads // kv_heads
    score_scale = 1.0 / math.sqrt(HEAD_DIM)
    offset = lax.axis_index("ctx") * span_len
    whole_segments = lax.all_gather(segment_ids, "ctx", axis=1, tiled=True)
    own_positions = lax.dynamic_slice_in_dim(positions_of(whole_segments), offset, span_len, 1)
    cosine, sine_table = rotary_tables(own_positions)
    cosine = cosine[:, :, None, :]
    sine_table = sine_table[:, :, None, :]
    hidden = inputs.astype(jnp.float32).reshape(row_count, model_width)
    inverse_one = lax.rsqrt(jnp.mean(hidden * hidden, axis=-1, keepdims=True) + epsilon)
    unit_one = hidden * inverse_one
    normed = (unit_one * attention_gain).astype(jnp.bfloat16)
    query_rows = rotate(
        jnp.dot(normed, query_weight, preferred_element_type=jnp.float32).reshape(
            seq_count, span_len, query_heads, HEAD_DIM
        ),
        cosine,
        sine_table,
    ).astype(jnp.bfloat16)
    key_rows = rotate(
        jnp.dot(normed, key_weight, preferred_element_type=jnp.float32).reshape(
            seq_count, span_len, kv_heads, HEAD_DIM
        ),
        cosine,
        sine_table,
    ).astype(jnp.bfloat16)
    value_rows = (
        jnp.dot(normed, value_weight, preferred_element_type=jnp.float32)
        .astype(jnp.bfloat16)
        .reshape(seq_count, span_len, kv_heads, HEAD_DIM)
    )
    all_keys, all_values = (
        lax.all_gather(key_rows, "ctx", axis=1, tiled=True),
        lax.all_gather(value_rows, "ctx", axis=1, tiled=True),
    )

    def attend(block_items):
        query_block, key_block, value_block, query_seg, key_seg = block_items
        allowed = visible(query_seg, key_seg, offset)
        grouped = query_block.reshape(span_len, kv_heads, group_size, HEAD_DIM)
        raw_scores = jnp.einsum(
            "qhgd,khd->hgqk", grouped, key_block, preferred_element_type=jnp.float32
        )
        scores = jnp.where(allowed, raw_scores * score_scale, masked_score)
        row_peak = jnp.max(scores, axis=-1, keepdims=True)
        shifted_exp = jnp.exp(scores - row_peak)
        denominator = jnp.sum(shifted_exp, axis=-1, keepdims=True)
        attn_probs = (shifted_exp / denominator).astype(jnp.bfloat16)
        mixed_block = jnp.einsum(
            "hgqk,khd->qhgd", attn_probs, value_block, preferred_element_type=jnp.float32
        )
        return (
            mixed_block.astype(jnp.bfloat16).reshape(span_len, query_heads * HEAD_DIM),
            row_peak + jnp.log(denominator),
        )

    mixed_heads, log_sums = lax.map(
        attend, (query_rows, all_keys, all_values, segment_ids, whole_segments)
    )
    mixed_flat = mixed_heads.reshape(row_count, query_heads * HEAD_DIM)
    attended = lax.psum(
        jnp.dot(mixed_flat, out_weight, preferred_element_type=jnp.float32), "tensor"
    )
    middle = hidden + attended
    inverse_two = lax.rsqrt(jnp.mean(middle * middle, axis=-1, keepdims=True) + epsilon)
    unit_two = middle * inverse_two
    normed_two = (unit_two * feedforward_gain).astype(jnp.bfloat16)
    gate_pre = jnp.dot(normed_two, gate_weight, preferred_element_type=jnp.float32)
    up_pre = jnp.dot(normed_two, up_weight, preferred_element_type=jnp.float32)
    sigmoid_gate = jax.nn.sigmoid(gate_pre)
    inner_act = (gate_pre * sigmoid_gate * up_pre).astype(jnp.bfloat16)
    feed_out = lax.psum(
        jnp.dot(inner_act, down_weight, preferred_element_type=jnp.float32).astype(jnp.bfloat16),
        "tensor",
    ).astype(jnp.float32)
    layer_out = (middle + feed_out).astype(jnp.bfloat16).reshape(seq_count, span_len, model_width)
    upstream = cotangent.reshape(row_count, model_width)
    grad_down = jnp.dot(inner_act.T, upstream, preferred_element_type=jnp.float32)
    grad_inner = jnp.dot(upstream, down_weight.T, preferred_element_type=jnp.float32)
    grad_up_pre = (grad_inner * gate_pre * sigmoid_gate).astype(jnp.bfloat16)
    grad_gate_pre = (
        grad_inner * up_pre * sigmoid_gate * (1.0 + gate_pre * (1.0 - sigmoid_gate))
    ).astype(jnp.bfloat16)
    grad_gate = jnp.dot(normed_two.T, grad_gate_pre, preferred_element_type=jnp.float32)
    grad_up = jnp.dot(normed_two.T, grad_up_pre, preferred_element_type=jnp.float32)
    grad_normed_two = lax.psum(
        jnp.dot(grad_gate_pre, gate_weight.T, preferred_element_type=jnp.float32)
        + jnp.dot(grad_up_pre, up_weight.T, preferred_element_type=jnp.float32),
        "tensor",
    )
    grad_ffn_gain = jnp.sum(grad_normed_two * unit_two, axis=0)
    scaled_two = grad_normed_two * feedforward_gain
    grad_middle = upstream.astype(jnp.float32) + inverse_two * (
        scaled_two - unit_two * jnp.mean(scaled_two * unit_two, axis=-1, keepdims=True)
    )
    grad_attended = grad_middle.astype(jnp.bfloat16)
    grad_out_part = jnp.dot(mixed_flat.T, grad_attended, preferred_element_type=jnp.float32)
    grad_mixed = (
        jnp.dot(grad_attended, out_weight.T, preferred_element_type=jnp.float32)
        .astype(jnp.bfloat16)
        .reshape(seq_count, span_len, query_heads, HEAD_DIM)
    )

    def attend_back(block_items):
        query_block, key_block, value_block, query_seg, key_seg, grad_block, log_block = block_items
        allowed = visible(query_seg, key_seg, offset)
        grouped = query_block.reshape(span_len, kv_heads, group_size, HEAD_DIM)
        grad_grouped = grad_block.reshape(span_len, kv_heads, group_size, HEAD_DIM)
        raw_scores = jnp.einsum(
            "qhgd,khd->hgqk", grouped, key_block, preferred_element_type=jnp.float32
        )
        scores = jnp.where(allowed, raw_scores * score_scale, masked_score)
        attn_probs = jnp.exp(scores - log_block)
        rounded = attn_probs.astype(jnp.bfloat16)
        grad_values = jnp.einsum(
            "hgqk,qhgd->khd", rounded, grad_grouped, preferred_element_type=jnp.float32
        )
        grad_probs = jnp.einsum(
            "qhgd,khd->hgqk", grad_grouped, value_block, preferred_element_type=jnp.float32
        )
        row_dot = jnp.sum(attn_probs * grad_probs, axis=-1, keepdims=True)
        grad_scores = (attn_probs * (grad_probs - row_dot) * score_scale).astype(jnp.bfloat16)
        grad_queries = jnp.einsum(
            "hgqk,khd->qhgd", grad_scores, key_block, preferred_element_type=jnp.float32
        ).reshape(span_len, query_heads, HEAD_DIM)
        grad_keys = jnp.einsum(
            "hgqk,qhgd->khd", grad_scores, grouped, preferred_element_type=jnp.float32
        )
        return (grad_queries, grad_keys, grad_values)

    grad_queries, grad_keys, grad_values = lax.map(
        attend_back,
        (query_rows, all_keys, all_values, segment_ids, whole_segments, grad_mixed, log_sums),
    )
    own_grad_keys, own_grad_values = (
        lax.psum_scatter(grad_keys, "ctx", scatter_dimension=1, tiled=True),
        lax.psum_scatter(grad_values, "ctx", scatter_dimension=1, tiled=True),
    )
    grad_query_pre = (
        rotate(grad_queries, cosine, -sine_table)
        .astype(jnp.bfloat16)
        .reshape(row_count, query_heads * HEAD_DIM)
    )
    grad_key_pre = (
        rotate(own_grad_keys, cosine, -sine_table)
        .astype(jnp.bfloat16)
        .reshape(row_count, kv_heads * HEAD_DIM)
    )
    grad_value_pre = own_grad_values.astype(jnp.bfloat16).reshape(row_count, kv_heads * HEAD_DIM)
    grad_query = jnp.dot(normed.T, grad_query_pre, preferred_element_type=jnp.float32)
    grad_key = jnp.dot(normed.T, grad_key_pre, preferred_element_type=jnp.float32)
    grad_value = jnp.dot(normed.T, grad_value_pre, preferred_element_type=jnp.float32)
    grad_normed = lax.psum(
        (
            jnp.dot(grad_query_pre, query_weight.T, preferred_element_type=jnp.float32)
            + jnp.dot(grad_key_pre, key_weight.T, preferred_element_type=jnp.float32)
            + jnp.dot(grad_value_pre, value_weight.T, preferred_element_type=jnp.float32)
        ).astype(jnp.bfloat16),
        "tensor",
    ).astype(jnp.float32)
    grad_attn_gain = jnp.sum(grad_normed * unit_one, axis=0)
    scaled_one = grad_normed * attention_gain
    grad_hidden = grad_middle + inverse_one * (
        scaled_one - unit_one * jnp.mean(scaled_one * unit_one, axis=-1, keepdims=True)
    )
    grad_inputs = grad_hidden.astype(jnp.bfloat16).reshape(seq_count, span_len, model_width)
    reduced = (
        lax.psum_scatter(
            grad_attn_gain.astype(jnp.bfloat16), ("dp", "ctx"), scatter_dimension=0, tiled=True
        ).astype(jnp.float32),
        lax.psum_scatter(
            grad_query.astype(jnp.bfloat16), ("dp", "ctx"), scatter_dimension=0, tiled=True
        ).astype(jnp.float32),
        lax.psum_scatter(
            grad_key.astype(jnp.bfloat16), ("dp", "ctx"), scatter_dimension=0, tiled=True
        ).astype(jnp.float32),
        lax.psum_scatter(
            grad_value.astype(jnp.bfloat16), ("dp", "ctx"), scatter_dimension=0, tiled=True
        ).astype(jnp.float32),
        lax.psum_scatter(
            grad_out_part.astype(jnp.bfloat16), ("dp", "ctx"), scatter_dimension=1, tiled=True
        ).astype(jnp.float32),
        lax.psum_scatter(
            grad_ffn_gain.astype(jnp.bfloat16), ("dp", "ctx"), scatter_dimension=0, tiled=True
        ).astype(jnp.float32),
        lax.psum_scatter(
            grad_gate.astype(jnp.bfloat16), ("dp", "ctx"), scatter_dimension=0, tiled=True
        ).astype(jnp.float32),
        lax.psum_scatter(
            grad_up.astype(jnp.bfloat16), ("dp", "ctx"), scatter_dimension=0, tiled=True
        ).astype(jnp.float32),
        lax.psum_scatter(
            grad_down.astype(jnp.bfloat16), ("dp", "ctx"), scatter_dimension=1, tiled=True
        ).astype(jnp.float32),
    )
    return (
        layer_out,
        grad_inputs,
        reduced[0],
        reduced[1],
        reduced[2],
        reduced[3],
        reduced[4],
        reduced[5],
        reduced[6],
        reduced[7],
        reduced[8],
    )


def fast_body(
    inputs, segment_ids, attention_gain, query_weight, key_weight, value_weight, out_weight, feedforward_gain,
    gate_weight, up_weight, down_weight, cotangent,
):
    _, span_len, model_width = inputs.shape
    line_size, dp_size = lax.axis_size("tensor"), lax.axis_size("dp")
    half_dim = HEAD_DIM // 2
    frequency = rope_base ** (-2.0 * jnp.arange(half_dim, dtype=jnp.float32) / HEAD_DIM)
    frequency = jnp.tile(frequency, 4).reshape(1, 128)
    flat_inputs = inputs.reshape(span_len, model_width)
    upstream = cotangent.reshape(span_len, model_width)
    gain_one, gain_two = attention_gain.reshape(1, -1), feedforward_gain.reshape(1, -1)
    key_turned, value_turned = key_weight.T, value_weight.T
    (
        seg_row, cosine, signed_sine, query, kv, logs, mixed, normed, two, upstream_cols, up, inner, second, attended,
        middle, grad_middle, land_gate, land_up, own_gate, gain_grad,
    ) = front_call(
        line_size, dp_size,
        (
            flat_inputs, segment_ids, frequency, gain_one, gain_two, query_weight, key_turned, value_turned, out_weight,
            gate_weight, up_weight, down_weight, upstream,
        ),
    )
    (
        layer_out, grad_inputs, gains, own_qkv, own_out, own_up, own_down, land_up_last, land_down, land_qkv,
        land_out,
    ) = back_call(
        line_size, dp_size,
        (
            query, kv, logs, mixed, cosine, signed_sine, seg_row, flat_inputs, normed, two, upstream_cols,
            up, inner, second, attended, middle, grad_middle, gain_one, gain_grad,
            query_weight, key_turned, value_turned, out_weight,
        ),
    )
    layer_out, grad_inputs, gain_a, grad_query, grad_key, grad_value, grad_out, gain_b, *ffn = settle_call(
        (
            layer_out, grad_inputs, gains, own_qkv, own_out, own_gate, own_up, own_down,
            land_gate, land_up, land_up_last, land_down, land_qkv, land_out,
        )
    )
    shape = (1, span_len, model_width)
    return (
        layer_out.reshape(shape), grad_inputs.reshape(shape), gain_a[0], grad_query, grad_key.T, grad_value.T,
        grad_out, gain_b[0], *ffn,
    )


def body(mesh, *arrays):
    inputs = arrays[0]
    span_len, model_width = inputs.shape[1:]
    dp_size, ctx_size, line_size = mesh.shape["dp"], mesh.shape["ctx"], mesh.shape["tensor"]
    piece = model_width // (dp_size * ctx_size)
    fits = inputs.shape[0] == 1 and ctx_size == 2 and dp_size > 2 and line_size > 1
    if fits and piece % 128 == 0 and span_len % 512 == 0:
        return fast_body(*arrays)
    return plain_body(*arrays)


def solution(mesh):
    return jax.shard_map(
        functools.partial(body, mesh),
        mesh=mesh,
        in_specs=(
            P("dp", "ctx", None),
            P("dp", "ctx"),
            P(),
            P(None, "tensor"),
            P(None, "tensor"),
            P(None, "tensor"),
            P("tensor", None),
            P(),
            P(None, "tensor"),
            P(None, "tensor"),
            P("tensor", None),
            P("dp", "ctx", None),
        ),
        out_specs=(
            P("dp", "ctx", None),
            P("dp", "ctx", None),
            P(("dp", "ctx")),
            P(("dp", "ctx"), "tensor"),
            P(("dp", "ctx"), "tensor"),
            P(("dp", "ctx"), "tensor"),
            P("tensor", ("dp", "ctx")),
            P(("dp", "ctx")),
            P(("dp", "ctx"), "tensor"),
            P(("dp", "ctx"), "tensor"),
            P("tensor", ("dp", "ctx")),
        ),
        check_vma=False,
    )
```

```python
import functools
import math

import jax
import jax.numpy as jnp
from jax import lax
from jax.experimental import pallas as pl
from jax.experimental.pallas import tpu as pltpu
from jax.sharding import PartitionSpec as P

HEAD_DIM = 64


epsilon = 1e-05
rope_base = 10000.0
masked_score = -1e30


def positions_of(segment):
    token_index = jnp.arange(segment.shape[-1], dtype=jnp.int32)
    previous = jnp.concatenate([segment[..., :1] - 1, segment[..., :-1]], axis=-1)
    starts = jnp.where(segment != previous, token_index, 0)
    earlier = token_index[None, :] <= token_index[:, None]
    run_start = jnp.max(jnp.where(earlier, starts[..., None, :], 0), axis=-1)
    return token_index - run_start


MESH = pl.DeviceIdType.MESH
CHUNK, HOP = 16, 2
BACK_CHUNK, BACK_HOP = 32, 2
TASKS = 1
RINGS = [1, 2, 4]
MIB = 1 << 20
FRONT_MIB, BACK_MIB = 62, 62


def rotary_tables(positions):
    half_dim = HEAD_DIM // 2
    frequency = rope_base ** (-2.0 * jnp.arange(half_dim, dtype=jnp.float32) / HEAD_DIM)
    angles = positions.astype(jnp.float32)[..., None] * frequency
    return (jnp.cos(angles), jnp.sin(angles))


def rotate(values, cosine, sine_table):
    half_dim = values.shape[-1] // 2
    first = values[..., :half_dim]
    second = values[..., half_dim:]
    return jnp.concatenate(
        [first * cosine - second * sine_table, second * cosine + first * sine_table], axis=-1
    )


def visible(query_seg, key_seg, first_row):
    query_pos = first_row + jnp.arange(query_seg.shape[0], dtype=jnp.int32)
    key_pos = jnp.arange(key_seg.shape[0], dtype=jnp.int32)
    same_doc = query_seg[:, None] == key_seg[None, :]
    causal = key_pos[None, :] <= query_pos[:, None]
    usable = (key_seg[None, :] >= 0) | (key_pos[None, :] == query_pos[:, None])
    return same_doc & causal & usable


def turned_dot(left, right):
    return lax.dot_general(
        left, right, (((1,), (1,)), ((), ())), preferred_element_type=jnp.float32
    )


def remote(src, dst, send, recv, **device):
    return pltpu.make_async_remote_copy(
        src_ref=src, dst_ref=dst, send_sem=send, recv_sem=recv, device_id=device, device_id_type=MESH
    )


class Line:
    def __init__(self, line_size, own, finish, place, out_ref, held, acc_send, acc_recv, back_send, back_recv, base=0, hop=HOP):
        self.base, self.hop = base, hop
        self.last = line_size - 1
        self.here = lax.axis_index("tensor")
        self.own, self.finish, self.place = own, finish, place
        self.out_ref, self.held = out_ref, held
        self.acc_sems, self.back_sems = (acc_send, acc_recv), (back_send, back_recv)
        self.count, self.chunk = held.shape[1:3]

    def parts(self, stream):
        if stream == 0:
            return self.here, self.here + 1, self.here - 1
        return self.last - self.here, self.here - 1, self.here + 1

    def acc_copy(self, stream, i, target):
        at = i - self.base
        ref = self.held.at[stream, at]
        return remote(ref, ref, self.acc_sems[0].at[stream, at], self.acc_sems[1].at[stream, at], tensor=target)

    def rows_of(self, stream, i):
        return pl.ds(pl.multiple_of(self.place(stream, i), self.chunk), self.chunk)

    def back_copy(self, stream, i, target):
        at = i - self.base
        ref = self.out_ref.at[self.rows_of(stream, i)]
        return remote(ref, ref, self.back_sems[0].at[stream, at], self.back_sems[1].at[stream, at], tensor=target)

    def step(self, k, begin=0, size=None):
        size = self.count if size is None else size

        @pl.when((k >= 0) & (k < size + 2 * self.hop * self.last))
        def _():
            for stream in (0, 1):
                self.stream_step(k, stream, begin, size)

    def stream_step(self, k, stream, begin, size):
        last, held = self.last, self.held
        place, after, before = self.parts(stream)
        due = k - self.hop * place
        i = begin + due
        at = i - self.base

        @pl.when((due >= 0) & (due < size))
        def _():
            @pl.when(place == 0)
            def _():
                held[stream, at] = self.own(stream, i).astype(jnp.bfloat16)
                self.acc_copy(stream, i, after).start()

            @pl.when(place > 0)
            def _():
                self.acc_copy(stream, i, after).wait_recv()

                @pl.when(place < last)
                def _():
                    held[stream, at] = (held[stream, at].astype(jnp.float32) + self.own(stream, i)).astype(jnp.bfloat16)
                    self.acc_copy(stream, i, after).start()

                @pl.when(place == last)
                def _():
                    total = held[stream, at].astype(jnp.float32) + self.own(stream, i)
                    self.out_ref[self.rows_of(stream, i)] = self.finish(stream, i, total).astype(jnp.bfloat16)
                    self.back_copy(stream, i, before).start()

        back = k - self.hop * (2 * last - place)
        j = begin + back

        @pl.when((back >= 0) & (back < size) & (place < last))
        def _():
            self.back_copy(stream, j, before).wait_recv()

            @pl.when(place > 0)
            def _():
                self.back_copy(stream, j, before).start()

    def drain(self):
        def sent(at, carry):
            i = at + self.base
            for stream in (0, 1):
                place, after, before = self.parts(stream)

                @pl.when(place < self.last)
                def _():
                    self.acc_copy(stream, i, after).wait_send()

                @pl.when(place > 0)
                def _():
                    self.back_copy(stream, i, before).wait_send()

            return carry

        lax.fori_loop(0, self.count, sent, 0)


def line_scratch(rows, width, share=1, chunk=CHUNK):
    count = rows // 2 // chunk // share
    return [
        pltpu.VMEM((2, count, chunk, width), jnp.bfloat16),
        *[pltpu.SemaphoreType.DMA((2, count))] * 4,
    ]


def greet(line, core, plane, full_line=False):
    here, row, side = lax.axis_index("tensor"), lax.axis_index("dp"), lax.axis_index("ctx")
    barrier = pltpu.get_barrier_semaphore()
    peers = 0

    def call(**device):
        pl.semaphore_signal(barrier, inc=1, device_id=device, device_id_type=MESH)

    if full_line:
        for hop in range(1, line):
            call(tensor=lax.rem(here + hop, line))
        peers += line - 1
    else:

        @pl.when(here > 0)
        def _():
            call(tensor=here - 1)

        @pl.when(here < line - 1)
        def _():
            call(tensor=here + 1)

        peers = jnp.where(here > 0, 1, 0) + jnp.where(here < line - 1, 1, 0)
    if plane:
        for hop in range(1, 2 * plane):
            peer = lax.rem(2 * row + side + hop, 2 * plane)
            call(dp=peer // 2, ctx=lax.rem(peer, 2))
        peers += 2 * plane - 1
    elif core:
        call(ctx=1 - side)
        peers += 1
    return lambda: pl.semaphore_wait(barrier, peers)


def kept_rows(i, chunk=CHUNK):
    return pl.ds(pl.multiple_of(i * chunk, chunk), chunk)


def rotate_lanes(values, cosine, signed_sine, back=False):
    lane = lax.broadcasted_iota(jnp.int32, values.shape, 1)
    swapped = jnp.where(
        lax.rem(lane, HEAD_DIM) < HEAD_DIM // 2,
        pltpu.roll(values, 128 - HEAD_DIM // 2, 1),
        pltpu.roll(values, HEAD_DIM // 2, 1),
    )
    turn = swapped * signed_sine
    return values * cosine - turn if back else values * cosine + turn


def key_lanes(values, turned):
    lane = lax.broadcasted_iota(jnp.int32, values.shape, 1)
    return jnp.where(lane < HEAD_DIM, turned, values)


def fill_bias(bias, seg_col, seg_row, first, keys, block):
    key_seg = seg_col[0:keys]
    query_seg = seg_row[:, first : first + block]
    key_pos = lax.broadcasted_iota(jnp.int32, (keys, block), 0)
    query_pos = first + lax.broadcasted_iota(jnp.int32, (keys, block), 1)
    usable = (key_seg >= 0) | (key_pos == query_pos)
    allowed = (key_seg == query_seg) & (key_pos <= query_pos) & usable
    bias[0:keys, :] = jnp.where(allowed, 0.0, masked_score)


def wide_tiles(width):
    return width // 256, width % 256


def inverse_rms(values):
    return lax.rsqrt(jnp.mean(values * values, axis=-1, keepdims=True) + epsilon)


def front_kernel(
    n, dp_size,
    inputs_any, segments, frequency, gain_one, gain_two,
    query_weight_any, key_weight_any, value_weight_any, out_weight_any, gate_weight_any, up_weight_any, down_weight_any, upstream_any,
    seg_out, cosine_out, sine_out, query_out, kv_out, log_out, mixed_out, normed_cols, two_cols, upstream_cols, up_out, inner_out, second_out,
    attended_out, middle_out, grad_middle_out, land_gate, land_up, own_gate, gain_out,
    seg_all, seg_row, seg_col, cosine, signed_sine,
    inputs, normed, kv_weight, query, kv, kv_turned, logs, mixed, bias,
    gate_weight, up_weight, down_weight, upstream, grad_inner, normed_two, gate, up, inner,
    partial, middle, grad_middle, two_other, turned, send_gate, send_up,
    load_sems, store_sems, core_send, core_recv, plane_send, plane_recv, *line_refs,
):
    span, width = inputs.shape
    hidden, piece = gate.shape[1], turned.shape[0]
    row, core = lax.axis_index("dp"), lax.axis_index("ctx")
    half, block = span // 2, span // 4
    second, attended = normed, inputs
    line_one, line_two, line_three = line_refs[:5], line_refs[5:10], line_refs[10:]
    count, heads = line_one[0].shape[1], query.shape[1]
    part = count // 2

    def load(at, src, dst):
        made = pltpu.make_async_copy(src, dst, load_sems.at[at])
        made.start()
        return made

    def ordered(stream, i):
        return (i // part) * half + stream * block + lax.rem(i, part) * CHUNK

    def moved(at):
        return (0, 2, 1, 3)[at] * block

    load_inputs = load(0, inputs_any, inputs)
    query_weight = gate_weight.at[:, pl.ds(0, heads)]
    out_weight = down_weight.at[pl.ds(0, heads)]
    load_query = load(1, query_weight_any, query_weight)
    load_kv = [
        load(2, key_weight_any, kv_weight.at[pl.ds(0, HEAD_DIM)]),
        load(11, value_weight_any, kv_weight.at[pl.ds(HEAD_DIM, HEAD_DIM)]),
    ]
    load_out = load(3, out_weight_any, out_weight)
    load_up = [
        load(4 + b, upstream_any.at[pl.ds(b * block, block)], upstream.at[pl.ds(moved(b), block)]) for b in range(4)
    ]
    load_up_weight = load(10, up_weight_any, up_weight)
    seg_all[core] = jnp.broadcast_to(segments[...], seg_all.shape[1:])
    meet = greet(n, True, dp_size)

    def seg_copy():
        return remote(seg_all.at[core], seg_all.at[core], core_send.at[1], core_recv.at[1], ctx=1 - core)

    load_inputs.wait()

    def norm_rows(b, carry):
        rows = pl.ds(pl.multiple_of(b * 64, 64), 64)
        value = inputs[rows].astype(jnp.float32)
        normed[rows] = (value * inverse_rms(value) * gain_one[...]).astype(jnp.bfloat16)
        return carry

    lax.fori_loop(0, span // 64, norm_rows, 0)
    meet()
    seg_copy().start()
    for made in load_kv:
        made.wait()
    raw_kv = turned_dot(normed[...], kv_weight[...])
    load_query.wait()
    for low in range(0, span, half):
        rows = slice(low, low + half)
        partial[rows, 0:heads] = jnp.dot(normed[rows], query_weight[...], preferred_element_type=jnp.float32)
    load_gate = load(9, gate_weight_any, gate_weight)
    seg_copy().wait()
    for side in (0, 1):
        seg_row[:, side * span : (side + 1) * span] = seg_all[side, 0:1]
        seg_col[side * span : (side + 1) * span] = seg_all[side].T[:, 0:1]
    own_seg = seg_all[core, 0:1]
    key_pos = lax.broadcasted_iota(jnp.int32, (2 * span, span), 0)
    query_pos = core * span + lax.broadcasted_iota(jnp.int32, (2 * span, span), 1)
    before = (seg_col[...] == own_seg) & (key_pos < query_pos)
    position = jnp.sum(jnp.where(before, 1.0, 0.0), axis=0, keepdims=True)
    angles = jnp.broadcast_to(position, (8, span)).T[:, 0:1] * frequency[...]
    lane = lax.broadcasted_iota(jnp.int32, angles.shape, 1)
    cosine[...] = jnp.cos(angles)
    sine = jnp.sin(angles)
    signed_sine[...] = jnp.where(lax.rem(lane, HEAD_DIM) < HEAD_DIM // 2, -sine, sine)
    own_rows = pl.ds(pl.multiple_of(core * span, span), span)
    kv[own_rows] = key_lanes(raw_kv, rotate_lanes(raw_kv, cosine[...], signed_sine[...])).astype(jnp.bfloat16)

    def kv_copy():
        return remote(kv.at[own_rows], kv.at[own_rows], core_send.at[0], core_recv.at[0], ctx=1 - core)

    def kv_arrival():
        rows = pl.ds(0, span)
        return remote(kv.at[rows], kv.at[rows], core_send.at[0], core_recv.at[0], ctx=1 - core)

    @pl.when(core == 0)
    def _():
        kv_copy().start()

    for lanes in range(0, heads, 128):
        rotated = rotate_lanes(partial[:, lanes : lanes + 128], cosine[...], signed_sine[...])
        query[:, lanes : lanes + 128] = rotated.astype(jnp.bfloat16) * (HEAD_DIM ** -0.5)

    @pl.when(core == 1)
    def _():
        kv_arrival().wait_recv()

    kv_turned[...] = kv[...].T

    def attend(side, at):
        keys = side * span + (at + 1) * half
        rows = slice(at * half, (at + 1) * half)
        fill_bias(bias, seg_col, seg_row, side * span + at * half, keys, half)

        def pair(index, carry):
            lanes = pl.ds(pl.multiple_of(index * 128, 128), 128)
            both = query[rows, lanes]
            outs = []
            for which in (0, 1):
                scores = turned_dot(kv[0:keys, 0:HEAD_DIM], both[:, which * HEAD_DIM : (which + 1) * HEAD_DIM])
                scores = scores + bias[0:keys, :]
                peak = jnp.max(scores, axis=0, keepdims=True)
                grown = jnp.exp(scores - peak)
                total = jnp.sum(grown, axis=0, keepdims=True)
                logs[pl.ds(2 * index + which, 1), rows] = peak + jnp.log(total)
                out = jnp.dot(
                    kv_turned[HEAD_DIM : 2 * HEAD_DIM, 0:keys],
                    grown.astype(jnp.bfloat16),
                    preferred_element_type=jnp.float32,
                )
                outs.append(out / total)
            mixed[rows, lanes] = jnp.concatenate(outs, axis=0).T.astype(jnp.bfloat16)
            return carry

        lax.fori_loop(0, query.shape[1] // 128, pair, 0)

    for side in (0, 1):

        @pl.when(core == side)
        def _():
            attend(side, 0)
            attend(side, 1)

    load_out.wait()

    def out_tile(t, carry):
        columns = pl.ds(pl.multiple_of(t * 512, 512), 512)
        for b in (0, 2):
            value = jnp.dot(
                mixed[b * block : (b + 2) * block], out_weight[:, columns], preferred_element_type=jnp.float32
            )
            partial[moved(b) : moved(b) + block, columns] = value[:block]
            partial[moved(b + 1) : moved(b + 1) + block, columns] = value[block:]
        return carry

    lax.fori_loop(0, width // 512, out_tile, 0)
    load_down = load(8, down_weight_any, down_weight)

    def rows_at(start):
        return pl.ds(pl.multiple_of(start, CHUNK), CHUNK)

    def own(stream, i):
        return partial[rows_at(ordered(stream, i))]

    def finish_one(stream, i, total):
        value = inputs[rows_at((stream * count + i) * CHUNK)].astype(jnp.float32) + total
        middle[kept_rows(i)] = value
        return value * inverse_rms(value) * gain_two[...]

    gain_out[...] = jnp.zeros_like(gain_out)

    def finish_two(stream, i, total):
        value = middle[kept_rows(i)]
        inverse = inverse_rms(value)
        unit = value * inverse
        gain_out[0:1, :] += jnp.sum(total * unit, axis=0, keepdims=True)
        scaled = total * gain_two[...]
        result = upstream[rows_at(ordered(stream, i))].astype(jnp.float32) + inverse * (
            scaled - unit * jnp.mean(scaled * unit, axis=-1, keepdims=True)
        )
        grad_middle[kept_rows(i)] = result
        return result

    first = Line(n, own, finish_one, ordered, normed_two, *line_one)
    then = Line(n, own, finish_two, ordered, attended, *line_two)
    third = Line(
        n,
        lambda stream, i: second[rows_at(ordered(stream, i))].astype(jnp.float32),
        lambda stream, i, total: middle[kept_rows(i)] + total,
        ordered, second, *line_three,
    )
    tiles, rest = wide_tiles(hidden)
    tile_count = tiles + (1 if rest else 0)

    def each_tile(t, work):
        @pl.when(t < tiles)
        def _():
            work(pl.ds(pl.multiple_of(t * 256, 256), 256))

        if rest:

            @pl.when(t == tiles)
            def _():
                work(pl.ds(tiles * 256, rest))

    def inner_tile(columns):
        grad_inner[:, columns] = turned_dot(upstream[...], down_weight[columns, :])

    def forward_tile(rows, columns):
        gated = jnp.dot(normed_two[rows], gate_weight[:, columns], preferred_element_type=jnp.float32)
        upped = jnp.dot(normed_two[rows], up_weight[:, columns], preferred_element_type=jnp.float32)
        sig = jax.nn.sigmoid(gated)
        act = gated * sig
        grad = grad_inner[rows, columns]
        inner[rows, columns] = (act * upped).astype(jnp.bfloat16)
        up[rows, columns] = (grad * act).astype(jnp.bfloat16)
        gate[rows, columns] = (grad * upped * sig * (1.0 + gated * (1.0 - sig))).astype(jnp.bfloat16)

    def back_tile(rows, t):
        columns = pl.ds(pl.multiple_of(t * 512, 512), 512)
        partial[rows, columns] = turned_dot(gate[rows], gate_weight[columns, :]) + turned_dot(
            up[rows], up_weight[columns, :]
        )

    def second_tile(rows, t):
        columns = pl.ds(pl.multiple_of(t * 512, 512), 512)
        second[rows, columns] = jnp.dot(
            inner[rows], down_weight[:, columns], preferred_element_type=jnp.float32
        ).astype(jnp.bfloat16)

    last = n - 1
    trip = 2 * HOP * last
    each = 2
    forward_steps, back_steps = -(-tile_count // each), width // 1024
    work = forward_steps + back_steps
    base_one = part + trip
    second_steps = width // 1024
    base_two = max(count + trip, base_one + work + second_steps)
    third_base = base_one + work + second_steps
    steps = max(base_two + work + part + trip, third_base + part + trip)

    def store(at, src, dst):
        return pltpu.make_async_copy(src, dst, store_sems.at[at])

    def stores(at, src, dst):
        return [
            store(at + b, src.at[pl.ds(moved(b), block)], dst.at[pl.ds(b * block, block)]) for b in range(4)
        ]

    early = [
        store(0, query, query_out), store(1, kv, kv_out), store(2, logs, log_out), store(3, mixed, mixed_out.at[pl.ds(0, span)]),
        store(31, seg_row, seg_out), store(32, cosine, cosine_out),
        store(33, signed_sine, sine_out),
    ]
    own_slots, far_slots = [], []

    def own_columns(src, dst):
        made = []
        for q in range(dp_size):
            columns = pl.ds(pl.multiple_of((2 * q + core) * piece, piece), piece)
            at = 34 + len(own_slots)
            own_slots.append(at)
            made.append(store(at, src.at[:, columns], dst.at[pl.ds(0, span), pl.ds(q * piece, piece)]))
        return made

    def far_copy(src, dst):
        at = 3 + dp_size + len(far_slots)
        far_slots.append(at)
        return remote(src, dst, core_send.at[at], core_recv.at[at], ctx=1 - core)

    def far_columns(src, dst):
        made = []
        for q in range(dp_size):
            columns = pl.ds(pl.multiple_of((2 * q + 1 - core) * piece, piece), piece)
            made.append(far_copy(src.at[:, columns], dst.at[pl.ds(span, span), pl.ds(q * piece, piece)]))
        return made

    normed_moves = [*own_columns(normed, normed_cols), *far_columns(normed, normed_cols)]
    upstream_moves = [*own_columns(upstream, upstream_cols), *far_columns(upstream, upstream_cols)]
    mixed_move = far_copy(mixed, mixed_out.at[pl.ds(span, span)])
    hidden_moves = [
        store(6, inner, inner_out.at[pl.ds(0, span)]), far_copy(inner, inner_out.at[pl.ds(span, span)]),
        *own_columns(normed_two, two_cols),
    ]
    up_slot = 3 + dp_size + len(far_slots)
    two_moves = [store(7, two_other, two_cols.at[pl.ds(span, span)]), store(5, up, up_out)]
    second_stores, attended_stores = stores(21, second, second_out), stores(25, attended, attended_out)
    middle_store = store(29, middle, middle_out)

    def gate_swaps():
        made = [
            remote(
                ref.at[pl.ds(0, span)], ref.at[pl.ds(span, span)], core_send.at[at], core_recv.at[at], ctx=1 - core
            )
            for ref, at in ((gate, 2), (up, up_slot))
        ]
        for q in range(dp_size):
            columns = pl.ds(pl.multiple_of((2 * q + 1 - core) * piece, piece), piece)
            made.append(
                remote(
                    normed_two.at[:, columns], two_other.at[:, pl.ds(q * piece, piece)],
                    core_send.at[3 + q], core_recv.at[3 + q], ctx=1 - core,
                )
            )
        return made

    def peer_of(r):
        return lax.rem(row + 1 + r, dp_size)

    sends, lands = (send_gate, send_up), (land_gate, land_up)

    def gate_copy(w, r):
        return remote(sends[w].at[r], lands[w].at[r], plane_send.at[w, r], plane_recv.at[w, r], dp=peer_of(r))

    def turn_two(r):
        peer = peer_of(r)
        columns = pl.ds(pl.multiple_of((2 * peer + core) * piece, piece), piece)
        turned[:, 0:span] = normed_two[:, columns].T
        turned[:, span : 2 * span] = two_other[:, pl.ds(pl.multiple_of(peer * piece, piece), piece)].T

    edges = [(low, min(low + 384, hidden)) for low in range(0, hidden, 384)]

    def gate_piece(w, r):
        for low, high in edges:
            sends[w][r, :, low:high] = jnp.dot(
                turned[...], (gate, up)[w][:, low:high], preferred_element_type=jnp.float32
            ).astype(jnp.bfloat16)
        gate_copy(w, r).start()

    def own_piece():
        for low, high in edges:
            partial[0:piece, low:high] = jnp.dot(turned[...], gate[:, low:high], preferred_element_type=jnp.float32)

    own_store = store(4, partial.at[pl.ds(0, piece), pl.ds(0, hidden)], own_gate)

    for made in [*early, *normed_moves, mixed_move]:
        made.start()

    def step(k, carry):
        first.step(k)
        if base_two == base_one + part:
            then.step(k - (base_one + work))
        else:
            then.step(k - (base_one + work), 0, part)
            then.step(k - (base_two + work), part, part)
        third.step(k - third_base)

        @pl.when(k == 0)
        def _():
            for made in load_up:
                made.wait()
            for made in upstream_moves:
                made.start()

        @pl.when(k == 2)
        def _():
            load_down.wait()
            load_gate.wait()
            load_up_weight.wait()

        @pl.when((k >= 2) & (k < 2 + tile_count))
        def _():
            each_tile(k - 2, inner_tile)

        @pl.when(k == base_one)
        def _():
            for made in normed_moves:
                made.wait()

        @pl.when(k == base_two)
        def _():
            middle_store.start()

        late = jnp.where(k >= base_two, 1, 0)
        phase = k - jnp.where(k >= base_two, base_two, base_one)
        rows = pl.ds(pl.multiple_of(late * half, half), half)

        @pl.when((phase >= 0) & (phase < forward_steps))
        def _():
            def tile(t, carry):
                each_tile(t, functools.partial(forward_tile, rows))
                return carry

            lax.fori_loop(phase * each, jnp.minimum((phase + 1) * each, tile_count), tile, 0)

        @pl.when((phase >= forward_steps) & (phase < work))
        def _():
            for t in (0, 1):
                back_tile(rows, 2 * (phase - forward_steps) + t)

        @pl.when((phase >= work) & (phase < work + second_steps))
        def _():
            for t in (0, 1):
                second_tile(rows, 2 * (phase - work) + t)

        @pl.when(k == base_two + work)
        def _():
            for made in hidden_moves:
                made.start()

        @pl.when(k == base_two + forward_steps)
        def _():
            for made in gate_swaps():
                made.start()

        @pl.when(k == base_two + work + 1)
        def _():
            for made in gate_swaps():
                made.wait()
            for made in two_moves:
                made.start()

        gate_task = k - (base_two + work + 1)

        @pl.when((gate_task >= 0) & (gate_task < dp_size - 1))
        def _():
            turn_two(gate_task)
            gate_piece(0, gate_task)

            @pl.when(gate_task < dp_size - 2)
            def _():
                gate_piece(1, gate_task)

        @pl.when(k == base_two + work + part + HOP * last)
        def _():
            turn_two(dp_size - 1)
            own_piece()
            own_store.start()

        @pl.when(k == base_two + work + second_steps)
        def _():
            for b in (1, 3):
                second_stores[b].start()

        @pl.when(k == max(base_one + work, third_base) + part + trip)
        def _():
            for b in (0, 2):
                second_stores[b].start()
                attended_stores[b].start()

        return carry

    lax.fori_loop(0, steps, step, 0)
    late_stores = [
        attended_stores[1], attended_stores[3], store(30, grad_middle, grad_middle_out),
    ]
    for made in late_stores:
        made.start()
    first.drain()
    then.drain()
    third.drain()

    @pl.when(core == 0)
    def _():
        kv_copy().wait_send()

    for r in range(dp_size - 1):
        for w in ((0, 1) if r < dp_size - 2 else (0,)):
            gate_copy(w, r).wait()
    for made in [
        *early, mixed_move, *upstream_moves, *hidden_moves, *two_moves, own_store, middle_store, *second_stores,
        attended_stores[0], attended_stores[2], *late_stores,
    ]:
        made.wait()


def front_call(line_size, dp_size, operands):
    inputs = operands[0]
    query_weight, out_weight, gate_weight = operands[5], operands[8], operands[9]
    span, width = inputs.shape
    heads, hidden = query_weight.shape[1], gate_weight.shape[1]
    piece = width // (2 * dp_size)
    low, full = jnp.bfloat16, jnp.float32
    vmem, outside = pl.BlockSpec(memory_space=pltpu.VMEM), pl.BlockSpec(memory_space=pl.ANY)
    dma = pltpu.SemaphoreType.DMA
    outs = [
        ((1, 2 * span), jnp.int32), ((span, 128), full), ((span, 128), full),
        ((span, heads), low), ((2 * span, 128), low), ((heads // HEAD_DIM, span), full), ((2 * span, heads), low),
        *[((2 * span, width // 2), low)] * 3, *[((2 * span, hidden), low)] * 2, ((span, width), low),
        ((span, width), low), ((span // 2, width), full), ((span // 2, width), full),
        ((dp_size - 1, piece, hidden), low), ((dp_size - 2, piece, hidden), low), ((piece, hidden), full), ((8, width), full),
    ]
    scratch = [
        pltpu.VMEM((2, 8, span), jnp.int32), pltpu.VMEM((1, 2 * span), jnp.int32),
        pltpu.VMEM((2 * span, 1), jnp.int32), pltpu.VMEM((span, 128), full), pltpu.VMEM((span, 128), full),
        pltpu.VMEM((span, width), low), pltpu.VMEM((span, width), low),
        pltpu.VMEM((128, width), low), pltpu.VMEM((span, heads), low),
        pltpu.VMEM((2 * span, 128), low), pltpu.VMEM((128, 2 * span), low),
        pltpu.VMEM((heads // HEAD_DIM, span), full), pltpu.VMEM((span, heads), low),
        pltpu.VMEM((2 * span, span // 2), full),
        pltpu.VMEM((width, hidden), low), pltpu.VMEM((width, hidden), low), pltpu.VMEM((hidden, width), low),
        pltpu.VMEM((span, width), low), pltpu.VMEM((span, hidden), full), pltpu.VMEM((span, width), low),
        *[pltpu.VMEM((2 * span, hidden), low)] * 2, pltpu.VMEM((span, hidden), low),
        pltpu.VMEM((span, width), full),
        pltpu.VMEM((span // 2, width), full), pltpu.VMEM((span // 2, width), full),
        pltpu.VMEM((span, width // 2), low), pltpu.VMEM((piece, 2 * span), low),
        pltpu.VMEM((dp_size - 1, piece, hidden), low), pltpu.VMEM((dp_size - 2, piece, hidden), low),
        dma((12,)), dma((34 + 3 * dp_size,)), dma((6 + 3 * dp_size,)), dma((6 + 3 * dp_size,)),
        dma((2, dp_size - 1)), dma((2, dp_size - 1)),
        *line_scratch(span, width), *line_scratch(span, width), *line_scratch(span, width, 2),
    ]
    return pl.pallas_call(
        functools.partial(front_kernel, line_size, dp_size),
        out_shape=[jax.ShapeDtypeStruct(s, d) for s, d in outs],
        in_specs=[outside] + [vmem] * 4 + [outside] * 8,
        out_specs=[outside] * 19 + [vmem],
        scratch_shapes=scratch,
        compiler_params=pltpu.CompilerParams(
            collective_id=1, has_side_effects=True, vmem_limit_bytes=FRONT_MIB * MIB
        ),
    )(*operands)


def back_kernel(
    n, dp_size,
    query_any, kv_any, logs, mixed_any, cosine, signed_sine, seg_row, inputs_any, normed_any, two_any, upstream_any,
    up_any, inner_any, second_any, attended_any, middle_any, grad_middle_any, gain_one, gain_two_grad,
    query_weight_any, key_weight_any, value_weight_any, out_weight_any,
    layer_out, grad_inputs, grad_gains, grad_qkv, own_out, grad_up, own_down,
    land_up, land_down, land_qkv, land_out,
    query, kv, kv_turned, grad_mixed, mixed, attended, normed_cols, two_cols, upstream_cols, attended_other,
    up, inner, pre, query_weight, kv_weight, out_weight, grad_middle, middle, inputs,
    ring, send_qkv, send_out, turned, seg_col, bias, kv_grad, kv_grad_other,
    gain_line, gain_land, gain_sum, gain_plane,
    load_sems, core_send, core_recv, ring_send, ring_recv, plane_send, plane_recv, line_send, line_recv,
    spread_send, spread_recv, *line_refs,
):
    span, width = attended.shape
    heads, piece = query.shape[1], turned.shape[0]
    here, row, core = lax.axis_index("tensor"), lax.axis_index("dp"), lax.axis_index("ctx")
    half = span // 2
    line_out, line_in = line_refs[:5], line_refs[5:]
    count, part = line_in[0].shape[1], line_out[0].shape[1]
    last = n - 1
    loads = []

    def load(src, dst):
        made = pltpu.make_async_copy(src, dst, load_sems.at[len(loads)])
        made.start()
        loads.append(made)
        return made

    own_half = pl.ds(pl.multiple_of(jnp.where(here == 0, half, 0), half), half)
    mixed_loads = [load(attended_any, attended), load(out_weight_any, out_weight)]
    attend_loads = [load(query_any, query), load(kv_any, kv), load(mixed_any, mixed)]
    line_loads = [load(second_any, layer_out), load(middle_any, middle)]

    up_loads = [load(two_any, two_cols), load(up_any, up)]
    inner_loads = [load(upstream_any, upstream_cols), load(inner_any, inner)]
    late_loads = [
        load(query_weight_any, query_weight), load(key_weight_any, kv_weight.at[pl.ds(0, HEAD_DIM)]),
        load(value_weight_any, kv_weight.at[pl.ds(HEAD_DIM, HEAD_DIM)]),
        load(grad_middle_any, grad_middle), load(inputs_any.at[own_half], inputs),
        load(normed_any, normed_cols),
    ]
    meet = greet(n, True, dp_size, full_line=True)
    pre_slot, kv_slot = dp_size, dp_size + 1

    def attended_swaps():
        made = []
        for q in range(dp_size):
            columns = pl.ds(pl.multiple_of((2 * q + 1 - core) * piece, piece), piece)
            made.append(
                remote(
                    attended.at[:, columns], attended_other.at[:, pl.ds(q * piece, piece)],
                    core_send.at[q], core_recv.at[q], ctx=1 - core,
                )
            )
        return made

    def pre_swap():
        return remote(
            pre.at[pl.ds(0, span)], pre.at[pl.ds(span, span)], core_send.at[pre_slot], core_recv.at[pre_slot],
            ctx=1 - core,
        )

    def kv_swap():
        return remote(
            kv_grad.at[pl.ds(0, span)], kv_grad_other, core_send.at[kv_slot], core_recv.at[kv_slot], ctx=1 - core
        )

    gain_line[...] = jnp.zeros_like(gain_line)
    gain_line[1:2, :] = gain_two_grad[0:1, :]
    kv_grad[...] = jnp.zeros_like(kv_grad)
    seg_col[...] = jnp.broadcast_to(seg_row[...], (8, 2 * span)).T[:, 0:1]
    for made in [*mixed_loads, *attend_loads]:
        made.wait()
    kv_turned[...] = kv[...].T
    grad_mixed[...] = turned_dot(attended[...], out_weight[...]).astype(jnp.bfloat16)
    for made in line_loads:
        made.wait()
    meet()
    for made in attended_swaps():
        made.start()

    def rows_at(start):
        return pl.ds(pl.multiple_of(start, BACK_CHUNK), BACK_CHUNK)

    def plain(stream, i):
        return (stream * count + i) * BACK_CHUNK

    def finish_out(stream, i, total):
        return middle[kept_rows(i, BACK_CHUNK)] + total

    def finish_in(stream, i, total):
        hidden = inputs[kept_rows(i, BACK_CHUNK)].astype(jnp.float32)
        inverse = inverse_rms(hidden)
        unit = hidden * inverse
        gain_line[0:1, :] += jnp.sum(total * unit, axis=0, keepdims=True)
        scaled = total * gain_one[...]
        return grad_middle[kept_rows(i, BACK_CHUNK)] + inverse * (
            scaled - unit * jnp.mean(scaled * unit, axis=-1, keepdims=True)
        )

    out_line = Line(
        n, lambda s, i: layer_out[rows_at(plain(s, i))].astype(jnp.float32), finish_out, plain, layer_out, *line_out,
        base=count - part, hop=BACK_HOP,
    )
    in_line = Line(
        n, lambda s, i: grad_inputs[rows_at(plain(s, i))].astype(jnp.float32), finish_in, plain, grad_inputs, *line_in,
        hop=BACK_HOP,
    )

    def attend_back(side, at, index):
        keys = side * span + (at + 1) * half
        rows = slice(at * half, (at + 1) * half)
        lanes = pl.ds(pl.multiple_of(index * 128, 128), 128)

        @pl.when(index == 0)
        def _():
            fill_bias(bias, seg_col, seg_row, side * span + at * half, keys, half)

        both_query, both_grad = query[rows, lanes], grad_mixed[rows, lanes]
        shared = (both_grad.astype(jnp.float32) * mixed[rows, lanes].astype(jnp.float32)).T
        outs, parts = [], None
        for which in (0, 1):
            head = slice(which * HEAD_DIM, (which + 1) * HEAD_DIM)
            query_head, grad_head = both_query[:, head], both_grad[:, head]
            scores = turned_dot(kv[0:keys, 0:HEAD_DIM], query_head) + bias[0:keys, :]
            probs = jnp.exp(scores - logs[pl.ds(2 * index + which, 1), rows])
            grad_probs = turned_dot(kv[0:keys, HEAD_DIM : 2 * HEAD_DIM], grad_head)
            row_dot = jnp.sum(shared[head], axis=0, keepdims=True)
            grad_scores = (probs * (grad_probs - row_dot)).astype(jnp.bfloat16)
            grad_key = jnp.dot(grad_scores, query_head, preferred_element_type=jnp.float32)
            grad_value = jnp.dot(probs.astype(jnp.bfloat16), grad_head, preferred_element_type=jnp.float32)
            part = jnp.concatenate([grad_key, grad_value], axis=1)
            parts = part if parts is None else parts + part
            outs.append(
                jnp.dot(kv_turned[0:HEAD_DIM, 0:keys], grad_scores, preferred_element_type=jnp.float32)
            )
        kv_grad[0:keys] += parts
        grad_query = jnp.concatenate(outs, axis=0).T * (HEAD_DIM ** -0.5)
        pre[rows, lanes] = rotate_lanes(grad_query, cosine[rows], signed_sine[rows], back=True).astype(jnp.bfloat16)

    pairs = heads // 128
    tasks = 2 * pairs

    def attend_task(task):
        for side in (0, 1):
            for at in (0, 1):

                @pl.when((core == side) & (task // pairs == at))
                def _():
                    attend_back(side, at, lax.rem(task, pairs))

    own_grad = pl.ds(pl.multiple_of(core * span, span), span)

    def finish_pre():
        @pl.when(core == 0)
        def _():
            kv_swap().wait_recv()
            kv_grad[0:span] += kv_grad_other[...]

        raw = kv_grad[own_grad]
        turned_back = rotate_lanes(raw, cosine[...], signed_sine[...], back=True)
        pre[0:span, heads : heads + 128] = key_lanes(raw, turned_back).astype(jnp.bfloat16)

    def in_products():
        def tile(t, carry):
            columns = pl.ds(pl.multiple_of(t * 512, 512), 512)
            for low in (0, half):
                rows = slice(low, low + half)
                grad_inputs[rows, columns] = (
                    turned_dot(pre[rows, 0:heads], query_weight[columns, :])
                    + jnp.dot(
                        pre[rows, heads : heads + 128], kv_weight[:, columns], preferred_element_type=jnp.float32
                    )
                ).astype(jnp.bfloat16)
            return carry

        lax.fori_loop(0, width // 512, tile, 0)

    def peer_of(r):
        return lax.rem(row + 1 + r, dp_size)

    def turn(r, cols):
        block = pl.multiple_of(peer_of(r) * piece, piece)
        turned[...] = cols[:, pl.ds(block, piece)].T

    def turn_attended(r):
        peer = peer_of(r)
        columns = pl.ds(pl.multiple_of((2 * peer + core) * piece, piece), piece)
        turned[:, 0:span] = attended[:, columns].T
        turned[:, span : 2 * span] = attended_other[:, pl.ds(pl.multiple_of(peer * piece, piece), piece)].T

    def tiles_of(stacked):
        wide = stacked.shape[1]
        return [(low, min(low + 384, wide)) for low in range(0, wide, 384)]

    def piece_value(stacked, low, high):
        return jnp.dot(turned[...], stacked[:, low:high], preferred_element_type=jnp.float32)

    others = dp_size - 1

    def ring_copy(at):
        r = others - 1 if at == 0 else at - 1
        land = land_up.at[0] if at == 0 else land_down.at[at - 1]
        return remote(ring.at[at], land, ring_send.at[at], ring_recv.at[at], dp=peer_of(r))

    def ring_piece(at, cols, stacked):
        turn(others - 1 if at == 0 else at - 1, cols)
        for low, high in tiles_of(stacked):
            ring[at, :, low:high] = piece_value(stacked, low, high).astype(jnp.bfloat16)
        ring_copy(at).start()

    def kept_piece(cols, stacked, own):
        turn(others, cols)
        for low, high in tiles_of(stacked):
            own[:, low:high] = piece_value(stacked, low, high)

    sends, lands = (send_qkv, send_out), (land_qkv, land_out)

    def plane_copy(w, r):
        return remote(sends[w].at[r], lands[w].at[r], plane_send.at[w, r], plane_recv.at[w, r], dp=peer_of(r))

    def plane_piece(w, r, stacked, own):
        @pl.when(r < dp_size - 1)
        def _():
            for low, high in tiles_of(stacked):
                sends[w][r, :, low:high] = piece_value(stacked, low, high).astype(jnp.bfloat16)
            plane_copy(w, r).start()

        @pl.when(r == dp_size - 1)
        def _():
            for low, high in tiles_of(stacked):
                own[:, low:high] = piece_value(stacked, low, high)

    def line_copies(owner, hops):
        slot = 0 if owner == 0 else 1
        return [
            remote(
                gain_line, gain_land.at[slot], line_send.at[slot, hop - 1], line_recv.at[slot],
                tensor=owner + hop if owner == 0 else owner - hop,
            )
            for hop in hops
        ]

    shard = width // (2 * dp_size)
    shards = 2 * dp_size
    place = 2 * row + core

    def spread(r):
        peer = lax.rem(place + 1 + r, shards)
        block = pl.multiple_of(peer * shard, shard)
        return remote(
            gain_sum.at[:, pl.ds(block, shard)], gain_plane.at[r], spread_send.at[r], spread_recv.at[r],
            dp=peer // 2, ctx=lax.rem(peer, 2),
        )

    def gather_gains():
        gain_sum[...] = jnp.zeros_like(gain_sum)
        for owner in (0, last):
            slot = 0 if owner == 0 else 1

            @pl.when(here == owner)
            def _():
                gain_sum[...] += gain_line[...]

            @pl.when(here != owner)
            def _():
                line_copies(owner, (1,))[0].wait_recv()
                gain_sum[...] += gain_land[slot]
        for r in range(shards - 1):
            spread(r).start()

    attend_steps = tasks // TASKS
    lag = attend_steps + 2
    ring_steps = RINGS + [lag + at for at in range(dp_size - 3)]
    out_base = lag + 1
    steps = max(lag + count + 2 * BACK_HOP * last, out_base + 2 * dp_size)

    def step(k, carry):
        out_line.step(k, count - part, part)
        in_line.step(k - lag)

        @pl.when((k >= 1) & (k <= attend_steps))
        def _():
            def task(more, carry):
                attend_task(TASKS * (k - 1) + more)
                return carry

            lax.fori_loop(0, TASKS, task, 0)

        @pl.when((k == attend_steps) & (core == 1))
        def _():
            kv_swap().start()

        @pl.when(k == 1)
        def _():
            for made in up_loads:
                made.wait()

        @pl.when(k == ring_steps[1])
        def _():
            for made in inner_loads:
                made.wait()

        @pl.when(k == attend_steps)
        def _():
            for made in [*late_loads, *attended_swaps()]:
                made.wait()

        @pl.when(k == attend_steps + 1)
        def _():
            finish_pre()
            in_products()
            pre_swap().start()

        for at in range(dp_size):

            @pl.when(k == ring_steps[at])
            def _():
                ring_piece(at, *((two_cols, up) if at == 0 else (upstream_cols, inner)))

        @pl.when(k == lag + dp_size)
        def _():
            kept_piece(two_cols, up, grad_up)

        @pl.when(k == lag + dp_size + 1)
        def _():
            kept_piece(upstream_cols, inner, own_down)

        @pl.when(k == out_base)
        def _():
            pre_swap().wait()

        at, kind = (k - out_base) // 2, lax.rem(k - out_base, 2)

        @pl.when((k >= out_base) & (at < dp_size) & (kind == 0))
        def _():
            turn_attended(at)
            plane_piece(1, at, mixed, own_out)

        @pl.when((k >= out_base) & (at < dp_size) & (kind == 1))
        def _():
            turn(at, normed_cols)
            plane_piece(0, at, pre, grad_qkv)

        @pl.when(k == lag + count + BACK_HOP * last - 1)
        def _():
            for owner in (0, last):

                @pl.when(here == owner)
                def _():
                    for made in line_copies(owner, range(1, n)):
                        made.start()

        @pl.when(k == min(lag + count + BACK_HOP * last + 3, steps - 1))
        def _():
            gather_gains()

        return carry

    lax.fori_loop(0, steps, step, 0)
    out_line.drain()
    in_line.drain()

    @pl.when(core == 1)
    def _():
        kv_swap().wait_send()

    for at in range(dp_size):
        ring_copy(at).wait()
    for r in range(others):
        for w in (0, 1):
            plane_copy(w, r).wait()
    grad_gains[...] = gain_sum[:, pl.ds(pl.multiple_of(place * shard, shard), shard)]
    for r in range(shards - 1):
        spread(r).wait()
        grad_gains[...] += gain_plane[r]
    for owner in (0, last):

        @pl.when(here == owner)
        def _():
            for made in line_copies(owner, range(1, n)):
                made.wait_send()


def back_call(line_size, dp_size, operands):
    query = operands[0]
    span, heads = query.shape
    width, hidden = operands[7].shape[1], operands[11].shape[1]
    piece = width // (2 * dp_size)
    wide = heads + 128
    low, full = jnp.bfloat16, jnp.float32
    vmem, outside = pl.BlockSpec(memory_space=pltpu.VMEM), pl.BlockSpec(memory_space=pl.ANY)
    dma = pltpu.SemaphoreType.DMA
    others = dp_size - 1
    outs = [
        ((span, width), low), ((span, width), low), ((8, piece), full), ((piece, wide), full), ((piece, heads), full),
        ((piece, hidden), full), ((piece, hidden), full),
        ((1, piece, hidden), low), ((others, piece, hidden), low), ((others, piece, wide), low), ((others, piece, heads), low),
    ]
    core_copies = dp_size + 2
    scratch = [
        pltpu.VMEM((span, heads), low), pltpu.VMEM((2 * span, 128), low), pltpu.VMEM((128, 2 * span), low),
        pltpu.VMEM((span, heads), low), pltpu.VMEM((2 * span, heads), low), pltpu.VMEM((span, width), low),
        *[pltpu.VMEM((2 * span, width // 2), low)] * 3, pltpu.VMEM((span, width // 2), low),
        *[pltpu.VMEM((2 * span, hidden), low)] * 2, pltpu.VMEM((2 * span, wide), low),
        pltpu.VMEM((width, heads), low), pltpu.VMEM((128, width), low), pltpu.VMEM((heads, width), low),
        pltpu.VMEM((span // 2, width), full), pltpu.VMEM((span // 2, width), full), pltpu.VMEM((span // 2, width), low),
        pltpu.VMEM((dp_size, piece, hidden), low), pltpu.VMEM((others, piece, wide), low),
        pltpu.VMEM((others, piece, heads), low),
        pltpu.VMEM((piece, 2 * span), low), pltpu.VMEM((2 * span, 1), jnp.int32), pltpu.VMEM((2 * span, span // 2), full),
        pltpu.VMEM((2 * span, 128), full), pltpu.VMEM((span, 128), full),
        pltpu.VMEM((8, width), full), pltpu.VMEM((2, 8, width), full), pltpu.VMEM((8, width), full),
        pltpu.VMEM((2 * dp_size - 1, 8, piece), full),
        dma((17,)), dma((core_copies,)), dma((core_copies,)),
        dma((dp_size,)), dma((dp_size,)), dma((2, others)), dma((2, others)),
        dma((2, line_size - 1)), dma((2,)), dma((2 * dp_size - 1,)), dma((2 * dp_size - 1,)),
        *line_scratch(span, width, 2, BACK_CHUNK), *line_scratch(span, width, 1, BACK_CHUNK),
    ]
    spaces = [outside, outside, vmem, outside, vmem, vmem, vmem] + [outside] * 10 + [vmem, vmem] + [outside] * 4
    return pl.pallas_call(
        functools.partial(back_kernel, line_size, dp_size),
        out_shape=[jax.ShapeDtypeStruct(s, d) for s, d in outs],
        in_specs=spaces,
        out_specs=[vmem] * 7 + [outside] * 4,
        scratch_shapes=scratch,
        compiler_params=pltpu.CompilerParams(
            collective_id=2, has_side_effects=True, vmem_limit_bytes=BACK_MIB * MIB
        ),
    )(*operands)


def settle_kernel(
    layer_any, inputs_any, gains, qkv_any, out_any, gate_any, up_any, down_any,
    land_gate, land_up, land_up_last, land_down, land_qkv, land_out,
    layer_out, grad_inputs, gain_one, grad_query, grad_key, grad_value, grad_out, gain_two, grad_gate, grad_up, grad_down,
    own_qkv, own_out, own_gate, own_up, own_down, far_qkv, far_out, far_gate, far_up, far_down,
    turned_kv, turned_out, turned_down, layer_held, inputs_held, in_sems, out_sems,
):
    whole, early = [], land_up.shape[0]
    passed = [
        pltpu.make_async_copy(layer_any, layer_held, in_sems.at[0, 5]),
        pltpu.make_async_copy(inputs_any, inputs_held, in_sems.at[1, 5]),
        pltpu.make_async_copy(land_up_last, far_up.at[pl.ds(early, 1)], in_sems.at[0, 6]),
    ]
    owns = ((qkv_any, own_qkv), (out_any, own_out), (gate_any, own_gate), (up_any, own_up), (down_any, own_down))
    fars = (
        (land_qkv, far_qkv), (land_out, far_out), (land_gate, far_gate), (land_up, far_up.at[pl.ds(0, early)]),
        (land_down, far_down),
    )
    loads = [
        (
            pltpu.make_async_copy(*own, in_sems.at[0, at]),
            pltpu.make_async_copy(*far, in_sems.at[1, at]),
        )
        for at, (own, far) in enumerate(zip(owns, fars))
    ]
    for pair in loads:
        for made in pair:
            made.start()
    for made in passed:
        made.start()
    gain_one[...] = gains[0:1]
    gain_two[...] = gains[1:2]

    def settle(at, own, far):
        for made in loads[at]:
            made.wait()
        total = own[...]
        for r in range(far.shape[0]):
            total = total + far[r].astype(jnp.float32)
        return total

    def put(at, src, dst):
        made = pltpu.make_async_copy(src, dst, out_sems.at[at])
        made.start()
        whole.append(made)

    heads = grad_query.shape[1]
    own_qkv[...] = settle(0, own_qkv, far_qkv)
    put(2, own_qkv.at[:, pl.ds(0, heads)], grad_query)
    turned_kv[...] = own_qkv[:, heads:].T
    put(3, turned_kv.at[pl.ds(0, HEAD_DIM)], grad_key)
    put(4, turned_kv.at[pl.ds(HEAD_DIM, HEAD_DIM)], grad_value)
    turned_out[...] = settle(1, own_out, far_out).T
    put(5, turned_out, grad_out)
    passed[0].wait()
    put(0, layer_held, layer_out)
    own_gate[...] = settle(2, own_gate, far_gate)
    put(6, own_gate, grad_gate)
    passed[2].wait()
    own_up[...] = settle(3, own_up, far_up)
    put(7, own_up, grad_up)
    passed[1].wait()
    put(1, inputs_held, grad_inputs)
    turned_down[...] = settle(4, own_down, far_down).T
    put(8, turned_down, grad_down)
    for made in whole:
        made.wait()


def settle_call(operands):
    layer_out, _, gains, qkv, out, gate = operands[:6]
    piece, wide = qkv.shape
    heads, hidden = out.shape[1], gate.shape[1]
    others = operands[8].shape[0]
    low, full = jnp.bfloat16, jnp.float32
    vmem, outside = pl.BlockSpec(memory_space=pltpu.VMEM), pl.BlockSpec(memory_space=pl.ANY)
    outs = [
        (layer_out.shape, low), (layer_out.shape, low), ((1, piece), full), ((piece, heads), full),
        ((HEAD_DIM, piece), full), ((HEAD_DIM, piece), full), ((heads, piece), full), ((1, piece), full),
        ((piece, hidden), full), ((piece, hidden), full), ((hidden, piece), full),
    ]
    shapes = [(piece, wide), (piece, heads), *[(piece, hidden)] * 3]
    scratch = [
        *[pltpu.VMEM(shape, full) for shape in shapes], *[pltpu.VMEM((others, *shape), low) for shape in shapes],
        pltpu.VMEM((wide - heads, piece), full), pltpu.VMEM((heads, piece), full), pltpu.VMEM((hidden, piece), full),
        pltpu.VMEM(layer_out.shape, low), pltpu.VMEM(layer_out.shape, low),
        pltpu.SemaphoreType.DMA((2, 7)), pltpu.SemaphoreType.DMA((9,)),
    ]
    return pl.pallas_call(
        settle_kernel,
        out_shape=[jax.ShapeDtypeStruct(s, d) for s, d in outs],
        in_specs=[outside, outside, vmem] + [outside] * 11,
        out_specs=[outside, outside, vmem] + [outside] * 4 + [vmem] + [outside] * 3,
        scratch_shapes=scratch,
        compiler_params=pltpu.CompilerParams(vmem_limit_bytes=62 * MIB),
    )(*operands)


def plain_body(
    inputs,
    segment_ids,
    attention_gain,
    query_weight,
    key_weight,
    value_weight,
    out_weight,
    feedforward_gain,
    gate_weight,
    up_weight,
    down_weight,
    cotangent,
):
    seq_count, span_len, model_width = inputs.shape
    row_count = seq_count * span_len
    query_heads = query_weight.shape[1] // HEAD_DIM
    kv_heads = key_weight.shape[1] // HEAD_DIM
    group_size = query_heads // kv_heads
    score_scale = 1.0 / math.sqrt(HEAD_DIM)
    offset = lax.axis_index("ctx") * span_len
    whole_segments = lax.all_gather(segment_ids, "ctx", axis=1, tiled=True)
    own_positions = lax.dynamic_slice_in_dim(positions_of(whole_segments), offset, span_len, 1)
    cosine, sine_table = rotary_tables(own_positions)
    cosine = cosine[:, :, None, :]
    sine_table = sine_table[:, :, None, :]
    hidden = inputs.astype(jnp.float32).reshape(row_count, model_width)
    inverse_one = lax.rsqrt(jnp.mean(hidden * hidden, axis=-1, keepdims=True) + epsilon)
    unit_one = hidden * inverse_one
    normed = (unit_one * attention_gain).astype(jnp.bfloat16)
    query_rows = rotate(
        jnp.dot(normed, query_weight, preferred_element_type=jnp.float32).reshape(
            seq_count, span_len, query_heads, HEAD_DIM
        ),
        cosine,
        sine_table,
    ).astype(jnp.bfloat16)
    key_rows = rotate(
        jnp.dot(normed, key_weight, preferred_element_type=jnp.float32).reshape(
            seq_count, span_len, kv_heads, HEAD_DIM
        ),
        cosine,
        sine_table,
    ).astype(jnp.bfloat16)
    value_rows = (
        jnp.dot(normed, value_weight, preferred_element_type=jnp.float32)
        .astype(jnp.bfloat16)
        .reshape(seq_count, span_len, kv_heads, HEAD_DIM)
    )
    all_keys, all_values = (
        lax.all_gather(key_rows, "ctx", axis=1, tiled=True),
        lax.all_gather(value_rows, "ctx", axis=1, tiled=True),
    )

    def attend(block_items):
        query_block, key_block, value_block, query_seg, key_seg = block_items
        allowed = visible(query_seg, key_seg, offset)
        grouped = query_block.reshape(span_len, kv_heads, group_size, HEAD_DIM)
        raw_scores = jnp.einsum(
            "qhgd,khd->hgqk", grouped, key_block, preferred_element_type=jnp.float32
        )
        scores = jnp.where(allowed, raw_scores * score_scale, masked_score)
        row_peak = jnp.max(scores, axis=-1, keepdims=True)
        shifted_exp = jnp.exp(scores - row_peak)
        denominator = jnp.sum(shifted_exp, axis=-1, keepdims=True)
        attn_probs = (shifted_exp / denominator).astype(jnp.bfloat16)
        mixed_block = jnp.einsum(
            "hgqk,khd->qhgd", attn_probs, value_block, preferred_element_type=jnp.float32
        )
        return (
            mixed_block.astype(jnp.bfloat16).reshape(span_len, query_heads * HEAD_DIM),
            row_peak + jnp.log(denominator),
        )

    mixed_heads, log_sums = lax.map(
        attend, (query_rows, all_keys, all_values, segment_ids, whole_segments)
    )
    mixed_flat = mixed_heads.reshape(row_count, query_heads * HEAD_DIM)
    attended = lax.psum(
        jnp.dot(mixed_flat, out_weight, preferred_element_type=jnp.float32), "tensor"
    )
    middle = hidden + attended
    inverse_two = lax.rsqrt(jnp.mean(middle * middle, axis=-1, keepdims=True) + epsilon)
    unit_two = middle * inverse_two
    normed_two = (unit_two * feedforward_gain).astype(jnp.bfloat16)
    gate_pre = jnp.dot(normed_two, gate_weight, preferred_element_type=jnp.float32)
    up_pre = jnp.dot(normed_two, up_weight, preferred_element_type=jnp.float32)
    sigmoid_gate = jax.nn.sigmoid(gate_pre)
    inner_act = (gate_pre * sigmoid_gate * up_pre).astype(jnp.bfloat16)
    feed_out = lax.psum(
        jnp.dot(inner_act, down_weight, preferred_element_type=jnp.float32).astype(jnp.bfloat16),
        "tensor",
    ).astype(jnp.float32)
    layer_out = (middle + feed_out).astype(jnp.bfloat16).reshape(seq_count, span_len, model_width)
    upstream = cotangent.reshape(row_count, model_width)
    grad_down = jnp.dot(inner_act.T, upstream, preferred_element_type=jnp.float32)
    grad_inner = jnp.dot(upstream, down_weight.T, preferred_element_type=jnp.float32)
    grad_up_pre = (grad_inner * gate_pre * sigmoid_gate).astype(jnp.bfloat16)
    grad_gate_pre = (
        grad_inner * up_pre * sigmoid_gate * (1.0 + gate_pre * (1.0 - sigmoid_gate))
    ).astype(jnp.bfloat16)
    grad_gate = jnp.dot(normed_two.T, grad_gate_pre, preferred_element_type=jnp.float32)
    grad_up = jnp.dot(normed_two.T, grad_up_pre, preferred_element_type=jnp.float32)
    grad_normed_two = lax.psum(
        jnp.dot(grad_gate_pre, gate_weight.T, preferred_element_type=jnp.float32)
        + jnp.dot(grad_up_pre, up_weight.T, preferred_element_type=jnp.float32),
        "tensor",
    )
    grad_ffn_gain = jnp.sum(grad_normed_two * unit_two, axis=0)
    scaled_two = grad_normed_two * feedforward_gain
    grad_middle = upstream.astype(jnp.float32) + inverse_two * (
        scaled_two - unit_two * jnp.mean(scaled_two * unit_two, axis=-1, keepdims=True)
    )
    grad_attended = grad_middle.astype(jnp.bfloat16)
    grad_out_part = jnp.dot(mixed_flat.T, grad_attended, preferred_element_type=jnp.float32)
    grad_mixed = (
        jnp.dot(grad_attended, out_weight.T, preferred_element_type=jnp.float32)
        .astype(jnp.bfloat16)
        .reshape(seq_count, span_len, query_heads, HEAD_DIM)
    )

    def attend_back(block_items):
        query_block, key_block, value_block, query_seg, key_seg, grad_block, log_block = block_items
        allowed = visible(query_seg, key_seg, offset)
        grouped = query_block.reshape(span_len, kv_heads, group_size, HEAD_DIM)
        grad_grouped = grad_block.reshape(span_len, kv_heads, group_size, HEAD_DIM)
        raw_scores = jnp.einsum(
            "qhgd,khd->hgqk", grouped, key_block, preferred_element_type=jnp.float32
        )
        scores = jnp.where(allowed, raw_scores * score_scale, masked_score)
        attn_probs = jnp.exp(scores - log_block)
        rounded = attn_probs.astype(jnp.bfloat16)
        grad_values = jnp.einsum(
            "hgqk,qhgd->khd", rounded, grad_grouped, preferred_element_type=jnp.float32
        )
        grad_probs = jnp.einsum(
            "qhgd,khd->hgqk", grad_grouped, value_block, preferred_element_type=jnp.float32
        )
        row_dot = jnp.sum(attn_probs * grad_probs, axis=-1, keepdims=True)
        grad_scores = (attn_probs * (grad_probs - row_dot) * score_scale).astype(jnp.bfloat16)
        grad_queries = jnp.einsum(
            "hgqk,khd->qhgd", grad_scores, key_block, preferred_element_type=jnp.float32
        ).reshape(span_len, query_heads, HEAD_DIM)
        grad_keys = jnp.einsum(
            "hgqk,qhgd->khd", grad_scores, grouped, preferred_element_type=jnp.float32
        )
        return (grad_queries, grad_keys, grad_values)

    grad_queries, grad_keys, grad_values = lax.map(
        attend_back,
        (query_rows, all_keys, all_values, segment_ids, whole_segments, grad_mixed, log_sums),
    )
    own_grad_keys, own_grad_values = (
        lax.psum_scatter(grad_keys, "ctx", scatter_dimension=1, tiled=True),
        lax.psum_scatter(grad_values, "ctx", scatter_dimension=1, tiled=True),
    )
    grad_query_pre = (
        rotate(grad_queries, cosine, -sine_table)
        .astype(jnp.bfloat16)
        .reshape(row_count, query_heads * HEAD_DIM)
    )
    grad_key_pre = (
        rotate(own_grad_keys, cosine, -sine_table)
        .astype(jnp.bfloat16)
        .reshape(row_count, kv_heads * HEAD_DIM)
    )
    grad_value_pre = own_grad_values.astype(jnp.bfloat16).reshape(row_count, kv_heads * HEAD_DIM)
    grad_query = jnp.dot(normed.T, grad_query_pre, preferred_element_type=jnp.float32)
    grad_key = jnp.dot(normed.T, grad_key_pre, preferred_element_type=jnp.float32)
    grad_value = jnp.dot(normed.T, grad_value_pre, preferred_element_type=jnp.float32)
    grad_normed = lax.psum(
        (
            jnp.dot(grad_query_pre, query_weight.T, preferred_element_type=jnp.float32)
            + jnp.dot(grad_key_pre, key_weight.T, preferred_element_type=jnp.float32)
            + jnp.dot(grad_value_pre, value_weight.T, preferred_element_type=jnp.float32)
        ).astype(jnp.bfloat16),
        "tensor",
    ).astype(jnp.float32)
    grad_attn_gain = jnp.sum(grad_normed * unit_one, axis=0)
    scaled_one = grad_normed * attention_gain
    grad_hidden = grad_middle + inverse_one * (
        scaled_one - unit_one * jnp.mean(scaled_one * unit_one, axis=-1, keepdims=True)
    )
    grad_inputs = grad_hidden.astype(jnp.bfloat16).reshape(seq_count, span_len, model_width)
    reduced = (
        lax.psum_scatter(
            grad_attn_gain.astype(jnp.bfloat16), ("dp", "ctx"), scatter_dimension=0, tiled=True
        ).astype(jnp.float32),
        lax.psum_scatter(
            grad_query.astype(jnp.bfloat16), ("dp", "ctx"), scatter_dimension=0, tiled=True
        ).astype(jnp.float32),
        lax.psum_scatter(
            grad_key.astype(jnp.bfloat16), ("dp", "ctx"), scatter_dimension=0, tiled=True
        ).astype(jnp.float32),
        lax.psum_scatter(
            grad_value.astype(jnp.bfloat16), ("dp", "ctx"), scatter_dimension=0, tiled=True
        ).astype(jnp.float32),
        lax.psum_scatter(
            grad_out_part.astype(jnp.bfloat16), ("dp", "ctx"), scatter_dimension=1, tiled=True
        ).astype(jnp.float32),
        lax.psum_scatter(
            grad_ffn_gain.astype(jnp.bfloat16), ("dp", "ctx"), scatter_dimension=0, tiled=True
        ).astype(jnp.float32),
        lax.psum_scatter(
            grad_gate.astype(jnp.bfloat16), ("dp", "ctx"), scatter_dimension=0, tiled=True
        ).astype(jnp.float32),
        lax.psum_scatter(
            grad_up.astype(jnp.bfloat16), ("dp", "ctx"), scatter_dimension=0, tiled=True
        ).astype(jnp.float32),
        lax.psum_scatter(
            grad_down.astype(jnp.bfloat16), ("dp", "ctx"), scatter_dimension=1, tiled=True
        ).astype(jnp.float32),
    )
    return (
        layer_out,
        grad_inputs,
        reduced[0],
        reduced[1],
        reduced[2],
        reduced[3],
        reduced[4],
        reduced[5],
        reduced[6],
        reduced[7],
        reduced[8],
    )


def fast_body(
    inputs, segment_ids, attention_gain, query_weight, key_weight, value_weight, out_weight, feedforward_gain,
    gate_weight, up_weight, down_weight, cotangent,
):
    _, span_len, model_width = inputs.shape
    line_size, dp_size = lax.axis_size("tensor"), lax.axis_size("dp")
    half_dim = HEAD_DIM // 2
    frequency = rope_base ** (-2.0 * jnp.arange(half_dim, dtype=jnp.float32) / HEAD_DIM)
    frequency = jnp.tile(frequency, 4).reshape(1, 128)
    flat_inputs = inputs.reshape(span_len, model_width)
    upstream = cotangent.reshape(span_len, model_width)
    gain_one, gain_two = attention_gain.reshape(1, -1), feedforward_gain.reshape(1, -1)
    key_turned, value_turned = key_weight.T, value_weight.T
    (
        seg_row, cosine, signed_sine, query, kv, logs, mixed, normed, two, upstream_cols, up, inner, second, attended,
        middle, grad_middle, land_gate, land_up, own_gate, gain_grad,
    ) = front_call(
        line_size, dp_size,
        (
            flat_inputs, segment_ids, frequency, gain_one, gain_two, query_weight, key_turned, value_turned, out_weight,
            gate_weight, up_weight, down_weight, upstream,
        ),
    )
    (
        layer_out, grad_inputs, gains, own_qkv, own_out, own_up, own_down, land_up_last, land_down, land_qkv,
        land_out,
    ) = back_call(
        line_size, dp_size,
        (
            query, kv, logs, mixed, cosine, signed_sine, seg_row, flat_inputs, normed, two, upstream_cols,
            up, inner, second, attended, middle, grad_middle, gain_one, gain_grad,
            query_weight, key_turned, value_turned, out_weight,
        ),
    )
    layer_out, grad_inputs, gain_a, grad_query, grad_key, grad_value, grad_out, gain_b, *ffn = settle_call(
        (
            layer_out, grad_inputs, gains, own_qkv, own_out, own_gate, own_up, own_down,
            land_gate, land_up, land_up_last, land_down, land_qkv, land_out,
        )
    )
    shape = (1, span_len, model_width)
    return (
        layer_out.reshape(shape), grad_inputs.reshape(shape), gain_a[0], grad_query, grad_key.T, grad_value.T,
        grad_out, gain_b[0], *ffn,
    )


def body(mesh, *arrays):
    inputs = arrays[0]
    span_len, model_width = inputs.shape[1:]
    dp_size, ctx_size, line_size = mesh.shape["dp"], mesh.shape["ctx"], mesh.shape["tensor"]
    piece = model_width // (dp_size * ctx_size)
    fits = inputs.shape[0] == 1 and ctx_size == 2 and dp_size > 2 and line_size > 1
    if fits and piece % 128 == 0 and span_len % 512 == 0:
        return fast_body(*arrays)
    return plain_body(*arrays)


def solution(mesh):
    return jax.shard_map(
        functools.partial(body, mesh),
        mesh=mesh,
        in_specs=(
            P("dp", "ctx", None),
            P("dp", "ctx"),
            P(),
            P(None, "tensor"),
            P(None, "tensor"),
            P(None, "tensor"),
            P("tensor", None),
            P(),
            P(None, "tensor"),
            P(None, "tensor"),
            P("tensor", None),
            P("dp", "ctx", None),
        ),
        out_specs=(
            P("dp", "ctx", None),
            P("dp", "ctx", None),
            P(("dp", "ctx")),
            P(("dp", "ctx"), "tensor"),
            P(("dp", "ctx"), "tensor"),
            P(("dp", "ctx"), "tensor"),
            P("tensor", ("dp", "ctx")),
            P(("dp", "ctx")),
            P(("dp", "ctx"), "tensor"),
            P(("dp", "ctx"), "tensor"),
            P("tensor", ("dp", "ctx")),
        ),
        check_vma=False,
    )
```

```python
import functools
import math

import jax
import jax.numpy as jnp
from jax import lax
from jax.experimental import pallas as pl
from jax.experimental.pallas import tpu as pltpu
from jax.sharding import PartitionSpec as P

HEAD_DIM = 64


epsilon = 1e-05
rope_base = 10000.0
masked_score = -1e30


def positions_of(segment):
    token_index = jnp.arange(segment.shape[-1], dtype=jnp.int32)
    previous = jnp.concatenate([segment[..., :1] - 1, segment[..., :-1]], axis=-1)
    starts = jnp.where(segment != previous, token_index, 0)
    earlier = token_index[None, :] <= token_index[:, None]
    run_start = jnp.max(jnp.where(earlier, starts[..., None, :], 0), axis=-1)
    return token_index - run_start


MESH = pl.DeviceIdType.MESH
CHUNK, HOP = 16, 2
BACK_CHUNK, BACK_HOP = 32, 2
TASKS = 1
RINGS = [1, 2, 4]
MIB = 1 << 20
FRONT_MIB, BACK_MIB = 62, 62


def rotary_tables(positions):
    half_dim = HEAD_DIM // 2
    frequency = rope_base ** (-2.0 * jnp.arange(half_dim, dtype=jnp.float32) / HEAD_DIM)
    angles = positions.astype(jnp.float32)[..., None] * frequency
    return (jnp.cos(angles), jnp.sin(angles))


def rotate(values, cosine, sine_table):
    half_dim = values.shape[-1] // 2
    first = values[..., :half_dim]
    second = values[..., half_dim:]
    return jnp.concatenate(
        [first * cosine - second * sine_table, second * cosine + first * sine_table], axis=-1
    )


def visible(query_seg, key_seg, first_row):
    query_pos = first_row + jnp.arange(query_seg.shape[0], dtype=jnp.int32)
    key_pos = jnp.arange(key_seg.shape[0], dtype=jnp.int32)
    same_doc = query_seg[:, None] == key_seg[None, :]
    causal = key_pos[None, :] <= query_pos[:, None]
    usable = (key_seg[None, :] >= 0) | (key_pos[None, :] == query_pos[:, None])
    return same_doc & causal & usable


def turned_dot(left, right):
    return lax.dot_general(
        left, right, (((1,), (1,)), ((), ())), preferred_element_type=jnp.float32
    )


def remote(src, dst, send, recv, **device):
    return pltpu.make_async_remote_copy(
        src_ref=src, dst_ref=dst, send_sem=send, recv_sem=recv, device_id=device, device_id_type=MESH
    )


class Line:
    def __init__(self, line_size, own, finish, place, out_ref, held, acc_send, acc_recv, back_send, back_recv, base=0, hop=HOP):
        self.base, self.hop = base, hop
        self.last = line_size - 1
        self.here = lax.axis_index("tensor")
        self.own, self.finish, self.place = own, finish, place
        self.out_ref, self.held = out_ref, held
        self.acc_sems, self.back_sems = (acc_send, acc_recv), (back_send, back_recv)
        self.count, self.chunk = held.shape[1:3]

    def parts(self, stream):
        if stream == 0:
            return self.here, self.here + 1, self.here - 1
        return self.last - self.here, self.here - 1, self.here + 1

    def acc_copy(self, stream, i, target):
        at = i - self.base
        ref = self.held.at[stream, at]
        return remote(ref, ref, self.acc_sems[0].at[stream, at], self.acc_sems[1].at[stream, at], tensor=target)

    def rows_of(self, stream, i):
        return pl.ds(pl.multiple_of(self.place(stream, i), self.chunk), self.chunk)

    def back_copy(self, stream, i, target):
        at = i - self.base
        ref = self.out_ref.at[self.rows_of(stream, i)]
        return remote(ref, ref, self.back_sems[0].at[stream, at], self.back_sems[1].at[stream, at], tensor=target)

    def step(self, k, begin=0, size=None):
        size = self.count if size is None else size

        @pl.when((k >= 0) & (k < size + 2 * self.hop * self.last))
        def _():
            for stream in (0, 1):
                self.stream_step(k, stream, begin, size)

    def stream_step(self, k, stream, begin, size):
        last, held = self.last, self.held
        place, after, before = self.parts(stream)
        due = k - self.hop * place
        i = begin + due
        at = i - self.base

        @pl.when((due >= 0) & (due < size))
        def _():
            @pl.when(place == 0)
            def _():
                held[stream, at] = self.own(stream, i).astype(jnp.bfloat16)
                self.acc_copy(stream, i, after).start()

            @pl.when(place > 0)
            def _():
                self.acc_copy(stream, i, after).wait_recv()

                @pl.when(place < last)
                def _():
                    held[stream, at] = (held[stream, at].astype(jnp.float32) + self.own(stream, i)).astype(jnp.bfloat16)
                    self.acc_copy(stream, i, after).start()

                @pl.when(place == last)
                def _():
                    total = held[stream, at].astype(jnp.float32) + self.own(stream, i)
                    self.out_ref[self.rows_of(stream, i)] = self.finish(stream, i, total).astype(jnp.bfloat16)
                    self.back_copy(stream, i, before).start()

        back = k - self.hop * (2 * last - place)
        j = begin + back

        @pl.when((back >= 0) & (back < size) & (place < last))
        def _():
            self.back_copy(stream, j, before).wait_recv()

            @pl.when(place > 0)
            def _():
                self.back_copy(stream, j, before).start()

    def drain(self):
        def sent(at, carry):
            i = at + self.base
            for stream in (0, 1):
                place, after, before = self.parts(stream)

                @pl.when(place < self.last)
                def _():
                    self.acc_copy(stream, i, after).wait_send()

                @pl.when(place > 0)
                def _():
                    self.back_copy(stream, i, before).wait_send()

            return carry

        lax.fori_loop(0, self.count, sent, 0)


def line_scratch(rows, width, share=1, chunk=CHUNK):
    count = rows // 2 // chunk // share
    return [
        pltpu.VMEM((2, count, chunk, width), jnp.bfloat16),
        *[pltpu.SemaphoreType.DMA((2, count))] * 4,
    ]


def greet(line, core, plane, full_line=False):
    here, row, side = lax.axis_index("tensor"), lax.axis_index("dp"), lax.axis_index("ctx")
    barrier = pltpu.get_barrier_semaphore()
    peers = 0

    def call(**device):
        pl.semaphore_signal(barrier, inc=1, device_id=device, device_id_type=MESH)

    if full_line:
        for hop in range(1, line):
            call(tensor=lax.rem(here + hop, line))
        peers += line - 1
    else:

        @pl.when(here > 0)
        def _():
            call(tensor=here - 1)

        @pl.when(here < line - 1)
        def _():
            call(tensor=here + 1)

        peers = jnp.where(here > 0, 1, 0) + jnp.where(here < line - 1, 1, 0)
    if plane:
        for hop in range(1, 2 * plane):
            peer = lax.rem(2 * row + side + hop, 2 * plane)
            call(dp=peer // 2, ctx=lax.rem(peer, 2))
        peers += 2 * plane - 1
    elif core:
        call(ctx=1 - side)
        peers += 1
    return lambda: pl.semaphore_wait(barrier, peers)


def kept_rows(i, chunk=CHUNK):
    return pl.ds(pl.multiple_of(i * chunk, chunk), chunk)


def rotate_lanes(values, cosine, signed_sine, back=False):
    lane = lax.broadcasted_iota(jnp.int32, values.shape, 1)
    swapped = jnp.where(
        lax.rem(lane, HEAD_DIM) < HEAD_DIM // 2,
        pltpu.roll(values, 128 - HEAD_DIM // 2, 1),
        pltpu.roll(values, HEAD_DIM // 2, 1),
    )
    turn = swapped * signed_sine
    return values * cosine - turn if back else values * cosine + turn


def key_lanes(values, turned):
    lane = lax.broadcasted_iota(jnp.int32, values.shape, 1)
    return jnp.where(lane < HEAD_DIM, turned, values)


def fill_bias(bias, seg_col, seg_row, first, keys, block):
    key_seg = seg_col[0:keys]
    query_seg = seg_row[:, first : first + block]
    key_pos = lax.broadcasted_iota(jnp.int32, (keys, block), 0)
    query_pos = first + lax.broadcasted_iota(jnp.int32, (keys, block), 1)
    usable = (key_seg >= 0) | (key_pos == query_pos)
    allowed = (key_seg == query_seg) & (key_pos <= query_pos) & usable
    bias[0:keys, :] = jnp.where(allowed, 0.0, masked_score)


def wide_tiles(width):
    return width // 256, width % 256


def inverse_rms(values):
    return lax.rsqrt(jnp.mean(values * values, axis=-1, keepdims=True) + epsilon)


def front_kernel(
    n, dp_size,
    inputs_any, segments, frequency, gain_one, gain_two,
    query_weight_any, key_weight_any, value_weight_any, out_weight_any, gate_weight_any, up_weight_any, down_weight_any, upstream_any,
    seg_out, cosine_out, sine_out, query_out, kv_out, log_out, mixed_out, normed_cols, two_cols, upstream_cols, up_out, inner_out, second_out,
    attended_out, middle_out, grad_middle_out, land_gate, land_up, own_gate, gain_out,
    seg_all, seg_row, seg_col, cosine, signed_sine,
    inputs, normed, kv_weight, query, kv, kv_turned, logs, mixed, bias,
    gate_weight, up_weight, down_weight, upstream, grad_inner, normed_two, gate, up, inner,
    partial, middle, grad_middle, two_other, turned, send_gate, send_up,
    load_sems, store_sems, core_send, core_recv, plane_send, plane_recv, *line_refs,
):
    span, width = inputs.shape
    hidden, piece = gate.shape[1], turned.shape[0]
    row, core = lax.axis_index("dp"), lax.axis_index("ctx")
    half, block = span // 2, span // 4
    second, attended = normed, inputs
    line_one, line_two, line_three = line_refs[:5], line_refs[5:10], line_refs[10:]
    count, heads = line_one[0].shape[1], query.shape[1]
    part = count // 2

    def load(at, src, dst):
        made = pltpu.make_async_copy(src, dst, load_sems.at[at])
        made.start()
        return made

    def ordered(stream, i):
        return (i // part) * half + stream * block + lax.rem(i, part) * CHUNK

    def moved(at):
        return (0, 2, 1, 3)[at] * block

    load_inputs = load(0, inputs_any, inputs)
    query_weight = gate_weight.at[:, pl.ds(0, heads)]
    out_weight = down_weight.at[pl.ds(0, heads)]
    load_query = load(1, query_weight_any, query_weight)
    load_kv = [
        load(2, key_weight_any, kv_weight.at[pl.ds(0, HEAD_DIM)]),
        load(11, value_weight_any, kv_weight.at[pl.ds(HEAD_DIM, HEAD_DIM)]),
    ]
    load_out = load(3, out_weight_any, out_weight)
    load_up = [
        load(4 + b, upstream_any.at[pl.ds(b * block, block)], upstream.at[pl.ds(moved(b), block)]) for b in range(4)
    ]
    load_up_weight = load(10, up_weight_any, up_weight)
    seg_all[core] = jnp.broadcast_to(segments[...], seg_all.shape[1:])
    meet = greet(n, True, dp_size)

    def seg_copy():
        return remote(seg_all.at[core], seg_all.at[core], core_send.at[1], core_recv.at[1], ctx=1 - core)

    load_inputs.wait()

    def norm_rows(b, carry):
        rows = pl.ds(pl.multiple_of(b * 64, 64), 64)
        value = inputs[rows].astype(jnp.float32)
        normed[rows] = (value * inverse_rms(value) * gain_one[...]).astype(jnp.bfloat16)
        return carry

    lax.fori_loop(0, span // 64, norm_rows, 0)
    meet()
    seg_copy().start()
    for made in load_kv:
        made.wait()
    raw_kv = turned_dot(normed[...], kv_weight[...])
    load_query.wait()
    for low in range(0, span, half):
        rows = slice(low, low + half)
        partial[rows, 0:heads] = jnp.dot(normed[rows], query_weight[...], preferred_element_type=jnp.float32)
    load_gate = load(9, gate_weight_any, gate_weight)
    seg_copy().wait()
    for side in (0, 1):
        seg_row[:, side * span : (side + 1) * span] = seg_all[side, 0:1]
        seg_col[side * span : (side + 1) * span] = seg_all[side].T[:, 0:1]
    own_seg = seg_all[core, 0:1]
    key_pos = lax.broadcasted_iota(jnp.int32, (2 * span, span), 0)
    query_pos = core * span + lax.broadcasted_iota(jnp.int32, (2 * span, span), 1)
    before = (seg_col[...] == own_seg) & (key_pos < query_pos)
    position = jnp.sum(jnp.where(before, 1.0, 0.0), axis=0, keepdims=True)
    angles = jnp.broadcast_to(position, (8, span)).T[:, 0:1] * frequency[...]
    lane = lax.broadcasted_iota(jnp.int32, angles.shape, 1)
    cosine[...] = jnp.cos(angles)
    sine = jnp.sin(angles)
    signed_sine[...] = jnp.where(lax.rem(lane, HEAD_DIM) < HEAD_DIM // 2, -sine, sine)
    own_rows = pl.ds(pl.multiple_of(core * span, span), span)
    kv[own_rows] = key_lanes(raw_kv, rotate_lanes(raw_kv, cosine[...], signed_sine[...])).astype(jnp.bfloat16)

    def kv_copy():
        return remote(kv.at[own_rows], kv.at[own_rows], core_send.at[0], core_recv.at[0], ctx=1 - core)

    def kv_arrival():
        rows = pl.ds(0, span)
        return remote(kv.at[rows], kv.at[rows], core_send.at[0], core_recv.at[0], ctx=1 - core)

    @pl.when(core == 0)
    def _():
        kv_copy().start()

    for lanes in range(0, heads, 128):
        rotated = rotate_lanes(partial[:, lanes : lanes + 128], cosine[...], signed_sine[...])
        query[:, lanes : lanes + 128] = rotated.astype(jnp.bfloat16) * (HEAD_DIM ** -0.5)

    @pl.when(core == 1)
    def _():
        kv_arrival().wait_recv()

    kv_turned[...] = kv[...].T

    def attend(side, at):
        keys = side * span + (at + 1) * half
        rows = slice(at * half, (at + 1) * half)
        fill_bias(bias, seg_col, seg_row, side * span + at * half, keys, half)

        def pair(index, carry):
            lanes = pl.ds(pl.multiple_of(index * 128, 128), 128)
            both = query[rows, lanes]
            outs = []
            for which in (0, 1):
                scores = turned_dot(kv[0:keys, 0:HEAD_DIM], both[:, which * HEAD_DIM : (which + 1) * HEAD_DIM])
                scores = scores + bias[0:keys, :]
                peak = jnp.max(scores, axis=0, keepdims=True)
                grown = jnp.exp(scores - peak)
                total = jnp.sum(grown, axis=0, keepdims=True)
                logs[pl.ds(2 * index + which, 1), rows] = peak + jnp.log(total)
                out = jnp.dot(
                    kv_turned[HEAD_DIM : 2 * HEAD_DIM, 0:keys],
                    grown.astype(jnp.bfloat16),
                    preferred_element_type=jnp.float32,
                )
                outs.append(out / total)
            mixed[rows, lanes] = jnp.concatenate(outs, axis=0).T.astype(jnp.bfloat16)
            return carry

        lax.fori_loop(0, query.shape[1] // 128, pair, 0)

    for side in (0, 1):

        @pl.when(core == side)
        def _():
            attend(side, 0)
            attend(side, 1)

    load_out.wait()

    def out_tile(t, carry):
        columns = pl.ds(pl.multiple_of(t * 512, 512), 512)
        for b in (0, 2):
            value = jnp.dot(
                mixed[b * block : (b + 2) * block], out_weight[:, columns], preferred_element_type=jnp.float32
            )
            partial[moved(b) : moved(b) + block, columns] = value[:block]
            partial[moved(b + 1) : moved(b + 1) + block, columns] = value[block:]
        return carry

    lax.fori_loop(0, width // 512, out_tile, 0)
    load_down = load(8, down_weight_any, down_weight)

    def rows_at(start):
        return pl.ds(pl.multiple_of(start, CHUNK), CHUNK)

    def own(stream, i):
        return partial[rows_at(ordered(stream, i))]

    def finish_one(stream, i, total):
        value = inputs[rows_at((stream * count + i) * CHUNK)].astype(jnp.float32) + total
        middle[kept_rows(i)] = value
        return value * inverse_rms(value) * gain_two[...]

    gain_out[...] = jnp.zeros_like(gain_out)

    def finish_two(stream, i, total):
        value = middle[kept_rows(i)]
        inverse = inverse_rms(value)
        unit = value * inverse
        gain_out[0:1, :] += jnp.sum(total * unit, axis=0, keepdims=True)
        scaled = total * gain_two[...]
        result = upstream[rows_at(ordered(stream, i))].astype(jnp.float32) + inverse * (
            scaled - unit * jnp.mean(scaled * unit, axis=-1, keepdims=True)
        )
        grad_middle[kept_rows(i)] = result
        return result

    first = Line(n, own, finish_one, ordered, normed_two, *line_one)
    then = Line(n, own, finish_two, ordered, attended, *line_two)
    third = Line(
        n,
        lambda stream, i: second[rows_at(ordered(stream, i))].astype(jnp.float32),
        lambda stream, i, total: middle[kept_rows(i)] + total,
        ordered, second, *line_three,
    )
    tiles, rest = wide_tiles(hidden)
    tile_count = tiles + (1 if rest else 0)

    def each_tile(t, work):
        @pl.when(t < tiles)
        def _():
            work(pl.ds(pl.multiple_of(t * 256, 256), 256))

        if rest:

            @pl.when(t == tiles)
            def _():
                work(pl.ds(tiles * 256, rest))

    def inner_tile(columns):
        grad_inner[:, columns] = turned_dot(upstream[...], down_weight[columns, :])

    def forward_tile(rows, columns):
        gated = jnp.dot(normed_two[rows], gate_weight[:, columns], preferred_element_type=jnp.float32)
        upped = jnp.dot(normed_two[rows], up_weight[:, columns], preferred_element_type=jnp.float32)
        sig = jax.nn.sigmoid(gated)
        act = gated * sig
        grad = grad_inner[rows, columns]
        inner[rows, columns] = (act * upped).astype(jnp.bfloat16)
        up[rows, columns] = (grad * act).astype(jnp.bfloat16)
        gate[rows, columns] = (grad * upped * sig * (1.0 + gated * (1.0 - sig))).astype(jnp.bfloat16)

    def back_tile(rows, t):
        columns = pl.ds(pl.multiple_of(t * 512, 512), 512)
        partial[rows, columns] = turned_dot(gate[rows], gate_weight[columns, :]) + turned_dot(
            up[rows], up_weight[columns, :]
        )

    def second_tile(rows, t):
        columns = pl.ds(pl.multiple_of(t * 512, 512), 512)
        second[rows, columns] = jnp.dot(
            inner[rows], down_weight[:, columns], preferred_element_type=jnp.float32
        ).astype(jnp.bfloat16)

    last = n - 1
    trip = 2 * HOP * last
    each = 2
    forward_steps, back_steps = -(-tile_count // each), width // 1024
    work = forward_steps + back_steps
    base_one = part + trip
    second_steps = width // 1024
    base_two = max(count + trip, base_one + work + second_steps)
    third_base = base_one + work + second_steps
    steps = max(base_two + work + part + trip, third_base + part + trip)

    def store(at, src, dst):
        return pltpu.make_async_copy(src, dst, store_sems.at[at])

    def stores(at, src, dst):
        return [
            store(at + b, src.at[pl.ds(moved(b), block)], dst.at[pl.ds(b * block, block)]) for b in range(4)
        ]

    early = [
        store(0, query, query_out), store(1, kv, kv_out), store(2, logs, log_out), store(3, mixed, mixed_out.at[pl.ds(0, span)]),
        store(31, seg_row, seg_out), store(32, cosine, cosine_out),
        store(33, signed_sine, sine_out),
    ]
    own_slots, far_slots = [], []

    def own_columns(src, dst):
        made = []
        for q in range(dp_size):
            columns = pl.ds(pl.multiple_of((2 * q + core) * piece, piece), piece)
            at = 34 + len(own_slots)
            own_slots.append(at)
            made.append(store(at, src.at[:, columns], dst.at[pl.ds(0, span), pl.ds(q * piece, piece)]))
        return made

    def far_copy(src, dst):
        at = 3 + dp_size + len(far_slots)
        far_slots.append(at)
        return remote(src, dst, core_send.at[at], core_recv.at[at], ctx=1 - core)

    def far_columns(src, dst):
        made = []
        for q in range(dp_size):
            columns = pl.ds(pl.multiple_of((2 * q + 1 - core) * piece, piece), piece)
            made.append(far_copy(src.at[:, columns], dst.at[pl.ds(span, span), pl.ds(q * piece, piece)]))
        return made

    normed_moves = [*own_columns(normed, normed_cols), *far_columns(normed, normed_cols)]
    upstream_moves = [*own_columns(upstream, upstream_cols), *far_columns(upstream, upstream_cols)]
    mixed_move = far_copy(mixed, mixed_out.at[pl.ds(span, span)])
    hidden_moves = [
        store(6, inner, inner_out.at[pl.ds(0, span)]), far_copy(inner, inner_out.at[pl.ds(span, span)]),
        *own_columns(normed_two, two_cols),
    ]
    up_slot = 3 + dp_size + len(far_slots)
    two_moves = [store(7, two_other, two_cols.at[pl.ds(span, span)]), store(5, up, up_out)]
    second_stores, attended_stores = stores(21, second, second_out), stores(25, attended, attended_out)
    middle_store = store(29, middle, middle_out)

    def gate_swaps():
        made = [
            remote(
                ref.at[pl.ds(0, span)], ref.at[pl.ds(span, span)], core_send.at[at], core_recv.at[at], ctx=1 - core
            )
            for ref, at in ((gate, 2), (up, up_slot))
        ]
        for q in range(dp_size):
            columns = pl.ds(pl.multiple_of((2 * q + 1 - core) * piece, piece), piece)
            made.append(
                remote(
                    normed_two.at[:, columns], two_other.at[:, pl.ds(q * piece, piece)],
                    core_send.at[3 + q], core_recv.at[3 + q], ctx=1 - core,
                )
            )
        return made

    def peer_of(r):
        return lax.rem(row + 1 + r, dp_size)

    sends, lands = (send_gate, send_up), (land_gate, land_up)

    def gate_copy(w, r):
        return remote(sends[w].at[r], lands[w].at[r], plane_send.at[w, r], plane_recv.at[w, r], dp=peer_of(r))

    def turn_two(r):
        peer = peer_of(r)
        columns = pl.ds(pl.multiple_of((2 * peer + core) * piece, piece), piece)
        turned[:, 0:span] = normed_two[:, columns].T
        turned[:, span : 2 * span] = two_other[:, pl.ds(pl.multiple_of(peer * piece, piece), piece)].T

    edges = [(low, min(low + 384, hidden)) for low in range(0, hidden, 384)]

    def gate_piece(w, r):
        for low, high in edges:
            sends[w][r, :, low:high] = jnp.dot(
                turned[...], (gate, up)[w][:, low:high], preferred_element_type=jnp.float32
            ).astype(jnp.bfloat16)
        gate_copy(w, r).start()

    def own_piece():
        for low, high in edges:
            partial[0:piece, low:high] = jnp.dot(turned[...], gate[:, low:high], preferred_element_type=jnp.float32)

    own_store = store(4, partial.at[pl.ds(0, piece), pl.ds(0, hidden)], own_gate)

    for made in [*early, *normed_moves, mixed_move]:
        made.start()

    def step(k, carry):
        first.step(k)
        if base_two == base_one + part:
            then.step(k - (base_one + work))
        else:
            then.step(k - (base_one + work), 0, part)
            then.step(k - (base_two + work), part, part)
        third.step(k - third_base)

        @pl.when(k == 0)
        def _():
            for made in load_up:
                made.wait()
            for made in upstream_moves:
                made.start()

        @pl.when(k == 2)
        def _():
            load_down.wait()
            load_gate.wait()
            load_up_weight.wait()

        @pl.when((k >= 2) & (k < 2 + tile_count))
        def _():
            each_tile(k - 2, inner_tile)

        @pl.when(k == base_one)
        def _():
            for made in normed_moves:
                made.wait()

        @pl.when(k == base_two)
        def _():
            middle_store.start()

        late = jnp.where(k >= base_two, 1, 0)
        phase = k - jnp.where(k >= base_two, base_two, base_one)
        rows = pl.ds(pl.multiple_of(late * half, half), half)

        @pl.when((phase >= 0) & (phase < forward_steps))
        def _():
            def tile(t, carry):
                each_tile(t, functools.partial(forward_tile, rows))
                return carry

            lax.fori_loop(phase * each, jnp.minimum((phase + 1) * each, tile_count), tile, 0)

        @pl.when((phase >= forward_steps) & (phase < work))
        def _():
            for t in (0, 1):
                back_tile(rows, 2 * (phase - forward_steps) + t)

        @pl.when((phase >= work) & (phase < work + second_steps))
        def _():
            for t in (0, 1):
                second_tile(rows, 2 * (phase - work) + t)

        @pl.when(k == base_two + work)
        def _():
            for made in hidden_moves:
                made.start()

        @pl.when(k == base_two + forward_steps)
        def _():
            for made in gate_swaps():
                made.start()

        @pl.when(k == base_two + work)
        def _():
            for made in gate_swaps():
                made.wait()
            for made in two_moves:
                made.start()

        gate_task = k - (base_two + work)

        @pl.when((gate_task >= 0) & (gate_task < dp_size - 1))
        def _():
            turn_two(gate_task)
            gate_piece(0, gate_task)

            @pl.when(gate_task < dp_size - 2)
            def _():
                gate_piece(1, gate_task)

        @pl.when(k == base_two + work + part + HOP * last)
        def _():
            turn_two(dp_size - 1)
            own_piece()
            own_store.start()

        @pl.when(k == base_two + work + second_steps)
        def _():
            for b in (1, 3):
                second_stores[b].start()

        @pl.when(k == max(base_one + work, third_base) + part + trip)
        def _():
            for b in (0, 2):
                second_stores[b].start()
                attended_stores[b].start()

        return carry

    lax.fori_loop(0, steps, step, 0)
    late_stores = [
        attended_stores[1], attended_stores[3], store(30, grad_middle, grad_middle_out),
    ]
    for made in late_stores:
        made.start()
    first.drain()
    then.drain()
    third.drain()

    @pl.when(core == 0)
    def _():
        kv_copy().wait_send()

    for r in range(dp_size - 1):
        for w in ((0, 1) if r < dp_size - 2 else (0,)):
            gate_copy(w, r).wait()
    for made in [
        *early, mixed_move, *upstream_moves, *hidden_moves, *two_moves, own_store, middle_store, *second_stores,
        attended_stores[0], attended_stores[2], *late_stores,
    ]:
        made.wait()


def front_call(line_size, dp_size, operands):
    inputs = operands[0]
    query_weight, out_weight, gate_weight = operands[5], operands[8], operands[9]
    span, width = inputs.shape
    heads, hidden = query_weight.shape[1], gate_weight.shape[1]
    piece = width // (2 * dp_size)
    low, full = jnp.bfloat16, jnp.float32
    vmem, outside = pl.BlockSpec(memory_space=pltpu.VMEM), pl.BlockSpec(memory_space=pl.ANY)
    dma = pltpu.SemaphoreType.DMA
    outs = [
        ((1, 2 * span), jnp.int32), ((span, 128), full), ((span, 128), full),
        ((span, heads), low), ((2 * span, 128), low), ((heads // HEAD_DIM, span), full), ((2 * span, heads), low),
        *[((2 * span, width // 2), low)] * 3, *[((2 * span, hidden), low)] * 2, ((span, width), low),
        ((span, width), low), ((span // 2, width), full), ((span // 2, width), full),
        ((dp_size - 1, piece, hidden), low), ((dp_size - 2, piece, hidden), low), ((piece, hidden), full), ((8, width), full),
    ]
    scratch = [
        pltpu.VMEM((2, 8, span), jnp.int32), pltpu.VMEM((1, 2 * span), jnp.int32),
        pltpu.VMEM((2 * span, 1), jnp.int32), pltpu.VMEM((span, 128), full), pltpu.VMEM((span, 128), full),
        pltpu.VMEM((span, width), low), pltpu.VMEM((span, width), low),
        pltpu.VMEM((128, width), low), pltpu.VMEM((span, heads), low),
        pltpu.VMEM((2 * span, 128), low), pltpu.VMEM((128, 2 * span), low),
        pltpu.VMEM((heads // HEAD_DIM, span), full), pltpu.VMEM((span, heads), low),
        pltpu.VMEM((2 * span, span // 2), full),
        pltpu.VMEM((width, hidden), low), pltpu.VMEM((width, hidden), low), pltpu.VMEM((hidden, width), low),
        pltpu.VMEM((span, width), low), pltpu.VMEM((span, hidden), full), pltpu.VMEM((span, width), low),
        *[pltpu.VMEM((2 * span, hidden), low)] * 2, pltpu.VMEM((span, hidden), low),
        pltpu.VMEM((span, width), full),
        pltpu.VMEM((span // 2, width), full), pltpu.VMEM((span // 2, width), full),
        pltpu.VMEM((span, width // 2), low), pltpu.VMEM((piece, 2 * span), low),
        pltpu.VMEM((dp_size - 1, piece, hidden), low), pltpu.VMEM((dp_size - 2, piece, hidden), low),
        dma((12,)), dma((34 + 3 * dp_size,)), dma((6 + 3 * dp_size,)), dma((6 + 3 * dp_size,)),
        dma((2, dp_size - 1)), dma((2, dp_size - 1)),
        *line_scratch(span, width), *line_scratch(span, width), *line_scratch(span, width, 2),
    ]
    return pl.pallas_call(
        functools.partial(front_kernel, line_size, dp_size),
        out_shape=[jax.ShapeDtypeStruct(s, d) for s, d in outs],
        in_specs=[outside] + [vmem] * 4 + [outside] * 8,
        out_specs=[outside] * 19 + [vmem],
        scratch_shapes=scratch,
        compiler_params=pltpu.CompilerParams(
            collective_id=1, has_side_effects=True, vmem_limit_bytes=FRONT_MIB * MIB
        ),
    )(*operands)


def back_kernel(
    n, dp_size,
    query_any, kv_any, logs, mixed_any, cosine, signed_sine, seg_row, inputs_any, normed_any, two_any, upstream_any,
    up_any, inner_any, second_any, attended_any, middle_any, grad_middle_any, gain_one, gain_two_grad,
    query_weight_any, key_weight_any, value_weight_any, out_weight_any,
    layer_out, grad_inputs, grad_gains, grad_qkv, own_out, grad_up, own_down,
    land_up, land_down, land_qkv, land_out,
    query, kv, kv_turned, grad_mixed, mixed, attended, normed_cols, two_cols, upstream_cols, attended_other,
    up, inner, pre, query_weight, kv_weight, out_weight, grad_middle, middle, inputs,
    ring, send_qkv, send_out, turned, seg_col, bias, kv_grad, kv_grad_other,
    gain_line, gain_land, gain_sum, gain_plane,
    load_sems, core_send, core_recv, ring_send, ring_recv, plane_send, plane_recv, line_send, line_recv,
    spread_send, spread_recv, *line_refs,
):
    span, width = attended.shape
    heads, piece = query.shape[1], turned.shape[0]
    here, row, core = lax.axis_index("tensor"), lax.axis_index("dp"), lax.axis_index("ctx")
    half = span // 2
    line_out, line_in = line_refs[:5], line_refs[5:]
    count, part = line_in[0].shape[1], line_out[0].shape[1]
    last = n - 1
    loads = []

    def load(src, dst):
        made = pltpu.make_async_copy(src, dst, load_sems.at[len(loads)])
        made.start()
        loads.append(made)
        return made

    own_half = pl.ds(pl.multiple_of(jnp.where(here == 0, half, 0), half), half)
    mixed_loads = [load(attended_any, attended), load(out_weight_any, out_weight)]
    attend_loads = [load(query_any, query), load(kv_any, kv), load(mixed_any, mixed)]
    line_loads = [load(second_any, layer_out), load(middle_any, middle)]

    up_loads = [load(two_any, two_cols), load(up_any, up)]
    inner_loads = [load(upstream_any, upstream_cols), load(inner_any, inner)]
    late_loads = [
        load(query_weight_any, query_weight), load(key_weight_any, kv_weight.at[pl.ds(0, HEAD_DIM)]),
        load(value_weight_any, kv_weight.at[pl.ds(HEAD_DIM, HEAD_DIM)]),
        load(grad_middle_any, grad_middle), load(inputs_any.at[own_half], inputs),
        load(normed_any, normed_cols),
    ]
    meet = greet(n, True, dp_size, full_line=True)
    pre_slot, kv_slot = dp_size, dp_size + 1

    def attended_swaps():
        made = []
        for q in range(dp_size):
            columns = pl.ds(pl.multiple_of((2 * q + 1 - core) * piece, piece), piece)
            made.append(
                remote(
                    attended.at[:, columns], attended_other.at[:, pl.ds(q * piece, piece)],
                    core_send.at[q], core_recv.at[q], ctx=1 - core,
                )
            )
        return made

    def pre_swap():
        return remote(
            pre.at[pl.ds(0, span)], pre.at[pl.ds(span, span)], core_send.at[pre_slot], core_recv.at[pre_slot],
            ctx=1 - core,
        )

    def kv_swap():
        return remote(
            kv_grad.at[pl.ds(0, span)], kv_grad_other, core_send.at[kv_slot], core_recv.at[kv_slot], ctx=1 - core
        )

    gain_line[...] = jnp.zeros_like(gain_line)
    gain_line[1:2, :] = gain_two_grad[0:1, :]
    kv_grad[...] = jnp.zeros_like(kv_grad)
    seg_col[...] = jnp.broadcast_to(seg_row[...], (8, 2 * span)).T[:, 0:1]
    for made in [*mixed_loads, *attend_loads]:
        made.wait()
    kv_turned[...] = kv[...].T
    grad_mixed[...] = turned_dot(attended[...], out_weight[...]).astype(jnp.bfloat16)
    for made in line_loads:
        made.wait()
    meet()
    for made in attended_swaps():
        made.start()

    def rows_at(start):
        return pl.ds(pl.multiple_of(start, BACK_CHUNK), BACK_CHUNK)

    def plain(stream, i):
        return (stream * count + i) * BACK_CHUNK

    def finish_out(stream, i, total):
        return middle[kept_rows(i, BACK_CHUNK)] + total

    def finish_in(stream, i, total):
        hidden = inputs[kept_rows(i, BACK_CHUNK)].astype(jnp.float32)
        inverse = inverse_rms(hidden)
        unit = hidden * inverse
        gain_line[0:1, :] += jnp.sum(total * unit, axis=0, keepdims=True)
        scaled = total * gain_one[...]
        return grad_middle[kept_rows(i, BACK_CHUNK)] + inverse * (
            scaled - unit * jnp.mean(scaled * unit, axis=-1, keepdims=True)
        )

    out_line = Line(
        n, lambda s, i: layer_out[rows_at(plain(s, i))].astype(jnp.float32), finish_out, plain, layer_out, *line_out,
        base=count - part, hop=BACK_HOP,
    )
    in_line = Line(
        n, lambda s, i: grad_inputs[rows_at(plain(s, i))].astype(jnp.float32), finish_in, plain, grad_inputs, *line_in,
        hop=BACK_HOP,
    )

    def attend_back(side, at, index):
        keys = side * span + (at + 1) * half
        rows = slice(at * half, (at + 1) * half)
        lanes = pl.ds(pl.multiple_of(index * 128, 128), 128)

        @pl.when(index == 0)
        def _():
            fill_bias(bias, seg_col, seg_row, side * span + at * half, keys, half)

        both_query, both_grad = query[rows, lanes], grad_mixed[rows, lanes]
        shared = (both_grad.astype(jnp.float32) * mixed[rows, lanes].astype(jnp.float32)).T
        outs, parts = [], None
        for which in (0, 1):
            head = slice(which * HEAD_DIM, (which + 1) * HEAD_DIM)
            query_head, grad_head = both_query[:, head], both_grad[:, head]
            scores = turned_dot(kv[0:keys, 0:HEAD_DIM], query_head) + bias[0:keys, :]
            probs = jnp.exp(scores - logs[pl.ds(2 * index + which, 1), rows])
            grad_probs = turned_dot(kv[0:keys, HEAD_DIM : 2 * HEAD_DIM], grad_head)
            row_dot = jnp.sum(shared[head], axis=0, keepdims=True)
            grad_scores = (probs * (grad_probs - row_dot)).astype(jnp.bfloat16)
            grad_key = jnp.dot(grad_scores, query_head, preferred_element_type=jnp.float32)
            grad_value = jnp.dot(probs.astype(jnp.bfloat16), grad_head, preferred_element_type=jnp.float32)
            part = jnp.concatenate([grad_key, grad_value], axis=1)
            parts = part if parts is None else parts + part
            outs.append(
                jnp.dot(kv_turned[0:HEAD_DIM, 0:keys], grad_scores, preferred_element_type=jnp.float32)
            )
        kv_grad[0:keys] += parts
        grad_query = jnp.concatenate(outs, axis=0).T * (HEAD_DIM ** -0.5)
        pre[rows, lanes] = rotate_lanes(grad_query, cosine[rows], signed_sine[rows], back=True).astype(jnp.bfloat16)

    pairs = heads // 128
    tasks = 2 * pairs

    def attend_task(task):
        for side in (0, 1):
            for at in (0, 1):

                @pl.when((core == side) & (task // pairs == at))
                def _():
                    attend_back(side, at, lax.rem(task, pairs))

    own_grad = pl.ds(pl.multiple_of(core * span, span), span)

    def finish_pre():
        @pl.when(core == 0)
        def _():
            kv_swap().wait_recv()
            kv_grad[0:span] += kv_grad_other[...]

        raw = kv_grad[own_grad]
        turned_back = rotate_lanes(raw, cosine[...], signed_sine[...], back=True)
        pre[0:span, heads : heads + 128] = key_lanes(raw, turned_back).astype(jnp.bfloat16)

    def in_products():
        def tile(t, carry):
            columns = pl.ds(pl.multiple_of(t * 512, 512), 512)
            for low in (0, half):
                rows = slice(low, low + half)
                grad_inputs[rows, columns] = (
                    turned_dot(pre[rows, 0:heads], query_weight[columns, :])
                    + jnp.dot(
                        pre[rows, heads : heads + 128], kv_weight[:, columns], preferred_element_type=jnp.float32
                    )
                ).astype(jnp.bfloat16)
            return carry

        lax.fori_loop(0, width // 512, tile, 0)

    def peer_of(r):
        return lax.rem(row + 1 + r, dp_size)

    def turn(r, cols):
        block = pl.multiple_of(peer_of(r) * piece, piece)
        turned[...] = cols[:, pl.ds(block, piece)].T

    def turn_attended(r):
        peer = peer_of(r)
        columns = pl.ds(pl.multiple_of((2 * peer + core) * piece, piece), piece)
        turned[:, 0:span] = attended[:, columns].T
        turned[:, span : 2 * span] = attended_other[:, pl.ds(pl.multiple_of(peer * piece, piece), piece)].T

    def tiles_of(stacked):
        wide = stacked.shape[1]
        return [(low, min(low + 384, wide)) for low in range(0, wide, 384)]

    def piece_value(stacked, low, high):
        return jnp.dot(turned[...], stacked[:, low:high], preferred_element_type=jnp.float32)

    others = dp_size - 1

    def ring_copy(at):
        r = others - 1 if at == 0 else at - 1
        land = land_up.at[0] if at == 0 else land_down.at[at - 1]
        return remote(ring.at[at], land, ring_send.at[at], ring_recv.at[at], dp=peer_of(r))

    def ring_piece(at, cols, stacked):
        turn(others - 1 if at == 0 else at - 1, cols)
        for low, high in tiles_of(stacked):
            ring[at, :, low:high] = piece_value(stacked, low, high).astype(jnp.bfloat16)
        ring_copy(at).start()

    def kept_piece(cols, stacked, own):
        turn(others, cols)
        for low, high in tiles_of(stacked):
            own[:, low:high] = piece_value(stacked, low, high)

    sends, lands = (send_qkv, send_out), (land_qkv, land_out)

    def plane_copy(w, r):
        return remote(sends[w].at[r], lands[w].at[r], plane_send.at[w, r], plane_recv.at[w, r], dp=peer_of(r))

    def plane_piece(w, r, stacked, own):
        @pl.when(r < dp_size - 1)
        def _():
            for low, high in tiles_of(stacked):
                sends[w][r, :, low:high] = piece_value(stacked, low, high).astype(jnp.bfloat16)
            plane_copy(w, r).start()

        @pl.when(r == dp_size - 1)
        def _():
            for low, high in tiles_of(stacked):
                own[:, low:high] = piece_value(stacked, low, high)

    def line_copies(owner, hops):
        slot = 0 if owner == 0 else 1
        return [
            remote(
                gain_line, gain_land.at[slot], line_send.at[slot, hop - 1], line_recv.at[slot],
                tensor=owner + hop if owner == 0 else owner - hop,
            )
            for hop in hops
        ]

    shard = width // (2 * dp_size)
    shards = 2 * dp_size
    place = 2 * row + core

    def spread(r):
        peer = lax.rem(place + 1 + r, shards)
        block = pl.multiple_of(peer * shard, shard)
        return remote(
            gain_sum.at[:, pl.ds(block, shard)], gain_plane.at[r], spread_send.at[r], spread_recv.at[r],
            dp=peer // 2, ctx=lax.rem(peer, 2),
        )

    def gather_gains():
        gain_sum[...] = jnp.zeros_like(gain_sum)
        for owner in (0, last):
            slot = 0 if owner == 0 else 1

            @pl.when(here == owner)
            def _():
                gain_sum[...] += gain_line[...]

            @pl.when(here != owner)
            def _():
                line_copies(owner, (1,))[0].wait_recv()
                gain_sum[...] += gain_land[slot]
        for r in range(shards - 1):
            spread(r).start()

    attend_steps = tasks // TASKS
    lag = attend_steps + 2
    ring_steps = RINGS + [lag + at for at in range(dp_size - 3)]
    out_base = lag + 1
    steps = max(lag + count + 2 * BACK_HOP * last, out_base + 2 * dp_size)

    def step(k, carry):
        out_line.step(k, count - part, part)
        in_line.step(k - lag)

        @pl.when((k >= 1) & (k <= attend_steps))
        def _():
            def task(more, carry):
                attend_task(TASKS * (k - 1) + more)
                return carry

            lax.fori_loop(0, TASKS, task, 0)

        @pl.when((k == attend_steps) & (core == 1))
        def _():
            kv_swap().start()

        @pl.when(k == 1)
        def _():
            for made in up_loads:
                made.wait()

        @pl.when(k == ring_steps[1])
        def _():
            for made in inner_loads:
                made.wait()

        @pl.when(k == attend_steps)
        def _():
            for made in [*late_loads, *attended_swaps()]:
                made.wait()

        @pl.when(k == attend_steps + 1)
        def _():
            finish_pre()
            in_products()
            pre_swap().start()

        for at in range(dp_size):

            @pl.when(k == ring_steps[at])
            def _():
                ring_piece(at, *((two_cols, up) if at == 0 else (upstream_cols, inner)))

        @pl.when(k == lag + dp_size)
        def _():
            kept_piece(two_cols, up, grad_up)

        @pl.when(k == lag + dp_size + 1)
        def _():
            kept_piece(upstream_cols, inner, own_down)

        @pl.when(k == out_base)
        def _():
            pre_swap().wait()

        at, kind = (k - out_base) // 2, lax.rem(k - out_base, 2)

        @pl.when((k >= out_base) & (at < dp_size) & (kind == 0))
        def _():
            turn_attended(at)
            plane_piece(1, at, mixed, own_out)

        @pl.when((k >= out_base) & (at < dp_size) & (kind == 1))
        def _():
            turn(at, normed_cols)
            plane_piece(0, at, pre, grad_qkv)

        @pl.when(k == lag + count + BACK_HOP * last - 1)
        def _():
            for owner in (0, last):

                @pl.when(here == owner)
                def _():
                    for made in line_copies(owner, range(1, n)):
                        made.start()

        @pl.when(k == min(lag + count + BACK_HOP * last + 3, steps - 1))
        def _():
            gather_gains()

        return carry

    lax.fori_loop(0, steps, step, 0)
    out_line.drain()
    in_line.drain()

    @pl.when(core == 1)
    def _():
        kv_swap().wait_send()

    for at in range(dp_size):
        ring_copy(at).wait()
    for r in range(others):
        for w in (0, 1):
            plane_copy(w, r).wait()
    grad_gains[...] = gain_sum[:, pl.ds(pl.multiple_of(place * shard, shard), shard)]
    for r in range(shards - 1):
        spread(r).wait()
        grad_gains[...] += gain_plane[r]
    for owner in (0, last):

        @pl.when(here == owner)
        def _():
            for made in line_copies(owner, range(1, n)):
                made.wait_send()


def back_call(line_size, dp_size, operands):
    query = operands[0]
    span, heads = query.shape
    width, hidden = operands[7].shape[1], operands[11].shape[1]
    piece = width // (2 * dp_size)
    wide = heads + 128
    low, full = jnp.bfloat16, jnp.float32
    vmem, outside = pl.BlockSpec(memory_space=pltpu.VMEM), pl.BlockSpec(memory_space=pl.ANY)
    dma = pltpu.SemaphoreType.DMA
    others = dp_size - 1
    outs = [
        ((span, width), low), ((span, width), low), ((8, piece), full), ((piece, wide), full), ((piece, heads), full),
        ((piece, hidden), full), ((piece, hidden), full),
        ((1, piece, hidden), low), ((others, piece, hidden), low), ((others, piece, wide), low), ((others, piece, heads), low),
    ]
    core_copies = dp_size + 2
    scratch = [
        pltpu.VMEM((span, heads), low), pltpu.VMEM((2 * span, 128), low), pltpu.VMEM((128, 2 * span), low),
        pltpu.VMEM((span, heads), low), pltpu.VMEM((2 * span, heads), low), pltpu.VMEM((span, width), low),
        *[pltpu.VMEM((2 * span, width // 2), low)] * 3, pltpu.VMEM((span, width // 2), low),
        *[pltpu.VMEM((2 * span, hidden), low)] * 2, pltpu.VMEM((2 * span, wide), low),
        pltpu.VMEM((width, heads), low), pltpu.VMEM((128, width), low), pltpu.VMEM((heads, width), low),
        pltpu.VMEM((span // 2, width), full), pltpu.VMEM((span // 2, width), full), pltpu.VMEM((span // 2, width), low),
        pltpu.VMEM((dp_size, piece, hidden), low), pltpu.VMEM((others, piece, wide), low),
        pltpu.VMEM((others, piece, heads), low),
        pltpu.VMEM((piece, 2 * span), low), pltpu.VMEM((2 * span, 1), jnp.int32), pltpu.VMEM((2 * span, span // 2), full),
        pltpu.VMEM((2 * span, 128), full), pltpu.VMEM((span, 128), full),
        pltpu.VMEM((8, width), full), pltpu.VMEM((2, 8, width), full), pltpu.VMEM((8, width), full),
        pltpu.VMEM((2 * dp_size - 1, 8, piece), full),
        dma((17,)), dma((core_copies,)), dma((core_copies,)),
        dma((dp_size,)), dma((dp_size,)), dma((2, others)), dma((2, others)),
        dma((2, line_size - 1)), dma((2,)), dma((2 * dp_size - 1,)), dma((2 * dp_size - 1,)),
        *line_scratch(span, width, 2, BACK_CHUNK), *line_scratch(span, width, 1, BACK_CHUNK),
    ]
    spaces = [outside, outside, vmem, outside, vmem, vmem, vmem] + [outside] * 10 + [vmem, vmem] + [outside] * 4
    return pl.pallas_call(
        functools.partial(back_kernel, line_size, dp_size),
        out_shape=[jax.ShapeDtypeStruct(s, d) for s, d in outs],
        in_specs=spaces,
        out_specs=[vmem] * 7 + [outside] * 4,
        scratch_shapes=scratch,
        compiler_params=pltpu.CompilerParams(
            collective_id=2, has_side_effects=True, vmem_limit_bytes=BACK_MIB * MIB
        ),
    )(*operands)


def settle_kernel(
    layer_any, inputs_any, gains, qkv_any, out_any, gate_any, up_any, down_any,
    land_gate, land_up, land_up_last, land_down, land_qkv, land_out,
    layer_out, grad_inputs, gain_one, grad_query, grad_key, grad_value, grad_out, gain_two, grad_gate, grad_up, grad_down,
    own_qkv, own_out, own_gate, own_up, own_down, far_qkv, far_out, far_gate, far_up, far_down,
    turned_kv, turned_out, turned_down, layer_held, inputs_held, in_sems, out_sems,
):
    whole, early = [], land_up.shape[0]
    passed = [
        pltpu.make_async_copy(layer_any, layer_held, in_sems.at[0, 5]),
        pltpu.make_async_copy(inputs_any, inputs_held, in_sems.at[1, 5]),
        pltpu.make_async_copy(land_up_last, far_up.at[pl.ds(early, 1)], in_sems.at[0, 6]),
    ]
    owns = ((qkv_any, own_qkv), (out_any, own_out), (gate_any, own_gate), (up_any, own_up), (down_any, own_down))
    fars = (
        (land_qkv, far_qkv), (land_out, far_out), (land_gate, far_gate), (land_up, far_up.at[pl.ds(0, early)]),
        (land_down, far_down),
    )
    loads = [
        (
            pltpu.make_async_copy(*own, in_sems.at[0, at]),
            pltpu.make_async_copy(*far, in_sems.at[1, at]),
        )
        for at, (own, far) in enumerate(zip(owns, fars))
    ]
    for made in passed:
        made.start()
    for at in (4, 2, 3, 0, 1):
        for made in loads[at]:
            made.start()
    gain_one[...] = gains[0:1]
    gain_two[...] = gains[1:2]

    def settle(at, own, far):
        for made in loads[at]:
            made.wait()
        total = own[...]
        for r in range(far.shape[0]):
            total = total + far[r].astype(jnp.float32)
        return total

    def put(at, src, dst):
        made = pltpu.make_async_copy(src, dst, out_sems.at[at])
        made.start()
        whole.append(made)

    heads = grad_query.shape[1]
    passed[0].wait()
    put(0, layer_held, layer_out)
    passed[1].wait()
    put(1, inputs_held, grad_inputs)
    turned_down[...] = settle(4, own_down, far_down).T
    put(8, turned_down, grad_down)
    own_gate[...] = settle(2, own_gate, far_gate)
    put(6, own_gate, grad_gate)
    passed[2].wait()
    own_up[...] = settle(3, own_up, far_up)
    put(7, own_up, grad_up)
    own_qkv[...] = settle(0, own_qkv, far_qkv)
    put(2, own_qkv.at[:, pl.ds(0, heads)], grad_query)
    turned_kv[...] = own_qkv[:, heads:].T
    put(3, turned_kv.at[pl.ds(0, HEAD_DIM)], grad_key)
    put(4, turned_kv.at[pl.ds(HEAD_DIM, HEAD_DIM)], grad_value)
    turned_out[...] = settle(1, own_out, far_out).T
    put(5, turned_out, grad_out)
    for made in whole:
        made.wait()


def settle_call(operands):
    layer_out, _, gains, qkv, out, gate = operands[:6]
    piece, wide = qkv.shape
    heads, hidden = out.shape[1], gate.shape[1]
    others = operands[8].shape[0]
    low, full = jnp.bfloat16, jnp.float32
    vmem, outside = pl.BlockSpec(memory_space=pltpu.VMEM), pl.BlockSpec(memory_space=pl.ANY)
    outs = [
        (layer_out.shape, low), (layer_out.shape, low), ((1, piece), full), ((piece, heads), full),
        ((HEAD_DIM, piece), full), ((HEAD_DIM, piece), full), ((heads, piece), full), ((1, piece), full),
        ((piece, hidden), full), ((piece, hidden), full), ((hidden, piece), full),
    ]
    shapes = [(piece, wide), (piece, heads), *[(piece, hidden)] * 3]
    scratch = [
        *[pltpu.VMEM(shape, full) for shape in shapes], *[pltpu.VMEM((others, *shape), low) for shape in shapes],
        pltpu.VMEM((wide - heads, piece), full), pltpu.VMEM((heads, piece), full), pltpu.VMEM((hidden, piece), full),
        pltpu.VMEM(layer_out.shape, low), pltpu.VMEM(layer_out.shape, low),
        pltpu.SemaphoreType.DMA((2, 7)), pltpu.SemaphoreType.DMA((9,)),
    ]
    return pl.pallas_call(
        settle_kernel,
        out_shape=[jax.ShapeDtypeStruct(s, d) for s, d in outs],
        in_specs=[outside, outside, vmem] + [outside] * 11,
        out_specs=[outside, outside, vmem] + [outside] * 4 + [vmem] + [outside] * 3,
        scratch_shapes=scratch,
        compiler_params=pltpu.CompilerParams(vmem_limit_bytes=62 * MIB),
    )(*operands)


def plain_body(
    inputs,
    segment_ids,
    attention_gain,
    query_weight,
    key_weight,
    value_weight,
    out_weight,
    feedforward_gain,
    gate_weight,
    up_weight,
    down_weight,
    cotangent,
):
    seq_count, span_len, model_width = inputs.shape
    row_count = seq_count * span_len
    query_heads = query_weight.shape[1] // HEAD_DIM
    kv_heads = key_weight.shape[1] // HEAD_DIM
    group_size = query_heads // kv_heads
    score_scale = 1.0 / math.sqrt(HEAD_DIM)
    offset = lax.axis_index("ctx") * span_len
    whole_segments = lax.all_gather(segment_ids, "ctx", axis=1, tiled=True)
    own_positions = lax.dynamic_slice_in_dim(positions_of(whole_segments), offset, span_len, 1)
    cosine, sine_table = rotary_tables(own_positions)
    cosine = cosine[:, :, None, :]
    sine_table = sine_table[:, :, None, :]
    hidden = inputs.astype(jnp.float32).reshape(row_count, model_width)
    inverse_one = lax.rsqrt(jnp.mean(hidden * hidden, axis=-1, keepdims=True) + epsilon)
    unit_one = hidden * inverse_one
    normed = (unit_one * attention_gain).astype(jnp.bfloat16)
    query_rows = rotate(
        jnp.dot(normed, query_weight, preferred_element_type=jnp.float32).reshape(
            seq_count, span_len, query_heads, HEAD_DIM
        ),
        cosine,
        sine_table,
    ).astype(jnp.bfloat16)
    key_rows = rotate(
        jnp.dot(normed, key_weight, preferred_element_type=jnp.float32).reshape(
            seq_count, span_len, kv_heads, HEAD_DIM
        ),
        cosine,
        sine_table,
    ).astype(jnp.bfloat16)
    value_rows = (
        jnp.dot(normed, value_weight, preferred_element_type=jnp.float32)
        .astype(jnp.bfloat16)
        .reshape(seq_count, span_len, kv_heads, HEAD_DIM)
    )
    all_keys, all_values = (
        lax.all_gather(key_rows, "ctx", axis=1, tiled=True),
        lax.all_gather(value_rows, "ctx", axis=1, tiled=True),
    )

    def attend(block_items):
        query_block, key_block, value_block, query_seg, key_seg = block_items
        allowed = visible(query_seg, key_seg, offset)
        grouped = query_block.reshape(span_len, kv_heads, group_size, HEAD_DIM)
        raw_scores = jnp.einsum(
            "qhgd,khd->hgqk", grouped, key_block, preferred_element_type=jnp.float32
        )
        scores = jnp.where(allowed, raw_scores * score_scale, masked_score)
        row_peak = jnp.max(scores, axis=-1, keepdims=True)
        shifted_exp = jnp.exp(scores - row_peak)
        denominator = jnp.sum(shifted_exp, axis=-1, keepdims=True)
        attn_probs = (shifted_exp / denominator).astype(jnp.bfloat16)
        mixed_block = jnp.einsum(
            "hgqk,khd->qhgd", attn_probs, value_block, preferred_element_type=jnp.float32
        )
        return (
            mixed_block.astype(jnp.bfloat16).reshape(span_len, query_heads * HEAD_DIM),
            row_peak + jnp.log(denominator),
        )

    mixed_heads, log_sums = lax.map(
        attend, (query_rows, all_keys, all_values, segment_ids, whole_segments)
    )
    mixed_flat = mixed_heads.reshape(row_count, query_heads * HEAD_DIM)
    attended = lax.psum(
        jnp.dot(mixed_flat, out_weight, preferred_element_type=jnp.float32), "tensor"
    )
    middle = hidden + attended
    inverse_two = lax.rsqrt(jnp.mean(middle * middle, axis=-1, keepdims=True) + epsilon)
    unit_two = middle * inverse_two
    normed_two = (unit_two * feedforward_gain).astype(jnp.bfloat16)
    gate_pre = jnp.dot(normed_two, gate_weight, preferred_element_type=jnp.float32)
    up_pre = jnp.dot(normed_two, up_weight, preferred_element_type=jnp.float32)
    sigmoid_gate = jax.nn.sigmoid(gate_pre)
    inner_act = (gate_pre * sigmoid_gate * up_pre).astype(jnp.bfloat16)
    feed_out = lax.psum(
        jnp.dot(inner_act, down_weight, preferred_element_type=jnp.float32).astype(jnp.bfloat16),
        "tensor",
    ).astype(jnp.float32)
    layer_out = (middle + feed_out).astype(jnp.bfloat16).reshape(seq_count, span_len, model_width)
    upstream = cotangent.reshape(row_count, model_width)
    grad_down = jnp.dot(inner_act.T, upstream, preferred_element_type=jnp.float32)
    grad_inner = jnp.dot(upstream, down_weight.T, preferred_element_type=jnp.float32)
    grad_up_pre = (grad_inner * gate_pre * sigmoid_gate).astype(jnp.bfloat16)
    grad_gate_pre = (
        grad_inner * up_pre * sigmoid_gate * (1.0 + gate_pre * (1.0 - sigmoid_gate))
    ).astype(jnp.bfloat16)
    grad_gate = jnp.dot(normed_two.T, grad_gate_pre, preferred_element_type=jnp.float32)
    grad_up = jnp.dot(normed_two.T, grad_up_pre, preferred_element_type=jnp.float32)
    grad_normed_two = lax.psum(
        jnp.dot(grad_gate_pre, gate_weight.T, preferred_element_type=jnp.float32)
        + jnp.dot(grad_up_pre, up_weight.T, preferred_element_type=jnp.float32),
        "tensor",
    )
    grad_ffn_gain = jnp.sum(grad_normed_two * unit_two, axis=0)
    scaled_two = grad_normed_two * feedforward_gain
    grad_middle = upstream.astype(jnp.float32) + inverse_two * (
        scaled_two - unit_two * jnp.mean(scaled_two * unit_two, axis=-1, keepdims=True)
    )
    grad_attended = grad_middle.astype(jnp.bfloat16)
    grad_out_part = jnp.dot(mixed_flat.T, grad_attended, preferred_element_type=jnp.float32)
    grad_mixed = (
        jnp.dot(grad_attended, out_weight.T, preferred_element_type=jnp.float32)
        .astype(jnp.bfloat16)
        .reshape(seq_count, span_len, query_heads, HEAD_DIM)
    )

    def attend_back(block_items):
        query_block, key_block, value_block, query_seg, key_seg, grad_block, log_block = block_items
        allowed = visible(query_seg, key_seg, offset)
        grouped = query_block.reshape(span_len, kv_heads, group_size, HEAD_DIM)
        grad_grouped = grad_block.reshape(span_len, kv_heads, group_size, HEAD_DIM)
        raw_scores = jnp.einsum(
            "qhgd,khd->hgqk", grouped, key_block, preferred_element_type=jnp.float32
        )
        scores = jnp.where(allowed, raw_scores * score_scale, masked_score)
        attn_probs = jnp.exp(scores - log_block)
        rounded = attn_probs.astype(jnp.bfloat16)
        grad_values = jnp.einsum(
            "hgqk,qhgd->khd", rounded, grad_grouped, preferred_element_type=jnp.float32
        )
        grad_probs = jnp.einsum(
            "qhgd,khd->hgqk", grad_grouped, value_block, preferred_element_type=jnp.float32
        )
        row_dot = jnp.sum(attn_probs * grad_probs, axis=-1, keepdims=True)
        grad_scores = (attn_probs * (grad_probs - row_dot) * score_scale).astype(jnp.bfloat16)
        grad_queries = jnp.einsum(
            "hgqk,khd->qhgd", grad_scores, key_block, preferred_element_type=jnp.float32
        ).reshape(span_len, query_heads, HEAD_DIM)
        grad_keys = jnp.einsum(
            "hgqk,qhgd->khd", grad_scores, grouped, preferred_element_type=jnp.float32
        )
        return (grad_queries, grad_keys, grad_values)

    grad_queries, grad_keys, grad_values = lax.map(
        attend_back,
        (query_rows, all_keys, all_values, segment_ids, whole_segments, grad_mixed, log_sums),
    )
    own_grad_keys, own_grad_values = (
        lax.psum_scatter(grad_keys, "ctx", scatter_dimension=1, tiled=True),
        lax.psum_scatter(grad_values, "ctx", scatter_dimension=1, tiled=True),
    )
    grad_query_pre = (
        rotate(grad_queries, cosine, -sine_table)
        .astype(jnp.bfloat16)
        .reshape(row_count, query_heads * HEAD_DIM)
    )
    grad_key_pre = (
        rotate(own_grad_keys, cosine, -sine_table)
        .astype(jnp.bfloat16)
        .reshape(row_count, kv_heads * HEAD_DIM)
    )
    grad_value_pre = own_grad_values.astype(jnp.bfloat16).reshape(row_count, kv_heads * HEAD_DIM)
    grad_query = jnp.dot(normed.T, grad_query_pre, preferred_element_type=jnp.float32)
    grad_key = jnp.dot(normed.T, grad_key_pre, preferred_element_type=jnp.float32)
    grad_value = jnp.dot(normed.T, grad_value_pre, preferred_element_type=jnp.float32)
    grad_normed = lax.psum(
        (
            jnp.dot(grad_query_pre, query_weight.T, preferred_element_type=jnp.float32)
            + jnp.dot(grad_key_pre, key_weight.T, preferred_element_type=jnp.float32)
            + jnp.dot(grad_value_pre, value_weight.T, preferred_element_type=jnp.float32)
        ).astype(jnp.bfloat16),
        "tensor",
    ).astype(jnp.float32)
    grad_attn_gain = jnp.sum(grad_normed * unit_one, axis=0)
    scaled_one = grad_normed * attention_gain
    grad_hidden = grad_middle + inverse_one * (
        scaled_one - unit_one * jnp.mean(scaled_one * unit_one, axis=-1, keepdims=True)
    )
    grad_inputs = grad_hidden.astype(jnp.bfloat16).reshape(seq_count, span_len, model_width)
    reduced = (
        lax.psum_scatter(
            grad_attn_gain.astype(jnp.bfloat16), ("dp", "ctx"), scatter_dimension=0, tiled=True
        ).astype(jnp.float32),
        lax.psum_scatter(
            grad_query.astype(jnp.bfloat16), ("dp", "ctx"), scatter_dimension=0, tiled=True
        ).astype(jnp.float32),
        lax.psum_scatter(
            grad_key.astype(jnp.bfloat16), ("dp", "ctx"), scatter_dimension=0, tiled=True
        ).astype(jnp.float32),
        lax.psum_scatter(
            grad_value.astype(jnp.bfloat16), ("dp", "ctx"), scatter_dimension=0, tiled=True
        ).astype(jnp.float32),
        lax.psum_scatter(
            grad_out_part.astype(jnp.bfloat16), ("dp", "ctx"), scatter_dimension=1, tiled=True
        ).astype(jnp.float32),
        lax.psum_scatter(
            grad_ffn_gain.astype(jnp.bfloat16), ("dp", "ctx"), scatter_dimension=0, tiled=True
        ).astype(jnp.float32),
        lax.psum_scatter(
            grad_gate.astype(jnp.bfloat16), ("dp", "ctx"), scatter_dimension=0, tiled=True
        ).astype(jnp.float32),
        lax.psum_scatter(
            grad_up.astype(jnp.bfloat16), ("dp", "ctx"), scatter_dimension=0, tiled=True
        ).astype(jnp.float32),
        lax.psum_scatter(
            grad_down.astype(jnp.bfloat16), ("dp", "ctx"), scatter_dimension=1, tiled=True
        ).astype(jnp.float32),
    )
    return (
        layer_out,
        grad_inputs,
        reduced[0],
        reduced[1],
        reduced[2],
        reduced[3],
        reduced[4],
        reduced[5],
        reduced[6],
        reduced[7],
        reduced[8],
    )


def fast_body(
    inputs, segment_ids, attention_gain, query_weight, key_weight, value_weight, out_weight, feedforward_gain,
    gate_weight, up_weight, down_weight, cotangent,
):
    _, span_len, model_width = inputs.shape
    line_size, dp_size = lax.axis_size("tensor"), lax.axis_size("dp")
    half_dim = HEAD_DIM // 2
    frequency = rope_base ** (-2.0 * jnp.arange(half_dim, dtype=jnp.float32) / HEAD_DIM)
    frequency = jnp.tile(frequency, 4).reshape(1, 128)
    flat_inputs = inputs.reshape(span_len, model_width)
    upstream = cotangent.reshape(span_len, model_width)
    gain_one, gain_two = attention_gain.reshape(1, -1), feedforward_gain.reshape(1, -1)
    key_turned, value_turned = key_weight.T, value_weight.T
    (
        seg_row, cosine, signed_sine, query, kv, logs, mixed, normed, two, upstream_cols, up, inner, second, attended,
        middle, grad_middle, land_gate, land_up, own_gate, gain_grad,
    ) = front_call(
        line_size, dp_size,
        (
            flat_inputs, segment_ids, frequency, gain_one, gain_two, query_weight, key_turned, value_turned, out_weight,
            gate_weight, up_weight, down_weight, upstream,
        ),
    )
    (
        layer_out, grad_inputs, gains, own_qkv, own_out, own_up, own_down, land_up_last, land_down, land_qkv,
        land_out,
    ) = back_call(
        line_size, dp_size,
        (
            query, kv, logs, mixed, cosine, signed_sine, seg_row, flat_inputs, normed, two, upstream_cols,
            up, inner, second, attended, middle, grad_middle, gain_one, gain_grad,
            query_weight, key_turned, value_turned, out_weight,
        ),
    )
    layer_out, grad_inputs, gain_a, grad_query, grad_key, grad_value, grad_out, gain_b, *ffn = settle_call(
        (
            layer_out, grad_inputs, gains, own_qkv, own_out, own_gate, own_up, own_down,
            land_gate, land_up, land_up_last, land_down, land_qkv, land_out,
        )
    )
    shape = (1, span_len, model_width)
    return (
        layer_out.reshape(shape), grad_inputs.reshape(shape), gain_a[0], grad_query, grad_key.T, grad_value.T,
        grad_out, gain_b[0], *ffn,
    )


def body(mesh, *arrays):
    inputs = arrays[0]
    span_len, model_width = inputs.shape[1:]
    dp_size, ctx_size, line_size = mesh.shape["dp"], mesh.shape["ctx"], mesh.shape["tensor"]
    piece = model_width // (dp_size * ctx_size)
    fits = inputs.shape[0] == 1 and ctx_size == 2 and dp_size > 2 and line_size > 1
    if fits and piece % 128 == 0 and span_len % 512 == 0:
        return fast_body(*arrays)
    return plain_body(*arrays)


def solution(mesh):
    return jax.shard_map(
        functools.partial(body, mesh),
        mesh=mesh,
        in_specs=(
            P("dp", "ctx", None),
            P("dp", "ctx"),
            P(),
            P(None, "tensor"),
            P(None, "tensor"),
            P(None, "tensor"),
            P("tensor", None),
            P(),
            P(None, "tensor"),
            P(None, "tensor"),
            P("tensor", None),
            P("dp", "ctx", None),
        ),
        out_specs=(
            P("dp", "ctx", None),
            P("dp", "ctx", None),
            P(("dp", "ctx")),
            P(("dp", "ctx"), "tensor"),
            P(("dp", "ctx"), "tensor"),
            P(("dp", "ctx"), "tensor"),
            P("tensor", ("dp", "ctx")),
            P(("dp", "ctx")),
            P(("dp", "ctx"), "tensor"),
            P(("dp", "ctx"), "tensor"),
            P("tensor", ("dp", "ctx")),
        ),
        check_vma=False,
    )
```

```python
import functools
import math

import jax
import jax.numpy as jnp
from jax import lax
from jax.experimental import pallas as pl
from jax.experimental.pallas import tpu as pltpu
from jax.sharding import PartitionSpec as P

HEAD_DIM = 64


epsilon = 1e-05
rope_base = 10000.0
masked_score = -1e30


def positions_of(segment):
    token_index = jnp.arange(segment.shape[-1], dtype=jnp.int32)
    previous = jnp.concatenate([segment[..., :1] - 1, segment[..., :-1]], axis=-1)
    starts = jnp.where(segment != previous, token_index, 0)
    earlier = token_index[None, :] <= token_index[:, None]
    run_start = jnp.max(jnp.where(earlier, starts[..., None, :], 0), axis=-1)
    return token_index - run_start


MESH = pl.DeviceIdType.MESH
CHUNK, HOP = 16, 2
BACK_CHUNK, BACK_HOP = 32, 2
TASKS = 1
RINGS = [1, 2, 4]
MIB = 1 << 20
FRONT_MIB, BACK_MIB = 62, 62


def rotary_tables(positions):
    half_dim = HEAD_DIM // 2
    frequency = rope_base ** (-2.0 * jnp.arange(half_dim, dtype=jnp.float32) / HEAD_DIM)
    angles = positions.astype(jnp.float32)[..., None] * frequency
    return (jnp.cos(angles), jnp.sin(angles))


def rotate(values, cosine, sine_table):
    half_dim = values.shape[-1] // 2
    first = values[..., :half_dim]
    second = values[..., half_dim:]
    return jnp.concatenate(
        [first * cosine - second * sine_table, second * cosine + first * sine_table], axis=-1
    )


def visible(query_seg, key_seg, first_row):
    query_pos = first_row + jnp.arange(query_seg.shape[0], dtype=jnp.int32)
    key_pos = jnp.arange(key_seg.shape[0], dtype=jnp.int32)
    same_doc = query_seg[:, None] == key_seg[None, :]
    causal = key_pos[None, :] <= query_pos[:, None]
    usable = (key_seg[None, :] >= 0) | (key_pos[None, :] == query_pos[:, None])
    return same_doc & causal & usable


def turned_dot(left, right):
    return lax.dot_general(
        left, right, (((1,), (1,)), ((), ())), preferred_element_type=jnp.float32
    )


def remote(src, dst, send, recv, **device):
    return pltpu.make_async_remote_copy(
        src_ref=src, dst_ref=dst, send_sem=send, recv_sem=recv, device_id=device, device_id_type=MESH
    )


class Line:
    def __init__(self, line_size, own, finish, place, out_ref, held, acc_send, acc_recv, back_send, back_recv, base=0, hop=HOP):
        self.base, self.hop = base, hop
        self.last = line_size - 1
        self.here = lax.axis_index("tensor")
        self.own, self.finish, self.place = own, finish, place
        self.out_ref, self.held = out_ref, held
        self.acc_sems, self.back_sems = (acc_send, acc_recv), (back_send, back_recv)
        self.count, self.chunk = held.shape[1:3]

    def parts(self, stream):
        if stream == 0:
            return self.here, self.here + 1, self.here - 1
        return self.last - self.here, self.here - 1, self.here + 1

    def acc_copy(self, stream, i, target):
        at = i - self.base
        ref = self.held.at[stream, at]
        return remote(ref, ref, self.acc_sems[0].at[stream, at], self.acc_sems[1].at[stream, at], tensor=target)

    def rows_of(self, stream, i):
        return pl.ds(pl.multiple_of(self.place(stream, i), self.chunk), self.chunk)

    def back_copy(self, stream, i, target):
        at = i - self.base
        ref = self.out_ref.at[self.rows_of(stream, i)]
        return remote(ref, ref, self.back_sems[0].at[stream, at], self.back_sems[1].at[stream, at], tensor=target)

    def step(self, k, begin=0, size=None):
        size = self.count if size is None else size

        @pl.when((k >= 0) & (k < size + 2 * self.hop * self.last))
        def _():
            for stream in (0, 1):
                self.stream_step(k, stream, begin, size)

    def stream_step(self, k, stream, begin, size):
        last, held = self.last, self.held
        place, after, before = self.parts(stream)
        due = k - self.hop * place
        i = begin + due
        at = i - self.base

        @pl.when((due >= 0) & (due < size))
        def _():
            @pl.when(place == 0)
            def _():
                held[stream, at] = self.own(stream, i).astype(jnp.bfloat16)
                self.acc_copy(stream, i, after).start()

            @pl.when(place > 0)
            def _():
                self.acc_copy(stream, i, after).wait_recv()

                @pl.when(place < last)
                def _():
                    held[stream, at] = (held[stream, at].astype(jnp.float32) + self.own(stream, i)).astype(jnp.bfloat16)
                    self.acc_copy(stream, i, after).start()

                @pl.when(place == last)
                def _():
                    total = held[stream, at].astype(jnp.float32) + self.own(stream, i)
                    self.out_ref[self.rows_of(stream, i)] = self.finish(stream, i, total).astype(jnp.bfloat16)
                    self.back_copy(stream, i, before).start()

        back = k - self.hop * (2 * last - place)
        j = begin + back

        @pl.when((back >= 0) & (back < size) & (place < last))
        def _():
            self.back_copy(stream, j, before).wait_recv()

            @pl.when(place > 0)
            def _():
                self.back_copy(stream, j, before).start()

    def drain(self):
        def sent(at, carry):
            i = at + self.base
            for stream in (0, 1):
                place, after, before = self.parts(stream)

                @pl.when(place < self.last)
                def _():
                    self.acc_copy(stream, i, after).wait_send()

                @pl.when(place > 0)
                def _():
                    self.back_copy(stream, i, before).wait_send()

            return carry

        lax.fori_loop(0, self.count, sent, 0)


def line_scratch(rows, width, share=1, chunk=CHUNK):
    count = rows // 2 // chunk // share
    return [
        pltpu.VMEM((2, count, chunk, width), jnp.bfloat16),
        *[pltpu.SemaphoreType.DMA((2, count))] * 4,
    ]


def greet(line, core, plane, full_line=False):
    here, row, side = lax.axis_index("tensor"), lax.axis_index("dp"), lax.axis_index("ctx")
    barrier = pltpu.get_barrier_semaphore()
    peers = 0

    def call(**device):
        pl.semaphore_signal(barrier, inc=1, device_id=device, device_id_type=MESH)

    if full_line:
        for hop in range(1, line):
            call(tensor=lax.rem(here + hop, line))
        peers += line - 1
    else:

        @pl.when(here > 0)
        def _():
            call(tensor=here - 1)

        @pl.when(here < line - 1)
        def _():
            call(tensor=here + 1)

        peers = jnp.where(here > 0, 1, 0) + jnp.where(here < line - 1, 1, 0)
    if plane:
        for hop in range(1, 2 * plane):
            peer = lax.rem(2 * row + side + hop, 2 * plane)
            call(dp=peer // 2, ctx=lax.rem(peer, 2))
        peers += 2 * plane - 1
    elif core:
        call(ctx=1 - side)
        peers += 1
    return lambda: pl.semaphore_wait(barrier, peers)


def kept_rows(i, chunk=CHUNK):
    return pl.ds(pl.multiple_of(i * chunk, chunk), chunk)


def rotate_lanes(values, cosine, signed_sine, back=False):
    lane = lax.broadcasted_iota(jnp.int32, values.shape, 1)
    swapped = jnp.where(
        lax.rem(lane, HEAD_DIM) < HEAD_DIM // 2,
        pltpu.roll(values, 128 - HEAD_DIM // 2, 1),
        pltpu.roll(values, HEAD_DIM // 2, 1),
    )
    turn = swapped * signed_sine
    return values * cosine - turn if back else values * cosine + turn


def key_lanes(values, turned):
    lane = lax.broadcasted_iota(jnp.int32, values.shape, 1)
    return jnp.where(lane < HEAD_DIM, turned, values)


def fill_bias(bias, seg_col, seg_row, first, keys, block):
    key_seg = seg_col[0:keys]
    query_seg = seg_row[:, first : first + block]
    key_pos = lax.broadcasted_iota(jnp.int32, (keys, block), 0)
    query_pos = first + lax.broadcasted_iota(jnp.int32, (keys, block), 1)
    usable = (key_seg >= 0) | (key_pos == query_pos)
    allowed = (key_seg == query_seg) & (key_pos <= query_pos) & usable
    bias[0:keys, :] = jnp.where(allowed, 0.0, masked_score)


def wide_tiles(width):
    return width // 256, width % 256


def inverse_rms(values):
    return lax.rsqrt(jnp.mean(values * values, axis=-1, keepdims=True) + epsilon)


def front_kernel(
    n, dp_size,
    inputs_any, segments, frequency, gain_one, gain_two,
    query_weight_any, key_weight_any, value_weight_any, out_weight_any, gate_weight_any, up_weight_any, down_weight_any, upstream_any,
    seg_out, cosine_out, sine_out, query_out, kv_out, log_out, mixed_out, normed_cols, two_cols, upstream_cols, up_out, inner_out, second_out,
    attended_out, middle_out, grad_middle_out, land_gate, land_up, own_gate, gain_out,
    seg_all, seg_row, seg_col, cosine, signed_sine,
    inputs, normed, kv_weight, query, kv, kv_turned, logs, mixed, bias,
    gate_weight, up_weight, down_weight, upstream, grad_inner, normed_two, gate, up, inner,
    partial, middle, grad_middle, two_other, turned, send_gate, send_up,
    load_sems, store_sems, core_send, core_recv, plane_send, plane_recv, *line_refs,
):
    span, width = inputs.shape
    hidden, piece = gate.shape[1], turned.shape[0]
    row, core = lax.axis_index("dp"), lax.axis_index("ctx")
    half, block = span // 2, span // 4
    second, attended = normed, inputs
    line_one, line_two, line_three = line_refs[:5], line_refs[5:10], line_refs[10:]
    count, heads = line_one[0].shape[1], query.shape[1]
    part = count // 2

    def load(at, src, dst):
        made = pltpu.make_async_copy(src, dst, load_sems.at[at])
        made.start()
        return made

    def ordered(stream, i):
        return (i // part) * half + stream * block + lax.rem(i, part) * CHUNK

    def moved(at):
        return (0, 2, 1, 3)[at] * block

    load_inputs = load(0, inputs_any, inputs)
    query_weight = gate_weight.at[:, pl.ds(0, heads)]
    out_weight = down_weight.at[pl.ds(0, heads)]
    load_query = load(1, query_weight_any, query_weight)
    load_kv = [
        load(2, key_weight_any, kv_weight.at[pl.ds(0, HEAD_DIM)]),
        load(11, value_weight_any, kv_weight.at[pl.ds(HEAD_DIM, HEAD_DIM)]),
    ]
    load_out = load(3, out_weight_any, out_weight)
    load_up = [
        load(4 + b, upstream_any.at[pl.ds(b * block, block)], upstream.at[pl.ds(moved(b), block)]) for b in range(4)
    ]
    load_up_weight = load(10, up_weight_any, up_weight)
    seg_all[core] = jnp.broadcast_to(segments[...], seg_all.shape[1:])
    meet = greet(n, True, dp_size)

    def seg_copy():
        return remote(seg_all.at[core], seg_all.at[core], core_send.at[1], core_recv.at[1], ctx=1 - core)

    load_inputs.wait()

    def norm_rows(b, carry):
        rows = pl.ds(pl.multiple_of(b * 64, 64), 64)
        value = inputs[rows].astype(jnp.float32)
        normed[rows] = (value * inverse_rms(value) * gain_one[...]).astype(jnp.bfloat16)
        return carry

    lax.fori_loop(0, span // 64, norm_rows, 0)
    meet()
    seg_copy().start()
    for made in load_kv:
        made.wait()
    raw_kv = turned_dot(normed[...], kv_weight[...])
    load_query.wait()
    for low in range(0, span, half):
        rows = slice(low, low + half)
        partial[rows, 0:heads] = jnp.dot(normed[rows], query_weight[...], preferred_element_type=jnp.float32)
    load_gate = load(9, gate_weight_any, gate_weight)
    seg_copy().wait()
    for side in (0, 1):
        seg_row[:, side * span : (side + 1) * span] = seg_all[side, 0:1]
        seg_col[side * span : (side + 1) * span] = seg_all[side].T[:, 0:1]
    own_seg = seg_all[core, 0:1]
    key_pos = lax.broadcasted_iota(jnp.int32, (2 * span, span), 0)
    query_pos = core * span + lax.broadcasted_iota(jnp.int32, (2 * span, span), 1)
    before = (seg_col[...] == own_seg) & (key_pos < query_pos)
    position = jnp.sum(jnp.where(before, 1.0, 0.0), axis=0, keepdims=True)
    angles = jnp.broadcast_to(position, (8, span)).T[:, 0:1] * frequency[...]
    lane = lax.broadcasted_iota(jnp.int32, angles.shape, 1)
    cosine[...] = jnp.cos(angles)
    sine = jnp.sin(angles)
    signed_sine[...] = jnp.where(lax.rem(lane, HEAD_DIM) < HEAD_DIM // 2, -sine, sine)
    own_rows = pl.ds(pl.multiple_of(core * span, span), span)
    kv[own_rows] = key_lanes(raw_kv, rotate_lanes(raw_kv, cosine[...], signed_sine[...])).astype(jnp.bfloat16)

    def kv_copy():
        return remote(kv.at[own_rows], kv.at[own_rows], core_send.at[0], core_recv.at[0], ctx=1 - core)

    def kv_arrival():
        rows = pl.ds(0, span)
        return remote(kv.at[rows], kv.at[rows], core_send.at[0], core_recv.at[0], ctx=1 - core)

    @pl.when(core == 0)
    def _():
        kv_copy().start()

    for lanes in range(0, heads, 128):
        rotated = rotate_lanes(partial[:, lanes : lanes + 128], cosine[...], signed_sine[...])
        query[:, lanes : lanes + 128] = rotated.astype(jnp.bfloat16) * (HEAD_DIM ** -0.5)

    @pl.when(core == 1)
    def _():
        kv_arrival().wait_recv()

    kv_turned[...] = kv[...].T

    def attend(side, at):
        keys = side * span + (at + 1) * half
        rows = slice(at * half, (at + 1) * half)
        fill_bias(bias, seg_col, seg_row, side * span + at * half, keys, half)

        def pair(index, carry):
            lanes = pl.ds(pl.multiple_of(index * 128, 128), 128)
            both = query[rows, lanes]
            outs = []
            for which in (0, 1):
                scores = turned_dot(kv[0:keys, 0:HEAD_DIM], both[:, which * HEAD_DIM : (which + 1) * HEAD_DIM])
                scores = scores + bias[0:keys, :]
                peak = jnp.max(scores, axis=0, keepdims=True)
                grown = jnp.exp(scores - peak)
                total = jnp.sum(grown, axis=0, keepdims=True)
                logs[pl.ds(2 * index + which, 1), rows] = peak + jnp.log(total)
                out = jnp.dot(
                    kv_turned[HEAD_DIM : 2 * HEAD_DIM, 0:keys],
                    grown.astype(jnp.bfloat16),
                    preferred_element_type=jnp.float32,
                )
                outs.append(out / total)
            mixed[rows, lanes] = jnp.concatenate(outs, axis=0).T.astype(jnp.bfloat16)
            return carry

        lax.fori_loop(0, query.shape[1] // 128, pair, 0)

    for side in (0, 1):

        @pl.when(core == side)
        def _():
            attend(side, 0)
            attend(side, 1)

    load_out.wait()

    def out_tile(t, carry):
        columns = pl.ds(pl.multiple_of(t * 512, 512), 512)
        for b in (0, 2):
            value = jnp.dot(
                mixed[b * block : (b + 2) * block], out_weight[:, columns], preferred_element_type=jnp.float32
            )
            partial[moved(b) : moved(b) + block, columns] = value[:block]
            partial[moved(b + 1) : moved(b + 1) + block, columns] = value[block:]
        return carry

    lax.fori_loop(0, width // 512, out_tile, 0)
    load_down = load(8, down_weight_any, down_weight)

    def rows_at(start):
        return pl.ds(pl.multiple_of(start, CHUNK), CHUNK)

    def own(stream, i):
        return partial[rows_at(ordered(stream, i))]

    def finish_one(stream, i, total):
        value = inputs[rows_at((stream * count + i) * CHUNK)].astype(jnp.float32) + total
        middle[kept_rows(i)] = value
        return value * inverse_rms(value) * gain_two[...]

    gain_out[...] = jnp.zeros_like(gain_out)

    def finish_two(stream, i, total):
        value = middle[kept_rows(i)]
        inverse = inverse_rms(value)
        unit = value * inverse
        gain_out[0:1, :] += jnp.sum(total * unit, axis=0, keepdims=True)
        scaled = total * gain_two[...]
        result = upstream[rows_at(ordered(stream, i))].astype(jnp.float32) + inverse * (
            scaled - unit * jnp.mean(scaled * unit, axis=-1, keepdims=True)
        )
        grad_middle[kept_rows(i)] = result
        return result

    first = Line(n, own, finish_one, ordered, normed_two, *line_one)
    then = Line(n, own, finish_two, ordered, attended, *line_two)
    third = Line(
        n,
        lambda stream, i: second[rows_at(ordered(stream, i))].astype(jnp.float32),
        lambda stream, i, total: middle[kept_rows(i)] + total,
        ordered, second, *line_three,
    )
    tiles, rest = wide_tiles(hidden)
    tile_count = tiles + (1 if rest else 0)

    def each_tile(t, work):
        @pl.when(t < tiles)
        def _():
            work(pl.ds(pl.multiple_of(t * 256, 256), 256))

        if rest:

            @pl.when(t == tiles)
            def _():
                work(pl.ds(tiles * 256, rest))

    def inner_tile(columns):
        grad_inner[:, columns] = turned_dot(upstream[...], down_weight[columns, :])

    def forward_tile(rows, columns):
        gated = jnp.dot(normed_two[rows], gate_weight[:, columns], preferred_element_type=jnp.float32)
        upped = jnp.dot(normed_two[rows], up_weight[:, columns], preferred_element_type=jnp.float32)
        sig = jax.nn.sigmoid(gated)
        act = gated * sig
        grad = grad_inner[rows, columns]
        inner[rows, columns] = (act * upped).astype(jnp.bfloat16)
        up[rows, columns] = (grad * act).astype(jnp.bfloat16)
        gate[rows, columns] = (grad * upped * sig * (1.0 + gated * (1.0 - sig))).astype(jnp.bfloat16)

    def back_tile(rows, t):
        columns = pl.ds(pl.multiple_of(t * 512, 512), 512)
        partial[rows, columns] = turned_dot(gate[rows], gate_weight[columns, :]) + turned_dot(
            up[rows], up_weight[columns, :]
        )

    def second_tile(rows, t):
        columns = pl.ds(pl.multiple_of(t * 512, 512), 512)
        second[rows, columns] = jnp.dot(
            inner[rows], down_weight[:, columns], preferred_element_type=jnp.float32
        ).astype(jnp.bfloat16)

    last = n - 1
    trip = 2 * HOP * last
    each = 2
    forward_steps, back_steps = -(-tile_count // each), width // 1024
    work = forward_steps + back_steps
    base_one = part + trip
    second_steps = width // 1024
    base_two = max(count + trip, base_one + work + second_steps)
    third_base = base_one + work + second_steps
    steps = max(base_two + work + part + trip, third_base + part + trip)

    def store(at, src, dst):
        return pltpu.make_async_copy(src, dst, store_sems.at[at])

    def stores(at, src, dst):
        return [
            store(at + b, src.at[pl.ds(moved(b), block)], dst.at[pl.ds(b * block, block)]) for b in range(4)
        ]

    early = [
        store(0, query, query_out), store(1, kv, kv_out), store(2, logs, log_out), store(3, mixed, mixed_out.at[pl.ds(0, span)]),
        store(31, seg_row, seg_out), store(32, cosine, cosine_out),
        store(33, signed_sine, sine_out),
    ]
    own_slots, far_slots = [], []

    def own_columns(src, dst):
        made = []
        for q in range(dp_size):
            columns = pl.ds(pl.multiple_of((2 * q + core) * piece, piece), piece)
            at = 34 + len(own_slots)
            own_slots.append(at)
            made.append(store(at, src.at[:, columns], dst.at[pl.ds(0, span), pl.ds(q * piece, piece)]))
        return made

    def far_copy(src, dst):
        at = 3 + dp_size + len(far_slots)
        far_slots.append(at)
        return remote(src, dst, core_send.at[at], core_recv.at[at], ctx=1 - core)

    def far_columns(src, dst):
        made = []
        for q in range(dp_size):
            columns = pl.ds(pl.multiple_of((2 * q + 1 - core) * piece, piece), piece)
            made.append(far_copy(src.at[:, columns], dst.at[pl.ds(span, span), pl.ds(q * piece, piece)]))
        return made

    normed_moves = [*own_columns(normed, normed_cols), *far_columns(normed, normed_cols)]
    upstream_moves = [*own_columns(upstream, upstream_cols), *far_columns(upstream, upstream_cols)]
    mixed_move = far_copy(mixed, mixed_out.at[pl.ds(span, span)])
    hidden_moves = [
        store(6, inner, inner_out.at[pl.ds(0, span)]), far_copy(inner, inner_out.at[pl.ds(span, span)]),
        *own_columns(normed_two, two_cols),
    ]
    up_slot = 3 + dp_size + len(far_slots)
    two_moves = [store(7, two_other, two_cols.at[pl.ds(span, span)]), store(5, up, up_out)]
    second_stores, attended_stores = stores(21, second, second_out), stores(25, attended, attended_out)
    middle_store = store(29, middle, middle_out)

    def gate_swaps():
        made = [
            remote(
                ref.at[pl.ds(0, span)], ref.at[pl.ds(span, span)], core_send.at[at], core_recv.at[at], ctx=1 - core
            )
            for ref, at in ((gate, 2), (up, up_slot))
        ]
        for q in range(dp_size):
            columns = pl.ds(pl.multiple_of((2 * q + 1 - core) * piece, piece), piece)
            made.append(
                remote(
                    normed_two.at[:, columns], two_other.at[:, pl.ds(q * piece, piece)],
                    core_send.at[3 + q], core_recv.at[3 + q], ctx=1 - core,
                )
            )
        return made

    def peer_of(r):
        return lax.rem(row + 1 + r, dp_size)

    sends, lands = (send_gate, send_up), (land_gate, land_up)

    def gate_copy(w, r):
        return remote(sends[w].at[r], lands[w].at[r], plane_send.at[w, r], plane_recv.at[w, r], dp=peer_of(r))

    def turn_two(r):
        peer = peer_of(r)
        columns = pl.ds(pl.multiple_of((2 * peer + core) * piece, piece), piece)
        turned[:, 0:span] = normed_two[:, columns].T
        turned[:, span : 2 * span] = two_other[:, pl.ds(pl.multiple_of(peer * piece, piece), piece)].T

    edges = [(low, min(low + 384, hidden)) for low in range(0, hidden, 384)]

    def gate_piece(w, r):
        for low, high in edges:
            sends[w][r, :, low:high] = jnp.dot(
                turned[...], (gate, up)[w][:, low:high], preferred_element_type=jnp.float32
            ).astype(jnp.bfloat16)
        gate_copy(w, r).start()

    def own_piece():
        for low, high in edges:
            partial[0:piece, low:high] = jnp.dot(turned[...], gate[:, low:high], preferred_element_type=jnp.float32)

    own_store = store(4, partial.at[pl.ds(0, piece), pl.ds(0, hidden)], own_gate)

    for made in [*early, *normed_moves, mixed_move]:
        made.start()

    def step(k, carry):
        first.step(k)
        if base_two == base_one + part:
            then.step(k - (base_one + work))
        else:
            then.step(k - (base_one + work), 0, part)
            then.step(k - (base_two + work), part, part)
        third.step(k - third_base)

        @pl.when(k == 0)
        def _():
            for made in load_up:
                made.wait()
            for made in upstream_moves:
                made.start()

        @pl.when(k == 2)
        def _():
            load_down.wait()
            load_gate.wait()
            load_up_weight.wait()

        @pl.when((k >= 2) & (k < 2 + tile_count))
        def _():
            each_tile(k - 2, inner_tile)

        @pl.when(k == base_one)
        def _():
            for made in normed_moves:
                made.wait()

        @pl.when(k == base_two)
        def _():
            middle_store.start()

        late = jnp.where(k >= base_two, 1, 0)
        phase = k - jnp.where(k >= base_two, base_two, base_one)
        rows = pl.ds(pl.multiple_of(late * half, half), half)

        @pl.when((phase >= 0) & (phase < forward_steps))
        def _():
            def tile(t, carry):
                each_tile(t, functools.partial(forward_tile, rows))
                return carry

            lax.fori_loop(phase * each, jnp.minimum((phase + 1) * each, tile_count), tile, 0)

        @pl.when((phase >= forward_steps) & (phase < work))
        def _():
            for t in (0, 1):
                back_tile(rows, 2 * (phase - forward_steps) + t)

        @pl.when((phase >= work) & (phase < work + second_steps))
        def _():
            for t in (0, 1):
                second_tile(rows, 2 * (phase - work) + t)

        @pl.when(k == base_two + work)
        def _():
            for made in hidden_moves:
                made.start()

        @pl.when(k == base_two + forward_steps)
        def _():
            for made in gate_swaps():
                made.start()

        @pl.when(k == base_two + work)
        def _():
            for made in gate_swaps():
                made.wait()
            for made in two_moves:
                made.start()

        gate_task = k - (base_two + work)

        @pl.when((gate_task >= 0) & (gate_task < dp_size - 1))
        def _():
            turn_two(gate_task)
            gate_piece(0, gate_task)

            @pl.when(gate_task < dp_size - 2)
            def _():
                gate_piece(1, gate_task)

        @pl.when(k == base_two + work + part + HOP * last)
        def _():
            turn_two(dp_size - 1)
            own_piece()
            own_store.start()

        @pl.when(k == base_two + work + second_steps)
        def _():
            for b in (1, 3):
                second_stores[b].start()

        @pl.when(k == max(base_one + work, third_base) + part + trip)
        def _():
            for b in (0, 2):
                second_stores[b].start()
                attended_stores[b].start()

        return carry

    lax.fori_loop(0, steps, step, 0)
    late_stores = [
        attended_stores[1], attended_stores[3], store(30, grad_middle, grad_middle_out),
    ]
    for made in late_stores:
        made.start()
    first.drain()
    then.drain()
    third.drain()

    @pl.when(core == 0)
    def _():
        kv_copy().wait_send()

    for r in range(dp_size - 1):
        for w in ((0, 1) if r < dp_size - 2 else (0,)):
            gate_copy(w, r).wait()
    for made in [
        *early, mixed_move, *upstream_moves, *hidden_moves, *two_moves, own_store, middle_store, *second_stores,
        attended_stores[0], attended_stores[2], *late_stores,
    ]:
        made.wait()


def front_call(line_size, dp_size, operands):
    inputs = operands[0]
    query_weight, out_weight, gate_weight = operands[5], operands[8], operands[9]
    span, width = inputs.shape
    heads, hidden = query_weight.shape[1], gate_weight.shape[1]
    piece = width // (2 * dp_size)
    low, full = jnp.bfloat16, jnp.float32
    vmem, outside = pl.BlockSpec(memory_space=pltpu.VMEM), pl.BlockSpec(memory_space=pl.ANY)
    dma = pltpu.SemaphoreType.DMA
    outs = [
        ((1, 2 * span), jnp.int32), ((span, 128), full), ((span, 128), full),
        ((span, heads), low), ((2 * span, 128), low), ((heads // HEAD_DIM, span), full), ((2 * span, heads), low),
        *[((2 * span, width // 2), low)] * 3, *[((2 * span, hidden), low)] * 2, ((span, width), low),
        ((span, width), low), ((span // 2, width), full), ((span // 2, width), full),
        ((dp_size - 1, piece, hidden), low), ((dp_size - 2, piece, hidden), low), ((piece, hidden), full), ((8, width), full),
    ]
    scratch = [
        pltpu.VMEM((2, 8, span), jnp.int32), pltpu.VMEM((1, 2 * span), jnp.int32),
        pltpu.VMEM((2 * span, 1), jnp.int32), pltpu.VMEM((span, 128), full), pltpu.VMEM((span, 128), full),
        pltpu.VMEM((span, width), low), pltpu.VMEM((span, width), low),
        pltpu.VMEM((128, width), low), pltpu.VMEM((span, heads), low),
        pltpu.VMEM((2 * span, 128), low), pltpu.VMEM((128, 2 * span), low),
        pltpu.VMEM((heads // HEAD_DIM, span), full), pltpu.VMEM((span, heads), low),
        pltpu.VMEM((2 * span, span // 2), full),
        pltpu.VMEM((width, hidden), low), pltpu.VMEM((width, hidden), low), pltpu.VMEM((hidden, width), low),
        pltpu.VMEM((span, width), low), pltpu.VMEM((span, hidden), full), pltpu.VMEM((span, width), low),
        *[pltpu.VMEM((2 * span, hidden), low)] * 2, pltpu.VMEM((span, hidden), low),
        pltpu.VMEM((span, width), full),
        pltpu.VMEM((span // 2, width), full), pltpu.VMEM((span // 2, width), full),
        pltpu.VMEM((span, width // 2), low), pltpu.VMEM((piece, 2 * span), low),
        pltpu.VMEM((dp_size - 1, piece, hidden), low), pltpu.VMEM((dp_size - 2, piece, hidden), low),
        dma((12,)), dma((34 + 3 * dp_size,)), dma((6 + 3 * dp_size,)), dma((6 + 3 * dp_size,)),
        dma((2, dp_size - 1)), dma((2, dp_size - 1)),
        *line_scratch(span, width), *line_scratch(span, width), *line_scratch(span, width, 2),
    ]
    return pl.pallas_call(
        functools.partial(front_kernel, line_size, dp_size),
        out_shape=[jax.ShapeDtypeStruct(s, d) for s, d in outs],
        in_specs=[outside] + [vmem] * 4 + [outside] * 8,
        out_specs=[outside] * 19 + [vmem],
        scratch_shapes=scratch,
        compiler_params=pltpu.CompilerParams(
            collective_id=1, has_side_effects=True, vmem_limit_bytes=FRONT_MIB * MIB
        ),
    )(*operands)


def back_kernel(
    n, dp_size,
    query_any, kv_any, logs, mixed_any, cosine, signed_sine, seg_row, inputs_any, normed_any, two_any, upstream_any,
    up_any, inner_any, second_any, attended_any, middle_any, grad_middle_any, gain_one, gain_two_grad,
    query_weight_any, key_weight_any, value_weight_any, out_weight_any,
    layer_out, grad_inputs, grad_gains, grad_qkv, own_out, grad_up, own_down,
    land_up, land_down, land_qkv, land_out,
    query, kv, kv_turned, grad_mixed, mixed, attended, normed_cols, two_cols, upstream_cols, attended_other,
    up, inner, pre, query_weight, kv_weight, out_weight, grad_middle, middle, inputs,
    ring, send_qkv, send_out, turned, seg_col, bias, kv_grad, kv_grad_other,
    gain_line, gain_land, gain_sum, gain_plane,
    load_sems, core_send, core_recv, ring_send, ring_recv, plane_send, plane_recv, line_send, line_recv,
    spread_send, spread_recv, *line_refs,
):
    span, width = attended.shape
    heads, piece = query.shape[1], turned.shape[0]
    here, row, core = lax.axis_index("tensor"), lax.axis_index("dp"), lax.axis_index("ctx")
    half = span // 2
    line_out, line_in = line_refs[:5], line_refs[5:]
    count, part = line_in[0].shape[1], line_out[0].shape[1]
    last = n - 1
    loads = []

    def load(src, dst):
        made = pltpu.make_async_copy(src, dst, load_sems.at[len(loads)])
        made.start()
        loads.append(made)
        return made

    own_half = pl.ds(pl.multiple_of(jnp.where(here == 0, half, 0), half), half)
    mixed_loads = [load(attended_any, attended), load(out_weight_any, out_weight)]
    attend_loads = [load(query_any, query), load(kv_any, kv), load(mixed_any, mixed)]
    line_loads = [load(second_any, layer_out), load(middle_any, middle)]

    up_loads = [load(two_any, two_cols), load(up_any, up)]
    inner_loads = [load(upstream_any, upstream_cols), load(inner_any, inner)]
    late_loads = [
        load(query_weight_any, query_weight), load(key_weight_any, kv_weight.at[pl.ds(0, HEAD_DIM)]),
        load(value_weight_any, kv_weight.at[pl.ds(HEAD_DIM, HEAD_DIM)]),
        load(grad_middle_any, grad_middle), load(inputs_any.at[own_half], inputs),
        load(normed_any, normed_cols),
    ]
    meet = greet(n, True, dp_size, full_line=True)
    pre_slot, kv_slot = dp_size, dp_size + 1

    def attended_swaps():
        made = []
        for q in range(dp_size):
            columns = pl.ds(pl.multiple_of((2 * q + 1 - core) * piece, piece), piece)
            made.append(
                remote(
                    attended.at[:, columns], attended_other.at[:, pl.ds(q * piece, piece)],
                    core_send.at[q], core_recv.at[q], ctx=1 - core,
                )
            )
        return made

    def pre_swap():
        return remote(
            pre.at[pl.ds(0, span)], pre.at[pl.ds(span, span)], core_send.at[pre_slot], core_recv.at[pre_slot],
            ctx=1 - core,
        )

    def kv_swap():
        return remote(
            kv_grad.at[pl.ds(0, span)], kv_grad_other, core_send.at[kv_slot], core_recv.at[kv_slot], ctx=1 - core
        )

    gain_line[...] = jnp.zeros_like(gain_line)
    gain_line[1:2, :] = gain_two_grad[0:1, :]
    kv_grad[...] = jnp.zeros_like(kv_grad)
    seg_col[...] = jnp.broadcast_to(seg_row[...], (8, 2 * span)).T[:, 0:1]
    for made in [*mixed_loads, *attend_loads]:
        made.wait()
    kv_turned[...] = kv[...].T
    grad_mixed[...] = turned_dot(attended[...], out_weight[...]).astype(jnp.bfloat16)
    for made in line_loads:
        made.wait()
    meet()
    for made in attended_swaps():
        made.start()

    def rows_at(start):
        return pl.ds(pl.multiple_of(start, BACK_CHUNK), BACK_CHUNK)

    def plain(stream, i):
        return (stream * count + i) * BACK_CHUNK

    def finish_out(stream, i, total):
        return middle[kept_rows(i, BACK_CHUNK)] + total

    def finish_in(stream, i, total):
        hidden = inputs[kept_rows(i, BACK_CHUNK)].astype(jnp.float32)
        inverse = inverse_rms(hidden)
        unit = hidden * inverse
        gain_line[0:1, :] += jnp.sum(total * unit, axis=0, keepdims=True)
        scaled = total * gain_one[...]
        return grad_middle[kept_rows(i, BACK_CHUNK)] + inverse * (
            scaled - unit * jnp.mean(scaled * unit, axis=-1, keepdims=True)
        )

    out_line = Line(
        n, lambda s, i: layer_out[rows_at(plain(s, i))].astype(jnp.float32), finish_out, plain, layer_out, *line_out,
        base=count - part, hop=BACK_HOP,
    )
    in_line = Line(
        n, lambda s, i: grad_inputs[rows_at(plain(s, i))].astype(jnp.float32), finish_in, plain, grad_inputs, *line_in,
        hop=BACK_HOP,
    )

    def attend_back(side, at, index):
        keys = side * span + (at + 1) * half
        rows = slice(at * half, (at + 1) * half)
        lanes = pl.ds(pl.multiple_of(index * 128, 128), 128)

        @pl.when(index == 0)
        def _():
            fill_bias(bias, seg_col, seg_row, side * span + at * half, keys, half)

        both_query, both_grad = query[rows, lanes], grad_mixed[rows, lanes]
        shared = (both_grad.astype(jnp.float32) * mixed[rows, lanes].astype(jnp.float32)).T
        outs, parts = [], None
        for which in (0, 1):
            head = slice(which * HEAD_DIM, (which + 1) * HEAD_DIM)
            query_head, grad_head = both_query[:, head], both_grad[:, head]
            scores = turned_dot(kv[0:keys, 0:HEAD_DIM], query_head) + bias[0:keys, :]
            probs = jnp.exp(scores - logs[pl.ds(2 * index + which, 1), rows])
            grad_probs = turned_dot(kv[0:keys, HEAD_DIM : 2 * HEAD_DIM], grad_head)
            row_dot = jnp.sum(shared[head], axis=0, keepdims=True)
            grad_scores = (probs * (grad_probs - row_dot)).astype(jnp.bfloat16)
            grad_key = jnp.dot(grad_scores, query_head, preferred_element_type=jnp.float32)
            grad_value = jnp.dot(probs.astype(jnp.bfloat16), grad_head, preferred_element_type=jnp.float32)
            part = jnp.concatenate([grad_key, grad_value], axis=1)
            parts = part if parts is None else parts + part
            outs.append(
                jnp.dot(kv_turned[0:HEAD_DIM, 0:keys], grad_scores, preferred_element_type=jnp.float32)
            )
        kv_grad[0:keys] += parts
        grad_query = jnp.concatenate(outs, axis=0).T * (HEAD_DIM ** -0.5)
        pre[rows, lanes] = rotate_lanes(grad_query, cosine[rows], signed_sine[rows], back=True).astype(jnp.bfloat16)

    pairs = heads // 128
    tasks = 2 * pairs

    def attend_task(task):
        for side in (0, 1):
            for at in (0, 1):

                @pl.when((core == side) & (task // pairs == at))
                def _():
                    attend_back(side, at, lax.rem(task, pairs))

    own_grad = pl.ds(pl.multiple_of(core * span, span), span)

    def finish_pre():
        @pl.when(core == 0)
        def _():
            kv_swap().wait_recv()
            kv_grad[0:span] += kv_grad_other[...]

        raw = kv_grad[own_grad]
        turned_back = rotate_lanes(raw, cosine[...], signed_sine[...], back=True)
        pre[0:span, heads : heads + 128] = key_lanes(raw, turned_back).astype(jnp.bfloat16)

    def in_products():
        def tile(t, carry):
            columns = pl.ds(pl.multiple_of(t * 512, 512), 512)
            for low in (0, half):
                rows = slice(low, low + half)
                grad_inputs[rows, columns] = (
                    turned_dot(pre[rows, 0:heads], query_weight[columns, :])
                    + jnp.dot(
                        pre[rows, heads : heads + 128], kv_weight[:, columns], preferred_element_type=jnp.float32
                    )
                ).astype(jnp.bfloat16)
            return carry

        lax.fori_loop(0, width // 512, tile, 0)

    def peer_of(r):
        return lax.rem(row + 1 + r, dp_size)

    def turn(r, cols):
        block = pl.multiple_of(peer_of(r) * piece, piece)
        turned[...] = cols[:, pl.ds(block, piece)].T

    def turn_attended(r):
        peer = peer_of(r)
        columns = pl.ds(pl.multiple_of((2 * peer + core) * piece, piece), piece)
        turned[:, 0:span] = attended[:, columns].T
        turned[:, span : 2 * span] = attended_other[:, pl.ds(pl.multiple_of(peer * piece, piece), piece)].T

    def tiles_of(stacked):
        wide = stacked.shape[1]
        return [(low, min(low + 384, wide)) for low in range(0, wide, 384)]

    def piece_value(stacked, low, high):
        return jnp.dot(turned[...], stacked[:, low:high], preferred_element_type=jnp.float32)

    others = dp_size - 1

    def ring_copy(at):
        r = others - 1 if at == 0 else at - 1
        land = land_up.at[0] if at == 0 else land_down.at[at - 1]
        return remote(ring.at[at], land, ring_send.at[at], ring_recv.at[at], dp=peer_of(r))

    def ring_piece(at, cols, stacked):
        turn(others - 1 if at == 0 else at - 1, cols)
        for low, high in tiles_of(stacked):
            ring[at, :, low:high] = piece_value(stacked, low, high).astype(jnp.bfloat16)
        ring_copy(at).start()

    def kept_piece(cols, stacked, own):
        turn(others, cols)
        for low, high in tiles_of(stacked):
            own[:, low:high] = piece_value(stacked, low, high)

    sends, lands = (send_qkv, send_out), (land_qkv, land_out)

    def plane_copy(w, r):
        return remote(sends[w].at[r], lands[w].at[r], plane_send.at[w, r], plane_recv.at[w, r], dp=peer_of(r))

    def plane_piece(w, r, stacked, own):
        @pl.when(r < dp_size - 1)
        def _():
            for low, high in tiles_of(stacked):
                sends[w][r, :, low:high] = piece_value(stacked, low, high).astype(jnp.bfloat16)
            plane_copy(w, r).start()

        @pl.when(r == dp_size - 1)
        def _():
            for low, high in tiles_of(stacked):
                own[:, low:high] = piece_value(stacked, low, high)

    def line_copies(owner, hops):
        slot = 0 if owner == 0 else 1
        return [
            remote(
                gain_line, gain_land.at[slot], line_send.at[slot, hop - 1], line_recv.at[slot],
                tensor=owner + hop if owner == 0 else owner - hop,
            )
            for hop in hops
        ]

    shard = width // (2 * dp_size)
    shards = 2 * dp_size
    place = 2 * row + core

    def spread(r):
        peer = lax.rem(place + 1 + r, shards)
        block = pl.multiple_of(peer * shard, shard)
        return remote(
            gain_sum.at[:, pl.ds(block, shard)], gain_plane.at[r], spread_send.at[r], spread_recv.at[r],
            dp=peer // 2, ctx=lax.rem(peer, 2),
        )

    def gather_gains():
        gain_sum[...] = jnp.zeros_like(gain_sum)
        for owner in (0, last):
            slot = 0 if owner == 0 else 1

            @pl.when(here == owner)
            def _():
                gain_sum[...] += gain_line[...]

            @pl.when(here != owner)
            def _():
                line_copies(owner, (1,))[0].wait_recv()
                gain_sum[...] += gain_land[slot]
        for r in range(shards - 1):
            spread(r).start()

    attend_steps = tasks // TASKS
    lag = attend_steps + 2
    ring_steps = RINGS + [lag + at for at in range(dp_size - 3)]
    out_base = lag + 1
    steps = max(lag + count + 2 * BACK_HOP * last, out_base + 2 * dp_size)

    def step(k, carry):
        out_line.step(k, count - part, part)
        in_line.step(k - lag)

        @pl.when((k >= 1) & (k <= attend_steps))
        def _():
            def task(more, carry):
                attend_task(TASKS * (k - 1) + more)
                return carry

            lax.fori_loop(0, TASKS, task, 0)

        @pl.when((k == attend_steps) & (core == 1))
        def _():
            kv_swap().start()

        @pl.when(k == 1)
        def _():
            for made in up_loads:
                made.wait()

        @pl.when(k == ring_steps[1])
        def _():
            for made in inner_loads:
                made.wait()

        @pl.when(k == attend_steps)
        def _():
            for made in [*late_loads, *attended_swaps()]:
                made.wait()

        @pl.when(k == attend_steps + 1)
        def _():
            finish_pre()
            in_products()
            pre_swap().start()

        for at in range(dp_size):

            @pl.when(k == ring_steps[at])
            def _():
                ring_piece(at, *((two_cols, up) if at == 0 else (upstream_cols, inner)))

        @pl.when(k == lag + dp_size)
        def _():
            kept_piece(two_cols, up, grad_up)

        @pl.when(k == lag + dp_size + 1)
        def _():
            kept_piece(upstream_cols, inner, own_down)

        @pl.when(k == out_base)
        def _():
            pre_swap().wait()

        at, kind = (k - out_base) // 2, lax.rem(k - out_base, 2)

        @pl.when((k >= out_base) & (at < dp_size) & (kind == 0))
        def _():
            turn_attended(at)
            plane_piece(1, at, mixed, own_out)

        @pl.when((k >= out_base) & (at < dp_size) & (kind == 1))
        def _():
            turn(at, normed_cols)
            plane_piece(0, at, pre, grad_qkv)

        @pl.when(k == lag + count + BACK_HOP * last - 1)
        def _():
            for owner in (0, last):

                @pl.when(here == owner)
                def _():
                    for made in line_copies(owner, range(1, n)):
                        made.start()

        @pl.when(k == min(lag + count + BACK_HOP * last + 3, steps - 1))
        def _():
            gather_gains()

        return carry

    lax.fori_loop(0, steps, step, 0)
    out_line.drain()
    in_line.drain()

    @pl.when(core == 1)
    def _():
        kv_swap().wait_send()

    for at in range(dp_size):
        ring_copy(at).wait()
    for r in range(others):
        for w in (0, 1):
            plane_copy(w, r).wait()
    grad_gains[...] = gain_sum[:, pl.ds(pl.multiple_of(place * shard, shard), shard)]
    for r in range(shards - 1):
        spread(r).wait()
        grad_gains[...] += gain_plane[r]
    for owner in (0, last):

        @pl.when(here == owner)
        def _():
            for made in line_copies(owner, range(1, n)):
                made.wait_send()


def back_call(line_size, dp_size, operands):
    query = operands[0]
    span, heads = query.shape
    width, hidden = operands[7].shape[1], operands[11].shape[1]
    piece = width // (2 * dp_size)
    wide = heads + 128
    low, full = jnp.bfloat16, jnp.float32
    vmem, outside = pl.BlockSpec(memory_space=pltpu.VMEM), pl.BlockSpec(memory_space=pl.ANY)
    dma = pltpu.SemaphoreType.DMA
    others = dp_size - 1
    outs = [
        ((span, width), low), ((span, width), low), ((8, piece), full), ((piece, wide), full), ((piece, heads), full),
        ((piece, hidden), full), ((piece, hidden), full),
        ((1, piece, hidden), low), ((others, piece, hidden), low), ((others, piece, wide), low), ((others, piece, heads), low),
    ]
    core_copies = dp_size + 2
    scratch = [
        pltpu.VMEM((span, heads), low), pltpu.VMEM((2 * span, 128), low), pltpu.VMEM((128, 2 * span), low),
        pltpu.VMEM((span, heads), low), pltpu.VMEM((2 * span, heads), low), pltpu.VMEM((span, width), low),
        *[pltpu.VMEM((2 * span, width // 2), low)] * 3, pltpu.VMEM((span, width // 2), low),
        *[pltpu.VMEM((2 * span, hidden), low)] * 2, pltpu.VMEM((2 * span, wide), low),
        pltpu.VMEM((width, heads), low), pltpu.VMEM((128, width), low), pltpu.VMEM((heads, width), low),
        pltpu.VMEM((span // 2, width), full), pltpu.VMEM((span // 2, width), full), pltpu.VMEM((span // 2, width), low),
        pltpu.VMEM((dp_size, piece, hidden), low), pltpu.VMEM((others, piece, wide), low),
        pltpu.VMEM((others, piece, heads), low),
        pltpu.VMEM((piece, 2 * span), low), pltpu.VMEM((2 * span, 1), jnp.int32), pltpu.VMEM((2 * span, span // 2), full),
        pltpu.VMEM((2 * span, 128), full), pltpu.VMEM((span, 128), full),
        pltpu.VMEM((8, width), full), pltpu.VMEM((2, 8, width), full), pltpu.VMEM((8, width), full),
        pltpu.VMEM((2 * dp_size - 1, 8, piece), full),
        dma((17,)), dma((core_copies,)), dma((core_copies,)),
        dma((dp_size,)), dma((dp_size,)), dma((2, others)), dma((2, others)),
        dma((2, line_size - 1)), dma((2,)), dma((2 * dp_size - 1,)), dma((2 * dp_size - 1,)),
        *line_scratch(span, width, 2, BACK_CHUNK), *line_scratch(span, width, 1, BACK_CHUNK),
    ]
    spaces = [outside, outside, vmem, outside, vmem, vmem, vmem] + [outside] * 10 + [vmem, vmem] + [outside] * 4
    return pl.pallas_call(
        functools.partial(back_kernel, line_size, dp_size),
        out_shape=[jax.ShapeDtypeStruct(s, d) for s, d in outs],
        in_specs=spaces,
        out_specs=[vmem] * 7 + [outside] * 4,
        scratch_shapes=scratch,
        compiler_params=pltpu.CompilerParams(
            collective_id=2, has_side_effects=True, vmem_limit_bytes=BACK_MIB * MIB
        ),
    )(*operands)


def settle_kernel(
    layer_any, inputs_any, gains, qkv_any, out_any, gate_any, up_any, down_any,
    land_gate, land_up, land_up_last, land_down, land_qkv, land_out,
    layer_out, grad_inputs, gain_one, grad_query, grad_key, grad_value, grad_out, gain_two, grad_gate, grad_up, grad_down,
    own_qkv, own_out, own_gate, own_up, own_down, far_qkv, far_out, far_gate, far_up, far_down,
    turned_kv, turned_out, turned_down, layer_held, inputs_held, in_sems, out_sems,
):
    whole, early = [], land_up.shape[0]
    passed = [
        pltpu.make_async_copy(layer_any, layer_held, in_sems.at[0, 5]),
        pltpu.make_async_copy(inputs_any, inputs_held, in_sems.at[1, 5]),
        pltpu.make_async_copy(land_up_last, far_up.at[pl.ds(early, 1)], in_sems.at[0, 6]),
    ]
    owns = ((qkv_any, own_qkv), (out_any, own_out), (gate_any, own_gate), (up_any, own_up), (down_any, own_down))
    fars = (
        (land_qkv, far_qkv), (land_out, far_out), (land_gate, far_gate), (land_up, far_up.at[pl.ds(0, early)]),
        (land_down, far_down),
    )
    loads = [
        (
            pltpu.make_async_copy(*own, in_sems.at[0, at]),
            pltpu.make_async_copy(*far, in_sems.at[1, at]),
        )
        for at, (own, far) in enumerate(zip(owns, fars))
    ]
    for pair in loads:
        for made in pair:
            made.start()
    for made in passed:
        made.start()
    gain_one[...] = gains[0:1]
    gain_two[...] = gains[1:2]

    def settle(at, own, far):
        for made in loads[at]:
            made.wait()
        total = own[...]
        for r in range(far.shape[0]):
            total = total + far[r].astype(jnp.float32)
        return total

    def put(at, src, dst):
        made = pltpu.make_async_copy(src, dst, out_sems.at[at])
        made.start()
        whole.append(made)

    heads = grad_query.shape[1]
    own_qkv[...] = settle(0, own_qkv, far_qkv)
    put(2, own_qkv.at[:, pl.ds(0, heads)], grad_query)
    turned_kv[...] = own_qkv[:, heads:].T
    put(3, turned_kv.at[pl.ds(0, HEAD_DIM)], grad_key)
    put(4, turned_kv.at[pl.ds(HEAD_DIM, HEAD_DIM)], grad_value)
    turned_out[...] = settle(1, own_out, far_out).T
    put(5, turned_out, grad_out)
    passed[0].wait()
    put(0, layer_held, layer_out)
    own_gate[...] = settle(2, own_gate, far_gate)
    put(6, own_gate, grad_gate)
    passed[2].wait()
    own_up[...] = settle(3, own_up, far_up)
    put(7, own_up, grad_up)
    passed[1].wait()
    put(1, inputs_held, grad_inputs)
    turned_down[...] = settle(4, own_down, far_down).T
    put(8, turned_down, grad_down)
    for made in whole:
        made.wait()


def settle_call(operands):
    layer_out, _, gains, qkv, out, gate = operands[:6]
    piece, wide = qkv.shape
    heads, hidden = out.shape[1], gate.shape[1]
    others = operands[8].shape[0]
    low, full = jnp.bfloat16, jnp.float32
    vmem, outside = pl.BlockSpec(memory_space=pltpu.VMEM), pl.BlockSpec(memory_space=pl.ANY)
    outs = [
        (layer_out.shape, low), (layer_out.shape, low), ((1, piece), full), ((piece, heads), full),
        ((HEAD_DIM, piece), full), ((HEAD_DIM, piece), full), ((heads, piece), full), ((1, piece), full),
        ((piece, hidden), full), ((piece, hidden), full), ((hidden, piece), full),
    ]
    shapes = [(piece, wide), (piece, heads), *[(piece, hidden)] * 3]
    scratch = [
        *[pltpu.VMEM(shape, full) for shape in shapes], *[pltpu.VMEM((others, *shape), low) for shape in shapes],
        pltpu.VMEM((wide - heads, piece), full), pltpu.VMEM((heads, piece), full), pltpu.VMEM((hidden, piece), full),
        pltpu.VMEM(layer_out.shape, low), pltpu.VMEM(layer_out.shape, low),
        pltpu.SemaphoreType.DMA((2, 7)), pltpu.SemaphoreType.DMA((9,)),
    ]
    return pl.pallas_call(
        settle_kernel,
        out_shape=[jax.ShapeDtypeStruct(s, d) for s, d in outs],
        in_specs=[outside, outside, vmem] + [outside] * 11,
        out_specs=[outside, outside, vmem] + [outside] * 4 + [vmem] + [outside] * 3,
        scratch_shapes=scratch,
        compiler_params=pltpu.CompilerParams(vmem_limit_bytes=62 * MIB),
    )(*operands)


def plain_body(
    inputs,
    segment_ids,
    attention_gain,
    query_weight,
    key_weight,
    value_weight,
    out_weight,
    feedforward_gain,
    gate_weight,
    up_weight,
    down_weight,
    cotangent,
):
    seq_count, span_len, model_width = inputs.shape
    row_count = seq_count * span_len
    query_heads = query_weight.shape[1] // HEAD_DIM
    kv_heads = key_weight.shape[1] // HEAD_DIM
    group_size = query_heads // kv_heads
    score_scale = 1.0 / math.sqrt(HEAD_DIM)
    offset = lax.axis_index("ctx") * span_len
    whole_segments = lax.all_gather(segment_ids, "ctx", axis=1, tiled=True)
    own_positions = lax.dynamic_slice_in_dim(positions_of(whole_segments), offset, span_len, 1)
    cosine, sine_table = rotary_tables(own_positions)
    cosine = cosine[:, :, None, :]
    sine_table = sine_table[:, :, None, :]
    hidden = inputs.astype(jnp.float32).reshape(row_count, model_width)
    inverse_one = lax.rsqrt(jnp.mean(hidden * hidden, axis=-1, keepdims=True) + epsilon)
    unit_one = hidden * inverse_one
    normed = (unit_one * attention_gain).astype(jnp.bfloat16)
    query_rows = rotate(
        jnp.dot(normed, query_weight, preferred_element_type=jnp.float32).reshape(
            seq_count, span_len, query_heads, HEAD_DIM
        ),
        cosine,
        sine_table,
    ).astype(jnp.bfloat16)
    key_rows = rotate(
        jnp.dot(normed, key_weight, preferred_element_type=jnp.float32).reshape(
            seq_count, span_len, kv_heads, HEAD_DIM
        ),
        cosine,
        sine_table,
    ).astype(jnp.bfloat16)
    value_rows = (
        jnp.dot(normed, value_weight, preferred_element_type=jnp.float32)
        .astype(jnp.bfloat16)
        .reshape(seq_count, span_len, kv_heads, HEAD_DIM)
    )
    all_keys, all_values = (
        lax.all_gather(key_rows, "ctx", axis=1, tiled=True),
        lax.all_gather(value_rows, "ctx", axis=1, tiled=True),
    )

    def attend(block_items):
        query_block, key_block, value_block, query_seg, key_seg = block_items
        allowed = visible(query_seg, key_seg, offset)
        grouped = query_block.reshape(span_len, kv_heads, group_size, HEAD_DIM)
        raw_scores = jnp.einsum(
            "qhgd,khd->hgqk", grouped, key_block, preferred_element_type=jnp.float32
        )
        scores = jnp.where(allowed, raw_scores * score_scale, masked_score)
        row_peak = jnp.max(scores, axis=-1, keepdims=True)
        shifted_exp = jnp.exp(scores - row_peak)
        denominator = jnp.sum(shifted_exp, axis=-1, keepdims=True)
        attn_probs = (shifted_exp / denominator).astype(jnp.bfloat16)
        mixed_block = jnp.einsum(
            "hgqk,khd->qhgd", attn_probs, value_block, preferred_element_type=jnp.float32
        )
        return (
            mixed_block.astype(jnp.bfloat16).reshape(span_len, query_heads * HEAD_DIM),
            row_peak + jnp.log(denominator),
        )

    mixed_heads, log_sums = lax.map(
        attend, (query_rows, all_keys, all_values, segment_ids, whole_segments)
    )
    mixed_flat = mixed_heads.reshape(row_count, query_heads * HEAD_DIM)
    attended = lax.psum(
        jnp.dot(mixed_flat, out_weight, preferred_element_type=jnp.float32), "tensor"
    )
    middle = hidden + attended
    inverse_two = lax.rsqrt(jnp.mean(middle * middle, axis=-1, keepdims=True) + epsilon)
    unit_two = middle * inverse_two
    normed_two = (unit_two * feedforward_gain).astype(jnp.bfloat16)
    gate_pre = jnp.dot(normed_two, gate_weight, preferred_element_type=jnp.float32)
    up_pre = jnp.dot(normed_two, up_weight, preferred_element_type=jnp.float32)
    sigmoid_gate = jax.nn.sigmoid(gate_pre)
    inner_act = (gate_pre * sigmoid_gate * up_pre).astype(jnp.bfloat16)
    feed_out = lax.psum(
        jnp.dot(inner_act, down_weight, preferred_element_type=jnp.float32).astype(jnp.bfloat16),
        "tensor",
    ).astype(jnp.float32)
    layer_out = (middle + feed_out).astype(jnp.bfloat16).reshape(seq_count, span_len, model_width)
    upstream = cotangent.reshape(row_count, model_width)
    grad_down = jnp.dot(inner_act.T, upstream, preferred_element_type=jnp.float32)
    grad_inner = jnp.dot(upstream, down_weight.T, preferred_element_type=jnp.float32)
    grad_up_pre = (grad_inner * gate_pre * sigmoid_gate).astype(jnp.bfloat16)
    grad_gate_pre = (
        grad_inner * up_pre * sigmoid_gate * (1.0 + gate_pre * (1.0 - sigmoid_gate))
    ).astype(jnp.bfloat16)
    grad_gate = jnp.dot(normed_two.T, grad_gate_pre, preferred_element_type=jnp.float32)
    grad_up = jnp.dot(normed_two.T, grad_up_pre, preferred_element_type=jnp.float32)
    grad_normed_two = lax.psum(
        jnp.dot(grad_gate_pre, gate_weight.T, preferred_element_type=jnp.float32)
        + jnp.dot(grad_up_pre, up_weight.T, preferred_element_type=jnp.float32),
        "tensor",
    )
    grad_ffn_gain = jnp.sum(grad_normed_two * unit_two, axis=0)
    scaled_two = grad_normed_two * feedforward_gain
    grad_middle = upstream.astype(jnp.float32) + inverse_two * (
        scaled_two - unit_two * jnp.mean(scaled_two * unit_two, axis=-1, keepdims=True)
    )
    grad_attended = grad_middle.astype(jnp.bfloat16)
    grad_out_part = jnp.dot(mixed_flat.T, grad_attended, preferred_element_type=jnp.float32)
    grad_mixed = (
        jnp.dot(grad_attended, out_weight.T, preferred_element_type=jnp.float32)
        .astype(jnp.bfloat16)
        .reshape(seq_count, span_len, query_heads, HEAD_DIM)
    )

    def attend_back(block_items):
        query_block, key_block, value_block, query_seg, key_seg, grad_block, log_block = block_items
        allowed = visible(query_seg, key_seg, offset)
        grouped = query_block.reshape(span_len, kv_heads, group_size, HEAD_DIM)
        grad_grouped = grad_block.reshape(span_len, kv_heads, group_size, HEAD_DIM)
        raw_scores = jnp.einsum(
            "qhgd,khd->hgqk", grouped, key_block, preferred_element_type=jnp.float32
        )
        scores = jnp.where(allowed, raw_scores * score_scale, masked_score)
        attn_probs = jnp.exp(scores - log_block)
        rounded = attn_probs.astype(jnp.bfloat16)
        grad_values = jnp.einsum(
            "hgqk,qhgd->khd", rounded, grad_grouped, preferred_element_type=jnp.float32
        )
        grad_probs = jnp.einsum(
            "qhgd,khd->hgqk", grad_grouped, value_block, preferred_element_type=jnp.float32
        )
        row_dot = jnp.sum(attn_probs * grad_probs, axis=-1, keepdims=True)
        grad_scores = (attn_probs * (grad_probs - row_dot) * score_scale).astype(jnp.bfloat16)
        grad_queries = jnp.einsum(
            "hgqk,khd->qhgd", grad_scores, key_block, preferred_element_type=jnp.float32
        ).reshape(span_len, query_heads, HEAD_DIM)
        grad_keys = jnp.einsum(
            "hgqk,qhgd->khd", grad_scores, grouped, preferred_element_type=jnp.float32
        )
        return (grad_queries, grad_keys, grad_values)

    grad_queries, grad_keys, grad_values = lax.map(
        attend_back,
        (query_rows, all_keys, all_values, segment_ids, whole_segments, grad_mixed, log_sums),
    )
    own_grad_keys, own_grad_values = (
        lax.psum_scatter(grad_keys, "ctx", scatter_dimension=1, tiled=True),
        lax.psum_scatter(grad_values, "ctx", scatter_dimension=1, tiled=True),
    )
    grad_query_pre = (
        rotate(grad_queries, cosine, -sine_table)
        .astype(jnp.bfloat16)
        .reshape(row_count, query_heads * HEAD_DIM)
    )
    grad_key_pre = (
        rotate(own_grad_keys, cosine, -sine_table)
        .astype(jnp.bfloat16)
        .reshape(row_count, kv_heads * HEAD_DIM)
    )
    grad_value_pre = own_grad_values.astype(jnp.bfloat16).reshape(row_count, kv_heads * HEAD_DIM)
    grad_query = jnp.dot(normed.T, grad_query_pre, preferred_element_type=jnp.float32)
    grad_key = jnp.dot(normed.T, grad_key_pre, preferred_element_type=jnp.float32)
    grad_value = jnp.dot(normed.T, grad_value_pre, preferred_element_type=jnp.float32)
    grad_normed = lax.psum(
        (
            jnp.dot(grad_query_pre, query_weight.T, preferred_element_type=jnp.float32)
            + jnp.dot(grad_key_pre, key_weight.T, preferred_element_type=jnp.float32)
            + jnp.dot(grad_value_pre, value_weight.T, preferred_element_type=jnp.float32)
        ).astype(jnp.bfloat16),
        "tensor",
    ).astype(jnp.float32)
    grad_attn_gain = jnp.sum(grad_normed * unit_one, axis=0)
    scaled_one = grad_normed * attention_gain
    grad_hidden = grad_middle + inverse_one * (
        scaled_one - unit_one * jnp.mean(scaled_one * unit_one, axis=-1, keepdims=True)
    )
    grad_inputs = grad_hidden.astype(jnp.bfloat16).reshape(seq_count, span_len, model_width)
    reduced = (
        lax.psum_scatter(
            grad_attn_gain.astype(jnp.bfloat16), ("dp", "ctx"), scatter_dimension=0, tiled=True
        ).astype(jnp.float32),
        lax.psum_scatter(
            grad_query.astype(jnp.bfloat16), ("dp", "ctx"), scatter_dimension=0, tiled=True
        ).astype(jnp.float32),
        lax.psum_scatter(
            grad_key.astype(jnp.bfloat16), ("dp", "ctx"), scatter_dimension=0, tiled=True
        ).astype(jnp.float32),
        lax.psum_scatter(
            grad_value.astype(jnp.bfloat16), ("dp", "ctx"), scatter_dimension=0, tiled=True
        ).astype(jnp.float32),
        lax.psum_scatter(
            grad_out_part.astype(jnp.bfloat16), ("dp", "ctx"), scatter_dimension=1, tiled=True
        ).astype(jnp.float32),
        lax.psum_scatter(
            grad_ffn_gain.astype(jnp.bfloat16), ("dp", "ctx"), scatter_dimension=0, tiled=True
        ).astype(jnp.float32),
        lax.psum_scatter(
            grad_gate.astype(jnp.bfloat16), ("dp", "ctx"), scatter_dimension=0, tiled=True
        ).astype(jnp.float32),
        lax.psum_scatter(
            grad_up.astype(jnp.bfloat16), ("dp", "ctx"), scatter_dimension=0, tiled=True
        ).astype(jnp.float32),
        lax.psum_scatter(
            grad_down.astype(jnp.bfloat16), ("dp", "ctx"), scatter_dimension=1, tiled=True
        ).astype(jnp.float32),
    )
    return (
        layer_out,
        grad_inputs,
        reduced[0],
        reduced[1],
        reduced[2],
        reduced[3],
        reduced[4],
        reduced[5],
        reduced[6],
        reduced[7],
        reduced[8],
    )


def fast_body(
    inputs, segment_ids, attention_gain, query_weight, key_weight, value_weight, out_weight, feedforward_gain,
    gate_weight, up_weight, down_weight, cotangent,
):
    _, span_len, model_width = inputs.shape
    line_size, dp_size = lax.axis_size("tensor"), lax.axis_size("dp")
    half_dim = HEAD_DIM // 2
    frequency = rope_base ** (-2.0 * jnp.arange(half_dim, dtype=jnp.float32) / HEAD_DIM)
    frequency = jnp.tile(frequency, 4).reshape(1, 128)
    flat_inputs = inputs.reshape(span_len, model_width)
    upstream = cotangent.reshape(span_len, model_width)
    gain_one, gain_two = attention_gain.reshape(1, -1), feedforward_gain.reshape(1, -1)
    key_turned, value_turned = key_weight.T, value_weight.T
    (
        seg_row, cosine, signed_sine, query, kv, logs, mixed, normed, two, upstream_cols, up, inner, second, attended,
        middle, grad_middle, land_gate, land_up, own_gate, gain_grad,
    ) = front_call(
        line_size, dp_size,
        (
            flat_inputs, segment_ids, frequency, gain_one, gain_two, query_weight, key_turned, value_turned, out_weight,
            gate_weight, up_weight, down_weight, upstream,
        ),
    )
    (
        layer_out, grad_inputs, gains, own_qkv, own_out, own_up, own_down, land_up_last, land_down, land_qkv,
        land_out,
    ) = back_call(
        line_size, dp_size,
        (
            query, kv, logs, mixed, cosine, signed_sine, seg_row, flat_inputs, normed, two, upstream_cols,
            up, inner, second, attended, middle, grad_middle, gain_one, gain_grad,
            query_weight, key_turned, value_turned, out_weight,
        ),
    )
    layer_out, grad_inputs, gain_a, grad_query, grad_key, grad_value, grad_out, gain_b, *ffn = settle_call(
        (
            layer_out, grad_inputs, gains, own_qkv, own_out, own_gate, own_up, own_down,
            land_gate, land_up, land_up_last, land_down, land_qkv, land_out,
        )
    )
    shape = (1, span_len, model_width)
    return (
        layer_out.reshape(shape), grad_inputs.reshape(shape), gain_a[0], grad_query, grad_key.T, grad_value.T,
        grad_out, gain_b[0], *ffn,
    )


def body(mesh, *arrays):
    inputs = arrays[0]
    span_len, model_width = inputs.shape[1:]
    dp_size, ctx_size, line_size = mesh.shape["dp"], mesh.shape["ctx"], mesh.shape["tensor"]
    piece = model_width // (dp_size * ctx_size)
    fits = inputs.shape[0] == 1 and ctx_size == 2 and dp_size > 2 and line_size > 1
    if fits and piece % 128 == 0 and span_len % 512 == 0:
        return fast_body(*arrays)
    return plain_body(*arrays)


def solution(mesh):
    return jax.shard_map(
        functools.partial(body, mesh),
        mesh=mesh,
        in_specs=(
            P("dp", "ctx", None),
            P("dp", "ctx"),
            P(),
            P(None, "tensor"),
            P(None, "tensor"),
            P(None, "tensor"),
            P("tensor", None),
            P(),
            P(None, "tensor"),
            P(None, "tensor"),
            P("tensor", None),
            P("dp", "ctx", None),
        ),
        out_specs=(
            P("dp", "ctx", None),
            P("dp", "ctx", None),
            P(("dp", "ctx")),
            P(("dp", "ctx"), "tensor"),
            P(("dp", "ctx"), "tensor"),
            P(("dp", "ctx"), "tensor"),
            P("tensor", ("dp", "ctx")),
            P(("dp", "ctx")),
            P(("dp", "ctx"), "tensor"),
            P(("dp", "ctx"), "tensor"),
            P("tensor", ("dp", "ctx")),
        ),
        check_vma=False,
    )
```
